256 devices in a mesh: section: 2 (over core), req: 32 (over z, x), head: 4 (over y).
Axes of the slice: x: 4, y: 4, z: 8, core: 2. Of those that a mesh axis runs over, the one named last changes fastest.
Arguments:
- tokens: bfloat16 [256, 1792], P('req', 'head'), may hold values from -6 to 6
- norm_gain: float32 [2, 1792], P('section'), may hold values from 0.1 to 1.9
- feature_w: bfloat16 [1792, 512], P(None, 'head'), may hold values from -0.125 to 0.125
- query_key_w: bfloat16 [1792, 3584], P(None, 'head'), may hold values from -0.125 to 0.125
- value_w: bfloat16 [2, 1792, 1792], P('section', None, 'head'), may hold values from -0.125 to 0.125
- out_w: bfloat16 [2, 1792, 1792], P('section', 'head'), may hold values from -0.125 to 0.125
- conv_w: float32 [3, 1792], P(None, 'head'), may hold values from -4 to 4
- conv_state: bfloat16 [256, 2, 1792], P('req', None, 'head'), may hold values from -6 to 6
- lin_state: bfloat16 [256, 16, 273, 112], P('req', 'head'), may hold values from -6 to 6
- lin_norm: float32 [256, 16, 273], P('req', 'head'), may hold values from -6 to 6, as said below
- own_pages: bfloat16 [512, 2, 128, 1792], P('req', None, None, 'head'), may hold values from -110 to 110
- prompt_pages: bfloat16 [32, 2, 128, 1792], P('req', None, None, 'head'), may hold values from -110 to 110
- page_table: int32 [256, 256], P('req'), may hold values from 0 to 543, as said below
- lengths: int32 [256], P('req'), may hold values from 129 to 32768, as said below
Outputs:
- hidden_states: bfloat16 [2, 256, 1792], P('section', 'req', 'head')
The draws below stay inside these ranges and needn't reach their ends.
Inputs may be any that keep to these rules, and one draw needn't show every extreme that they name: `page_table`: entry 0 of a request's row is its prompt group, whose page is prompt_pages row (entry 0). Entries of logical pages 1 and above are 32 plus a row of own_pages within the block of 16 rows that matches the request's block of 8 rows; two consecutive logical pages of a request are different pages. `lengths`: the new token sits at position length - 1; positions below 128 are the group's prompt. Some request has length 32768. `lin_norm`: the inner product with the feature vector phi(u) of any 16-vector u is at least one half.
All inputs are finite; a program needn't handle non-finite values.
Results may differ from the reference program's by a relative error of at most 0.024.
Values may be sent and summed in bfloat16 or wider, within the bound.
No kernel may reach another device: no remote copies, remote signals or barrier semaphores. Data moves between devices by JAX's collectives and lax.ppermute only.
A program may use at most 128 MiB of HBM per device.

```python
from functools import partial
import jax
import jax.numpy as jnp
from jax import lax

D = 1792
H = 16
HD = 112
FEAT = 16
KERNEL = 3
WINDOW = 64
PAGE = 128
MAXLEN = 32768
REQ_DEV = 8
TAYLOR = 273
REQS = 256
GROUPS = 32
OWN = 512
MAXP = 256


def taylor_draw(raw_feats):
    scaled = raw_feats * FEAT ** (-0.25)
    outer = scaled[..., :, None] * scaled[..., None, :]
    flat = outer.reshape(scaled.shape[:-1] + (FEAT * FEAT,)) * 0.5 ** 0.5
    constant = jnp.ones(scaled.shape[:-1] + (1,), jnp.float32)
    return jnp.concatenate([constant, scaled, flat], axis=-1)


def draw_lin_norm(key, part):
    local_key = jax.random.fold_in(key, 11)
    pseudo = jnp.clip(jax.random.normal(local_key, (8, REQS, H, FEAT), jnp.float32), -2.0, 2.0)
    summed = taylor_draw(pseudo[0])
    for member in range(1, 8):
        summed = summed + taylor_draw(pseudo[member])
    return summed * 0.125


def page_draw(key, page_count):
    shape = (page_count, 2, PAGE, H * HD)
    base = jnp.clip(jax.random.normal(key, shape, jnp.float32), -6.0, 6.0)
    return base.astype(jnp.bfloat16)


def draw_own_pages(key, part):
    return page_draw(jax.random.fold_in(key, 21), OWN)


def draw_prompt_pages(key, part):
    return page_draw(jax.random.fold_in(key, 31), GROUPS)


def draw_page_table(key, part):
    subkeys = jax.random.split(jax.random.fold_in(key, 41), 3)
    first_pick = jax.random.randint(subkeys[0], (REQS,), 0, GROUPS)
    second_pick = jax.random.randint(subkeys[1], (REQS,), 0, GROUPS)
    group_ids = jnp.minimum(first_pick, second_pick)
    flips = jax.random.randint(subkeys[2], (REQS,), 0, 2)
    requests = jnp.arange(REQS, dtype=jnp.int32)
    devices = requests // REQ_DEV
    within = requests % REQ_DEV
    logical = jnp.arange(MAXP, dtype=jnp.int32)
    slots = (logical[None, :] + flips[:, None]) % 2
    own_ids = GROUPS + devices[:, None] * (2 * REQ_DEV) + 2 * within[:, None] + slots
    return jnp.where(logical[None, :] == 0, group_ids[:, None], own_ids).astype(jnp.int32)


def draw_lengths(key, part):
    subkeys = jax.random.split(jax.random.fold_in(key, 51), 4)
    near = jax.random.randint(subkeys[0], (REQS,), PAGE + 1, PAGE + WINDOW)
    far = jax.random.randint(subkeys[1], (REQS,), PAGE + WINDOW, MAXLEN + 1)
    which = jax.random.randint(subkeys[2], (REQS,), 0, 2)
    picked = jnp.where(which == 1, far, near)
    longest = jax.random.randint(subkeys[3], (), 0, REQS)
    return jnp.where(jnp.arange(REQS) == longest, MAXLEN, picked).astype(jnp.int32)


def levels(rng, extent, pieces, low, top_value):
    factor_of, own = 1.0, jax.random.fold_in(rng, 6)
    for axis_at, shards_of in pieces:
        heights = jnp.exp(jax.random.uniform(jax.random.fold_in(own, axis_at), (shards_of,), jnp.float32, low / len(pieces), top_value / len(pieces)))
        factor_of = factor_of * jnp.repeat(heights, extent[axis_at] // shards_of).reshape([-1 if axis == axis_at else 1 for axis in range(len(extent))])
    return factor_of


def bell_draw(own_key, dims, spread, bound, cuts=(), kind=jnp.bfloat16):
    drawn = jax.random.normal(own_key, dims, jnp.float32) * spread
    if len(cuts) > 0:
        drawn = levels(own_key, dims, cuts, -0.22, 0.18) * drawn
    return jnp.clip(drawn, min=-bound, max=bound).astype(kind)


def setup_inputs(seed: int = 0) -> dict:
    seeds = jax.random.split(jax.random.key(seed), 15)
    return {
        "tokens": bell_draw(seeds[0], (REQS, D), 1.0, 6.0, ((0, 32), (1, 4))),
        "norm_gain": jnp.clip(1.0 + 0.18 * jax.random.normal(seeds[1], (2, D), jnp.float32), 0.1, 1.9),
        "feature_w": bell_draw(seeds[2], (D, H * 2 * FEAT), D ** -0.5, 0.125, ((1, 4),)),
        "query_key_w": bell_draw(seeds[3], (D, H * 2 * HD), D ** -0.5, 0.125, ((1, 4),)),
        "value_w": bell_draw(seeds[4], (2, D, H * HD), D ** -0.5, 0.125, ((0, 2), (2, 4))),
        "out_w": bell_draw(seeds[5], (2, H * HD, D), (H * HD) ** -0.5, 0.125, ((0, 2), (1, 4))),
        "conv_w": bell_draw(seeds[6], (KERNEL, H * HD), 0.6, 4.0, ((1, 4),), jnp.float32),
        "conv_state": bell_draw(seeds[7], (REQS, KERNEL - 1, H * HD), 1.0, 6.0, ((0, 32), (2, 4))),
        "lin_state": bell_draw(seeds[8], (REQS, H, TAYLOR, HD), 0.4, 6.0, ((0, 32), (1, 4))),
        "lin_norm": draw_lin_norm(jax.random.fold_in(seeds[14], 71), 0),
        "own_pages": draw_own_pages(jax.random.fold_in(seeds[14], 71), 0),
        "prompt_pages": draw_prompt_pages(jax.random.fold_in(seeds[14], 71), 0),
        "page_table": draw_page_table(jax.random.fold_in(seeds[14], 71), 0),
        "lengths": draw_lengths(jax.random.fold_in(seeds[14], 71), 0),
    }


EPSILON = 1e-06
MASKED = -1e+30

def rms_norm(token_rows, gain_row):
    values = token_rows.astype(jnp.float32)
    factor = lax.rsqrt(lax.optimization_barrier(jnp.mean(values * values, axis=-1, keepdims=True)) + EPSILON)
    return (values * factor * gain_row.astype(jnp.float32)).astype(jnp.bfloat16)

def taylor(raw_feats):
    scaled = raw_feats * FEAT ** (-0.25)
    outer = scaled[..., :, None] * scaled[..., None, :]
    flat = outer.reshape(scaled.shape[:-1] + (FEAT * FEAT,)) * 0.5 ** 0.5
    constant = jnp.ones(scaled.shape[:-1] + (1,), jnp.float32)
    return jnp.concatenate([constant, scaled, flat], axis=-1)

def linear_layer(tokens, gain_row, feature_w, value_w, out_w, conv_w, conv_state, lin_state, lin_norm):
    normed = rms_norm(tokens, gain_row)
    features = jnp.dot(normed, feature_w, preferred_element_type=jnp.float32).reshape(REQS, H, 2, FEAT)
    query_feats = taylor(features[:, :, 0])
    key_feats = taylor(features[:, :, 1])
    fresh_values = jnp.dot(normed, value_w, preferred_element_type=jnp.float32)
    older_values = conv_state.astype(jnp.float32)
    mixed_values = conv_w[0] * older_values[:, 0] + conv_w[1] * older_values[:, 1] + conv_w[2] * fresh_values
    mixed_values = mixed_values.reshape(REQS, H, HD)
    query_low = query_feats.astype(jnp.bfloat16)
    from_state = jnp.einsum('rhf,rhfd->rhd', query_low.astype(jnp.float32), lin_state.astype(jnp.float32))
    intersection = lax.optimization_barrier(jnp.sum(query_feats * key_feats, axis=-1))
    denominator = lax.optimization_barrier(jnp.sum(query_feats * lin_norm, axis=-1)) + intersection
    attended = ((from_state + intersection[..., None] * mixed_values) / denominator[..., None]).astype(jnp.bfloat16)
    update = jnp.dot(attended.reshape(REQS, H * HD), out_w, preferred_element_type=jnp.float32)
    return (tokens.astype(jnp.float32) + update).astype(jnp.bfloat16)

def window_one(inputs, own_pages, prompt_pages):
    query_row, key_new, value_new, table_row, length = inputs
    window_start = length - WINDOW
    first_page = jnp.maximum(window_start // PAGE, 1)
    last_page = jnp.maximum((length - 2) // PAGE, 1)
    page_picks = jnp.stack([first_page, last_page]).astype(jnp.int32)
    own_rows = own_pages[(table_row[page_picks] - GROUPS).astype(jnp.int32)]
    prompt = prompt_pages[table_row[0]]
    key_rows = jnp.concatenate([prompt[0], own_rows[0, 0], own_rows[1, 0]], axis=0).reshape(3 * PAGE, H, HD)
    values = jnp.concatenate([prompt[1], own_rows[0, 1], own_rows[1, 1]], axis=0).reshape(3 * PAGE, H, HD)
    offsets = jnp.arange(PAGE, dtype=jnp.int32)
    prompt_usable = offsets >= window_start
    own_positions = (page_picks[:, None] * PAGE + offsets[None, :]).reshape(2 * PAGE)
    second = jnp.concatenate([jnp.ones((PAGE,), bool), jnp.full((PAGE,), last_page != first_page)])
    own_usable = (own_positions >= window_start) & (own_positions <= length - 2) & second
    usable = jnp.concatenate([prompt_usable, own_usable])
    score_scale = HD ** (-0.5)
    scores = jnp.einsum('hd,thd->ht', query_row.astype(jnp.float32), key_rows.astype(jnp.float32)) * score_scale
    new_score = lax.optimization_barrier(jnp.sum(query_row.astype(jnp.float32) * key_new.astype(jnp.float32), axis=-1)) * score_scale
    scores = jnp.where(usable[None, :], scores, MASKED)
    highest = jnp.maximum(lax.optimization_barrier(jnp.max(scores, axis=-1)), new_score)
    exp_scores = jnp.exp(scores - highest[:, None])
    exp_new = jnp.exp(new_score - highest)
    exp_total = lax.optimization_barrier(jnp.sum(exp_scores, axis=-1)) + exp_new
    weights = (exp_scores / exp_total[:, None]).astype(jnp.bfloat16)
    weight_new = (exp_new / exp_total).astype(jnp.bfloat16)
    summed = jnp.einsum('ht,thd->hd', weights.astype(jnp.float32), values.astype(jnp.float32))
    summed = summed + weight_new.astype(jnp.float32)[:, None] * value_new.astype(jnp.float32)
    return summed.astype(jnp.bfloat16)

def window_layer(hidden, gain_row, query_key_w, value_w, out_w, own_pages, prompt_pages, page_table, lengths):
    normed = rms_norm(hidden, gain_row)
    query_key = jnp.dot(normed, query_key_w, preferred_element_type=jnp.float32).reshape(REQS, H, 2, HD).astype(jnp.bfloat16)
    value_new = jnp.dot(normed, value_w, preferred_element_type=jnp.float32).reshape(REQS, H, HD).astype(jnp.bfloat16)
    attended = lax.map(partial(window_one, own_pages=own_pages, prompt_pages=prompt_pages), (query_key[:, :, 0], query_key[:, :, 1], value_new, page_table, lengths))
    update = jnp.dot(attended.reshape(REQS, H * HD), out_w, preferred_element_type=jnp.float32)
    return (hidden.astype(jnp.float32) + update).astype(jnp.bfloat16)

def reference(tokens, norm_gain, feature_w, query_key_w, value_w, out_w, conv_w, conv_state, lin_state, lin_norm, own_pages, prompt_pages, page_table, lengths):
    layer_one = linear_layer(tokens, norm_gain[0], feature_w, value_w[0], out_w[0], conv_w, conv_state, lin_state, lin_norm)
    layer_two = window_layer(layer_one, norm_gain[1], query_key_w, value_w[1], out_w[1], own_pages, prompt_pages, page_table, lengths)
    return jnp.stack([layer_one, layer_two])
```

```python
import jax
import jax.numpy as jnp
from jax import lax
from jax.sharding import PartitionSpec as P

HD = 112
FEAT = 16
WINDOW = 64
PAGE = 128
HALF = 64
XN = 4
ZN = 8
LANES = 512

EPSILON = 1e-06
MASKED = -1e30
Z_OFFSETS = (-1, 0, 1, 2, 3, 4, -3, -2)


def head_shift(value, steps):
    count = lax.axis_size("head")
    return lax.ppermute(value, "head", [(i, (i + steps) % count) for i in range(count)])


def x_shift(value, steps):
    return lax.ppermute(
        value,
        "req",
        [(z * XN + i, z * XN + (i + steps) % XN) for z in range(ZN) for i in range(XN)],
    )


def z_shift(value, steps):
    base = XN * ZN
    return lax.ppermute(
        value,
        ("section", "req"),
        [
            (base + z * XN + i, base + ((z + steps) % ZN) * XN + i)
            for z in range(ZN)
            for i in range(XN)
        ],
    )


def section_swap(value, steps):
    count = lax.axis_size("head")
    there = [(i, count + (i + steps) % count) for i in range(count)]
    return lax.ppermute(value, ("section", "head"), there + [(b, a) for a, b in there])


def rms_norm(token_rows, gain_row):
    values = token_rows.astype(jnp.float32)
    factor = lax.rsqrt(jnp.mean(values * values, axis=-1, keepdims=True) + EPSILON)
    return (values * factor * gain_row).astype(jnp.bfloat16)


def taylor(raw_feats):
    scaled = raw_feats * FEAT ** (-0.25)
    outer = scaled[..., :, None] * scaled[..., None, :]
    flat = outer.reshape(scaled.shape[:-1] + (FEAT * FEAT,)) * 0.5**0.5
    constant = jnp.ones(scaled.shape[:-1] + (1,), jnp.float32)
    return jnp.concatenate([constant, scaled, flat], axis=-1)


def linear_local(normed, feature_w, value_w, out_w, conv_w, conv_part, state_part, norm_part):
    batch_rows = normed.shape[0]
    heads = state_part.shape[1]
    features = jnp.dot(normed, feature_w, preferred_element_type=jnp.float32).reshape(
        batch_rows, heads, 2, FEAT
    )
    query_feats = taylor(features[:, :, 0])
    key_feats = taylor(features[:, :, 1])
    fresh_values = jnp.dot(normed, value_w, preferred_element_type=jnp.float32)
    older_values = conv_part.astype(jnp.float32)
    mixed_values = (
        conv_w[0] * older_values[:, 0] + conv_w[1] * older_values[:, 1] + conv_w[2] * fresh_values
    )
    mixed_values = mixed_values.reshape(batch_rows, heads, HD)
    from_state = jnp.einsum(
        "rhf,rhfd->rhd",
        query_feats.astype(jnp.bfloat16),
        state_part,
        preferred_element_type=jnp.float32,
    )
    intersection = jnp.sum(query_feats * key_feats, axis=-1)
    denominator = jnp.sum(query_feats * norm_part, axis=-1) + intersection
    attended = (
        (from_state + intersection[..., None] * mixed_values) / denominator[..., None]
    ).astype(jnp.bfloat16)
    return jnp.dot(
        attended.reshape(batch_rows, heads * HD), out_w, preferred_element_type=jnp.float32
    )


def gather_own(own_pages, page_table, lengths, groups, req_index):
    rows = lengths.shape[0]
    window_start = lengths - WINDOW
    halves = jnp.stack([window_start // HALF, (lengths - 2) // HALF], axis=1)
    pages = halves // 2
    own_ids = jnp.take_along_axis(page_table, pages, axis=1) - groups
    own_ids = jnp.clip(own_ids - req_index * own_pages.shape[0], 0, own_pages.shape[0] - 1)
    split = own_pages.reshape(own_pages.shape[0], 2, 2, HALF, own_pages.shape[-1])
    picked = split[own_ids, :, halves % 2]
    positions = (halves[:, :, None] * HALF + jnp.arange(HALF, dtype=jnp.int32)).reshape(
        rows, 2 * HALF
    )
    second = jnp.concatenate(
        [
            jnp.ones((rows, HALF), bool),
            jnp.broadcast_to((halves[:, 1] != halves[:, 0])[:, None], (rows, HALF)),
        ],
        axis=1,
    )
    usable = (
        (positions >= jnp.maximum(window_start, PAGE)[:, None])
        & (positions <= (lengths - 2)[:, None])
        & second
    )
    keys = picked[:, :, 0].reshape(rows, 2 * HALF, -1)
    values = picked[:, :, 1].reshape(rows, 2 * HALF, -1)
    return keys, values, usable


def project(layer_one, gain, query_key_w, value_w):
    rows = layer_one.shape[0]
    normed = rms_norm(layer_one, gain)
    query_key = jnp.dot(normed, query_key_w, preferred_element_type=jnp.float32).reshape(
        rows, -1, 2, HD
    )
    value_new = jnp.dot(normed, value_w, preferred_element_type=jnp.float32)
    return (
        query_key[:, :, 0].reshape(rows, -1).astype(jnp.bfloat16),
        query_key[:, :, 1].reshape(rows, -1).astype(jnp.bfloat16),
        value_new.astype(jnp.bfloat16),
    )


def prompt_local(queries, groups_of, starts, pages, slot_groups):
    rows = queries.shape[0]
    heads = queries.shape[1] // HD
    keys = pages[:, :HALF].reshape(ZN * HALF, heads, HD)
    values = pages[:, HALF:].reshape(ZN * HALF, heads, HD)
    scores = jnp.einsum(
        "rhd,thd->rht", queries.reshape(rows, heads, HD), keys, preferred_element_type=jnp.float32
    ) * HD ** (-0.5)
    offsets = jnp.arange(ZN * HALF, dtype=jnp.int32) % HALF + HALF
    usable = (groups_of[:, None] == jnp.repeat(slot_groups, HALF)[None]) & (
        offsets[None] >= starts[:, None]
    )
    scores = jnp.where(usable[:, None], scores, MASKED)
    highest = jnp.max(scores, axis=-1)
    exps = jnp.where(usable[:, None], jnp.exp(scores - highest[..., None]), 0.0)
    total = jnp.sum(exps, axis=-1)
    summed = jnp.einsum(
        "rht,thd->rhd", exps.astype(jnp.bfloat16), values, preferred_element_type=jnp.float32
    )
    pad = jnp.zeros((rows, LANES - heads * HD - 2 * heads), jnp.float32)
    return jnp.concatenate([summed.reshape(rows, heads * HD), highest, total, pad], axis=1)


def own_local(query, key_new, value_new, keys, values, usable):
    rows = query.shape[0]
    heads = query.shape[1] // HD
    query = query.reshape(rows, heads, HD)
    key_new = key_new.reshape(rows, heads, HD)
    value_new = value_new.reshape(rows, heads, HD)
    keys = keys.reshape(rows, 2 * HALF, heads, HD)
    values = values.reshape(rows, 2 * HALF, heads, HD)
    scale = HD ** (-0.5)
    scores = jnp.einsum("rhd,rthd->rht", query, keys, preferred_element_type=jnp.float32) * scale
    new_score = jnp.sum(query.astype(jnp.float32) * key_new.astype(jnp.float32), axis=-1) * scale
    scores = jnp.where(usable[:, None], scores, MASKED)
    highest = jnp.maximum(jnp.max(scores, axis=-1), new_score)
    exps = jnp.exp(scores - highest[..., None])
    exp_new = jnp.exp(new_score - highest)
    total = jnp.sum(exps, axis=-1) + exp_new
    summed = jnp.einsum(
        "rht,rthd->rhd", exps.astype(jnp.bfloat16), values, preferred_element_type=jnp.float32
    ) + exp_new.astype(jnp.bfloat16).astype(jnp.float32)[..., None] * value_new.astype(jnp.float32)
    return summed, highest, total


def combine(own_summed, own_highest, own_total, parts, out_w):
    rows, heads = own_highest.shape
    wide = heads * HD
    prompt_highest = parts[0][:, wide : wide + heads]
    merged = parts[0]
    for part in parts[1:]:
        prompt_highest = jnp.maximum(prompt_highest, part[:, wide : wide + heads])
        merged = merged + part
    prompt_total = merged[:, wide + heads : wide + 2 * heads]
    prompt_summed = merged[:, :wide].reshape(rows, heads, HD)
    highest = jnp.maximum(own_highest, prompt_highest)
    own_factor = jnp.exp(own_highest - highest)
    prompt_factor = jnp.exp(prompt_highest - highest)
    total = own_total * own_factor + prompt_total * prompt_factor
    attended = (
        own_summed * (own_factor / total)[..., None]
        + prompt_summed * (prompt_factor / total)[..., None]
    )
    attended = attended.astype(jnp.bfloat16).reshape(rows, wide)
    return jnp.dot(attended, out_w, preferred_element_type=jnp.float32)


def on_section(index, wanted, run, *operands):
    shapes = jax.eval_shape(run, *operands)

    def skip(*_):
        return jax.tree.map(lambda leaf: jnp.zeros(leaf.shape, leaf.dtype), shapes)

    return lax.cond(index == wanted, run, skip, *operands)


def body(
    tokens,
    norm_gain,
    feature_w,
    query_key_w,
    value_w,
    out_w,
    conv_w,
    conv_state,
    lin_state,
    lin_norm,
    own_pages,
    prompt_pages,
    page_table,
    lengths,
):
    section_index = lax.axis_index("section")
    req_index = lax.axis_index("req")
    head_index = lax.axis_index("head")
    groups = lax.axis_size("req")
    head_count = lax.axis_size("head")
    rows, share = tokens.shape
    gain = norm_gain[0]

    pieces = [tokens] + [head_shift(tokens, k) for k in (1, 3, 2)]
    order = jnp.stack([(head_index - k) % head_count for k in (0, 1, 3, 2)])
    whole = jnp.zeros((head_count, rows, share), tokens.dtype)
    for at, piece in enumerate(pieces):
        whole = lax.dynamic_update_slice(whole, piece[None], (order[at], 0, 0))
    whole = whole.transpose(1, 0, 2).reshape(rows, head_count * share)

    page = prompt_pages[0, :, HALF:, :].reshape(2 * HALF, share)
    trio = jnp.stack([z_shift(page, 1), page, z_shift(page, -1)])
    pages = jnp.concatenate([trio, z_shift(trio, -3), z_shift(trio[1:], 3)])
    slot_groups = (req_index // XN + jnp.array(Z_OFFSETS, jnp.int32)) % ZN * XN + req_index % XN
    own_keys, own_values, usable = on_section(
        section_index,
        1,
        lambda *a: gather_own(*a, groups, req_index),
        own_pages,
        page_table,
        lengths,
    )

    def run_linear(whole_rows):
        normed = rms_norm(whole_rows, gain)
        return linear_local(
            normed, feature_w, value_w[0], out_w[0], conv_w, conv_state, lin_state, lin_norm
        )

    update = on_section(section_index, 0, run_linear, whole)
    swapped = [section_swap(update, k) for k in (0, 1, 3, 2)]
    summed = whole.astype(jnp.float32)
    for piece in swapped:
        summed = summed + piece
    layer_one = summed.astype(jnp.bfloat16)
    one_share = lax.dynamic_slice(layer_one, (0, head_index * share), (rows, share))
    one_back = lax.ppermute(one_share, "section", [(1, 0)])

    query, key_new, value_new = on_section(
        section_index, 1, lambda a: project(a, gain, query_key_w, value_w[0]), layer_one
    )
    window_start = jnp.minimum(lengths - WINDOW, PAGE)
    tags = jnp.stack([page_table[:, 0], window_start], axis=1).astype(jnp.bfloat16)
    packed = jnp.concatenate(
        [query, tags, jnp.zeros((rows, LANES - share - 2), jnp.bfloat16)], axis=1
    )
    asked = [packed] + [x_shift(packed, k) for k in (1, 3, 2)]

    def run_own(*operands):
        return own_local(*operands)

    own_summed, own_highest, own_total = on_section(
        section_index, 1, run_own, query, key_new, value_new, own_keys, own_values, usable
    )

    def run_prompt(asked_rows, pages_here):
        return prompt_local(
            asked_rows[:, :share],
            asked_rows[:, share].astype(jnp.int32),
            asked_rows[:, share + 1].astype(jnp.int32),
            pages_here,
            slot_groups,
        )

    answers = on_section(section_index, 1, run_prompt, jnp.concatenate(asked), pages)
    parts = [answers[:rows]] + [
        x_shift(answers[(at + 1) * rows : (at + 2) * rows], -k) for at, k in enumerate((1, 3, 2))
    ]
    second = on_section(
        section_index,
        1,
        lambda a, b, c, d: combine(a, b, c, d, out_w[0]),
        own_summed,
        own_highest,
        own_total,
        parts,
    )
    by_head = second.reshape(rows, head_count, share).transpose(1, 0, 2)

    def slab(k):
        return lax.dynamic_index_in_dim(by_head, (head_index + k) % head_count, 0, keepdims=False)

    total = one_share.astype(jnp.float32) + slab(0)
    for piece in [head_shift(slab(k), k) for k in (1, 3, 2)]:
        total = total + piece
    output = jnp.where(section_index == 0, one_back, total.astype(jnp.bfloat16))
    return output[None]


def solution(mesh):
    placed = (
        P("req", "head"),
        P("section", None),
        P(None, "head"),
        P(None, "head"),
        P("section", None, "head"),
        P("section", "head", None),
        P(None, "head"),
        P("req", None, "head"),
        P("req", "head", None, None),
        P("req", "head", None),
        P("req", None, None, "head"),
        P("req", None, None, "head"),
        P("req", None),
        P("req"),
    )
    return jax.shard_map(
        body, mesh=mesh, in_specs=placed, out_specs=P("section", "req", "head"), check_vma=False
    )
```

```python
import jax
import jax.numpy as jnp
from jax import lax
from jax.experimental import pallas as pl
from jax.experimental.pallas import tpu as pltpu
from jax.sharding import PartitionSpec as P

HD = 112
FEAT = 16
WINDOW = 64
PAGE = 128
HALF = 64
XN = 4
ZN = 8
LANES = 512
GROUPS = 32
TAYLOR = 273
TAYLOR_LANES = 384
SPREAD = 1152

EPSILON = 1e-06
MASKED = -1e30


def head_shift(value, steps):
    count = lax.axis_size("head")
    return lax.ppermute(value, "head", [(i, (i + steps) % count) for i in range(count)])


def x_shift(value, steps):
    return lax.ppermute(
        value,
        "req",
        [(z * XN + i, z * XN + (i + steps) % XN) for z in range(ZN) for i in range(XN)],
    )


def z_shift(value, steps):
    base = XN * ZN
    return lax.ppermute(
        value,
        ("section", "req"),
        [
            (base + z * XN + i, base + ((z + steps) % ZN) * XN + i)
            for z in range(ZN)
            for i in range(XN)
        ],
    )


def section_swap(value, steps):
    count = lax.axis_size("head")
    there = [(i, count + (i + steps) % count) for i in range(count)]
    return lax.ppermute(value, ("section", "head"), there + [(b, a) for a, b in there])


VMEM = pl.BlockSpec(memory_space=pltpu.VMEM)
SMEM = pl.BlockSpec(memory_space=pltpu.SMEM)
HBM = pl.BlockSpec(memory_space=pl.ANY)
FLAT = (((1,), (1,)), ((), ()))


def normed_rows(values, gain_row):
    factor = lax.rsqrt(jnp.mean(values * values, axis=-1, keepdims=True) + EPSILON)
    return (values * factor * gain_row).astype(jnp.bfloat16)


def lanes_of(shape):
    return lax.broadcasted_iota(jnp.int32, shape, len(shape) - 1)


def in_head(lane, h):
    return (lane >= h * HD) & (lane < (h + 1) * HD)


def kernel_call(kernel, section, name, out_shape, in_specs, scratch_shapes, args, vmem=24 << 20):
    def run(ids, *refs):
        @pl.when(ids[0] == section)
        def _():
            kernel(ids, *refs)

    return pl.pallas_call(
        run,
        out_shape=out_shape,
        in_specs=[SMEM] + in_specs,
        out_specs=jax.tree.map(lambda _: VMEM, out_shape),
        scratch_shapes=scratch_shapes,
        compiler_params=pltpu.CompilerParams(vmem_limit_bytes=vmem),
        name=name,
    )(*args)


def expansion(features, width, repeat):
    lane = lax.broadcasted_iota(jnp.int32, (features, 2 * width), 1)
    source = lax.broadcasted_iota(jnp.int32, (features, 2 * width), 0)
    left = lane < width
    at = jnp.where(left, lane, lane - width) >> (repeat.bit_length() - 1)
    linear = left & (at > 0) & (at <= FEAT) & (source == at - 1)
    pair = at - (FEAT + 1)
    wanted = jnp.where(left, pair >> 4, pair & (FEAT - 1))
    quad = (pair >= 0) & (pair < FEAT * FEAT) & (source == wanted)
    return jnp.where(linear | quad, 1.0, 0.0).astype(jnp.bfloat16)


def taylor_rows(left, right, feature):
    scale = FEAT ** (-0.25)
    left, right = left * scale, right * scale
    return jnp.where(
        feature == 0, 1.0, jnp.where(feature <= FEAT, left, left * right * 0.5**0.5)
    )


def linear_kernel(
    ids,
    t0,
    t1,
    t2,
    t3,
    gain,
    conv_w,
    conv_state,
    lin_norm,
    feature_w,
    value_w,
    out_w,
    state_hbm,
    update,
    state,
    sem,
):
    rows, share = t0.shape
    heads = share // HD
    span = TAYLOR * heads
    copy = pltpu.make_async_copy(state_hbm, state, sem)
    copy.start()
    by_state = expansion(128, SPREAD, heads)
    by_norm = expansion(128, TAYLOR_LANES, 1)
    expand = jnp.concatenate([by_state, by_norm], axis=1)

    own = ids[2]
    got = [ref[...].astype(jnp.float32) for ref in (t0, t1, t3, t2)]
    whole = []
    for place in range(heads):
        piece = got[0]
        for back in range(1, heads):
            piece = jnp.where(((own - back) & (heads - 1)) == place, got[back], piece)
        whole.append(piece)
    tokens = jnp.concatenate(whole, axis=1)
    normed = normed_rows(tokens, gain[...])
    feats = jnp.dot(normed, feature_w[...], preferred_element_type=jnp.float32)
    by_head = jnp.concatenate(
        [feats] + [pltpu.roll(feats, 128 - 2 * FEAT * h, 1) for h in range(1, heads)], axis=0
    )
    high = by_head.astype(jnp.bfloat16)
    rest = by_head - high.astype(jnp.float32)
    middle = rest.astype(jnp.bfloat16)
    low = (rest - middle.astype(jnp.float32)).astype(jnp.bfloat16)
    spread = jnp.dot(
        jnp.concatenate([high, middle, low], axis=0), expand, preferred_element_type=jnp.float32
    )
    count = heads * rows
    spread = spread[:count] + spread[count : 2 * count] + spread[2 * count :]
    lane = lanes_of((count, SPREAD))
    head = lax.broadcasted_iota(jnp.int32, (count, SPREAD), 0) >> 3
    query_wide = taylor_rows(spread[:, :SPREAD], spread[:, SPREAD : 2 * SPREAD], lane >> 2)
    query_wide = jnp.where(((lane & (heads - 1)) == head) & (lane < span), query_wide, 0.0)
    query_feats = taylor_rows(
        spread[:, 2 * SPREAD : 2 * SPREAD + TAYLOR_LANES],
        spread[:, 2 * SPREAD + TAYLOR_LANES :],
        lanes_of((count, TAYLOR_LANES)),
    )[:, :TAYLOR]
    both = by_head * pltpu.roll(by_head, 128 - FEAT, 1)
    near = jnp.sum(
        jnp.where(lanes_of(both.shape) < FEAT, both, 0.0), axis=-1, keepdims=True
    ) * FEAT ** (-0.5)
    intersection = 1.0 + near + 0.5 * near * near

    fresh = lax.dot_general(normed, value_w[0], FLAT, preferred_element_type=jnp.float32)
    older = conv_state[...].astype(jnp.float32)
    mixed = conv_w[0:1] * older[:, 0] + conv_w[1:2] * older[:, 1] + conv_w[2:3] * fresh

    length = span + 12
    queries = []
    for shift in range(0, 16, 4):
        moved = query_wide if shift == 0 else pltpu.roll(query_wide, shift, 1)
        queries.append(moved[:, :length].astype(jnp.bfloat16))
    row = lax.broadcasted_iota(jnp.int32, (count, HD), 0) & (rows - 1)
    found = jnp.zeros((count, HD), jnp.float32)
    copy.wait()
    for r in range(rows):
        first = span * r
        shift = first % 16
        product = jnp.dot(
            queries[shift // 4],
            state[first - shift : first - shift + length, :],
            preferred_element_type=jnp.float32,
        )
        found = jnp.where(row == r, product, found)
    total = tokens * 0.25
    for h in range(heads):
        here = slice(h * rows, (h + 1) * rows)
        denominator = (
            jnp.sum(query_feats[here] * lin_norm[:, h, :], axis=-1, keepdims=True)
            + intersection[here]
        )
        attended = (
            (found[here] + intersection[here] * mixed[:, h * HD : (h + 1) * HD]) / denominator
        ).astype(jnp.bfloat16)
        total = total + jnp.dot(
            attended, out_w[0, h * HD : (h + 1) * HD, :], preferred_element_type=jnp.float32
        )
    update[...] = total


def linear_layer(ids, pieces, gain, feature_w, value_w, out_w, conv_w, conv_state, state, norm):
    rows = pieces[0].shape[0]
    return kernel_call(
        linear_kernel,
        0,
        "linear_layer",
        jax.ShapeDtypeStruct((rows, out_w.shape[2]), jnp.float32),
        [VMEM] * 11 + [HBM],
        [pltpu.VMEM(state.shape, jnp.bfloat16), pltpu.SemaphoreType.DMA],
        (ids, *pieces, gain, conv_w, conv_state, norm, feature_w, value_w, out_w, state),
    )


def project_kernel(
    ids, table, lengths, p0, p1, p2, p3, gain, qk_w, v_w, one, asked, key_new, value_new
):
    rows, share = one.shape
    heads = share // HD
    layer_one = (p0[...] + p1[...] + p2[...] + p3[...]).astype(jnp.bfloat16)
    rounded = layer_one.astype(jnp.float32)
    mine = rounded[:, :share]
    for h in range(1, heads):
        mine = jnp.where(ids[2] == h, rounded[:, h * share : (h + 1) * share], mine)
    one[...] = mine.astype(jnp.bfloat16)
    normed = normed_rows(rounded, gain[...])
    query_key = jnp.dot(normed, qk_w[...], preferred_element_type=jnp.float32)
    width = query_key.shape[1]
    lane = lanes_of((rows, LANES))
    query = jnp.where(in_head(lane, 0), query_key[:, :LANES], 0.0)
    key = query
    for h in range(heads):
        if h:
            moved = pltpu.roll(query_key, width - h * HD, 1)[:, :LANES]
            query = jnp.where(in_head(lane, h), moved, query)
        moved = pltpu.roll(query_key, width - (h + 1) * HD, 1)[:, :LANES]
        key = jnp.where(in_head(lane, h), moved, key)
    row = lax.broadcasted_iota(jnp.int32, (rows, LANES), 0)
    for r in range(rows):
        group = table[r, 0].astype(jnp.float32)
        start = jnp.minimum(lengths[r] - WINDOW, PAGE).astype(jnp.float32)
        query = jnp.where((row == r) & (lane == share), group, query)
        query = jnp.where((row == r) & (lane == share + 1), start, query)
    asked[...] = query.astype(jnp.bfloat16)
    key_new[...] = key[:, :share].astype(jnp.bfloat16)
    value_new[...] = lax.dot_general(
        normed, v_w[0], FLAT, preferred_element_type=jnp.float32
    ).astype(jnp.bfloat16)


def project(ids, table, lengths, pieces, gain, query_key_w, value_w):
    rows = pieces[0].shape[0]
    share = value_w.shape[1]
    return kernel_call(
        project_kernel,
        1,
        "project",
        [
            jax.ShapeDtypeStruct((rows, share), jnp.bfloat16),
            jax.ShapeDtypeStruct((rows, LANES), jnp.bfloat16),
            jax.ShapeDtypeStruct((rows, share), jnp.bfloat16),
            jax.ShapeDtypeStruct((rows, share), jnp.bfloat16),
        ],
        [SMEM] * 2 + [VMEM] * 7,
        [],
        (ids, table, lengths, *pieces, gain, query_key_w, value_w),
    )


def own_kernel(
    ids,
    table,
    lengths,
    asked,
    key_new,
    value_new,
    own_pages,
    summed_out,
    highest_out,
    total_out,
    pages,
    sems,
):
    rows, share = key_new.shape
    count = own_pages.shape[0]
    bounds = []
    copies = []
    for r in range(rows):
        length = lengths[r]
        first = jnp.maximum((length - WINDOW) // PAGE, 1)
        last = jnp.maximum((length - 2) // PAGE, 1)
        bounds.append((length, first, last))
        for slot, logical in enumerate((first, last)):
            page = jnp.clip(table[r, logical] - GROUPS - ids[1] * count, 0, count - 1)
            copies.append(
                pltpu.make_async_copy(own_pages.at[page], pages.at[r, slot], sems.at[r, slot])
            )
            copies[-1].start()
    head = lax.broadcasted_iota(jnp.int32, (8, share), 0)
    lane = lanes_of((8, share))
    mine = (lane >= head * HD) & (lane < (head + 1) * HD)
    token = lanes_of((8, 2 * PAGE))
    scale = HD ** (-0.5)
    query = asked[:, :share].astype(jnp.float32)
    new_key = key_new[...].astype(jnp.float32)
    new_value = value_new[...].astype(jnp.float32)
    for r in range(rows):
        query_here = jnp.where(mine, query[r : r + 1], 0.0)
        new_score = jnp.sum(query_here * new_key[r : r + 1], axis=-1, keepdims=True) * scale
        low = query_here.astype(jnp.bfloat16)
        copies[2 * r].wait()
        copies[2 * r + 1].wait()
        scores = (
            jnp.concatenate(
                [
                    jnp.dot(low, pages[r, slot, 0], preferred_element_type=jnp.float32)
                    for slot in range(2)
                ],
                axis=1,
            )
            * scale
        )
        length, first, last = bounds[r]
        position = jnp.where(
            token < PAGE,
            first * PAGE + token,
            jnp.where(last != first, last * PAGE + token - PAGE, -1),
        )
        usable = (position >= length - WINDOW) & (position <= length - 2)
        scores = jnp.where(usable, scores, MASKED)
        highest = jnp.maximum(jnp.max(scores, axis=-1, keepdims=True), new_score)
        exps = jnp.where(usable, jnp.exp(scores - highest), 0.0)
        exp_new = jnp.exp(new_score - highest)
        total = jnp.sum(exps, axis=-1, keepdims=True) + exp_new
        exps = exps.astype(jnp.bfloat16)
        found = exp_new * new_value[r : r + 1]
        for slot in range(2):
            found = found + lax.dot_general(
                exps[:, slot * PAGE : (slot + 1) * PAGE],
                pages[r, slot, 1],
                FLAT,
                preferred_element_type=jnp.float32,
            )
        for ref, value in ((summed_out, found), (highest_out, highest), (total_out, total)):
            ref[r : r + 1, :] = jnp.sum(jnp.where(mine, value, 0.0), axis=0, keepdims=True)


def own_attention(ids, table, lengths, asked, key_new, value_new, own_pages):
    rows, share = key_new.shape
    return kernel_call(
        own_kernel,
        1,
        "own_attention",
        [jax.ShapeDtypeStruct((rows, share), jnp.float32)] * 3,
        [SMEM] * 2 + [VMEM] * 3 + [HBM],
        [
            pltpu.VMEM((rows, 2) + own_pages.shape[1:], jnp.bfloat16),
            pltpu.SemaphoreType.DMA((rows, 2)),
        ],
        (ids, table, lengths, asked, key_new, value_new, own_pages),
    )


def prompt_kernel(ids, a0, a1, a2, a3, near_pages, above, below, o0, o1, o2, o3):
    rows = a0.shape[0]
    share = near_pages.shape[1]
    heads = share // HD
    pages = jnp.concatenate(
        [near_pages[i] for i in range(3)]
        + [above[i] for i in range(3)]
        + [below[i] for i in range(2)],
        axis=1,
    )
    asked = jnp.concatenate([ref[...].astype(jnp.float32) for ref in (a0, a1, a2, a3)], axis=0)
    count = asked.shape[0]
    lane = lanes_of(asked.shape)
    group = jnp.sum(jnp.where(lane == share, asked, 0.0), axis=-1, keepdims=True)
    start = jnp.sum(jnp.where(lane == share + 1, asked, 0.0), axis=-1, keepdims=True)
    group, start = group.astype(jnp.int32), start.astype(jnp.int32)
    query = jnp.concatenate(
        [jnp.where(in_head(lane, h), asked, 0.0)[:, :share] for h in range(heads)], axis=0
    ).astype(jnp.bfloat16)
    scores = jnp.dot(query, pages, preferred_element_type=jnp.float32) * HD ** (-0.5)
    token = lanes_of((count, ZN * PAGE))
    z, x = ids[1] // XN, ids[1] % XN
    slot_group = (((token >> 7) + (z + ZN - 1)) & (ZN - 1)) * XN + x
    offset = token & (PAGE - 1)
    usable = (slot_group == group) & (offset < HALF) & (offset + HALF >= start)
    lane = lanes_of((count, share))
    stat_lane = lanes_of((count, 128))
    weights = []
    stats = jnp.zeros((count, 128), jnp.float32)
    for h in range(heads):
        here = jnp.where(usable, scores[h * count : (h + 1) * count], MASKED)
        highest = jnp.max(here, axis=-1, keepdims=True)
        exps = jnp.where(usable, jnp.exp(here - highest), 0.0)
        total = jnp.sum(exps, axis=-1, keepdims=True)
        stats = jnp.where(stat_lane == h, highest, stats)
        stats = jnp.where(stat_lane == heads + h, total, stats)
        weights.append(pltpu.roll(exps, HALF, 1))
    found = lax.dot_general(
        jnp.concatenate(weights, axis=0).astype(jnp.bfloat16),
        pages,
        FLAT,
        preferred_element_type=jnp.float32,
    )
    summed = jnp.zeros((count, share), jnp.float32)
    for h in range(heads):
        summed = jnp.where(in_head(lane, h), found[h * count : (h + 1) * count], summed)
    for at, ref in enumerate((o0, o1, o2, o3)):
        ref[:, :share] = summed[at * rows : (at + 1) * rows]
        ref[:, share:LANES] = jnp.zeros((rows, LANES - share), jnp.float32)
        ref[:, LANES:] = stats[at * rows : (at + 1) * rows]


def prompt_attention(ids, asked, near_pages, above, below):
    rows = asked[0].shape[0]
    return kernel_call(
        prompt_kernel,
        1,
        "prompt_attention",
        [jax.ShapeDtypeStruct((rows, LANES + 128), jnp.float32)] * 4,
        [VMEM] * 7,
        [],
        (ids, *asked, near_pages, above, below),
    )


def combine_kernel(ids, summed, highest, total, r0, r1, r2, r3, out_w, s0, s1, s2, s3):
    rows, share = summed.shape
    heads = share // HD
    refs = (r0, r1, r2, r3)
    prompt_summed = sum(ref[:, :share] for ref in refs)
    stats = [ref[:, LANES:] for ref in refs]
    top = jnp.maximum(jnp.maximum(stats[0], stats[1]), jnp.maximum(stats[2], stats[3]))
    added = stats[0] + stats[1] + stats[2] + stats[3]
    lane = lanes_of((rows, share))
    prompt_highest = jnp.zeros((rows, share), jnp.float32)
    prompt_total = jnp.zeros((rows, share), jnp.float32)
    for h in range(heads):
        here = in_head(lane, h)
        prompt_highest = jnp.where(here, top[:, h : h + 1], prompt_highest)
        prompt_total = jnp.where(here, added[:, heads + h : heads + h + 1], prompt_total)
    peak = jnp.maximum(highest[...], prompt_highest)
    own_factor = jnp.exp(highest[...] - peak)
    prompt_factor = jnp.exp(prompt_highest - peak)
    whole = total[...] * own_factor + prompt_total * prompt_factor
    attended = (summed[...] * own_factor + prompt_summed * prompt_factor) / whole
    second = jnp.dot(attended.astype(jnp.bfloat16), out_w[0], preferred_element_type=jnp.float32)
    for steps, ref in enumerate((s0, s1, s2, s3)):
        slab = second[:, :share]
        for h in range(1, heads):
            slab = jnp.where(
                ((ids[2] + steps) & (heads - 1)) == h, second[:, h * share : (h + 1) * share], slab
            )
        ref[...] = slab


def combine(ids, own, parts, out_w):
    return kernel_call(
        combine_kernel,
        1,
        "combine",
        [jax.ShapeDtypeStruct(own[0].shape, jnp.float32)] * 4,
        [VMEM] * 8,
        [],
        (ids, *own, *parts, out_w),
    )


def body(
    tokens,
    norm_gain,
    feature_w,
    query_key_w,
    value_w,
    out_w,
    conv_w,
    conv_state,
    lin_state,
    lin_norm,
    own_pages,
    prompt_pages,
    page_table,
    lengths,
):
    section_index = lax.axis_index("section")
    ids = jnp.stack([section_index, lax.axis_index("req"), lax.axis_index("head")])
    value_w = value_w.transpose(0, 2, 1)
    lin_state = lin_state.transpose(0, 2, 1, 3).reshape(-1, HD)
    own_pages = own_pages.transpose(0, 1, 3, 2)
    prompt_pages = prompt_pages.transpose(0, 1, 3, 2)

    received = [head_shift(tokens, k) for k in (1, 3, 2)]
    page = jnp.concatenate([prompt_pages[0, 0, :, HALF:], prompt_pages[0, 1, :, HALF:]], axis=1)
    near_pages = jnp.stack([z_shift(page, 1), page, z_shift(page, -1)])
    near_pages, received = lax.optimization_barrier((near_pages, received))
    above = z_shift(near_pages, -3)
    below = z_shift(near_pages[1:], 3)

    update = linear_layer(
        ids,
        [tokens] + received,
        norm_gain,
        feature_w,
        value_w,
        out_w,
        conv_w,
        conv_state,
        lin_state,
        lin_norm,
    )
    swapped = [section_swap(update, k) for k in (0, 1, 3, 2)]
    one_share, packed, key_new, value_new = project(
        ids, page_table, lengths, swapped, norm_gain, query_key_w, value_w
    )
    asked = [packed] + [x_shift(packed, k) for k in (1, 3, 2)]
    own = own_attention(ids, page_table, lengths, packed, key_new, value_new, own_pages)
    answers = prompt_attention(ids, asked, near_pages, above, below)
    parts = [answers[0]] + [x_shift(answers[at], -k) for at, k in ((1, 1), (2, 3), (3, 2))]
    slabs = combine(ids, own, parts, out_w)
    one_back = lax.ppermute(one_share, "section", [(1, 0)])
    total = one_share.astype(jnp.float32) + slabs[0]
    for piece in [head_shift(slabs[k], k) for k in (1, 3, 2)]:
        total = total + piece
    output = jnp.where(section_index == 0, one_back, total.astype(jnp.bfloat16))
    return output[None]


def solution(mesh):
    placed = (
        P("req", "head"),
        P("section", None),
        P(None, "head"),
        P(None, "head"),
        P("section", None, "head"),
        P("section", "head", None),
        P(None, "head"),
        P("req", None, "head"),
        P("req", "head", None, None),
        P("req", "head", None),
        P("req", None, None, "head"),
        P("req", None, None, "head"),
        P("req", None),
        P("req"),
    )
    return jax.shard_map(
        body, mesh=mesh, in_specs=placed, out_specs=P("section", "req", "head"), check_vma=False
    )
```

```python
import jax
import jax.numpy as jnp
from jax import lax
from jax.experimental import pallas as pl
from jax.experimental.pallas import tpu as pltpu
from jax.sharding import PartitionSpec as P

HD = 112
FEAT = 16
WINDOW = 64
PAGE = 128
HALF = 64
MAXP = 256
GROUPS = 32
XN = 4
ZN = 8
LANES = 512
TAYLOR = 273
TAYLOR_LANES = 384
SPREAD = 1152

EPSILON = 1e-06
MASKED = -1e30


def head_shift(value, steps):
    count = lax.axis_size("head")
    return lax.ppermute(value, "head", [(i, (i + steps) % count) for i in range(count)])


def token_shift(value, steps):
    count = lax.axis_size("head")
    return lax.ppermute(
        value, ("section", "head"), [(i, (i + steps) % count) for i in range(count)]
    )


def z_shift(value, steps):
    return lax.ppermute(
        value,
        "req",
        [(z * XN + i, (z + steps) % ZN * XN + i) for z in range(ZN) for i in range(XN)],
    )


def page_shift(value, z_steps, x_steps):
    base = XN * ZN
    return lax.ppermute(
        value,
        ("section", "req"),
        [
            (base + z * XN + i, base + (z + z_steps) % ZN * XN + (i + x_steps) % XN)
            for z in range(ZN)
            for i in range(XN)
        ],
    )


def section_swap(value, steps):
    count = lax.axis_size("head")
    there = [(i, count + (i + steps) % count) for i in range(count)]
    return lax.ppermute(value, ("section", "head"), there + [(b, a) for a, b in there])


VMEM = pl.BlockSpec(memory_space=pltpu.VMEM)
SMEM = pl.BlockSpec(memory_space=pltpu.SMEM)
HBM = pl.BlockSpec(memory_space=pltpu.HBM)
FLAT = (((1,), (1,)), ((), ()))


def normed_rows(values, gain_row):
    factor = lax.rsqrt(jnp.mean(values * values, axis=-1, keepdims=True) + EPSILON)
    return (values * factor * gain_row).astype(jnp.bfloat16)


def lanes_of(shape):
    return lax.broadcasted_iota(jnp.int32, shape, len(shape) - 1)


def in_head(lane, h):
    return (lane >= h * HD) & (lane < (h + 1) * HD)


def place():
    return lax.axis_index("section"), lax.axis_index("req"), lax.axis_index("head")


def kernel_call(
    kernel, section, name, out_shape, in_specs, scratch_shapes, args, vmem=24 << 20, cost=None
):
    def run(*refs):
        ids = place()

        @pl.when(ids[0] == section)
        def _():
            kernel(ids, *refs)

    args = [
        pltpu.with_memory_space_constraint(arg, pltpu.HBM) if spec is HBM else arg
        for arg, spec in zip(args, in_specs, strict=True)
    ]
    return pl.pallas_call(
        run,
        out_shape=out_shape,
        in_specs=in_specs,
        out_specs=jax.tree.map(lambda _: VMEM, out_shape),
        scratch_shapes=scratch_shapes,
        compiler_params=pltpu.CompilerParams(vmem_limit_bytes=vmem),
        cost_estimate=cost,
        name=name,
    )(*args)


def expansion(features, width, repeat):
    lane = lax.broadcasted_iota(jnp.int32, (features, 2 * width), 1)
    source = lax.broadcasted_iota(jnp.int32, (features, 2 * width), 0)
    left = lane < width
    at = jnp.where(left, lane, lane - width) >> (repeat.bit_length() - 1)
    linear = left & (at > 0) & (at <= FEAT) & (source == at - 1)
    pair = at - (FEAT + 1)
    wanted = jnp.where(left, pair >> 4, pair & (FEAT - 1))
    quad = (pair >= 0) & (pair < FEAT * FEAT) & (source == wanted)
    return jnp.where(linear | quad, 1.0, 0.0).astype(jnp.bfloat16)


def taylor_rows(left, right, feature):
    scale = FEAT ** (-0.25)
    left, right = left * scale, right * scale
    return jnp.where(
        feature == 0, 1.0, jnp.where(feature <= FEAT, left, left * right * 0.5**0.5)
    )


def linear_kernel(
    ids,
    t1,
    t2,
    t3,
    t0_hbm,
    gain_hbm,
    feature_hbm,
    state_hbm,
    norm_hbm,
    conv_w_hbm,
    conv_state_hbm,
    value_hbm,
    out_hbm,
    update,
    t0,
    gain,
    feature_w,
    state,
    lin_norm,
    conv_w,
    conv_state,
    value_w,
    out_w,
    sems,
):
    rows, share = t0.shape
    heads = share // HD
    span = TAYLOR * heads
    copies = [
        pltpu.make_async_copy(source, target, sems.at[at])
        for at, (source, target) in enumerate(
            [
                (t0_hbm, t0),
                (gain_hbm, gain),
                (feature_hbm, feature_w),
                (state_hbm, state),
                (norm_hbm, lin_norm),
                (conv_w_hbm, conv_w),
                (conv_state_hbm, conv_state),
                (value_hbm.at[0], value_w),
                (out_hbm.at[0], out_w),
            ]
        )
    ]
    for copy in copies:
        copy.start()
    by_state = expansion(128, SPREAD, heads)
    by_norm = expansion(128, TAYLOR_LANES, 1)
    expand = jnp.concatenate([by_state, by_norm], axis=1)

    for copy in copies[:3]:
        copy.wait()
    own = ids[2]
    got = [ref[...].astype(jnp.float32) for ref in (t0, t1, t3, t2)]
    whole = []
    for place in range(heads):
        piece = got[0]
        for back in range(1, heads):
            piece = jnp.where(((own - back) & (heads - 1)) == place, got[back], piece)
        whole.append(piece)
    tokens = jnp.concatenate(whole, axis=1)
    normed = normed_rows(tokens, gain[...])
    feats = jnp.dot(normed, feature_w[...], preferred_element_type=jnp.float32)
    by_head = jnp.concatenate(
        [feats] + [pltpu.roll(feats, 128 - 2 * FEAT * h, 1) for h in range(1, heads)], axis=0
    )
    high = by_head.astype(jnp.bfloat16)
    rest = by_head - high.astype(jnp.float32)
    middle = rest.astype(jnp.bfloat16)
    low = (rest - middle.astype(jnp.float32)).astype(jnp.bfloat16)
    spread = jnp.dot(
        jnp.concatenate([high, middle, low], axis=0), expand, preferred_element_type=jnp.float32
    )
    count = heads * rows
    spread = spread[:count] + spread[count : 2 * count] + spread[2 * count :]
    lane = lanes_of((count, SPREAD))
    head = lax.broadcasted_iota(jnp.int32, (count, SPREAD), 0) >> 3
    query_wide = taylor_rows(spread[:, :SPREAD], spread[:, SPREAD : 2 * SPREAD], lane >> 2)
    query_wide = jnp.where(((lane & (heads - 1)) == head) & (lane < span), query_wide, 0.0)
    query_feats = taylor_rows(
        spread[:, 2 * SPREAD : 2 * SPREAD + TAYLOR_LANES],
        spread[:, 2 * SPREAD + TAYLOR_LANES :],
        lanes_of((count, TAYLOR_LANES)),
    )[:, :TAYLOR]
    both = by_head * pltpu.roll(by_head, 128 - FEAT, 1)
    near = jnp.sum(
        jnp.where(lanes_of(both.shape) < FEAT, both, 0.0), axis=-1, keepdims=True
    ) * FEAT ** (-0.5)
    intersection = 1.0 + near + 0.5 * near * near

    length = span + 12
    queries = []
    for shift in range(0, 16, 4):
        moved = query_wide if shift == 0 else pltpu.roll(query_wide, shift, 1)
        queries.append(moved[:, :length].astype(jnp.bfloat16))
    row = lax.broadcasted_iota(jnp.int32, (count, HD), 0) & (rows - 1)
    found = jnp.zeros((count, HD), jnp.float32)
    copies[3].wait()
    for r in range(rows):
        first = span * r
        shift = first % 16
        product = jnp.dot(
            queries[shift // 4],
            state[first - shift : first - shift + length, :],
            preferred_element_type=jnp.float32,
        )
        found = jnp.where(row == r, product, found)
    for copy in copies[4:8]:
        copy.wait()
    fresh = lax.dot_general(normed, value_w[...], FLAT, preferred_element_type=jnp.float32)
    older = conv_state[...].astype(jnp.float32)
    mixed = conv_w[0:1] * older[:, 0] + conv_w[1:2] * older[:, 1] + conv_w[2:3] * fresh
    total = tokens * 0.25
    copies[8].wait()
    for h in range(heads):
        here = slice(h * rows, (h + 1) * rows)
        denominator = (
            jnp.sum(query_feats[here] * lin_norm[:, h, :], axis=-1, keepdims=True)
            + intersection[here]
        )
        attended = (
            (found[here] + intersection[here] * mixed[:, h * HD : (h + 1) * HD]) / denominator
        ).astype(jnp.bfloat16)
        total = total + jnp.dot(
            attended, out_w[h * HD : (h + 1) * HD, :], preferred_element_type=jnp.float32
        )
    update[...] = total


def linear_layer(pieces, gain, feature_w, value_w, out_w, conv_w, conv_state, state, norm):
    rows = pieces[0].shape[0]
    near = (pieces[0], gain, feature_w, state, norm, conv_w, conv_state, value_w, out_w)
    return kernel_call(
        linear_kernel,
        0,
        "linear_layer",
        jax.ShapeDtypeStruct((rows, out_w.shape[2]), jnp.float32),
        [VMEM] * 3 + [HBM] * len(near),
        [
            *(pltpu.VMEM(array.shape, array.dtype) for array in near[:-2]),
            pltpu.VMEM(value_w.shape[1:], jnp.bfloat16),
            pltpu.VMEM(out_w.shape[1:], jnp.bfloat16),
            pltpu.SemaphoreType.DMA((len(near),)),
        ],
        (*pieces[1:], *near),
    )


def project_kernel(
    ids,
    tags,
    p0,
    p1,
    p2,
    p3,
    gain,
    qk_hbm,
    v_hbm,
    one,
    asked,
    key_new,
    value_new,
    v_w,
    qk_w,
    sems,
):
    rows, share = one.shape
    copy_value = pltpu.make_async_copy(v_hbm.at[0], v_w, sems.at[0])
    copy_query = pltpu.make_async_copy(qk_hbm, qk_w, sems.at[1])
    copy_value.start()
    copy_query.start()
    heads = share // HD
    layer_one = (p0[...] + p1[...] + p2[...] + p3[...]).astype(jnp.bfloat16)
    rounded = layer_one.astype(jnp.float32)
    mine = rounded[:, :share]
    for h in range(1, heads):
        mine = jnp.where(ids[2] == h, rounded[:, h * share : (h + 1) * share], mine)
    one[...] = mine.astype(jnp.bfloat16)
    normed = normed_rows(rounded, gain[...])
    copy_value.wait()
    value_new[...] = lax.dot_general(
        normed, v_w[...], FLAT, preferred_element_type=jnp.float32
    ).astype(jnp.bfloat16)
    copy_query.wait()
    query_key = jnp.dot(normed, qk_w[...], preferred_element_type=jnp.float32)
    width = query_key.shape[1]
    lane = lanes_of((rows, LANES))
    query = jnp.where(in_head(lane, 0), query_key[:, :LANES], 0.0)
    key = query
    for h in range(heads):
        if h:
            moved = pltpu.roll(query_key, width - h * HD, 1)[:, :LANES]
            query = jnp.where(in_head(lane, h), moved, query)
        moved = pltpu.roll(query_key, width - (h + 1) * HD, 1)[:, :LANES]
        key = jnp.where(in_head(lane, h), moved, key)
    group = tags[:, 0:1].astype(jnp.float32)
    start = jnp.minimum(tags[:, 1:2] - WINDOW, PAGE).astype(jnp.float32)
    query = jnp.where(lane == share, group, query)
    query = jnp.where(lane == share + 1, start, query)
    asked[...] = query.astype(jnp.bfloat16)
    key_new[...] = key[:, :share].astype(jnp.bfloat16)


def project(tags, pieces, gain, query_key_w, value_w):
    rows = pieces[0].shape[0]
    share = value_w.shape[1]
    return kernel_call(
        project_kernel,
        1,
        "project",
        [
            jax.ShapeDtypeStruct((rows, share), jnp.bfloat16),
            jax.ShapeDtypeStruct((rows, LANES), jnp.bfloat16),
            jax.ShapeDtypeStruct((rows, share), jnp.bfloat16),
            jax.ShapeDtypeStruct((rows, share), jnp.bfloat16),
        ],
        [VMEM] * 6 + [HBM] * 2,
        [
            pltpu.VMEM(value_w.shape[1:], jnp.bfloat16),
            pltpu.VMEM(query_key_w.shape, jnp.bfloat16),
            pltpu.SemaphoreType.DMA((2,)),
        ],
        (tags, *pieces, gain, query_key_w, value_w),
    )


def own_kernel(
    ids,
    table,
    lengths,
    asked,
    key_new,
    value_new,
    own_pages,
    summed_out,
    highest_out,
    total_out,
    pages,
    sems,
):
    rows, share = key_new.shape
    count = own_pages.shape[0]
    bounds = []
    copies = []
    for r in range(rows):
        length = lengths[r]
        first = jnp.maximum((length - WINDOW) // PAGE, 1)
        last = jnp.maximum((length - 2) // PAGE, 1)
        bounds.append((length, first, last))
        for slot, logical in enumerate((first, last)):
            page = jnp.clip(table[r, logical] - GROUPS - ids[1] * count, 0, count - 1)
            copies.append(
                pltpu.make_async_copy(own_pages.at[page], pages.at[r, slot], sems.at[r, slot])
            )
            copies[-1].start()
    head = lax.broadcasted_iota(jnp.int32, (8, share), 0)
    lane = lanes_of((8, share))
    mine = (lane >= head * HD) & (lane < (head + 1) * HD)
    scale = HD ** (-0.5)
    query = asked[:, :share].astype(jnp.float32)
    new_key = key_new[...].astype(jnp.float32)
    new_value = value_new[...].astype(jnp.float32)
    wide = jnp.concatenate([jnp.where(mine, query[r : r + 1], 0.0) for r in range(rows)], axis=0)
    keys = jnp.concatenate(
        [jnp.broadcast_to(new_key[r : r + 1], (8, share)) for r in range(rows)], axis=0
    )
    new_score = jnp.sum(wide * keys, axis=-1, keepdims=True) * scale
    token = lanes_of((8 * rows, 2 * PAGE))
    request = lax.broadcasted_iota(jnp.int32, (8 * rows, 2 * PAGE), 0) >> 3
    length = jnp.zeros(token.shape, jnp.int32)
    base = jnp.zeros(token.shape, jnp.int32)
    for r in range(rows):
        length = jnp.where(request == r, bounds[r][0], length)
        second = jnp.where(bounds[r][1] != bounds[r][2], bounds[r][2] - 1, -MAXP) * PAGE
        base = jnp.where(request == r, jnp.where(token < PAGE, bounds[r][1] * PAGE, second), base)
    position = base + token
    usable = (position >= length - WINDOW) & (position <= length - 2)
    scores = []
    for r in range(rows):
        low = wide[8 * r : 8 * r + 8].astype(jnp.bfloat16)
        copies[2 * r].wait()
        copies[2 * r + 1].wait()
        scores.append(
            jnp.concatenate(
                [
                    jnp.dot(low, pages[r, slot, 0], preferred_element_type=jnp.float32)
                    for slot in range(2)
                ],
                axis=1,
            )
        )
    scores = jnp.where(usable, jnp.concatenate(scores, axis=0) * scale, MASKED)
    highest = jnp.maximum(jnp.max(scores, axis=-1, keepdims=True), new_score)
    exps = jnp.where(usable, jnp.exp(scores - highest), 0.0)
    exp_new = jnp.exp(new_score - highest)
    total = jnp.sum(exps, axis=-1, keepdims=True) + exp_new
    for r in range(rows):
        here = slice(8 * r, 8 * r + 8)
        low = exps[here].astype(jnp.bfloat16)
        found = exp_new[here] * new_value[r : r + 1]
        for slot in range(2):
            found = found + lax.dot_general(
                low[:, slot * PAGE : (slot + 1) * PAGE],
                pages[r, slot, 1],
                FLAT,
                preferred_element_type=jnp.float32,
            )
        for ref, value in (
            (summed_out, found),
            (highest_out, highest[here]),
            (total_out, total[here]),
        ):
            ref[r : r + 1, :] = jnp.sum(jnp.where(mine, value, 0.0), axis=0, keepdims=True)


def own_attention(table, lengths, asked, key_new, value_new, own_pages):
    rows, share = key_new.shape
    return kernel_call(
        own_kernel,
        1,
        "own_attention",
        [jax.ShapeDtypeStruct((rows, share), jnp.float32)] * 3,
        [SMEM] * 2 + [VMEM] * 3 + [HBM],
        [
            pltpu.VMEM((rows, 2) + own_pages.shape[1:], jnp.bfloat16),
            pltpu.SemaphoreType.DMA((rows, 2)),
        ],
        (table, lengths, asked, key_new, value_new, own_pages),
    )


def prompt_kernel(ids, a0, a1, a2, a3, near_pages, far_pages, o0, o1, o2, o3):
    rows = a0.shape[0]
    share = near_pages.shape[1]
    heads = share // HD
    pages = jnp.concatenate(
        [near_pages[i] for i in range(XN)] + [far_pages[i] for i in range(XN)], axis=1
    )
    asked = jnp.concatenate([ref[...].astype(jnp.float32) for ref in (a0, a1, a2, a3)], axis=0)
    count = asked.shape[0]
    lane = lanes_of(asked.shape)
    group = jnp.sum(jnp.where(lane == share, asked, 0.0), axis=-1, keepdims=True)
    start = jnp.sum(jnp.where(lane == share + 1, asked, 0.0), axis=-1, keepdims=True)
    group, start = group.astype(jnp.int32), start.astype(jnp.int32)
    query = jnp.concatenate(
        [jnp.where(in_head(lane, h), asked, 0.0)[:, :share] for h in range(heads)], axis=0
    ).astype(jnp.bfloat16)
    scores = jnp.dot(query, pages, preferred_element_type=jnp.float32) * HD ** (-0.5)
    token = lanes_of((count, 2 * XN * PAGE))
    z, x = ids[1] // XN, ids[1] % XN
    slot = token >> 7
    slot_group = jnp.where(slot < XN, z, (z + ZN // 2) & (ZN - 1)) * XN
    slot_group = slot_group + ((slot + x + XN - 1) & (XN - 1))
    offset = token & (PAGE - 1)
    usable = (slot_group == group) & (offset < HALF) & (offset + HALF >= start)
    lane = lanes_of((count, share))
    stat_lane = lanes_of((count, 128))
    weights = []
    stats = jnp.zeros((count, 128), jnp.float32)
    for h in range(heads):
        here = jnp.where(usable, scores[h * count : (h + 1) * count], MASKED)
        highest = jnp.max(here, axis=-1, keepdims=True)
        exps = jnp.where(usable, jnp.exp(here - highest), 0.0)
        total = jnp.sum(exps, axis=-1, keepdims=True)
        stats = jnp.where(stat_lane == h, highest, stats)
        stats = jnp.where(stat_lane == heads + h, total, stats)
        weights.append(pltpu.roll(exps, HALF, 1))
    found = lax.dot_general(
        jnp.concatenate(weights, axis=0).astype(jnp.bfloat16),
        pages,
        FLAT,
        preferred_element_type=jnp.float32,
    )
    summed = jnp.zeros((count, share), jnp.float32)
    for h in range(heads):
        summed = jnp.where(in_head(lane, h), found[h * count : (h + 1) * count], summed)
    for at, ref in enumerate((o0, o1, o2, o3)):
        ref[:, :share] = summed[at * rows : (at + 1) * rows]
        ref[:, share:LANES] = jnp.zeros((rows, LANES - share), jnp.float32)
        ref[:, LANES:] = stats[at * rows : (at + 1) * rows]


def prompt_attention(asked, near_pages, far_pages):
    rows = asked[0].shape[0]
    return kernel_call(
        prompt_kernel,
        1,
        "prompt_attention",
        [jax.ShapeDtypeStruct((rows, LANES + 128), jnp.float32)] * 4,
        [VMEM] * 6,
        [],
        (*asked, near_pages, far_pages),
    )


def combine_kernel(ids, summed, highest, total, r0, r1, r2, r3, out_w, s0, s1, s2, s3):
    rows, share = summed.shape
    heads = share // HD
    refs = (r0, r1, r2, r3)
    prompt_summed = sum(ref[:, :share] for ref in refs)
    stats = [ref[:, LANES:] for ref in refs]
    top = jnp.maximum(jnp.maximum(stats[0], stats[1]), jnp.maximum(stats[2], stats[3]))
    added = stats[0] + stats[1] + stats[2] + stats[3]
    lane = lanes_of((rows, share))
    prompt_highest = jnp.zeros((rows, share), jnp.float32)
    prompt_total = jnp.zeros((rows, share), jnp.float32)
    for h in range(heads):
        here = in_head(lane, h)
        prompt_highest = jnp.where(here, top[:, h : h + 1], prompt_highest)
        prompt_total = jnp.where(here, added[:, heads + h : heads + h + 1], prompt_total)
    peak = jnp.maximum(highest[...], prompt_highest)
    own_factor = jnp.exp(highest[...] - peak)
    prompt_factor = jnp.exp(prompt_highest - peak)
    whole = total[...] * own_factor + prompt_total * prompt_factor
    attended = (summed[...] * own_factor + prompt_summed * prompt_factor) / whole
    second = jnp.dot(attended.astype(jnp.bfloat16), out_w[0], preferred_element_type=jnp.float32)
    for steps, ref in enumerate((s0, s1, s2, s3)):
        slab = second[:, :share]
        for h in range(1, heads):
            slab = jnp.where(
                ((ids[2] + steps) & (heads - 1)) == h, second[:, h * share : (h + 1) * share], slab
            )
        ref[...] = slab


def combine(own, parts, out_w):
    return kernel_call(
        combine_kernel,
        1,
        "combine",
        [jax.ShapeDtypeStruct(own[0].shape, jnp.float32)] * 4,
        [VMEM] * 8,
        [],
        (*own, *parts, out_w),
    )


def page_kernel(ids, pages_hbm, page, pages, sem):
    copy = pltpu.make_async_copy(pages_hbm.at[0], pages, sem)
    copy.start()
    copy.wait()
    lane = lanes_of(page.shape)
    keys = pltpu.roll(pages[0].astype(jnp.float32), HALF, 1)
    page[...] = jnp.where(lane < HALF, keys, pages[1].astype(jnp.float32)).astype(jnp.bfloat16)


def window_page(prompt_pages):
    shape = prompt_pages.shape[1:]
    return kernel_call(
        page_kernel,
        1,
        "window_page",
        jax.ShapeDtypeStruct(shape[1:], jnp.bfloat16),
        [HBM],
        [pltpu.VMEM(shape, jnp.bfloat16), pltpu.SemaphoreType.DMA],
        (prompt_pages,),
        cost=pl.CostEstimate(flops=0, bytes_accessed=16 << 20, transcendentals=0),
    )


def body(
    tokens,
    norm_gain,
    feature_w,
    query_key_w,
    value_w,
    out_w,
    conv_w,
    conv_state,
    lin_state,
    lin_norm,
    own_pages,
    prompt_pages,
    page_table,
    lengths,
):
    value_w = value_w.transpose(0, 2, 1)
    lin_state = lin_state.transpose(0, 2, 1, 3).reshape(-1, HD)
    own_pages = own_pages.transpose(0, 1, 3, 2)
    prompt_pages = prompt_pages.transpose(0, 1, 3, 2)

    received = [token_shift(tokens, k) for k in (1, 3, 2)]
    page = window_page(prompt_pages)
    row_pages = [page_shift(page, 0, k) for k in (1, 3, 2)]
    near_pages = jnp.stack([row_pages[0], page, row_pages[1], row_pages[2]])
    near_pages, received = lax.optimization_barrier((near_pages, received))
    far_pages = page_shift(near_pages, ZN // 2, 0)

    update = linear_layer(
        [tokens] + received,
        norm_gain,
        feature_w,
        value_w,
        out_w,
        conv_w,
        conv_state,
        lin_state,
        lin_norm,
    )
    table, ends, update = lax.optimization_barrier((page_table, lengths, update))
    tags = jnp.concatenate([table[:, :1], ends[:, None]], axis=1)
    swapped = [section_swap(update, k) for k in (0, 1, 3, 2)]
    one_share, packed, key_new, value_new = project(
        tags, swapped, norm_gain, query_key_w, value_w
    )
    asked = [packed] + [z_shift(packed, k) for k in (1, 7, 2)]
    one_back = lax.ppermute(one_share, "section", [(1, 0)])
    own_query, one_back = lax.optimization_barrier((packed, one_back))
    own = own_attention(page_table, lengths, own_query, key_new, value_new, own_pages)
    asked, own = lax.optimization_barrier((asked, own))
    answers = prompt_attention(asked, near_pages, far_pages)
    parts = [answers[0]] + [z_shift(answers[at], -k) for at, k in ((1, 1), (2, 7), (3, 2))]
    slabs = combine(own, parts, out_w)
    section_index = lax.axis_index("section")
    total = one_share.astype(jnp.float32) + slabs[0]
    for piece in [head_shift(slabs[k], k) for k in (1, 3, 2)]:
        total = total + piece
    output = jnp.where(section_index == 0, one_back, total.astype(jnp.bfloat16))
    return output[None]


def solution(mesh):
    placed = (
        P("req", "head"),
        P("section", None),
        P(None, "head"),
        P(None, "head"),
        P("section", None, "head"),
        P("section", "head", None),
        P(None, "head"),
        P("req", None, "head"),
        P("req", "head", None, None),
        P("req", "head", None),
        P("req", None, None, "head"),
        P("req", None, None, "head"),
        P("req", None),
        P("req"),
    )
    return jax.shard_map(
        body, mesh=mesh, in_specs=placed, out_specs=P("section", "req", "head"), check_vma=False
    )
```

```python
import jax
import jax.numpy as jnp
from jax import lax
from jax.experimental import pallas as pl
from jax.experimental.pallas import tpu as pltpu
from jax.sharding import PartitionSpec as P

HD = 112
FEAT = 16
WINDOW = 64
PAGE = 128
HALF = 64
MAXP = 256
GROUPS = 32
XN = 4
ZN = 8
LANES = 512
TAYLOR = 273
TAYLOR_LANES = 384
SPREAD = 1152

EPSILON = 1e-06
MASKED = -1e30


def head_shift(value, steps):
    count = lax.axis_size("head")
    return lax.ppermute(value, "head", [(i, (i + steps) % count) for i in range(count)])


def z_shift(value, steps):
    return lax.ppermute(
        value,
        "req",
        [(z * XN + i, (z + steps) % ZN * XN + i) for z in range(ZN) for i in range(XN)],
    )


def x_shift(value, steps):
    return lax.ppermute(
        value,
        "req",
        [(z * XN + i, z * XN + (i + steps) % XN) for z in range(ZN) for i in range(XN)],
    )


def section_swap(value, steps):
    count = lax.axis_size("head")
    there = [(i, count + (i + steps) % count) for i in range(count)]
    return lax.ppermute(value, ("section", "head"), there + [(b, a) for a, b in there])


VMEM = pl.BlockSpec(memory_space=pltpu.VMEM)
SMEM = pl.BlockSpec(memory_space=pltpu.SMEM)
HBM = pl.BlockSpec(memory_space=pltpu.HBM)
FLAT = (((1,), (1,)), ((), ()))


def normed_rows(values, gain_row):
    factor = lax.rsqrt(jnp.mean(values * values, axis=-1, keepdims=True) + EPSILON)
    return (values * factor * gain_row).astype(jnp.bfloat16)


def lanes_of(shape):
    return lax.broadcasted_iota(jnp.int32, shape, len(shape) - 1)


def in_head(lane, h):
    return (lane >= h * HD) & (lane < (h + 1) * HD)


def place():
    return lax.axis_index("section"), lax.axis_index("req"), lax.axis_index("head")


def kernel_call(
    kernel,
    section,
    name,
    out_shape,
    in_specs,
    scratch_shapes,
    args,
    vmem=10 << 20,
    cost=None,
    elsewhere=None,
):
    def run(*refs):
        ids = place()

        @pl.when(ids[0] == section)
        def _():
            kernel(ids, *refs)

        if elsewhere is not None:

            @pl.when(ids[0] != section)
            def _():
                elsewhere(ids, *refs)

    args = [
        pltpu.with_memory_space_constraint(arg, pltpu.HBM) if spec is HBM else arg
        for arg, spec in zip(args, in_specs, strict=True)
    ]
    return pl.pallas_call(
        run,
        out_shape=out_shape,
        in_specs=in_specs,
        out_specs=jax.tree.map(lambda _: VMEM, out_shape),
        scratch_shapes=scratch_shapes,
        compiler_params=pltpu.CompilerParams(vmem_limit_bytes=vmem),
        cost_estimate=cost,
        name=name,
    )(*args)


def expansion(features, width, repeat):
    lane = lax.broadcasted_iota(jnp.int32, (features, 2 * width), 1)
    source = lax.broadcasted_iota(jnp.int32, (features, 2 * width), 0)
    left = lane < width
    at = jnp.where(left, lane, lane - width) >> (repeat.bit_length() - 1)
    linear = left & (at > 0) & (at <= FEAT) & (source == at - 1)
    pair = at - (FEAT + 1)
    wanted = jnp.where(left, pair >> 4, pair & (FEAT - 1))
    quad = (pair >= 0) & (pair < FEAT * FEAT) & (source == wanted)
    return jnp.where(linear | quad, 1.0, 0.0).astype(jnp.bfloat16)


def taylor_rows(left, right, feature):
    scale = FEAT ** (-0.25)
    left, right = left * scale, right * scale
    return jnp.where(
        feature == 0, 1.0, jnp.where(feature <= FEAT, left, left * right * 0.5**0.5)
    )


def linear_kernel(
    ids,
    t0,
    t1,
    t2,
    t3,
    gain,
    feature_w,
    state,
    lin_norm,
    conv_w,
    conv_state,
    value_w,
    out_w,
    update,
):
    rows, share = t0.shape
    heads = share // HD
    span = TAYLOR * heads
    by_state = expansion(128, SPREAD, heads)
    by_norm = expansion(128, TAYLOR_LANES, 1)
    expand = jnp.concatenate([by_state, by_norm], axis=1)

    own = ids[2]
    got = [ref[...].astype(jnp.float32) for ref in (t0, t1, t3, t2)]
    whole = []
    for place in range(heads):
        piece = got[0]
        for back in range(1, heads):
            piece = jnp.where(((own - back) & (heads - 1)) == place, got[back], piece)
        whole.append(piece)
    tokens = jnp.concatenate(whole, axis=1)
    normed = normed_rows(tokens, gain[...])
    feats = jnp.dot(normed, feature_w[...], preferred_element_type=jnp.float32)
    by_head = jnp.concatenate(
        [feats] + [pltpu.roll(feats, 128 - 2 * FEAT * h, 1) for h in range(1, heads)], axis=0
    )
    high = by_head.astype(jnp.bfloat16)
    rest = by_head - high.astype(jnp.float32)
    middle = rest.astype(jnp.bfloat16)
    low = (rest - middle.astype(jnp.float32)).astype(jnp.bfloat16)
    spread = jnp.dot(
        jnp.concatenate([high, middle, low], axis=0), expand, preferred_element_type=jnp.float32
    )
    count = heads * rows
    spread = spread[:count] + spread[count : 2 * count] + spread[2 * count :]
    lane = lanes_of((count, SPREAD))
    head = lax.broadcasted_iota(jnp.int32, (count, SPREAD), 0) >> 3
    query_wide = taylor_rows(spread[:, :SPREAD], spread[:, SPREAD : 2 * SPREAD], lane >> 2)
    query_wide = jnp.where(((lane & (heads - 1)) == head) & (lane < span), query_wide, 0.0)
    query_feats = taylor_rows(
        spread[:, 2 * SPREAD : 2 * SPREAD + TAYLOR_LANES],
        spread[:, 2 * SPREAD + TAYLOR_LANES :],
        lanes_of((count, TAYLOR_LANES)),
    )[:, :TAYLOR]
    both = by_head * pltpu.roll(by_head, 128 - FEAT, 1)
    near = jnp.sum(
        jnp.where(lanes_of(both.shape) < FEAT, both, 0.0), axis=-1, keepdims=True
    ) * FEAT ** (-0.5)
    intersection = 1.0 + near + 0.5 * near * near

    length = span + 12
    queries = []
    for shift in range(0, 16, 4):
        moved = query_wide if shift == 0 else pltpu.roll(query_wide, shift, 1)
        queries.append(moved[:, :length].astype(jnp.bfloat16))
    row = lax.broadcasted_iota(jnp.int32, (count, HD), 0) & (rows - 1)
    found = jnp.zeros((count, HD), jnp.float32)
    for r in range(rows):
        first = span * r
        shift = first % 16
        product = jnp.dot(
            queries[shift // 4],
            state[first - shift : first - shift + length, :],
            preferred_element_type=jnp.float32,
        )
        found = jnp.where(row == r, product, found)
    fresh = lax.dot_general(normed, value_w[...], FLAT, preferred_element_type=jnp.float32)
    older = conv_state[...].astype(jnp.float32)
    mixed = conv_w[0:1] * older[:, 0] + conv_w[1:2] * older[:, 1] + conv_w[2:3] * fresh
    total = tokens * 0.25
    for h in range(heads):
        here = slice(h * rows, (h + 1) * rows)
        denominator = (
            jnp.sum(query_feats[here] * lin_norm[:, h, :], axis=-1, keepdims=True)
            + intersection[here]
        )
        attended = (
            (found[here] + intersection[here] * mixed[:, h * HD : (h + 1) * HD]) / denominator
        ).astype(jnp.bfloat16)
        total = total + jnp.dot(
            attended, out_w[h * HD : (h + 1) * HD, :], preferred_element_type=jnp.float32
        )
    update[...] = total


def linear_layer(pieces, near):
    return kernel_call(
        linear_kernel,
        0,
        "linear_layer",
        jax.ShapeDtypeStruct((pieces[0].shape[0], near["out_w"].shape[1]), jnp.float32),
        [VMEM] * 12,
        [],
        (*pieces, *(near[name] for name in LINEAR_NEAR)),
    )


def project_kernel(
    ids,
    tags,
    p0,
    p1,
    p2,
    p3,
    gain,
    v_w,
    qk_w,
    one,
    asked,
    key_new,
    value_new,
):
    rows, share = one.shape
    heads = share // HD
    layer_one = (p0[...] + p1[...] + p2[...] + p3[...]).astype(jnp.bfloat16)
    rounded = layer_one.astype(jnp.float32)
    mine = rounded[:, :share]
    for h in range(1, heads):
        mine = jnp.where(ids[2] == h, rounded[:, h * share : (h + 1) * share], mine)
    one[...] = mine.astype(jnp.bfloat16)
    normed = normed_rows(rounded, gain[...])
    value_new[...] = lax.dot_general(
        normed, v_w[...], FLAT, preferred_element_type=jnp.float32
    ).astype(jnp.bfloat16)
    query_key = jnp.dot(normed, qk_w[...], preferred_element_type=jnp.float32)
    width = query_key.shape[1]
    lane = lanes_of((rows, LANES))
    query = jnp.where(in_head(lane, 0), query_key[:, :LANES], 0.0)
    key = query
    for h in range(heads):
        if h:
            moved = pltpu.roll(query_key, width - h * HD, 1)[:, :LANES]
            query = jnp.where(in_head(lane, h), moved, query)
        moved = pltpu.roll(query_key, width - (h + 1) * HD, 1)[:, :LANES]
        key = jnp.where(in_head(lane, h), moved, key)
    group = tags[:, 0:1].astype(jnp.float32)
    start = jnp.minimum(tags[:, 1:2] - WINDOW, PAGE).astype(jnp.float32)
    query = jnp.where(lane == share, group, query)
    query = jnp.where(lane == share + 1, start, query)
    asked[...] = query.astype(jnp.bfloat16)
    key_new[...] = key[:, :share].astype(jnp.bfloat16)


def project(tags, pieces, near):
    rows = pieces[0].shape[0]
    share = near["value_w"].shape[0]
    return kernel_call(
        project_kernel,
        1,
        "project",
        [
            jax.ShapeDtypeStruct((rows, share), jnp.bfloat16),
            jax.ShapeDtypeStruct((rows, LANES), jnp.bfloat16),
            jax.ShapeDtypeStruct((rows, share), jnp.bfloat16),
            jax.ShapeDtypeStruct((rows, share), jnp.bfloat16),
        ],
        [VMEM] * 8,
        [],
        (tags, *pieces, near["gain"], near["value_w"], near["query_key_w"]),
    )


def window_pages(lengths, r):
    length = lengths[r]
    return jnp.maximum((length - WINDOW) // PAGE, 1), jnp.maximum((length - 2) // PAGE, 1)


def own_kernel(
    ids, lengths, asked, key_new, value_new, pages, summed_out, highest_out, total_out
):
    rows, share = key_new.shape
    bounds = [(lengths[r], *window_pages(lengths, r)) for r in range(rows)]
    head = lax.broadcasted_iota(jnp.int32, (8, share), 0)
    lane = lanes_of((8, share))
    mine = (lane >= head * HD) & (lane < (head + 1) * HD)
    scale = HD ** (-0.5)
    query = asked[:, :share].astype(jnp.float32)
    new_key = key_new[...].astype(jnp.float32)
    new_value = value_new[...].astype(jnp.float32)
    wide = jnp.concatenate([jnp.where(mine, query[r : r + 1], 0.0) for r in range(rows)], axis=0)
    keys = jnp.concatenate(
        [jnp.broadcast_to(new_key[r : r + 1], (8, share)) for r in range(rows)], axis=0
    )
    new_score = jnp.sum(wide * keys, axis=-1, keepdims=True) * scale
    token = lanes_of((8 * rows, 2 * PAGE))
    request = lax.broadcasted_iota(jnp.int32, (8 * rows, 2 * PAGE), 0) >> 3
    length = jnp.zeros(token.shape, jnp.int32)
    base = jnp.zeros(token.shape, jnp.int32)
    for r in range(rows):
        length = jnp.where(request == r, bounds[r][0], length)
        second = jnp.where(bounds[r][1] != bounds[r][2], bounds[r][2] - 1, -MAXP) * PAGE
        base = jnp.where(request == r, jnp.where(token < PAGE, bounds[r][1] * PAGE, second), base)
    position = base + token
    usable = (position >= length - WINDOW) & (position <= length - 2)
    scores = []
    for r in range(rows):
        low = wide[8 * r : 8 * r + 8].astype(jnp.bfloat16)
        scores.append(
            jnp.concatenate(
                [
                    jnp.dot(low, pages[r, slot, 0], preferred_element_type=jnp.float32)
                    for slot in range(2)
                ],
                axis=1,
            )
        )
    scores = jnp.where(usable, jnp.concatenate(scores, axis=0) * scale, MASKED)
    highest = jnp.maximum(jnp.max(scores, axis=-1, keepdims=True), new_score)
    exps = jnp.where(usable, jnp.exp(scores - highest), 0.0)
    exp_new = jnp.exp(new_score - highest)
    total = jnp.sum(exps, axis=-1, keepdims=True) + exp_new
    for r in range(rows):
        here = slice(8 * r, 8 * r + 8)
        low = exps[here].astype(jnp.bfloat16)
        found = exp_new[here] * new_value[r : r + 1]
        for slot in range(2):
            found = found + lax.dot_general(
                low[:, slot * PAGE : (slot + 1) * PAGE],
                pages[r, slot, 1],
                FLAT,
                preferred_element_type=jnp.float32,
            )
        for ref, value in (
            (summed_out, found),
            (highest_out, highest[here]),
            (total_out, total[here]),
        ):
            ref[r : r + 1, :] = jnp.sum(jnp.where(mine, value, 0.0), axis=0, keepdims=True)


def own_attention(lengths, asked, key_new, value_new, near):
    rows, share = key_new.shape
    return kernel_call(
        own_kernel,
        1,
        "own_attention",
        [jax.ShapeDtypeStruct((rows, share), jnp.float32)] * 3,
        [SMEM] + [VMEM] * 4,
        [],
        (lengths, asked, key_new, value_new, near["own_pages"]),
    )


def prompt_kernel(ids, a0, a1, a2, a3, near_pages, far_pages, o0, o1, o2, o3):
    rows = a0.shape[0]
    share = near_pages.shape[1]
    heads = share // HD
    pages = jnp.concatenate(
        [near_pages[i] for i in range(XN)] + [far_pages[i] for i in range(XN)], axis=1
    )
    asked = jnp.concatenate([ref[...].astype(jnp.float32) for ref in (a0, a1, a2, a3)], axis=0)
    count = asked.shape[0]
    lane = lanes_of(asked.shape)
    group = jnp.sum(jnp.where(lane == share, asked, 0.0), axis=-1, keepdims=True)
    start = jnp.sum(jnp.where(lane == share + 1, asked, 0.0), axis=-1, keepdims=True)
    group, start = group.astype(jnp.int32), start.astype(jnp.int32)
    query = jnp.concatenate(
        [jnp.where(in_head(lane, h), asked, 0.0)[:, :share] for h in range(heads)], axis=0
    ).astype(jnp.bfloat16)
    scores = jnp.dot(query, pages, preferred_element_type=jnp.float32) * HD ** (-0.5)
    token = lanes_of((count, 2 * XN * PAGE))
    z, x = ids[1] // XN, ids[1] % XN
    slot = token >> 7
    slot_group = jnp.where(slot < XN, z, (z + ZN // 2) & (ZN - 1)) * XN
    slot_group = slot_group + ((slot + x + XN - 1) & (XN - 1))
    offset = token & (PAGE - 1)
    usable = (slot_group == group) & (offset < HALF) & (offset + HALF >= start)
    lane = lanes_of((count, share))
    stat_lane = lanes_of((count, 128))
    weights = []
    stats = jnp.zeros((count, 128), jnp.float32)
    for h in range(heads):
        here = jnp.where(usable, scores[h * count : (h + 1) * count], MASKED)
        highest = jnp.max(here, axis=-1, keepdims=True)
        exps = jnp.where(usable, jnp.exp(here - highest), 0.0)
        total = jnp.sum(exps, axis=-1, keepdims=True)
        stats = jnp.where(stat_lane == h, highest, stats)
        stats = jnp.where(stat_lane == heads + h, total, stats)
        weights.append(pltpu.roll(exps, HALF, 1))
    found = lax.dot_general(
        jnp.concatenate(weights, axis=0).astype(jnp.bfloat16),
        pages,
        FLAT,
        preferred_element_type=jnp.float32,
    )
    summed = jnp.zeros((count, share), jnp.float32)
    for h in range(heads):
        summed = jnp.where(in_head(lane, h), found[h * count : (h + 1) * count], summed)
    for at, ref in enumerate((o0, o1, o2, o3)):
        ref[:, :share] = summed[at * rows : (at + 1) * rows]
        ref[:, share:LANES] = jnp.zeros((rows, LANES - share), jnp.float32)
        ref[:, LANES:] = stats[at * rows : (at + 1) * rows]


def prompt_attention(asked, near_pages, far_pages):
    rows = asked[0].shape[0]
    return kernel_call(
        prompt_kernel,
        1,
        "prompt_attention",
        [jax.ShapeDtypeStruct((rows, LANES + 128), jnp.float32)] * 4,
        [VMEM] * 6,
        [],
        (*asked, near_pages, far_pages),
    )


def combine_kernel(ids, summed, highest, total, r0, r1, r2, r3, out_w, s0, s1, s2, s3):
    rows, share = summed.shape
    heads = share // HD
    refs = (r0, r1, r2, r3)
    prompt_summed = sum(ref[:, :share] for ref in refs)
    stats = [ref[:, LANES:] for ref in refs]
    top = jnp.maximum(jnp.maximum(stats[0], stats[1]), jnp.maximum(stats[2], stats[3]))
    added = stats[0] + stats[1] + stats[2] + stats[3]
    lane = lanes_of((rows, share))
    prompt_highest = jnp.zeros((rows, share), jnp.float32)
    prompt_total = jnp.zeros((rows, share), jnp.float32)
    for h in range(heads):
        here = in_head(lane, h)
        prompt_highest = jnp.where(here, top[:, h : h + 1], prompt_highest)
        prompt_total = jnp.where(here, added[:, heads + h : heads + h + 1], prompt_total)
    peak = jnp.maximum(highest[...], prompt_highest)
    own_factor = jnp.exp(highest[...] - peak)
    prompt_factor = jnp.exp(prompt_highest - peak)
    whole = total[...] * own_factor + prompt_total * prompt_factor
    attended = (summed[...] * own_factor + prompt_summed * prompt_factor) / whole
    second = jnp.dot(attended.astype(jnp.bfloat16), out_w[...], preferred_element_type=jnp.float32)
    for steps, ref in enumerate((s0, s1, s2, s3)):
        slab = second[:, :share]
        for h in range(1, heads):
            slab = jnp.where(
                ((ids[2] + steps) & (heads - 1)) == h, second[:, h * share : (h + 1) * share], slab
            )
        ref[...] = slab


def combine(own, parts, near):
    return kernel_call(
        combine_kernel,
        1,
        "combine",
        [jax.ShapeDtypeStruct(own[0].shape, jnp.float32)] * 4,
        [VMEM] * 8,
        [],
        (*own, *parts, near["out_w"]),
    )


LINEAR_NEAR = (
    "gain",
    "feature_w",
    "state",
    "lin_norm",
    "conv_w",
    "conv_state",
    "value_w",
    "out_w",
)
SHARED_NEAR = ("gain", "value_w", "out_w")


def bring_near(arrays):
    names = list(arrays)
    count = len(names)
    both = [at for at, name in enumerate(names) if name in SHARED_NEAR]

    def copy_some(chosen, refs):
        sems = refs[-1]
        copies = [
            pltpu.make_async_copy(refs[at], refs[count + at], sems.at[at]) for at in chosen
        ]
        for copy in copies:
            copy.start()
        for copy in copies:
            copy.wait()

    near = kernel_call(
        lambda ids, *refs: copy_some(range(count), refs),
        0,
        "bring_near",
        [jax.ShapeDtypeStruct(array.shape, array.dtype) for array in arrays.values()],
        [HBM] * count,
        [pltpu.SemaphoreType.DMA((count,))],
        tuple(arrays.values()),
        4 << 20,
        bytes_only(arrays.values()),
        lambda ids, *refs: copy_some(both, refs),
    )
    return dict(zip(names, near))


def bytes_only(arrays):
    moved = sum(array.size * array.dtype.itemsize for array in arrays)
    return pl.CostEstimate(flops=0, bytes_accessed=2 * moved, transcendentals=0)


def window_kernel(
    ids, table, lengths, query_key_hbm, own_hbm, query_key_near, own_near, key_sem, sems
):
    rows = lengths.shape[0]
    total = own_hbm.shape[0]
    copies = [pltpu.make_async_copy(query_key_hbm, query_key_near, key_sem)]
    for r in range(rows):
        for slot, logical in enumerate(window_pages(lengths, r)):
            page = jnp.clip(table[r, logical] - GROUPS - ids[1] * total, 0, total - 1)
            copies.append(
                pltpu.make_async_copy(own_hbm.at[page], own_near.at[r, slot], sems.at[r, slot])
            )
    for copy in copies:
        copy.start()
    for copy in copies:
        copy.wait()


def bring_windows(table, lengths, query_key_w, own_pages):
    rows = lengths.shape[0]
    windows = jax.ShapeDtypeStruct((rows, 2) + own_pages.shape[1:], own_pages.dtype)
    return kernel_call(
        window_kernel,
        1,
        "bring_windows",
        [jax.ShapeDtypeStruct(query_key_w.shape, query_key_w.dtype), windows],
        [SMEM] * 2 + [HBM] * 2,
        [pltpu.SemaphoreType.DMA, pltpu.SemaphoreType.DMA((rows, 2))],
        (table, lengths, query_key_w, own_pages),
        4 << 20,
        bytes_only([query_key_w, windows]),
    )


def page_kernel(ids, pages_hbm, page, pages, sem):
    copy = pltpu.make_async_copy(pages_hbm.at[0], pages, sem)
    copy.start()
    copy.wait()
    lane = lanes_of(page.shape)
    keys = pltpu.roll(pages[0].astype(jnp.float32), HALF, 1)
    page[...] = jnp.where(lane < HALF, keys, pages[1].astype(jnp.float32)).astype(jnp.bfloat16)


def window_page(prompt_pages):
    shape = prompt_pages.shape[1:]
    return kernel_call(
        page_kernel,
        1,
        "window_page",
        jax.ShapeDtypeStruct(shape[1:], jnp.bfloat16),
        [HBM],
        [pltpu.VMEM(shape, jnp.bfloat16), pltpu.SemaphoreType.DMA],
        (prompt_pages,),
        cost=pl.CostEstimate(flops=0, bytes_accessed=16 << 20, transcendentals=0),
    )


def body(
    tokens,
    norm_gain,
    feature_w,
    query_key_w,
    value_w,
    out_w,
    conv_w,
    conv_state,
    lin_state,
    lin_norm,
    own_pages,
    prompt_pages,
    page_table,
    lengths,
):
    pages_first = prompt_pages.transpose(0, 1, 3, 2)
    near = bring_near(
        {
            "gain": norm_gain,
            "feature_w": feature_w,
            "state": lin_state.transpose(0, 2, 1, 3).reshape(-1, HD),
            "lin_norm": lin_norm,
            "conv_w": conv_w,
            "conv_state": conv_state,
            "value_w": value_w.transpose(0, 2, 1)[0],
            "out_w": out_w[0],
        }
    )

    received = [head_shift(tokens, k) for k in (1, 3, 2)]
    page = window_page(pages_first)
    near, received = lax.optimization_barrier((near, received))
    page, received = lax.optimization_barrier((page, received))
    row_pages = [x_shift(page, k) for k in (1, 3, 2)]
    update = linear_layer([tokens] + received, near)
    row_pages, update = lax.optimization_barrier((row_pages, update))
    near_pages = jnp.stack([row_pages[0], page, row_pages[1], row_pages[2]])
    far_pages = z_shift(near_pages, ZN // 2)
    own_pages = own_pages.transpose(0, 1, 3, 2)
    query_key_w, own_pages, page_table, ends, update = lax.optimization_barrier(
        (query_key_w, own_pages, page_table, lengths, update)
    )
    near["query_key_w"], near["own_pages"] = bring_windows(
        page_table, ends, query_key_w, own_pages
    )
    tags = jnp.concatenate([page_table[:, :1], ends[:, None]], axis=1)
    swapped = [section_swap(update, k) for k in (0, 1, 3, 2)]
    one_share, packed, key_new, value_new = project(tags, swapped, near)
    asked = [packed] + [z_shift(packed, k) for k in (1, 7, 2)]
    own = own_attention(lengths, packed, key_new, value_new, near)
    asked, own = lax.optimization_barrier((asked, own))
    answers = prompt_attention(asked, near_pages, far_pages)
    answers, one_share = lax.optimization_barrier((answers, one_share))
    parts = [answers[0]] + [z_shift(answers[at], -k) for at, k in ((1, 1), (2, 7), (3, 2))]
    one_back = lax.ppermute(one_share, "section", [(1, 0), (0, 1)])
    parts, one_back = lax.optimization_barrier((parts, one_back))
    slabs = combine(own, parts, near)
    section_index = lax.axis_index("section")
    total = one_share.astype(jnp.float32) + slabs[0]
    for piece in [head_shift(slabs[k], k) for k in (1, 3, 2)]:
        total = total + piece
    output = jnp.where(section_index == 0, one_back, total.astype(jnp.bfloat16))
    return output[None]


def solution(mesh):
    placed = (
        P("req", "head"),
        P("section", None),
        P(None, "head"),
        P(None, "head"),
        P("section", None, "head"),
        P("section", "head", None),
        P(None, "head"),
        P("req", None, "head"),
        P("req", "head", None, None),
        P("req", "head", None),
        P("req", None, None, "head"),
        P("req", None, None, "head"),
        P("req", None),
        P("req"),
    )
    return jax.shard_map(
        body, mesh=mesh, in_specs=placed, out_specs=P("section", "req", "head"), check_vma=False
    )
```

```python
import jax
import jax.numpy as jnp
from jax import lax
from jax.experimental import pallas as pl
from jax.experimental.pallas import tpu as pltpu
from jax.sharding import PartitionSpec as P

HD = 112
FEAT = 16
WINDOW = 64
PAGE = 128
HALF = 64
MAXP = 256
GROUPS = 32
XN = 4
ZN = 8
LANES = 512
TAYLOR = 273
TAYLOR_LANES = 384
SPREAD = 1152

EPSILON = 1e-06
MASKED = -1e30


def shift_on(section, value, axis, moves):
    count = lax.axis_size(axis)
    pairs = [(section * count + i, section * count + j) for i, j in moves]
    pairs += [((1 - section) * count + i,) * 2 for i in range(count)]
    return lax.ppermute(value, ("section", axis), pairs)


def head_shift(section, value, steps):
    count = lax.axis_size("head")
    return shift_on(section, value, "head", [(i, (i + steps) % count) for i in range(count)])


def z_shift(value, steps):
    return shift_on(
        1,
        value,
        "req",
        [(z * XN + i, (z + steps) % ZN * XN + i) for z in range(ZN) for i in range(XN)],
    )


def x_shift(value, steps):
    return shift_on(
        1,
        value,
        "req",
        [(z * XN + i, z * XN + (i + steps) % XN) for z in range(ZN) for i in range(XN)],
    )


def section_swap(value, steps):
    count = lax.axis_size("head")
    there = [(i, count + (i + steps) % count) for i in range(count)]
    return lax.ppermute(value, ("section", "head"), there + [(b, a) for a, b in there])


VMEM = pl.BlockSpec(memory_space=pltpu.VMEM)
SMEM = pl.BlockSpec(memory_space=pltpu.SMEM)
HBM = pl.BlockSpec(memory_space=pltpu.HBM)
FLAT = (((1,), (1,)), ((), ()))


def normed_rows(values, gain_row):
    factor = lax.rsqrt(jnp.mean(values * values, axis=-1, keepdims=True) + EPSILON)
    return (values * factor * gain_row).astype(jnp.bfloat16)


def lanes_of(shape):
    return lax.broadcasted_iota(jnp.int32, shape, len(shape) - 1)


def in_head(lane, h):
    return (lane >= h * HD) & (lane < (h + 1) * HD)


def place():
    return lax.axis_index("section"), lax.axis_index("req"), lax.axis_index("head")


def kernel_call(
    kernel,
    section,
    name,
    out_shape,
    in_specs,
    scratch_shapes,
    args,
    vmem=10 << 20,
    cost=None,
    elsewhere=None,
):
    def run(*refs):
        ids = place()

        @pl.when(ids[0] == section)
        def _():
            kernel(ids, *refs)

        if elsewhere is not None:

            @pl.when(ids[0] != section)
            def _():
                elsewhere(ids, *refs)

    args = [
        pltpu.with_memory_space_constraint(arg, pltpu.HBM) if spec is HBM else arg
        for arg, spec in zip(args, in_specs, strict=True)
    ]
    return pl.pallas_call(
        run,
        out_shape=out_shape,
        in_specs=in_specs,
        out_specs=jax.tree.map(lambda _: VMEM, out_shape),
        scratch_shapes=scratch_shapes,
        compiler_params=pltpu.CompilerParams(vmem_limit_bytes=vmem),
        cost_estimate=cost,
        name=name,
    )(*args)


def expansion(features, width, repeat):
    lane = lax.broadcasted_iota(jnp.int32, (features, 2 * width), 1)
    source = lax.broadcasted_iota(jnp.int32, (features, 2 * width), 0)
    left = lane < width
    at = jnp.where(left, lane, lane - width) >> (repeat.bit_length() - 1)
    linear = left & (at > 0) & (at <= FEAT) & (source == at - 1)
    pair = at - (FEAT + 1)
    wanted = jnp.where(left, pair >> 4, pair & (FEAT - 1))
    quad = (pair >= 0) & (pair < FEAT * FEAT) & (source == wanted)
    return jnp.where(linear | quad, 1.0, 0.0).astype(jnp.bfloat16)


def taylor_rows(left, right, feature):
    scale = FEAT ** (-0.25)
    left, right = left * scale, right * scale
    return jnp.where(
        feature == 0, 1.0, jnp.where(feature <= FEAT, left, left * right * 0.5**0.5)
    )


def linear_kernel(
    ids,
    t0,
    t1,
    t2,
    t3,
    gain,
    feature_w,
    state,
    lin_norm,
    conv_w,
    conv_state,
    value_w,
    out_w,
    update,
):
    rows, share = t0.shape
    heads = share // HD
    span = TAYLOR * heads
    by_state = expansion(128, SPREAD, heads)
    by_norm = expansion(128, TAYLOR_LANES, 1)
    expand = jnp.concatenate([by_state, by_norm], axis=1)

    own = ids[2]
    got = [ref[...].astype(jnp.float32) for ref in (t0, t1, t3, t2)]
    whole = []
    for place in range(heads):
        piece = got[0]
        for back in range(1, heads):
            piece = jnp.where(((own - back) & (heads - 1)) == place, got[back], piece)
        whole.append(piece)
    tokens = jnp.concatenate(whole, axis=1)
    normed = normed_rows(tokens, gain[...])
    feats = jnp.dot(normed, feature_w[...], preferred_element_type=jnp.float32)
    by_head = jnp.concatenate(
        [feats] + [pltpu.roll(feats, 128 - 2 * FEAT * h, 1) for h in range(1, heads)], axis=0
    )
    high = by_head.astype(jnp.bfloat16)
    rest = by_head - high.astype(jnp.float32)
    middle = rest.astype(jnp.bfloat16)
    low = (rest - middle.astype(jnp.float32)).astype(jnp.bfloat16)
    spread = jnp.dot(
        jnp.concatenate([high, middle, low], axis=0), expand, preferred_element_type=jnp.float32
    )
    count = heads * rows
    spread = spread[:count] + spread[count : 2 * count] + spread[2 * count :]
    lane = lanes_of((count, SPREAD))
    head = lax.broadcasted_iota(jnp.int32, (count, SPREAD), 0) >> 3
    query_wide = taylor_rows(spread[:, :SPREAD], spread[:, SPREAD : 2 * SPREAD], lane >> 2)
    query_wide = jnp.where(((lane & (heads - 1)) == head) & (lane < span), query_wide, 0.0)
    query_feats = taylor_rows(
        spread[:, 2 * SPREAD : 2 * SPREAD + TAYLOR_LANES],
        spread[:, 2 * SPREAD + TAYLOR_LANES :],
        lanes_of((count, TAYLOR_LANES)),
    )[:, :TAYLOR]
    both = by_head * pltpu.roll(by_head, 128 - FEAT, 1)
    near = jnp.sum(
        jnp.where(lanes_of(both.shape) < FEAT, both, 0.0), axis=-1, keepdims=True
    ) * FEAT ** (-0.5)
    intersection = 1.0 + near + 0.5 * near * near

    length = span + 12
    queries = []
    for shift in range(0, 16, 4):
        moved = query_wide if shift == 0 else pltpu.roll(query_wide, shift, 1)
        queries.append(moved[:, :length].astype(jnp.bfloat16))
    row = lax.broadcasted_iota(jnp.int32, (count, HD), 0) & (rows - 1)
    found = jnp.zeros((count, HD), jnp.float32)
    for r in range(rows):
        first = span * r
        shift = first % 16
        product = jnp.dot(
            queries[shift // 4],
            state[first - shift : first - shift + length, :],
            preferred_element_type=jnp.float32,
        )
        found = jnp.where(row == r, product, found)
    fresh = lax.dot_general(normed, value_w[...], FLAT, preferred_element_type=jnp.float32)
    older = conv_state[...].astype(jnp.float32)
    mixed = conv_w[0:1] * older[:, 0] + conv_w[1:2] * older[:, 1] + conv_w[2:3] * fresh
    total = tokens * 0.25
    for h in range(heads):
        here = slice(h * rows, (h + 1) * rows)
        denominator = (
            jnp.sum(query_feats[here] * lin_norm[:, h, :], axis=-1, keepdims=True)
            + intersection[here]
        )
        attended = (
            (found[here] + intersection[here] * mixed[:, h * HD : (h + 1) * HD]) / denominator
        ).astype(jnp.bfloat16)
        total = total + jnp.dot(
            attended, out_w[h * HD : (h + 1) * HD, :], preferred_element_type=jnp.float32
        )
    update[...] = total


def linear_layer(pieces, near):
    return kernel_call(
        linear_kernel,
        0,
        "linear_layer",
        jax.ShapeDtypeStruct((pieces[0].shape[0], near["out_w"].shape[1]), jnp.float32),
        [VMEM] * 12,
        [],
        (*pieces, *(near[name] for name in LINEAR_NEAR)),
    )


def project_kernel(
    ids,
    tags,
    p0,
    p1,
    p2,
    p3,
    gain,
    v_w,
    qk_w,
    one,
    asked,
    key_new,
    value_new,
):
    rows, share = one.shape
    heads = share // HD
    layer_one = (p0[...] + p1[...] + p2[...] + p3[...]).astype(jnp.bfloat16)
    rounded = layer_one.astype(jnp.float32)
    mine = rounded[:, :share]
    for h in range(1, heads):
        mine = jnp.where(ids[2] == h, rounded[:, h * share : (h + 1) * share], mine)
    one[...] = mine.astype(jnp.bfloat16)
    normed = normed_rows(rounded, gain[...])
    value_new[...] = lax.dot_general(
        normed, v_w[...], FLAT, preferred_element_type=jnp.float32
    ).astype(jnp.bfloat16)
    query_key = jnp.dot(normed, qk_w[...], preferred_element_type=jnp.float32)
    width = query_key.shape[1]
    lane = lanes_of((rows, LANES))
    query = jnp.where(in_head(lane, 0), query_key[:, :LANES], 0.0)
    key = query
    for h in range(heads):
        if h:
            moved = pltpu.roll(query_key, width - h * HD, 1)[:, :LANES]
            query = jnp.where(in_head(lane, h), moved, query)
        moved = pltpu.roll(query_key, width - (h + 1) * HD, 1)[:, :LANES]
        key = jnp.where(in_head(lane, h), moved, key)
    query = jnp.where(lane == share, tags[:, 0:1], query)
    query = jnp.where(lane == share + 1, tags[:, 1:2], query)
    asked[...] = query.astype(jnp.bfloat16)
    key_new[...] = key[:, :share].astype(jnp.bfloat16)


def project(tags, pieces, near):
    rows = pieces[0].shape[0]
    share = near["value_w"].shape[0]
    return kernel_call(
        project_kernel,
        1,
        "project",
        [
            jax.ShapeDtypeStruct((rows, share), jnp.bfloat16),
            jax.ShapeDtypeStruct((rows, LANES), jnp.bfloat16),
            jax.ShapeDtypeStruct((rows, share), jnp.bfloat16),
            jax.ShapeDtypeStruct((rows, share), jnp.bfloat16),
        ],
        [VMEM] * 8,
        [],
        (tags, *pieces, near["gain"], near["value_w"], near["query_key_w"]),
    )


def window_pages(lengths, r):
    length = lengths[r]
    return jnp.maximum((length - WINDOW) // PAGE, 1), jnp.maximum((length - 2) // PAGE, 1)


def own_kernel(
    ids,
    table,
    lengths,
    asked,
    key_new,
    value_new,
    own_pages,
    summed_out,
    highest_out,
    total_out,
    pages,
    sems,
):
    rows, share = key_new.shape
    count = own_pages.shape[0]
    bounds = []
    copies = []
    for r in range(rows):
        first, last = window_pages(lengths, r)
        bounds.append((lengths[r], first, last))
        for slot, logical in enumerate((first, last)):
            page = jnp.clip(table[r, logical] - GROUPS - ids[1] * count, 0, count - 1)
            copies.append(
                pltpu.make_async_copy(own_pages.at[page], pages.at[r, slot], sems.at[r, slot])
            )
            copies[-1].start()
    head = lax.broadcasted_iota(jnp.int32, (8, share), 0)
    lane = lanes_of((8, share))
    mine = (lane >= head * HD) & (lane < (head + 1) * HD)
    scale = HD ** (-0.5)
    query = asked[:, :share].astype(jnp.float32)
    new_key = key_new[...].astype(jnp.float32)
    new_value = value_new[...].astype(jnp.float32)
    wide = jnp.concatenate([jnp.where(mine, query[r : r + 1], 0.0) for r in range(rows)], axis=0)
    keys = jnp.concatenate(
        [jnp.broadcast_to(new_key[r : r + 1], (8, share)) for r in range(rows)], axis=0
    )
    new_score = jnp.sum(wide * keys, axis=-1, keepdims=True) * scale
    token = lanes_of((8 * rows, 2 * PAGE))
    request = lax.broadcasted_iota(jnp.int32, (8 * rows, 2 * PAGE), 0) >> 3
    length = jnp.zeros(token.shape, jnp.int32)
    base = jnp.zeros(token.shape, jnp.int32)
    for r in range(rows):
        length = jnp.where(request == r, bounds[r][0], length)
        second = jnp.where(bounds[r][1] != bounds[r][2], bounds[r][2] - 1, -MAXP) * PAGE
        base = jnp.where(request == r, jnp.where(token < PAGE, bounds[r][1] * PAGE, second), base)
    position = base + token
    usable = (position >= length - WINDOW) & (position <= length - 2)
    scores = []
    for r in range(rows):
        low = wide[8 * r : 8 * r + 8].astype(jnp.bfloat16)
        copies[2 * r].wait()
        copies[2 * r + 1].wait()
        scores.append(
            jnp.concatenate(
                [
                    jnp.dot(low, pages[r, slot, 0], preferred_element_type=jnp.float32)
                    for slot in range(2)
                ],
                axis=1,
            )
        )
    scores = jnp.where(usable, jnp.concatenate(scores, axis=0) * scale, MASKED)
    highest = jnp.maximum(jnp.max(scores, axis=-1, keepdims=True), new_score)
    exps = jnp.where(usable, jnp.exp(scores - highest), 0.0)
    exp_new = jnp.exp(new_score - highest)
    total = jnp.sum(exps, axis=-1, keepdims=True) + exp_new
    for r in range(rows):
        here = slice(8 * r, 8 * r + 8)
        low = exps[here].astype(jnp.bfloat16)
        found = exp_new[here] * new_value[r : r + 1]
        for slot in range(2):
            found = found + lax.dot_general(
                low[:, slot * PAGE : (slot + 1) * PAGE],
                pages[r, slot, 1],
                FLAT,
                preferred_element_type=jnp.float32,
            )
        for ref, value in (
            (summed_out, found),
            (highest_out, highest[here]),
            (total_out, total[here]),
        ):
            ref[r : r + 1, :] = jnp.sum(jnp.where(mine, value, 0.0), axis=0, keepdims=True)


def own_attention(table, lengths, asked, key_new, value_new, own_pages):
    rows, share = key_new.shape
    return kernel_call(
        own_kernel,
        1,
        "own_attention",
        [jax.ShapeDtypeStruct((rows, share), jnp.float32)] * 3,
        [SMEM] * 2 + [VMEM] * 3 + [HBM],
        [
            pltpu.VMEM((rows, 2) + own_pages.shape[1:], jnp.bfloat16),
            pltpu.SemaphoreType.DMA((rows, 2)),
        ],
        (table, lengths, asked, key_new, value_new, own_pages),
    )


def prompt_kernel(ids, a0, a1, a2, a3, near_pages, far_pages, o0, o1, o2, o3):
    rows = a0.shape[0]
    share = near_pages.shape[1]
    heads = share // HD
    pages = jnp.concatenate(
        [near_pages[i] for i in range(XN)] + [far_pages[i] for i in range(XN)], axis=1
    )
    asked = jnp.concatenate([ref[...].astype(jnp.float32) for ref in (a0, a1, a2, a3)], axis=0)
    count = asked.shape[0]
    lane = lanes_of(asked.shape)
    group = jnp.sum(jnp.where(lane == share, asked, 0.0), axis=-1, keepdims=True)
    start = jnp.sum(jnp.where(lane == share + 1, asked, 0.0), axis=-1, keepdims=True)
    group, start = group.astype(jnp.int32), start.astype(jnp.int32)
    query = jnp.concatenate(
        [jnp.where(in_head(lane, h), asked, 0.0)[:, :share] for h in range(heads)], axis=0
    ).astype(jnp.bfloat16)
    scores = jnp.dot(query, pages, preferred_element_type=jnp.float32) * HD ** (-0.5)
    token = lanes_of((count, 2 * XN * PAGE))
    z, x = ids[1] // XN, ids[1] % XN
    slot = token >> 7
    slot_group = jnp.where(slot < XN, z, (z + ZN // 2) & (ZN - 1)) * XN
    slot_group = slot_group + ((slot + x + XN - 1) & (XN - 1))
    offset = token & (PAGE - 1)
    usable = (slot_group == group) & (offset < HALF) & (offset + HALF >= start)
    lane = lanes_of((count, share))
    stat_lane = lanes_of((count, 128))
    weights = []
    stats = jnp.zeros((count, 128), jnp.float32)
    for h in range(heads):
        here = jnp.where(usable, scores[h * count : (h + 1) * count], MASKED)
        highest = jnp.max(here, axis=-1, keepdims=True)
        exps = jnp.where(usable, jnp.exp(here - highest), 0.0)
        total = jnp.sum(exps, axis=-1, keepdims=True)
        stats = jnp.where(stat_lane == h, highest, stats)
        stats = jnp.where(stat_lane == heads + h, total, stats)
        weights.append(pltpu.roll(exps, HALF, 1))
    found = lax.dot_general(
        jnp.concatenate(weights, axis=0).astype(jnp.bfloat16),
        pages,
        FLAT,
        preferred_element_type=jnp.float32,
    )
    summed = jnp.zeros((count, share), jnp.float32)
    for h in range(heads):
        summed = jnp.where(in_head(lane, h), found[h * count : (h + 1) * count], summed)
    for at, ref in enumerate((o0, o1, o2, o3)):
        ref[:, :share] = summed[at * rows : (at + 1) * rows]
        ref[:, share:LANES] = jnp.zeros((rows, LANES - share), jnp.float32)
        ref[:, LANES:] = stats[at * rows : (at + 1) * rows]


def prompt_attention(asked, near_pages, far_pages):
    rows = asked[0].shape[0]
    return kernel_call(
        prompt_kernel,
        1,
        "prompt_attention",
        [jax.ShapeDtypeStruct((rows, LANES + 128), jnp.float32)] * 4,
        [VMEM] * 6,
        [],
        (*asked, near_pages, far_pages),
    )


def combine_kernel(ids, summed, highest, total, r0, r1, r2, r3, out_w, s0, s1, s2, s3):
    rows, share = summed.shape
    heads = share // HD
    refs = (r0, r1, r2, r3)
    prompt_summed = sum(ref[:, :share] for ref in refs)
    stats = [ref[:, LANES:] for ref in refs]
    top = jnp.maximum(jnp.maximum(stats[0], stats[1]), jnp.maximum(stats[2], stats[3]))
    added = stats[0] + stats[1] + stats[2] + stats[3]
    lane = lanes_of((rows, share))
    prompt_highest = jnp.zeros((rows, share), jnp.float32)
    prompt_total = jnp.zeros((rows, share), jnp.float32)
    for h in range(heads):
        here = in_head(lane, h)
        prompt_highest = jnp.where(here, top[:, h : h + 1], prompt_highest)
        prompt_total = jnp.where(here, added[:, heads + h : heads + h + 1], prompt_total)
    peak = jnp.maximum(highest[...], prompt_highest)
    own_factor = jnp.exp(highest[...] - peak)
    prompt_factor = jnp.exp(prompt_highest - peak)
    whole = total[...] * own_factor + prompt_total * prompt_factor
    attended = (summed[...] * own_factor + prompt_summed * prompt_factor) / whole
    second = jnp.dot(attended.astype(jnp.bfloat16), out_w[...], preferred_element_type=jnp.float32)
    for steps, ref in enumerate((s0, s1, s2, s3)):
        slab = second[:, :share]
        for h in range(1, heads):
            slab = jnp.where(
                ((ids[2] + steps) & (heads - 1)) == h, second[:, h * share : (h + 1) * share], slab
            )
        ref[...] = slab


def combine(own, parts, near):
    return kernel_call(
        combine_kernel,
        1,
        "combine",
        [jax.ShapeDtypeStruct(own[0].shape, jnp.float32)] * 4,
        [VMEM] * 8,
        [],
        (*own, *parts, near["out_w"]),
    )


LINEAR_NEAR = (
    "gain",
    "feature_w",
    "state",
    "lin_norm",
    "conv_w",
    "conv_state",
    "value_w",
    "out_w",
)
SHARED_NEAR = ("gain", "value_w", "out_w")


def bring_near(arrays):
    names = list(arrays)
    count = len(names)
    both = [at for at, name in enumerate(names) if name in SHARED_NEAR]

    def copy_some(chosen, refs):
        sems = refs[-1]
        copies = [
            pltpu.make_async_copy(refs[at], refs[count + at], sems.at[at]) for at in chosen
        ]
        for copy in copies:
            copy.start()
        for copy in copies:
            copy.wait()

    near = kernel_call(
        lambda ids, *refs: copy_some(range(count), refs),
        0,
        "bring_near",
        [jax.ShapeDtypeStruct(array.shape, array.dtype) for array in arrays.values()],
        [HBM] * count,
        [pltpu.SemaphoreType.DMA((count,))],
        tuple(arrays.values()),
        4 << 20,
        bytes_only(arrays.values()),
        lambda ids, *refs: copy_some(both, refs),
    )
    return dict(zip(names, near))


def bytes_only(arrays):
    moved = sum(array.size * array.dtype.itemsize for array in arrays)
    return pl.CostEstimate(flops=0, bytes_accessed=2 * moved, transcendentals=0)


def query_kernel(ids, table, lengths, query_key_hbm, query_key_near, tags, sem):
    copy = pltpu.make_async_copy(query_key_hbm, query_key_near, sem)
    copy.start()
    row = lax.broadcasted_iota(jnp.int32, tags.shape, 0)
    first = lanes_of(tags.shape) == 0
    marks = jnp.zeros(tags.shape, jnp.int32)
    for r in range(tags.shape[0]):
        start = jnp.minimum(lengths[r] - WINDOW, PAGE)
        marks = jnp.where(row == r, jnp.where(first, table[r, 0], start), marks)
    tags[...] = marks.astype(jnp.float32)
    copy.wait()


def bring_queries(table, lengths, query_key_w):
    return kernel_call(
        query_kernel,
        1,
        "bring_queries",
        [
            jax.ShapeDtypeStruct(query_key_w.shape, query_key_w.dtype),
            jax.ShapeDtypeStruct((lengths.shape[0], 128), jnp.float32),
        ],
        [SMEM] * 2 + [HBM],
        [pltpu.SemaphoreType.DMA],
        (table, lengths, query_key_w),
        4 << 20,
        bytes_only([query_key_w]),
    )


def page_kernel(ids, pages_hbm, page, pages, sem):
    copy = pltpu.make_async_copy(pages_hbm.at[0], pages, sem)
    copy.start()
    copy.wait()
    lane = lanes_of(page.shape)
    keys = pltpu.roll(pages[0].astype(jnp.float32), HALF, 1)
    page[...] = jnp.where(lane < HALF, keys, pages[1].astype(jnp.float32)).astype(jnp.bfloat16)


def window_page(prompt_pages):
    shape = prompt_pages.shape[1:]
    return kernel_call(
        page_kernel,
        1,
        "window_page",
        jax.ShapeDtypeStruct(shape[1:], jnp.bfloat16),
        [HBM],
        [pltpu.VMEM(shape, jnp.bfloat16), pltpu.SemaphoreType.DMA],
        (prompt_pages,),
        cost=pl.CostEstimate(flops=0, bytes_accessed=16 << 20, transcendentals=0),
    )


def body(
    tokens,
    norm_gain,
    feature_w,
    query_key_w,
    value_w,
    out_w,
    conv_w,
    conv_state,
    lin_state,
    lin_norm,
    own_pages,
    prompt_pages,
    page_table,
    lengths,
):
    pages_first = prompt_pages.transpose(0, 1, 3, 2)
    near = bring_near(
        {
            "gain": norm_gain,
            "feature_w": feature_w,
            "state": lin_state.transpose(0, 2, 1, 3).reshape(-1, HD),
            "lin_norm": lin_norm,
            "conv_w": conv_w,
            "conv_state": conv_state,
            "value_w": value_w.transpose(0, 2, 1)[0],
            "out_w": out_w[0],
        }
    )

    received = [head_shift(0, tokens, k) for k in (1, 3, 2)]
    page = window_page(pages_first)
    near, received = lax.optimization_barrier((near, received))
    page, received = lax.optimization_barrier((page, received))
    row_pages = [x_shift(page, k) for k in (1, 3, 2)]
    update = linear_layer([tokens] + received, near)
    row_pages, update = lax.optimization_barrier((row_pages, update))
    near_pages = jnp.stack([row_pages[0], page, row_pages[1], row_pages[2]])
    far_pages = z_shift(near_pages, ZN // 2)
    own_pages = own_pages.transpose(0, 1, 3, 2)
    query_key_w, table, ends, update = lax.optimization_barrier(
        (query_key_w, page_table, lengths, update)
    )
    near["query_key_w"], tags = bring_queries(table, ends, query_key_w)
    swapped = [section_swap(update, k) for k in (0, 1, 3, 2)]
    one_share, packed, key_new, value_new = project(tags, swapped, near)
    asked = [packed] + [z_shift(packed, k) for k in (1, 7, 2)]
    own = own_attention(page_table, lengths, packed, key_new, value_new, own_pages)
    asked, own = lax.optimization_barrier((asked, own))
    answers = prompt_attention(asked, near_pages, far_pages)
    answers, one_share = lax.optimization_barrier((answers, one_share))
    parts = [answers[0]] + [z_shift(answers[at], -k) for at, k in ((1, 1), (2, 7), (3, 2))]
    one_back = lax.ppermute(one_share, "section", [(1, 0), (0, 1)])
    parts, one_back = lax.optimization_barrier((parts, one_back))
    slabs = combine(own, parts, near)
    section_index = lax.axis_index("section")
    total = one_share.astype(jnp.float32) + slabs[0]
    for piece in [head_shift(1, slabs[k], k) for k in (1, 3, 2)]:
        total = total + piece
    output = jnp.where(section_index == 0, one_back, total.astype(jnp.bfloat16))
    return output[None]


def solution(mesh):
    placed = (
        P("req", "head"),
        P("section", None),
        P(None, "head"),
        P(None, "head"),
        P("section", None, "head"),
        P("section", "head", None),
        P(None, "head"),
        P("req", None, "head"),
        P("req", "head", None, None),
        P("req", "head", None),
        P("req", None, None, "head"),
        P("req", None, None, "head"),
        P("req", None),
        P("req"),
    )
    return jax.shard_map(
        body, mesh=mesh, in_specs=placed, out_specs=P("section", "req", "head"), check_vma=False
    )
```

```python
import jax
import jax.numpy as jnp
from jax import lax
from jax.experimental import pallas as pl
from jax.experimental.pallas import tpu as pltpu
from jax.sharding import PartitionSpec as P

HD = 112
FEAT = 16
WINDOW = 64
PAGE = 128
HALF = 64
MAXP = 256
GROUPS = 32
XN = 4
ZN = 8
LANES = 512
TAYLOR = 273
TAYLOR_LANES = 384
SPREAD = 1152

EPSILON = 1e-06
MASKED = -1e30


def head_shift(value, steps):
    count = lax.axis_size("head")
    return lax.ppermute(value, "head", [(i, (i + steps) % count) for i in range(count)])


def z_shift(value, steps):
    return lax.ppermute(
        value,
        "req",
        [(z * XN + i, (z + steps) % ZN * XN + i) for z in range(ZN) for i in range(XN)],
    )


def x_swap(value, flip):
    return lax.ppermute(value, "req", [(i, i ^ flip) for i in range(XN * ZN)])


def far_swap(value):
    count = XN * ZN
    return lax.ppermute(
        value,
        ("section", "req"),
        [(count + i, count + (i + count // 2) % count) for i in range(count)],
    )


def section_swap(value, steps):
    count = lax.axis_size("head")
    there = [(i, count + (i + steps) % count) for i in range(count)]
    return lax.ppermute(value, ("section", "head"), there + [(b, a) for a, b in there])


VMEM = pl.BlockSpec(memory_space=pltpu.VMEM)
SMEM = pl.BlockSpec(memory_space=pltpu.SMEM)
HBM = pl.BlockSpec(memory_space=pltpu.HBM)
FLAT = (((1,), (1,)), ((), ()))


def normed_rows(values, gain_row):
    factor = lax.rsqrt(jnp.mean(values * values, axis=-1, keepdims=True) + EPSILON)
    return (values * factor * gain_row).astype(jnp.bfloat16)


def lanes_of(shape):
    return lax.broadcasted_iota(jnp.int32, shape, len(shape) - 1)


def in_head(lane, h):
    return (lane >= h * HD) & (lane < (h + 1) * HD)


def place():
    return lax.axis_index("section"), lax.axis_index("req"), lax.axis_index("head")


def kernel_call(
    kernel,
    section,
    name,
    out_shape,
    in_specs,
    scratch_shapes,
    args,
    vmem=10 << 20,
    cost=None,
    elsewhere=None,
):
    def run(*refs):
        ids = place()

        @pl.when(ids[0] == section)
        def _():
            kernel(ids, *refs)

        if elsewhere is not None:

            @pl.when(ids[0] != section)
            def _():
                elsewhere(ids, *refs)

    args = [
        pltpu.with_memory_space_constraint(arg, pltpu.HBM) if spec is HBM else arg
        for arg, spec in zip(args, in_specs, strict=True)
    ]
    return pl.pallas_call(
        run,
        out_shape=out_shape,
        in_specs=in_specs,
        out_specs=jax.tree.map(lambda _: VMEM, out_shape),
        scratch_shapes=scratch_shapes,
        compiler_params=pltpu.CompilerParams(vmem_limit_bytes=vmem),
        cost_estimate=cost,
        name=name,
    )(*args)


def expansion(features, width, repeat):
    lane = lax.broadcasted_iota(jnp.int32, (features, 2 * width), 1)
    source = lax.broadcasted_iota(jnp.int32, (features, 2 * width), 0)
    left = lane < width
    at = jnp.where(left, lane, lane - width) >> (repeat.bit_length() - 1)
    linear = left & (at > 0) & (at <= FEAT) & (source == at - 1)
    pair = at - (FEAT + 1)
    wanted = jnp.where(left, pair >> 4, pair & (FEAT - 1))
    quad = (pair >= 0) & (pair < FEAT * FEAT) & (source == wanted)
    return jnp.where(linear | quad, 1.0, 0.0).astype(jnp.bfloat16)


def taylor_rows(left, right, feature):
    scale = FEAT ** (-0.25)
    left, right = left * scale, right * scale
    return jnp.where(
        feature == 0, 1.0, jnp.where(feature <= FEAT, left, left * right * 0.5**0.5)
    )


def linear_kernel(
    ids,
    t0,
    t1,
    t2,
    t3,
    gain,
    feature_w,
    state,
    lin_norm,
    conv_w,
    conv_state,
    value_w,
    out_w,
    update,
):
    rows, share = t0.shape
    heads = share // HD
    span = TAYLOR * heads
    by_state = expansion(128, SPREAD, heads)
    by_norm = expansion(128, TAYLOR_LANES, 1)
    expand = jnp.concatenate([by_state, by_norm], axis=1)

    own = ids[2]
    got = [ref[...].astype(jnp.float32) for ref in (t0, t1, t3, t2)]
    whole = []
    for place in range(heads):
        piece = got[0]
        for back in range(1, heads):
            piece = jnp.where(((own - back) & (heads - 1)) == place, got[back], piece)
        whole.append(piece)
    tokens = jnp.concatenate(whole, axis=1)
    normed = normed_rows(tokens, gain[...])
    feats = jnp.dot(normed, feature_w[...], preferred_element_type=jnp.float32)
    by_head = jnp.concatenate(
        [feats] + [pltpu.roll(feats, 128 - 2 * FEAT * h, 1) for h in range(1, heads)], axis=0
    )
    high = by_head.astype(jnp.bfloat16)
    rest = by_head - high.astype(jnp.float32)
    middle = rest.astype(jnp.bfloat16)
    low = (rest - middle.astype(jnp.float32)).astype(jnp.bfloat16)
    spread = jnp.dot(
        jnp.concatenate([high, middle, low], axis=0), expand, preferred_element_type=jnp.float32
    )
    count = heads * rows
    spread = spread[:count] + spread[count : 2 * count] + spread[2 * count :]
    lane = lanes_of((count, SPREAD))
    head = lax.broadcasted_iota(jnp.int32, (count, SPREAD), 0) >> 3
    query_wide = taylor_rows(spread[:, :SPREAD], spread[:, SPREAD : 2 * SPREAD], lane >> 2)
    query_wide = jnp.where(((lane & (heads - 1)) == head) & (lane < span), query_wide, 0.0)
    query_feats = taylor_rows(
        spread[:, 2 * SPREAD : 2 * SPREAD + TAYLOR_LANES],
        spread[:, 2 * SPREAD + TAYLOR_LANES :],
        lanes_of((count, TAYLOR_LANES)),
    )[:, :TAYLOR]
    both = by_head * pltpu.roll(by_head, 128 - FEAT, 1)
    near = jnp.sum(
        jnp.where(lanes_of(both.shape) < FEAT, both, 0.0), axis=-1, keepdims=True
    ) * FEAT ** (-0.5)
    intersection = 1.0 + near + 0.5 * near * near

    length = span + 12
    queries = []
    for shift in range(0, 16, 4):
        moved = query_wide if shift == 0 else pltpu.roll(query_wide, shift, 1)
        queries.append(moved[:, :length].astype(jnp.bfloat16))
    row = lax.broadcasted_iota(jnp.int32, (count, HD), 0) & (rows - 1)
    found = jnp.zeros((count, HD), jnp.float32)
    for r in range(rows):
        first = span * r
        shift = first % 16
        product = jnp.dot(
            queries[shift // 4],
            state[first - shift : first - shift + length, :],
            preferred_element_type=jnp.float32,
        )
        found = jnp.where(row == r, product, found)
    fresh = lax.dot_general(normed, value_w[...], FLAT, preferred_element_type=jnp.float32)
    older = conv_state[...].astype(jnp.float32)
    mixed = conv_w[0:1] * older[:, 0] + conv_w[1:2] * older[:, 1] + conv_w[2:3] * fresh
    total = tokens * 0.25
    for h in range(heads):
        here = slice(h * rows, (h + 1) * rows)
        denominator = (
            jnp.sum(query_feats[here] * lin_norm[:, h, :], axis=-1, keepdims=True)
            + intersection[here]
        )
        attended = (
            (found[here] + intersection[here] * mixed[:, h * HD : (h + 1) * HD]) / denominator
        ).astype(jnp.bfloat16)
        total = total + jnp.dot(
            attended, out_w[h * HD : (h + 1) * HD, :], preferred_element_type=jnp.float32
        )
    update[...] = total


def linear_layer(pieces, near):
    return kernel_call(
        linear_kernel,
        0,
        "linear_layer",
        jax.ShapeDtypeStruct((pieces[0].shape[0], near["out_w"].shape[1]), jnp.float32),
        [VMEM] * 12,
        [],
        (*pieces, *(near[name] for name in LINEAR_NEAR)),
    )


def project_kernel(
    ids,
    tags,
    p0,
    p1,
    p2,
    p3,
    gain,
    v_w,
    qk_w,
    one,
    asked,
    key_new,
    value_new,
):
    rows, share = one.shape
    heads = share // HD
    layer_one = (p0[...] + p1[...] + p2[...] + p3[...]).astype(jnp.bfloat16)
    rounded = layer_one.astype(jnp.float32)
    mine = rounded[:, :share]
    for h in range(1, heads):
        mine = jnp.where(ids[2] == h, rounded[:, h * share : (h + 1) * share], mine)
    one[...] = mine.astype(jnp.bfloat16)
    normed = normed_rows(rounded, gain[...])
    value_new[...] = lax.dot_general(
        normed, v_w[...], FLAT, preferred_element_type=jnp.float32
    ).astype(jnp.bfloat16)
    query_key = jnp.dot(normed, qk_w[...], preferred_element_type=jnp.float32)
    width = query_key.shape[1]
    lane = lanes_of((rows, LANES))
    query = jnp.where(in_head(lane, 0), query_key[:, :LANES], 0.0)
    key = query
    for h in range(heads):
        if h:
            moved = pltpu.roll(query_key, width - h * HD, 1)[:, :LANES]
            query = jnp.where(in_head(lane, h), moved, query)
        moved = pltpu.roll(query_key, width - (h + 1) * HD, 1)[:, :LANES]
        key = jnp.where(in_head(lane, h), moved, key)
    query = jnp.where(lane == share, tags[:, 0:1], query)
    query = jnp.where(lane == share + 1, tags[:, 1:2], query)
    asked[...] = query.astype(jnp.bfloat16)
    key_new[...] = key[:, :share].astype(jnp.bfloat16)


def project(tags, pieces, near):
    rows = pieces[0].shape[0]
    share = near["value_w"].shape[0]
    return kernel_call(
        project_kernel,
        1,
        "project",
        [
            jax.ShapeDtypeStruct((rows, share), jnp.bfloat16),
            jax.ShapeDtypeStruct((rows, LANES), jnp.bfloat16),
            jax.ShapeDtypeStruct((rows, share), jnp.bfloat16),
            jax.ShapeDtypeStruct((rows, share), jnp.bfloat16),
        ],
        [VMEM] * 8,
        [],
        (tags, *pieces, near["gain"], near["value_w"], near["query_key_w"]),
    )


def window_pages(lengths, r):
    length = lengths[r]
    return jnp.maximum((length - WINDOW) // PAGE, 1), jnp.maximum((length - 2) // PAGE, 1)


def own_kernel(
    ids,
    table,
    lengths,
    asked,
    key_new,
    value_new,
    own_pages,
    summed_out,
    highest_out,
    total_out,
    pages,
    sems,
):
    rows, share = key_new.shape
    count = own_pages.shape[0]
    bounds = []
    copies = []
    for r in range(rows):
        first, last = window_pages(lengths, r)
        bounds.append((lengths[r], first, last))
        for slot, logical in enumerate((first, last)):
            page = jnp.clip(table[r, logical] - GROUPS - ids[1] * count, 0, count - 1)
            copies.append(
                pltpu.make_async_copy(own_pages.at[page], pages.at[r, slot], sems.at[r, slot])
            )
            copies[-1].start()
    head = lax.broadcasted_iota(jnp.int32, (8, share), 0)
    lane = lanes_of((8, share))
    mine = (lane >= head * HD) & (lane < (head + 1) * HD)
    scale = HD ** (-0.5)
    query = asked[:, :share].astype(jnp.float32)
    new_key = key_new[...].astype(jnp.float32)
    new_value = value_new[...].astype(jnp.float32)
    wide = jnp.concatenate([jnp.where(mine, query[r : r + 1], 0.0) for r in range(rows)], axis=0)
    keys = jnp.concatenate(
        [jnp.broadcast_to(new_key[r : r + 1], (8, share)) for r in range(rows)], axis=0
    )
    new_score = jnp.sum(wide * keys, axis=-1, keepdims=True) * scale
    token = lanes_of((8 * rows, 2 * PAGE))
    request = lax.broadcasted_iota(jnp.int32, (8 * rows, 2 * PAGE), 0) >> 3
    length = jnp.zeros(token.shape, jnp.int32)
    base = jnp.zeros(token.shape, jnp.int32)
    for r in range(rows):
        length = jnp.where(request == r, bounds[r][0], length)
        second = jnp.where(bounds[r][1] != bounds[r][2], bounds[r][2] - 1, -MAXP) * PAGE
        base = jnp.where(request == r, jnp.where(token < PAGE, bounds[r][1] * PAGE, second), base)
    position = base + token
    usable = (position >= length - WINDOW) & (position <= length - 2)
    scores = []
    for r in range(rows):
        low = wide[8 * r : 8 * r + 8].astype(jnp.bfloat16)
        copies[2 * r].wait()
        copies[2 * r + 1].wait()
        scores.append(
            jnp.concatenate(
                [
                    jnp.dot(low, pages[r, slot, 0], preferred_element_type=jnp.float32)
                    for slot in range(2)
                ],
                axis=1,
            )
        )
    scores = jnp.where(usable, jnp.concatenate(scores, axis=0) * scale, MASKED)
    highest = jnp.maximum(jnp.max(scores, axis=-1, keepdims=True), new_score)
    exps = jnp.where(usable, jnp.exp(scores - highest), 0.0)
    exp_new = jnp.exp(new_score - highest)
    total = jnp.sum(exps, axis=-1, keepdims=True) + exp_new
    for r in range(rows):
        here = slice(8 * r, 8 * r + 8)
        low = exps[here].astype(jnp.bfloat16)
        found = exp_new[here] * new_value[r : r + 1]
        for slot in range(2):
            found = found + lax.dot_general(
                low[:, slot * PAGE : (slot + 1) * PAGE],
                pages[r, slot, 1],
                FLAT,
                preferred_element_type=jnp.float32,
            )
        for ref, value in (
            (summed_out, found),
            (highest_out, highest[here]),
            (total_out, total[here]),
        ):
            ref[r : r + 1, :] = jnp.sum(jnp.where(mine, value, 0.0), axis=0, keepdims=True)


def own_attention(table, lengths, asked, key_new, value_new, own_pages):
    rows, share = key_new.shape
    return kernel_call(
        own_kernel,
        1,
        "own_attention",
        [jax.ShapeDtypeStruct((rows, share), jnp.float32)] * 3,
        [SMEM] * 2 + [VMEM] * 3 + [HBM],
        [
            pltpu.VMEM((rows, 2) + own_pages.shape[1:], jnp.bfloat16),
            pltpu.SemaphoreType.DMA((rows, 2)),
        ],
        (table, lengths, asked, key_new, value_new, own_pages),
    )


def prompt_kernel(ids, a0, a1, a2, a3, near_pages, far_pages, o0, o1, o2, o3):
    rows = a0.shape[0]
    share = near_pages.shape[1]
    heads = share // HD
    pages = jnp.concatenate(
        [near_pages[i] for i in range(XN)] + [far_pages[i] for i in range(XN)], axis=1
    )
    asked = jnp.concatenate([ref[...].astype(jnp.float32) for ref in (a0, a1, a2, a3)], axis=0)
    count = asked.shape[0]
    lane = lanes_of(asked.shape)
    group = jnp.sum(jnp.where(lane == share, asked, 0.0), axis=-1, keepdims=True)
    start = jnp.sum(jnp.where(lane == share + 1, asked, 0.0), axis=-1, keepdims=True)
    group, start = group.astype(jnp.int32), start.astype(jnp.int32)
    query = jnp.concatenate(
        [jnp.where(in_head(lane, h), asked, 0.0)[:, :share] for h in range(heads)], axis=0
    ).astype(jnp.bfloat16)
    scores = jnp.dot(query, pages, preferred_element_type=jnp.float32) * HD ** (-0.5)
    token = lanes_of((count, 2 * XN * PAGE))
    z, x = ids[1] // XN, ids[1] % XN
    slot = token >> 7
    slot_group = jnp.where(slot < XN, z, (z + ZN // 2) & (ZN - 1)) * XN
    slot_group = slot_group + (x ^ (slot & (XN - 1)))
    offset = token & (PAGE - 1)
    usable = (slot_group == group) & (offset < HALF) & (offset + HALF >= start)
    lane = lanes_of((count, share))
    stat_lane = lanes_of((count, 128))
    weights = []
    stats = jnp.zeros((count, 128), jnp.float32)
    for h in range(heads):
        here = jnp.where(usable, scores[h * count : (h + 1) * count], MASKED)
        highest = jnp.max(here, axis=-1, keepdims=True)
        exps = jnp.where(usable, jnp.exp(here - highest), 0.0)
        total = jnp.sum(exps, axis=-1, keepdims=True)
        stats = jnp.where(stat_lane == h, highest, stats)
        stats = jnp.where(stat_lane == heads + h, total, stats)
        weights.append(pltpu.roll(exps, HALF, 1))
    found = lax.dot_general(
        jnp.concatenate(weights, axis=0).astype(jnp.bfloat16),
        pages,
        FLAT,
        preferred_element_type=jnp.float32,
    )
    summed = jnp.zeros((count, share), jnp.float32)
    for h in range(heads):
        summed = jnp.where(in_head(lane, h), found[h * count : (h + 1) * count], summed)
    for at, ref in enumerate((o0, o1, o2, o3)):
        ref[:, :share] = summed[at * rows : (at + 1) * rows]
        ref[:, share:LANES] = jnp.zeros((rows, LANES - share), jnp.float32)
        ref[:, LANES:] = stats[at * rows : (at + 1) * rows]


def prompt_attention(asked, near_pages, far_pages):
    rows = asked[0].shape[0]
    return kernel_call(
        prompt_kernel,
        1,
        "prompt_attention",
        [jax.ShapeDtypeStruct((rows, LANES + 128), jnp.float32)] * 4,
        [VMEM] * 6,
        [],
        (*asked, near_pages, far_pages),
    )


def combine_kernel(ids, summed, highest, total, r0, r1, r2, r3, out_w, s0, s1, s2, s3):
    rows, share = summed.shape
    heads = share // HD
    refs = (r0, r1, r2, r3)
    prompt_summed = sum(ref[:, :share] for ref in refs)
    stats = [ref[:, LANES:] for ref in refs]
    top = jnp.maximum(jnp.maximum(stats[0], stats[1]), jnp.maximum(stats[2], stats[3]))
    added = stats[0] + stats[1] + stats[2] + stats[3]
    lane = lanes_of((rows, share))
    prompt_highest = jnp.zeros((rows, share), jnp.float32)
    prompt_total = jnp.zeros((rows, share), jnp.float32)
    for h in range(heads):
        here = in_head(lane, h)
        prompt_highest = jnp.where(here, top[:, h : h + 1], prompt_highest)
        prompt_total = jnp.where(here, added[:, heads + h : heads + h + 1], prompt_total)
    peak = jnp.maximum(highest[...], prompt_highest)
    own_factor = jnp.exp(highest[...] - peak)
    prompt_factor = jnp.exp(prompt_highest - peak)
    whole = total[...] * own_factor + prompt_total * prompt_factor
    attended = (summed[...] * own_factor + prompt_summed * prompt_factor) / whole
    second = jnp.dot(attended.astype(jnp.bfloat16), out_w[...], preferred_element_type=jnp.float32)
    for steps, ref in enumerate((s0, s1, s2, s3)):
        slab = second[:, :share]
        for h in range(1, heads):
            slab = jnp.where(
                ((ids[2] + steps) & (heads - 1)) == h, second[:, h * share : (h + 1) * share], slab
            )
        ref[...] = slab


def combine(own, parts, near):
    return kernel_call(
        combine_kernel,
        1,
        "combine",
        [jax.ShapeDtypeStruct(own[0].shape, jnp.float32)] * 4,
        [VMEM] * 8,
        [],
        (*own, *parts, near["out_w"]),
    )


LINEAR_NEAR = (
    "gain",
    "feature_w",
    "state",
    "lin_norm",
    "conv_w",
    "conv_state",
    "value_w",
    "out_w",
)
SHARED_NEAR = ("gain", "value_w", "out_w")


def bring_near(arrays):
    names = list(arrays)
    count = len(names)
    both = [at for at, name in enumerate(names) if name in SHARED_NEAR]

    def copy_some(chosen, refs):
        sems = refs[-1]
        copies = [
            pltpu.make_async_copy(refs[at], refs[count + at], sems.at[at]) for at in chosen
        ]
        for copy in copies:
            copy.start()
        for copy in copies:
            copy.wait()

    near = kernel_call(
        lambda ids, *refs: copy_some(range(count), refs),
        0,
        "bring_near",
        [jax.ShapeDtypeStruct(array.shape, array.dtype) for array in arrays.values()],
        [HBM] * count,
        [pltpu.SemaphoreType.DMA((count,))],
        tuple(arrays.values()),
        4 << 20,
        bytes_only(arrays.values()),
        lambda ids, *refs: copy_some(both, refs),
    )
    return dict(zip(names, near))


def bytes_only(arrays):
    moved = sum(array.size * array.dtype.itemsize for array in arrays)
    return pl.CostEstimate(flops=0, bytes_accessed=2 * moved, transcendentals=0)


def query_kernel(ids, table, lengths, query_key_hbm, query_key_near, tags, sem):
    copy = pltpu.make_async_copy(query_key_hbm, query_key_near, sem)
    copy.start()
    row = lax.broadcasted_iota(jnp.int32, tags.shape, 0)
    first = lanes_of(tags.shape) == 0
    marks = jnp.zeros(tags.shape, jnp.int32)
    for r in range(tags.shape[0]):
        start = jnp.minimum(lengths[r] - WINDOW, PAGE)
        marks = jnp.where(row == r, jnp.where(first, table[r, 0], start), marks)
    tags[...] = marks.astype(jnp.float32)
    copy.wait()


def bring_queries(table, lengths, query_key_w):
    return kernel_call(
        query_kernel,
        1,
        "bring_queries",
        [
            jax.ShapeDtypeStruct(query_key_w.shape, query_key_w.dtype),
            jax.ShapeDtypeStruct((lengths.shape[0], 128), jnp.float32),
        ],
        [SMEM] * 2 + [HBM],
        [pltpu.SemaphoreType.DMA],
        (table, lengths, query_key_w),
        4 << 20,
        bytes_only([query_key_w]),
    )


def page_kernel(ids, pages_hbm, page, pages, sem):
    copy = pltpu.make_async_copy(pages_hbm.at[0], pages, sem)
    copy.start()
    copy.wait()
    lane = lanes_of(page.shape)
    keys = pltpu.roll(pages[0].astype(jnp.float32), HALF, 1)
    page[...] = jnp.where(lane < HALF, keys, pages[1].astype(jnp.float32)).astype(jnp.bfloat16)


def window_page(prompt_pages):
    shape = prompt_pages.shape[1:]
    return kernel_call(
        page_kernel,
        1,
        "window_page",
        jax.ShapeDtypeStruct(shape[1:], jnp.bfloat16),
        [HBM],
        [pltpu.VMEM(shape, jnp.bfloat16), pltpu.SemaphoreType.DMA],
        (prompt_pages,),
        cost=pl.CostEstimate(flops=0, bytes_accessed=16 << 20, transcendentals=0),
    )


def body(
    tokens,
    norm_gain,
    feature_w,
    query_key_w,
    value_w,
    out_w,
    conv_w,
    conv_state,
    lin_state,
    lin_norm,
    own_pages,
    prompt_pages,
    page_table,
    lengths,
):
    pages_first = prompt_pages.transpose(0, 1, 3, 2)
    near = bring_near(
        {
            "gain": norm_gain,
            "feature_w": feature_w,
            "state": lin_state.transpose(0, 2, 1, 3).reshape(-1, HD),
            "lin_norm": lin_norm,
            "conv_w": conv_w,
            "conv_state": conv_state,
            "value_w": value_w.transpose(0, 2, 1)[0],
            "out_w": out_w[0],
        }
    )

    page = window_page(pages_first)
    two_pages = jnp.stack([page, x_swap(page, 1)])
    received = [head_shift(tokens, k) for k in (1, 3, 2)]
    near_pages = jnp.concatenate([two_pages, x_swap(two_pages, 2)])
    near, received = lax.optimization_barrier((near, received))
    near_pages, received = lax.optimization_barrier((near_pages, received))
    far_pages = far_swap(near_pages)
    update = linear_layer([tokens] + received, near)
    own_pages = own_pages.transpose(0, 1, 3, 2)
    query_key_w, table, ends, update = lax.optimization_barrier(
        (query_key_w, page_table, lengths, update)
    )
    near["query_key_w"], tags = bring_queries(table, ends, query_key_w)
    swapped = [section_swap(update, k) for k in (0, 1, 3, 2)]
    one_share, packed, key_new, value_new = project(tags, swapped, near)
    asked = [packed] + [z_shift(packed, k) for k in (1, 7, 2)]
    own = own_attention(page_table, lengths, packed, key_new, value_new, own_pages)
    asked, own = lax.optimization_barrier((asked, own))
    answers = prompt_attention(asked, near_pages, far_pages)
    answers, one_share = lax.optimization_barrier((answers, one_share))
    parts = [answers[0]] + [z_shift(answers[at], -k) for at, k in ((1, 1), (2, 7), (3, 2))]
    one_back = lax.ppermute(one_share, "section", [(1, 0), (0, 1)])
    parts, one_back = lax.optimization_barrier((parts, one_back))
    slabs = combine(own, parts, near)
    section_index = lax.axis_index("section")
    total = one_share.astype(jnp.float32) + slabs[0]
    for piece in [head_shift(slabs[k], k) for k in (1, 3, 2)]:
        total = total + piece
    output = jnp.where(section_index == 0, one_back, total.astype(jnp.bfloat16))
    return output[None]


def solution(mesh):
    placed = (
        P("req", "head"),
        P("section", None),
        P(None, "head"),
        P(None, "head"),
        P("section", None, "head"),
        P("section", "head", None),
        P(None, "head"),
        P("req", None, "head"),
        P("req", "head", None, None),
        P("req", "head", None),
        P("req", None, None, "head"),
        P("req", None, None, "head"),
        P("req", None),
        P("req"),
    )
    return jax.shard_map(
        body, mesh=mesh, in_specs=placed, out_specs=P("section", "req", "head"), check_vma=False
    )
```

```python
import jax
import jax.numpy as jnp
from jax import lax
from jax.experimental import pallas as pl
from jax.experimental.pallas import tpu as pltpu
from jax.sharding import PartitionSpec as P

HD = 112
FEAT = 16
WINDOW = 64
PAGE = 128
HALF = 64
MAXP = 256
GROUPS = 32
XN = 4
ZN = 8
LANES = 512
TAYLOR = 273
TAYLOR_LANES = 384
SPREAD = 1152

EPSILON = 1e-06
MASKED = -1e30


def head_shift(value, steps):
    count = lax.axis_size("head")
    return lax.ppermute(value, "head", [(i, (i + steps) % count) for i in range(count)])


def z_shift(value, steps):
    return lax.ppermute(
        value,
        "req",
        [(z * XN + i, (z + steps) % ZN * XN + i) for z in range(ZN) for i in range(XN)],
    )


def x_swap(value, flip):
    return lax.ppermute(value, "req", [(i, i ^ flip) for i in range(XN * ZN)])


def far_swap(value):
    count = XN * ZN
    return lax.ppermute(
        value,
        ("section", "req"),
        [(count + i, count + (i + count // 2) % count) for i in range(count)],
    )


def section_swap(value, steps):
    count = lax.axis_size("head")
    there = [(i, count + (i + steps) % count) for i in range(count)]
    return lax.ppermute(value, ("section", "head"), there + [(b, a) for a, b in there])


VMEM = pl.BlockSpec(memory_space=pltpu.VMEM)
SMEM = pl.BlockSpec(memory_space=pltpu.SMEM)
HBM = pl.BlockSpec(memory_space=pltpu.HBM)
FLAT = (((1,), (1,)), ((), ()))


def normed_rows(values, gain_row):
    factor = lax.rsqrt(jnp.mean(values * values, axis=-1, keepdims=True) + EPSILON)
    return (values * factor * gain_row).astype(jnp.bfloat16)


def lanes_of(shape):
    return lax.broadcasted_iota(jnp.int32, shape, len(shape) - 1)


def in_head(lane, h):
    return (lane >= h * HD) & (lane < (h + 1) * HD)


def place():
    return lax.axis_index("section"), lax.axis_index("req"), lax.axis_index("head")


def kernel_call(
    kernel,
    section,
    name,
    out_shape,
    in_specs,
    scratch_shapes,
    args,
    vmem=6 << 20,
    cost=None,
    elsewhere=None,
):
    def run(*refs):
        ids = place()

        @pl.when(ids[0] == section)
        def _():
            kernel(ids, *refs)

        if elsewhere is not None:

            @pl.when(ids[0] != section)
            def _():
                elsewhere(ids, *refs)

    args = [
        pltpu.with_memory_space_constraint(arg, pltpu.HBM) if spec is HBM else arg
        for arg, spec in zip(args, in_specs, strict=True)
    ]
    return pl.pallas_call(
        run,
        out_shape=out_shape,
        in_specs=in_specs,
        out_specs=jax.tree.map(lambda _: VMEM, out_shape),
        scratch_shapes=scratch_shapes,
        compiler_params=pltpu.CompilerParams(vmem_limit_bytes=vmem),
        cost_estimate=cost,
        name=name,
    )(*args)


def expansion(features, width, repeat):
    lane = lax.broadcasted_iota(jnp.int32, (features, 2 * width), 1)
    source = lax.broadcasted_iota(jnp.int32, (features, 2 * width), 0)
    left = lane < width
    at = jnp.where(left, lane, lane - width) >> (repeat.bit_length() - 1)
    linear = left & (at > 0) & (at <= FEAT) & (source == at - 1)
    pair = at - (FEAT + 1)
    wanted = jnp.where(left, pair >> 4, pair & (FEAT - 1))
    quad = (pair >= 0) & (pair < FEAT * FEAT) & (source == wanted)
    return jnp.where(linear | quad, 1.0, 0.0).astype(jnp.bfloat16)


def taylor_rows(left, right, feature):
    scale = FEAT ** (-0.25)
    left, right = left * scale, right * scale
    return jnp.where(
        feature == 0, 1.0, jnp.where(feature <= FEAT, left, left * right * 0.5**0.5)
    )


def linear_kernel(
    ids,
    t0,
    t1,
    t2,
    t3,
    gain,
    feature_w,
    state,
    lin_norm,
    conv_w,
    conv_state,
    value_w,
    out_w,
    update,
):
    rows, share = t0.shape
    heads = share // HD
    span = TAYLOR * heads
    by_state = expansion(128, SPREAD, heads)
    by_norm = expansion(128, TAYLOR_LANES, 1)
    expand = jnp.concatenate([by_state, by_norm], axis=1)

    own = ids[2]
    got = [ref[...].astype(jnp.float32) for ref in (t0, t1, t3, t2)]
    whole = []
    for place in range(heads):
        piece = got[0]
        for back in range(1, heads):
            piece = jnp.where(((own - back) & (heads - 1)) == place, got[back], piece)
        whole.append(piece)
    tokens = jnp.concatenate(whole, axis=1)
    normed = normed_rows(tokens, gain[...])
    feats = jnp.dot(normed, feature_w[...], preferred_element_type=jnp.float32)
    by_head = jnp.concatenate(
        [feats] + [pltpu.roll(feats, 128 - 2 * FEAT * h, 1) for h in range(1, heads)], axis=0
    )
    high = by_head.astype(jnp.bfloat16)
    rest = by_head - high.astype(jnp.float32)
    middle = rest.astype(jnp.bfloat16)
    low = (rest - middle.astype(jnp.float32)).astype(jnp.bfloat16)
    spread = jnp.dot(
        jnp.concatenate([high, middle, low], axis=0), expand, preferred_element_type=jnp.float32
    )
    count = heads * rows
    spread = spread[:count] + spread[count : 2 * count] + spread[2 * count :]
    lane = lanes_of((count, SPREAD))
    head = lax.broadcasted_iota(jnp.int32, (count, SPREAD), 0) >> 3
    query_wide = taylor_rows(spread[:, :SPREAD], spread[:, SPREAD : 2 * SPREAD], lane >> 2)
    query_wide = jnp.where(((lane & (heads - 1)) == head) & (lane < span), query_wide, 0.0)
    query_feats = taylor_rows(
        spread[:, 2 * SPREAD : 2 * SPREAD + TAYLOR_LANES],
        spread[:, 2 * SPREAD + TAYLOR_LANES :],
        lanes_of((count, TAYLOR_LANES)),
    )[:, :TAYLOR]
    both = by_head * pltpu.roll(by_head, 128 - FEAT, 1)
    near = jnp.sum(
        jnp.where(lanes_of(both.shape) < FEAT, both, 0.0), axis=-1, keepdims=True
    ) * FEAT ** (-0.5)
    intersection = 1.0 + near + 0.5 * near * near

    length = span + 12
    queries = []
    for shift in range(0, 16, 4):
        moved = query_wide if shift == 0 else pltpu.roll(query_wide, shift, 1)
        queries.append(moved[:, :length].astype(jnp.bfloat16))
    row = lax.broadcasted_iota(jnp.int32, (count, HD), 0) & (rows - 1)
    found = jnp.zeros((count, HD), jnp.float32)
    for r in range(rows):
        first = span * r
        shift = first % 16
        product = jnp.dot(
            queries[shift // 4],
            state[first - shift : first - shift + length, :],
            preferred_element_type=jnp.float32,
        )
        found = jnp.where(row == r, product, found)
    fresh = lax.dot_general(normed, value_w[...], FLAT, preferred_element_type=jnp.float32)
    older = conv_state[...].astype(jnp.float32)
    mixed = conv_w[0:1] * older[:, 0] + conv_w[1:2] * older[:, 1] + conv_w[2:3] * fresh
    total = tokens * 0.25
    for h in range(heads):
        here = slice(h * rows, (h + 1) * rows)
        denominator = (
            jnp.sum(query_feats[here] * lin_norm[:, h, :], axis=-1, keepdims=True)
            + intersection[here]
        )
        attended = (
            (found[here] + intersection[here] * mixed[:, h * HD : (h + 1) * HD]) / denominator
        ).astype(jnp.bfloat16)
        total = total + jnp.dot(
            attended, out_w[h * HD : (h + 1) * HD, :], preferred_element_type=jnp.float32
        )
    update[...] = total


def linear_layer(pieces, near):
    return kernel_call(
        linear_kernel,
        0,
        "linear_layer",
        jax.ShapeDtypeStruct((pieces[0].shape[0], near["out_w"].shape[1]), jnp.float32),
        [VMEM] * 12,
        [],
        (*pieces, *(near[name] for name in LINEAR_NEAR)),
    )


def project_kernel(
    ids,
    tags,
    p0,
    p1,
    p2,
    p3,
    gain,
    v_w,
    qk_w,
    one,
    asked,
    key_new,
    value_new,
):
    rows, share = one.shape
    heads = share // HD
    layer_one = (p0[...] + p1[...] + p2[...] + p3[...]).astype(jnp.bfloat16)
    rounded = layer_one.astype(jnp.float32)
    mine = rounded[:, :share]
    for h in range(1, heads):
        mine = jnp.where(ids[2] == h, rounded[:, h * share : (h + 1) * share], mine)
    one[...] = mine.astype(jnp.bfloat16)
    normed = normed_rows(rounded, gain[...])
    value_new[...] = lax.dot_general(
        normed, v_w[...], FLAT, preferred_element_type=jnp.float32
    ).astype(jnp.bfloat16)
    query_key = jnp.dot(normed, qk_w[...], preferred_element_type=jnp.float32)
    width = query_key.shape[1]
    lane = lanes_of((rows, LANES))
    query = jnp.where(in_head(lane, 0), query_key[:, :LANES], 0.0)
    key = query
    for h in range(heads):
        if h:
            moved = pltpu.roll(query_key, width - h * HD, 1)[:, :LANES]
            query = jnp.where(in_head(lane, h), moved, query)
        moved = pltpu.roll(query_key, width - (h + 1) * HD, 1)[:, :LANES]
        key = jnp.where(in_head(lane, h), moved, key)
    query = jnp.where(lane == share, tags[:, 0:1], query)
    query = jnp.where(lane == share + 1, tags[:, 1:2], query)
    asked[...] = query.astype(jnp.bfloat16)
    key_new[...] = key[:, :share].astype(jnp.bfloat16)


def project(tags, pieces, near):
    rows = pieces[0].shape[0]
    share = near["value_w"].shape[0]
    return kernel_call(
        project_kernel,
        1,
        "project",
        [
            jax.ShapeDtypeStruct((rows, share), jnp.bfloat16),
            jax.ShapeDtypeStruct((rows, LANES), jnp.bfloat16),
            jax.ShapeDtypeStruct((rows, share), jnp.bfloat16),
            jax.ShapeDtypeStruct((rows, share), jnp.bfloat16),
        ],
        [VMEM] * 8,
        [],
        (tags, *pieces, near["gain"], near["value_w"], near["query_key_w"]),
    )


def window_pages(lengths, r):
    length = lengths[r]
    return jnp.maximum((length - WINDOW) // PAGE, 1), jnp.maximum((length - 2) // PAGE, 1)


def own_kernel(
    ids, lengths, asked, key_new, value_new, pages, summed_out, highest_out, total_out
):
    rows, share = key_new.shape
    bounds = [(lengths[r], *window_pages(lengths, r)) for r in range(rows)]
    head = lax.broadcasted_iota(jnp.int32, (8, share), 0)
    lane = lanes_of((8, share))
    mine = (lane >= head * HD) & (lane < (head + 1) * HD)
    scale = HD ** (-0.5)
    query = asked[:, :share].astype(jnp.float32)
    new_key = key_new[...].astype(jnp.float32)
    new_value = value_new[...].astype(jnp.float32)
    wide = jnp.concatenate([jnp.where(mine, query[r : r + 1], 0.0) for r in range(rows)], axis=0)
    keys = jnp.concatenate(
        [jnp.broadcast_to(new_key[r : r + 1], (8, share)) for r in range(rows)], axis=0
    )
    new_score = jnp.sum(wide * keys, axis=-1, keepdims=True) * scale
    token = lanes_of((8 * rows, 2 * PAGE))
    request = lax.broadcasted_iota(jnp.int32, (8 * rows, 2 * PAGE), 0) >> 3
    length = jnp.zeros(token.shape, jnp.int32)
    base = jnp.zeros(token.shape, jnp.int32)
    for r in range(rows):
        length = jnp.where(request == r, bounds[r][0], length)
        second = jnp.where(bounds[r][1] != bounds[r][2], bounds[r][2] - 1, -MAXP) * PAGE
        base = jnp.where(request == r, jnp.where(token < PAGE, bounds[r][1] * PAGE, second), base)
    position = base + token
    usable = (position >= length - WINDOW) & (position <= length - 2)
    scores = []
    for r in range(rows):
        low = wide[8 * r : 8 * r + 8].astype(jnp.bfloat16)
        scores.append(
            jnp.concatenate(
                [
                    jnp.dot(low, pages[r, slot, 0], preferred_element_type=jnp.float32)
                    for slot in range(2)
                ],
                axis=1,
            )
        )
    scores = jnp.where(usable, jnp.concatenate(scores, axis=0) * scale, MASKED)
    highest = jnp.maximum(jnp.max(scores, axis=-1, keepdims=True), new_score)
    exps = jnp.where(usable, jnp.exp(scores - highest), 0.0)
    exp_new = jnp.exp(new_score - highest)
    total = jnp.sum(exps, axis=-1, keepdims=True) + exp_new
    for r in range(rows):
        here = slice(8 * r, 8 * r + 8)
        low = exps[here].astype(jnp.bfloat16)
        found = exp_new[here] * new_value[r : r + 1]
        for slot in range(2):
            found = found + lax.dot_general(
                low[:, slot * PAGE : (slot + 1) * PAGE],
                pages[r, slot, 1],
                FLAT,
                preferred_element_type=jnp.float32,
            )
        for ref, value in (
            (summed_out, found),
            (highest_out, highest[here]),
            (total_out, total[here]),
        ):
            ref[r : r + 1, :] = jnp.sum(jnp.where(mine, value, 0.0), axis=0, keepdims=True)


def own_attention(lengths, asked, key_new, value_new, near):
    rows, share = key_new.shape
    return kernel_call(
        own_kernel,
        1,
        "own_attention",
        [jax.ShapeDtypeStruct((rows, share), jnp.float32)] * 3,
        [SMEM] + [VMEM] * 4,
        [],
        (lengths, asked, key_new, value_new, near["own_pages"]),
    )


def prompt_kernel(ids, a0, a1, a2, a3, near_pages, far_pages, o0, o1, o2, o3):
    rows = a0.shape[0]
    share = near_pages.shape[1]
    heads = share // HD
    pages = jnp.concatenate(
        [near_pages[i] for i in range(XN)] + [far_pages[i] for i in range(XN)], axis=1
    )
    asked = jnp.concatenate([ref[...].astype(jnp.float32) for ref in (a0, a1, a2, a3)], axis=0)
    count = asked.shape[0]
    lane = lanes_of(asked.shape)
    group = jnp.sum(jnp.where(lane == share, asked, 0.0), axis=-1, keepdims=True)
    start = jnp.sum(jnp.where(lane == share + 1, asked, 0.0), axis=-1, keepdims=True)
    group, start = group.astype(jnp.int32), start.astype(jnp.int32)
    query = jnp.concatenate(
        [jnp.where(in_head(lane, h), asked, 0.0)[:, :share] for h in range(heads)], axis=0
    ).astype(jnp.bfloat16)
    scores = jnp.dot(query, pages, preferred_element_type=jnp.float32) * HD ** (-0.5)
    token = lanes_of((count, 2 * XN * PAGE))
    z, x = ids[1] // XN, ids[1] % XN
    slot = token >> 7
    slot_group = jnp.where(slot < XN, z, (z + ZN // 2) & (ZN - 1)) * XN
    slot_group = slot_group + (x ^ (slot & (XN - 1)))
    offset = token & (PAGE - 1)
    usable = (slot_group == group) & (offset < HALF) & (offset + HALF >= start)
    lane = lanes_of((count, share))
    stat_lane = lanes_of((count, 128))
    weights = []
    stats = jnp.zeros((count, 128), jnp.float32)
    for h in range(heads):
        here = jnp.where(usable, scores[h * count : (h + 1) * count], MASKED)
        highest = jnp.max(here, axis=-1, keepdims=True)
        exps = jnp.where(usable, jnp.exp(here - highest), 0.0)
        total = jnp.sum(exps, axis=-1, keepdims=True)
        stats = jnp.where(stat_lane == h, highest, stats)
        stats = jnp.where(stat_lane == heads + h, total, stats)
        weights.append(pltpu.roll(exps, HALF, 1))
    found = lax.dot_general(
        jnp.concatenate(weights, axis=0).astype(jnp.bfloat16),
        pages,
        FLAT,
        preferred_element_type=jnp.float32,
    )
    summed = jnp.zeros((count, share), jnp.float32)
    for h in range(heads):
        summed = jnp.where(in_head(lane, h), found[h * count : (h + 1) * count], summed)
    for at, ref in enumerate((o0, o1, o2, o3)):
        ref[:, :share] = summed[at * rows : (at + 1) * rows]
        ref[:, share:LANES] = jnp.zeros((rows, LANES - share), jnp.float32)
        ref[:, LANES:] = stats[at * rows : (at + 1) * rows]


def prompt_attention(asked, near_pages, far_pages):
    rows = asked[0].shape[0]
    return kernel_call(
        prompt_kernel,
        1,
        "prompt_attention",
        [jax.ShapeDtypeStruct((rows, LANES + 128), jnp.float32)] * 4,
        [VMEM] * 6,
        [],
        (*asked, near_pages, far_pages),
    )


def combine_kernel(ids, summed, highest, total, r0, r1, r2, r3, out_w, s0, s1, s2, s3):
    rows, share = summed.shape
    heads = share // HD
    refs = (r0, r1, r2, r3)
    prompt_summed = sum(ref[:, :share] for ref in refs)
    stats = [ref[:, LANES:] for ref in refs]
    top = jnp.maximum(jnp.maximum(stats[0], stats[1]), jnp.maximum(stats[2], stats[3]))
    added = stats[0] + stats[1] + stats[2] + stats[3]
    lane = lanes_of((rows, share))
    prompt_highest = jnp.zeros((rows, share), jnp.float32)
    prompt_total = jnp.zeros((rows, share), jnp.float32)
    for h in range(heads):
        here = in_head(lane, h)
        prompt_highest = jnp.where(here, top[:, h : h + 1], prompt_highest)
        prompt_total = jnp.where(here, added[:, heads + h : heads + h + 1], prompt_total)
    peak = jnp.maximum(highest[...], prompt_highest)
    own_factor = jnp.exp(highest[...] - peak)
    prompt_factor = jnp.exp(prompt_highest - peak)
    whole = total[...] * own_factor + prompt_total * prompt_factor
    attended = (summed[...] * own_factor + prompt_summed * prompt_factor) / whole
    second = jnp.dot(attended.astype(jnp.bfloat16), out_w[...], preferred_element_type=jnp.float32)
    for steps, ref in enumerate((s0, s1, s2, s3)):
        slab = second[:, :share]
        for h in range(1, heads):
            slab = jnp.where(
                ((ids[2] + steps) & (heads - 1)) == h, second[:, h * share : (h + 1) * share], slab
            )
        ref[...] = slab


def combine(own, parts, near):
    return kernel_call(
        combine_kernel,
        1,
        "combine",
        [jax.ShapeDtypeStruct(own[0].shape, jnp.float32)] * 4,
        [VMEM] * 8,
        [],
        (*own, *parts, near["out_w"]),
    )


LINEAR_NEAR = (
    "gain",
    "feature_w",
    "state",
    "lin_norm",
    "conv_w",
    "conv_state",
    "value_w",
    "out_w",
)
SHARED_NEAR = ("gain", "value_w", "out_w")


def bring_near(arrays):
    names = list(arrays)
    count = len(names)
    both = [at for at, name in enumerate(names) if name in SHARED_NEAR]

    def copy_some(chosen, refs):
        sems = refs[-1]
        copies = [
            pltpu.make_async_copy(refs[at], refs[count + at], sems.at[at]) for at in chosen
        ]
        for copy in copies:
            copy.start()
        for copy in copies:
            copy.wait()

    near = kernel_call(
        lambda ids, *refs: copy_some(range(count), refs),
        0,
        "bring_near",
        [jax.ShapeDtypeStruct(array.shape, array.dtype) for array in arrays.values()],
        [HBM] * count,
        [pltpu.SemaphoreType.DMA((count,))],
        tuple(arrays.values()),
        4 << 20,
        bytes_only(arrays.values()),
        lambda ids, *refs: copy_some(both, refs),
    )
    return dict(zip(names, near))


def bytes_only(arrays):
    moved = sum(array.size * array.dtype.itemsize for array in arrays)
    return pl.CostEstimate(flops=0, bytes_accessed=2 * moved, transcendentals=0)


def window_kernel(
    ids, table, lengths, query_key_hbm, own_hbm, query_key_near, own_near, tags, key_sem, sems
):
    rows = tags.shape[0]
    total = own_hbm.shape[0]
    copies = [pltpu.make_async_copy(query_key_hbm, query_key_near, key_sem)]
    for r in range(rows):
        for slot, logical in enumerate(window_pages(lengths, r)):
            page = jnp.clip(table[r, logical] - GROUPS - ids[1] * total, 0, total - 1)
            copies.append(
                pltpu.make_async_copy(own_hbm.at[page], own_near.at[r, slot], sems.at[r, slot])
            )
    for copy in copies:
        copy.start()
    row = lax.broadcasted_iota(jnp.int32, tags.shape, 0)
    first = lanes_of(tags.shape) == 0
    marks = jnp.zeros(tags.shape, jnp.int32)
    for r in range(rows):
        start = jnp.minimum(lengths[r] - WINDOW, PAGE)
        marks = jnp.where(row == r, jnp.where(first, table[r, 0], start), marks)
    tags[...] = marks.astype(jnp.float32)
    for copy in copies:
        copy.wait()


def bring_windows(table, lengths, query_key_w, own_pages):
    rows = lengths.shape[0]
    windows = jax.ShapeDtypeStruct((rows, 2) + own_pages.shape[1:], own_pages.dtype)
    return kernel_call(
        window_kernel,
        1,
        "bring_windows",
        [
            jax.ShapeDtypeStruct(query_key_w.shape, query_key_w.dtype),
            windows,
            jax.ShapeDtypeStruct((rows, 128), jnp.float32),
        ],
        [SMEM] * 2 + [HBM] * 2,
        [pltpu.SemaphoreType.DMA, pltpu.SemaphoreType.DMA((rows, 2))],
        (table, lengths, query_key_w, own_pages),
        1 << 20,
        bytes_only([query_key_w, windows]),
    )


def page_kernel(ids, pages_hbm, page, pages, sem):
    copy = pltpu.make_async_copy(pages_hbm.at[0], pages, sem)
    copy.start()
    copy.wait()
    lane = lanes_of(page.shape)
    keys = pltpu.roll(pages[0].astype(jnp.float32), HALF, 1)
    page[...] = jnp.where(lane < HALF, keys, pages[1].astype(jnp.float32)).astype(jnp.bfloat16)


def window_page(prompt_pages):
    shape = prompt_pages.shape[1:]
    return kernel_call(
        page_kernel,
        1,
        "window_page",
        jax.ShapeDtypeStruct(shape[1:], jnp.bfloat16),
        [HBM],
        [pltpu.VMEM(shape, jnp.bfloat16), pltpu.SemaphoreType.DMA],
        (prompt_pages,),
        cost=pl.CostEstimate(flops=0, bytes_accessed=16 << 20, transcendentals=0),
    )


def body(
    tokens,
    norm_gain,
    feature_w,
    query_key_w,
    value_w,
    out_w,
    conv_w,
    conv_state,
    lin_state,
    lin_norm,
    own_pages,
    prompt_pages,
    page_table,
    lengths,
):
    pages_first = prompt_pages.transpose(0, 1, 3, 2)
    stored = {
        "gain": norm_gain,
        "feature_w": feature_w,
        "state": lin_state.transpose(0, 2, 1, 3).reshape(-1, HD),
        "lin_norm": lin_norm,
        "conv_w": conv_w,
        "conv_state": conv_state,
        "value_w": value_w.transpose(0, 2, 1)[0],
        "out_w": out_w[0],
    }

    page = window_page(pages_first)
    other = x_swap(page, 1)
    received = [head_shift(tokens, k) for k in (1, 3, 2)]
    other, received = lax.optimization_barrier((other, received))
    stored, two_pages = lax.optimization_barrier((stored, jnp.stack([page, other])))
    near = bring_near(stored)
    update = linear_layer([tokens] + received, near)
    next_pages, update = lax.optimization_barrier((x_swap(two_pages, 2), update))
    near_pages = jnp.concatenate([two_pages, next_pages])
    far_pages = far_swap(near_pages)
    own_pages = own_pages.transpose(0, 1, 3, 2)
    query_key_w, own_pages, table, ends, update = lax.optimization_barrier(
        (query_key_w, own_pages, page_table, lengths, update)
    )
    near["query_key_w"], near["own_pages"], tags = bring_windows(
        table, ends, query_key_w, own_pages
    )
    swapped = [section_swap(update, k) for k in (0, 1, 3, 2)]
    one_share, packed, key_new, value_new = project(tags, swapped, near)
    asked = [packed] + [z_shift(packed, k) for k in (1, 7, 2)]
    own = own_attention(lengths, packed, key_new, value_new, near)
    asked, own = lax.optimization_barrier((asked, own))
    answers = prompt_attention(asked, near_pages, far_pages)
    answers, one_share = lax.optimization_barrier((answers, one_share))
    parts = [answers[0]] + [z_shift(answers[at], -k) for at, k in ((1, 1), (2, 7), (3, 2))]
    one_back = lax.ppermute(one_share, "section", [(1, 0), (0, 1)])
    parts, one_back = lax.optimization_barrier((parts, one_back))
    slabs = combine(own, parts, near)
    section_index = lax.axis_index("section")
    total = one_share.astype(jnp.float32) + slabs[0]
    for piece in [head_shift(slabs[k], k) for k in (1, 3, 2)]:
        total = total + piece
    output = jnp.where(section_index == 0, one_back, total.astype(jnp.bfloat16))
    return output[None]


def solution(mesh):
    placed = (
        P("req", "head"),
        P("section", None),
        P(None, "head"),
        P(None, "head"),
        P("section", None, "head"),
        P("section", "head", None),
        P(None, "head"),
        P("req", None, "head"),
        P("req", "head", None, None),
        P("req", "head", None),
        P("req", None, None, "head"),
        P("req", None, None, "head"),
        P("req", None),
        P("req"),
    )
    return jax.shard_map(
        body, mesh=mesh, in_specs=placed, out_specs=P("section", "req", "head"), check_vma=False
    )
```

```python
import jax
import jax.numpy as jnp
from jax import lax
from jax.experimental import pallas as pl
from jax.experimental.pallas import tpu as pltpu
from jax.sharding import PartitionSpec as P

HD = 112
FEAT = 16
WINDOW = 64
PAGE = 128
HALF = 64
MAXP = 256
GROUPS = 32
XN = 4
ZN = 8
LANES = 512
TAYLOR = 273
TAYLOR_LANES = 384
SPREAD = 1152

EPSILON = 1e-06
MASKED = -1e30


def head_shift(value, steps):
    count = lax.axis_size("head")
    return lax.ppermute(value, "head", [(i, (i + steps) % count) for i in range(count)])


def z_shift(value, steps):
    return lax.ppermute(
        value,
        "req",
        [(z * XN + i, (z + steps) % ZN * XN + i) for z in range(ZN) for i in range(XN)],
    )


def x_swap(value, flip):
    return lax.ppermute(value, "req", [(i, i ^ flip) for i in range(XN * ZN)])


def section_swap(value, steps):
    count = lax.axis_size("head")
    there = [(i, count + (i + steps) % count) for i in range(count)]
    return lax.ppermute(value, ("section", "head"), there + [(b, a) for a, b in there])


VMEM = pl.BlockSpec(memory_space=pltpu.VMEM)
SMEM = pl.BlockSpec(memory_space=pltpu.SMEM)
HBM = pl.BlockSpec(memory_space=pltpu.HBM)
FLAT = (((1,), (1,)), ((), ()))


def normed_rows(values, gain_row):
    factor = lax.rsqrt(jnp.mean(values * values, axis=-1, keepdims=True) + EPSILON)
    return (values * factor * gain_row).astype(jnp.bfloat16)


def lanes_of(shape):
    return lax.broadcasted_iota(jnp.int32, shape, len(shape) - 1)


def in_head(lane, h):
    return (lane >= h * HD) & (lane < (h + 1) * HD)


def place():
    return lax.axis_index("section"), lax.axis_index("req"), lax.axis_index("head")


def kernel_call(
    kernel,
    section,
    name,
    out_shape,
    in_specs,
    scratch_shapes,
    args,
    vmem=6 << 20,
    cost=None,
    elsewhere=None,
):
    def run(*refs):
        ids = place()

        @pl.when(section is None or ids[0] == section)
        def _():
            kernel(ids, *refs)

        if elsewhere is not None:

            @pl.when(ids[0] != section)
            def _():
                elsewhere(ids, *refs)

    args = [
        pltpu.with_memory_space_constraint(arg, pltpu.HBM) if spec is HBM else arg
        for arg, spec in zip(args, in_specs, strict=True)
    ]
    return pl.pallas_call(
        run,
        out_shape=out_shape,
        in_specs=in_specs,
        out_specs=jax.tree.map(lambda _: VMEM, out_shape),
        scratch_shapes=scratch_shapes,
        compiler_params=pltpu.CompilerParams(vmem_limit_bytes=vmem),
        cost_estimate=cost,
        name=name,
    )(*args)


def expansion(features, width, repeat):
    lane = lax.broadcasted_iota(jnp.int32, (features, 2 * width), 1)
    source = lax.broadcasted_iota(jnp.int32, (features, 2 * width), 0)
    left = lane < width
    at = jnp.where(left, lane, lane - width) >> (repeat.bit_length() - 1)
    linear = left & (at > 0) & (at <= FEAT) & (source == at - 1)
    pair = at - (FEAT + 1)
    wanted = jnp.where(left, pair >> 4, pair & (FEAT - 1))
    quad = (pair >= 0) & (pair < FEAT * FEAT) & (source == wanted)
    return jnp.where(linear | quad, 1.0, 0.0).astype(jnp.bfloat16)


def taylor_rows(left, right, feature):
    scale = FEAT ** (-0.25)
    left, right = left * scale, right * scale
    return jnp.where(
        feature == 0, 1.0, jnp.where(feature <= FEAT, left, left * right * 0.5**0.5)
    )


def linear_kernel(
    ids,
    t0,
    t1,
    t2,
    t3,
    gain,
    feature_w,
    state,
    lin_norm,
    conv_w,
    conv_state,
    value_w,
    out_w,
    update,
):
    rows, share = t0.shape
    heads = share // HD
    span = TAYLOR * heads
    by_state = expansion(128, SPREAD, heads)
    by_norm = expansion(128, TAYLOR_LANES, 1)
    expand = jnp.concatenate([by_state, by_norm], axis=1)

    own = ids[2]
    got = [ref[...].astype(jnp.float32) for ref in (t0, t1, t3, t2)]
    whole = []
    for place in range(heads):
        piece = got[0]
        for back in range(1, heads):
            piece = jnp.where(((own - back) & (heads - 1)) == place, got[back], piece)
        whole.append(piece)
    tokens = jnp.concatenate(whole, axis=1)
    normed = normed_rows(tokens, gain[...])
    feats = jnp.dot(normed, feature_w[...], preferred_element_type=jnp.float32)
    by_head = jnp.concatenate(
        [feats] + [pltpu.roll(feats, 128 - 2 * FEAT * h, 1) for h in range(1, heads)], axis=0
    )
    high = by_head.astype(jnp.bfloat16)
    rest = by_head - high.astype(jnp.float32)
    middle = rest.astype(jnp.bfloat16)
    low = (rest - middle.astype(jnp.float32)).astype(jnp.bfloat16)
    spread = jnp.dot(
        jnp.concatenate([high, middle, low], axis=0), expand, preferred_element_type=jnp.float32
    )
    count = heads * rows
    spread = spread[:count] + spread[count : 2 * count] + spread[2 * count :]
    lane = lanes_of((count, SPREAD))
    head = lax.broadcasted_iota(jnp.int32, (count, SPREAD), 0) >> 3
    query_wide = taylor_rows(spread[:, :SPREAD], spread[:, SPREAD : 2 * SPREAD], lane >> 2)
    query_wide = jnp.where(((lane & (heads - 1)) == head) & (lane < span), query_wide, 0.0)
    query_feats = taylor_rows(
        spread[:, 2 * SPREAD : 2 * SPREAD + TAYLOR_LANES],
        spread[:, 2 * SPREAD + TAYLOR_LANES :],
        lanes_of((count, TAYLOR_LANES)),
    )[:, :TAYLOR]
    both = by_head * pltpu.roll(by_head, 128 - FEAT, 1)
    near = jnp.sum(
        jnp.where(lanes_of(both.shape) < FEAT, both, 0.0), axis=-1, keepdims=True
    ) * FEAT ** (-0.5)
    intersection = 1.0 + near + 0.5 * near * near

    length = span + 12
    queries = []
    for shift in range(0, 16, 4):
        moved = query_wide if shift == 0 else pltpu.roll(query_wide, shift, 1)
        queries.append(moved[:, :length].astype(jnp.bfloat16))
    row = lax.broadcasted_iota(jnp.int32, (count, HD), 0) & (rows - 1)
    found = jnp.zeros((count, HD), jnp.float32)
    for r in range(rows):
        first = span * r
        shift = first % 16
        product = jnp.dot(
            queries[shift // 4],
            state[first - shift : first - shift + length, :],
            preferred_element_type=jnp.float32,
        )
        found = jnp.where(row == r, product, found)
    fresh = lax.dot_general(normed, value_w[...], FLAT, preferred_element_type=jnp.float32)
    older = conv_state[...].astype(jnp.float32)
    mixed = conv_w[0:1] * older[:, 0] + conv_w[1:2] * older[:, 1] + conv_w[2:3] * fresh
    total = tokens * 0.25
    for h in range(heads):
        here = slice(h * rows, (h + 1) * rows)
        denominator = (
            jnp.sum(query_feats[here] * lin_norm[:, h, :], axis=-1, keepdims=True)
            + intersection[here]
        )
        attended = (
            (found[here] + intersection[here] * mixed[:, h * HD : (h + 1) * HD]) / denominator
        ).astype(jnp.bfloat16)
        total = total + jnp.dot(
            attended, out_w[h * HD : (h + 1) * HD, :], preferred_element_type=jnp.float32
        )
    update[...] = total


def linear_layer(pieces, near):
    return kernel_call(
        linear_kernel,
        0,
        "linear_layer",
        jax.ShapeDtypeStruct((pieces[0].shape[0], near["out_w"].shape[1]), jnp.float32),
        [VMEM] * 12,
        [],
        (*pieces, *(near[name] for name in LINEAR_NEAR)),
    )


def project_kernel(
    ids,
    tags,
    p0,
    p1,
    p2,
    p3,
    gain,
    v_w,
    qk_w,
    one,
    asked,
    key_new,
    value_new,
):
    rows, share = one.shape
    heads = share // HD
    layer_one = (p0[...] + p1[...] + p2[...] + p3[...]).astype(jnp.bfloat16)
    rounded = layer_one.astype(jnp.float32)
    mine = rounded[:, :share]
    for h in range(1, heads):
        mine = jnp.where(ids[2] == h, rounded[:, h * share : (h + 1) * share], mine)
    one[...] = mine.astype(jnp.bfloat16)
    normed = normed_rows(rounded, gain[...])
    value_new[...] = lax.dot_general(
        normed, v_w[...], FLAT, preferred_element_type=jnp.float32
    ).astype(jnp.bfloat16)
    query_key = jnp.dot(normed, qk_w[...], preferred_element_type=jnp.float32)
    width = query_key.shape[1]
    lane = lanes_of((rows, LANES))
    query = jnp.where(in_head(lane, 0), query_key[:, :LANES], 0.0)
    key = query
    for h in range(heads):
        if h:
            moved = pltpu.roll(query_key, width - h * HD, 1)[:, :LANES]
            query = jnp.where(in_head(lane, h), moved, query)
        moved = pltpu.roll(query_key, width - (h + 1) * HD, 1)[:, :LANES]
        key = jnp.where(in_head(lane, h), moved, key)
    query = jnp.where(lane == share, tags[:, 0:1], query)
    query = jnp.where(lane == share + 1, tags[:, 1:2], query)
    asked[...] = query.astype(jnp.bfloat16)
    key_new[...] = key[:, :share].astype(jnp.bfloat16)


def project(tags, pieces, near):
    rows = pieces[0].shape[0]
    share = near["value_w"].shape[0]
    return kernel_call(
        project_kernel,
        1,
        "project",
        [
            jax.ShapeDtypeStruct((rows, share), jnp.bfloat16),
            jax.ShapeDtypeStruct((rows, LANES), jnp.bfloat16),
            jax.ShapeDtypeStruct((rows, share), jnp.bfloat16),
            jax.ShapeDtypeStruct((rows, share), jnp.bfloat16),
        ],
        [VMEM] * 8,
        [],
        (tags, *pieces, near["gain"], near["value_w"], near["query_key_w"]),
    )


def window_pages(lengths, r):
    length = lengths[r]
    return jnp.maximum((length - WINDOW) // PAGE, 1), jnp.maximum((length - 2) // PAGE, 1)


def own_kernel(
    ids, lengths, asked, key_new, value_new, pages, summed_out, highest_out, total_out
):
    rows, share = key_new.shape
    bounds = [(lengths[r], *window_pages(lengths, r)) for r in range(rows)]
    head = lax.broadcasted_iota(jnp.int32, (8, share), 0)
    lane = lanes_of((8, share))
    mine = (lane >= head * HD) & (lane < (head + 1) * HD)
    scale = HD ** (-0.5)
    query = asked[:, :share].astype(jnp.float32)
    new_key = key_new[...].astype(jnp.float32)
    new_value = value_new[...].astype(jnp.float32)
    wide = jnp.concatenate([jnp.where(mine, query[r : r + 1], 0.0) for r in range(rows)], axis=0)
    keys = jnp.concatenate(
        [jnp.broadcast_to(new_key[r : r + 1], (8, share)) for r in range(rows)], axis=0
    )
    new_score = jnp.sum(wide * keys, axis=-1, keepdims=True) * scale
    token = lanes_of((8 * rows, 2 * PAGE))
    request = lax.broadcasted_iota(jnp.int32, (8 * rows, 2 * PAGE), 0) >> 3
    length = jnp.zeros(token.shape, jnp.int32)
    base = jnp.zeros(token.shape, jnp.int32)
    for r in range(rows):
        length = jnp.where(request == r, bounds[r][0], length)
        second = jnp.where(bounds[r][1] != bounds[r][2], bounds[r][2] - 1, -MAXP) * PAGE
        base = jnp.where(request == r, jnp.where(token < PAGE, bounds[r][1] * PAGE, second), base)
    position = base + token
    usable = (position >= length - WINDOW) & (position <= length - 2)
    scores = []
    for r in range(rows):
        low = wide[8 * r : 8 * r + 8].astype(jnp.bfloat16)
        scores.append(
            jnp.concatenate(
                [
                    jnp.dot(low, pages[r, slot, 0], preferred_element_type=jnp.float32)
                    for slot in range(2)
                ],
                axis=1,
            )
        )
    scores = jnp.where(usable, jnp.concatenate(scores, axis=0) * scale, MASKED)
    highest = jnp.maximum(jnp.max(scores, axis=-1, keepdims=True), new_score)
    exps = jnp.where(usable, jnp.exp(scores - highest), 0.0)
    exp_new = jnp.exp(new_score - highest)
    total = jnp.sum(exps, axis=-1, keepdims=True) + exp_new
    for r in range(rows):
        here = slice(8 * r, 8 * r + 8)
        low = exps[here].astype(jnp.bfloat16)
        found = exp_new[here] * new_value[r : r + 1]
        for slot in range(2):
            found = found + lax.dot_general(
                low[:, slot * PAGE : (slot + 1) * PAGE],
                pages[r, slot, 1],
                FLAT,
                preferred_element_type=jnp.float32,
            )
        for ref, value in (
            (summed_out, found),
            (highest_out, highest[here]),
            (total_out, total[here]),
        ):
            ref[r : r + 1, :] = jnp.sum(jnp.where(mine, value, 0.0), axis=0, keepdims=True)


def own_attention(lengths, asked, key_new, value_new, near):
    rows, share = key_new.shape
    return kernel_call(
        own_kernel,
        1,
        "own_attention",
        [jax.ShapeDtypeStruct((rows, share), jnp.float32)] * 3,
        [SMEM] + [VMEM] * 4,
        [],
        (lengths, asked, key_new, value_new, near["own_pages"]),
    )


def prompt_kernel(ids, a0, a1, a2, a3, near_pages, far_pages, o0, o1, o2, o3):
    rows = a0.shape[0]
    share = near_pages.shape[1]
    heads = share // HD
    pages = jnp.concatenate(
        [near_pages[i] for i in range(XN)] + [far_pages[i] for i in range(XN)], axis=1
    )
    asked = jnp.concatenate([ref[...].astype(jnp.float32) for ref in (a0, a1, a2, a3)], axis=0)
    count = asked.shape[0]
    lane = lanes_of(asked.shape)
    group = jnp.sum(jnp.where(lane == share, asked, 0.0), axis=-1, keepdims=True)
    start = jnp.sum(jnp.where(lane == share + 1, asked, 0.0), axis=-1, keepdims=True)
    group, start = group.astype(jnp.int32), start.astype(jnp.int32)
    query = jnp.concatenate(
        [jnp.where(in_head(lane, h), asked, 0.0)[:, :share] for h in range(heads)], axis=0
    ).astype(jnp.bfloat16)
    scores = jnp.dot(query, pages, preferred_element_type=jnp.float32) * HD ** (-0.5)
    token = lanes_of((count, 2 * XN * PAGE))
    z, x = ids[1] // XN, ids[1] % XN
    slot = token >> 7
    slot_group = jnp.where(slot < XN, z, (z + ZN // 2) & (ZN - 1)) * XN
    slot_group = slot_group + (x ^ (slot & (XN - 1)))
    offset = token & (PAGE - 1)
    usable = (slot_group == group) & (offset < HALF) & (offset + HALF >= start)
    lane = lanes_of((count, share))
    stat_lane = lanes_of((count, 128))
    weights = []
    stats = jnp.zeros((count, 128), jnp.float32)
    for h in range(heads):
        here = jnp.where(usable, scores[h * count : (h + 1) * count], MASKED)
        highest = jnp.max(here, axis=-1, keepdims=True)
        exps = jnp.where(usable, jnp.exp(here - highest), 0.0)
        total = jnp.sum(exps, axis=-1, keepdims=True)
        stats = jnp.where(stat_lane == h, highest, stats)
        stats = jnp.where(stat_lane == heads + h, total, stats)
        weights.append(pltpu.roll(exps, HALF, 1))
    found = lax.dot_general(
        jnp.concatenate(weights, axis=0).astype(jnp.bfloat16),
        pages,
        FLAT,
        preferred_element_type=jnp.float32,
    )
    summed = jnp.zeros((count, share), jnp.float32)
    for h in range(heads):
        summed = jnp.where(in_head(lane, h), found[h * count : (h + 1) * count], summed)
    for at, ref in enumerate((o0, o1, o2, o3)):
        ref[:, :share] = summed[at * rows : (at + 1) * rows]
        ref[:, share:LANES] = jnp.zeros((rows, LANES - share), jnp.float32)
        ref[:, LANES:] = stats[at * rows : (at + 1) * rows]


def prompt_attention(asked, near_pages, far_pages):
    rows = asked[0].shape[0]
    return kernel_call(
        prompt_kernel,
        1,
        "prompt_attention",
        [jax.ShapeDtypeStruct((rows, LANES + 128), jnp.float32)] * 4,
        [VMEM] * 6,
        [],
        (*asked, near_pages, far_pages),
    )


def combine_kernel(ids, summed, highest, total, r0, r1, r2, r3, out_w, s0, s1, s2, s3):
    rows, share = summed.shape
    heads = share // HD
    refs = (r0, r1, r2, r3)
    prompt_summed = sum(ref[:, :share] for ref in refs)
    stats = [ref[:, LANES:] for ref in refs]
    top = jnp.maximum(jnp.maximum(stats[0], stats[1]), jnp.maximum(stats[2], stats[3]))
    added = stats[0] + stats[1] + stats[2] + stats[3]
    lane = lanes_of((rows, share))
    prompt_highest = jnp.zeros((rows, share), jnp.float32)
    prompt_total = jnp.zeros((rows, share), jnp.float32)
    for h in range(heads):
        here = in_head(lane, h)
        prompt_highest = jnp.where(here, top[:, h : h + 1], prompt_highest)
        prompt_total = jnp.where(here, added[:, heads + h : heads + h + 1], prompt_total)
    peak = jnp.maximum(highest[...], prompt_highest)
    own_factor = jnp.exp(highest[...] - peak)
    prompt_factor = jnp.exp(prompt_highest - peak)
    whole = total[...] * own_factor + prompt_total * prompt_factor
    attended = (summed[...] * own_factor + prompt_summed * prompt_factor) / whole
    second = jnp.dot(attended.astype(jnp.bfloat16), out_w[...], preferred_element_type=jnp.float32)
    for steps, ref in enumerate((s0, s1, s2, s3)):
        slab = second[:, :share]
        for h in range(1, heads):
            slab = jnp.where(
                ((ids[2] + steps) & (heads - 1)) == h, second[:, h * share : (h + 1) * share], slab
            )
        ref[...] = slab


def combine(own, parts, near):
    return kernel_call(
        combine_kernel,
        1,
        "combine",
        [jax.ShapeDtypeStruct(own[0].shape, jnp.float32)] * 4,
        [VMEM] * 8,
        [],
        (*own, *parts, near["out_w"]),
    )


LINEAR_NEAR = (
    "gain",
    "feature_w",
    "state",
    "lin_norm",
    "conv_w",
    "conv_state",
    "value_w",
    "out_w",
)
SHARED_NEAR = ("gain", "value_w", "out_w")


def bring_near(arrays):
    names = list(arrays)
    count = len(names)
    both = [at for at, name in enumerate(names) if name in SHARED_NEAR]

    def copy_some(chosen, refs):
        sems = refs[-1]
        copies = [
            pltpu.make_async_copy(refs[at], refs[count + at], sems.at[at]) for at in chosen
        ]
        for copy in copies:
            copy.start()
        for copy in copies:
            copy.wait()

    near = kernel_call(
        lambda ids, *refs: copy_some(range(count), refs),
        0,
        "bring_near",
        [jax.ShapeDtypeStruct(array.shape, array.dtype) for array in arrays.values()],
        [HBM] * count,
        [pltpu.SemaphoreType.DMA((count,))],
        tuple(arrays.values()),
        4 << 20,
        bytes_only(arrays.values()),
        lambda ids, *refs: copy_some(both, refs),
    )
    return dict(zip(names, near))


def bytes_only(arrays):
    moved = sum(array.size * array.dtype.itemsize for array in arrays)
    return pl.CostEstimate(flops=0, bytes_accessed=2 * moved, transcendentals=0)


def window_kernel(
    ids, table, lengths, query_key_hbm, own_hbm, query_key_near, own_near, tags, key_sem, sems
):
    rows = tags.shape[0]
    total = own_hbm.shape[0]
    copies = [pltpu.make_async_copy(query_key_hbm, query_key_near, key_sem)]
    for r in range(rows):
        for slot, logical in enumerate(window_pages(lengths, r)):
            page = jnp.clip(table[r, logical] - GROUPS - ids[1] * total, 0, total - 1)
            copies.append(
                pltpu.make_async_copy(own_hbm.at[page], own_near.at[r, slot], sems.at[r, slot])
            )
    for copy in copies:
        copy.start()
    row = lax.broadcasted_iota(jnp.int32, tags.shape, 0)
    first = lanes_of(tags.shape) == 0
    marks = jnp.zeros(tags.shape, jnp.int32)
    for r in range(rows):
        start = jnp.minimum(lengths[r] - WINDOW, PAGE)
        marks = jnp.where(row == r, jnp.where(first, table[r, 0], start), marks)
    tags[...] = marks.astype(jnp.float32)
    for copy in copies:
        copy.wait()


def bring_windows(table, lengths, query_key_w, own_pages):
    rows = lengths.shape[0]
    windows = jax.ShapeDtypeStruct((rows, 2) + own_pages.shape[1:], own_pages.dtype)
    return kernel_call(
        window_kernel,
        1,
        "bring_windows",
        [
            jax.ShapeDtypeStruct(query_key_w.shape, query_key_w.dtype),
            windows,
            jax.ShapeDtypeStruct((rows, 128), jnp.float32),
        ],
        [SMEM] * 2 + [HBM] * 2,
        [pltpu.SemaphoreType.DMA, pltpu.SemaphoreType.DMA((rows, 2))],
        (table, lengths, query_key_w, own_pages),
        1 << 20,
        bytes_only([query_key_w, windows]),
    )


def page_kernel(ids, pages_hbm, page, pages, sem):
    copy = pltpu.make_async_copy(pages_hbm.at[0], pages, sem)
    copy.start()
    copy.wait()
    lane = lanes_of(page.shape)
    keys = pltpu.roll(pages[0].astype(jnp.float32), HALF, 1)
    page[...] = jnp.where(lane < HALF, keys, pages[1].astype(jnp.float32)).astype(jnp.bfloat16)


def window_page(prompt_pages):
    shape = prompt_pages.shape[1:]
    return kernel_call(
        page_kernel,
        None,
        "window_page",
        jax.ShapeDtypeStruct(shape[1:], jnp.bfloat16),
        [HBM],
        [pltpu.VMEM(shape, jnp.bfloat16), pltpu.SemaphoreType.DMA],
        (prompt_pages,),
        cost=pl.CostEstimate(flops=0, bytes_accessed=16 << 20, transcendentals=0),
    )


def body(
    tokens,
    norm_gain,
    feature_w,
    query_key_w,
    value_w,
    out_w,
    conv_w,
    conv_state,
    lin_state,
    lin_norm,
    own_pages,
    prompt_pages,
    page_table,
    lengths,
):
    pages_first = prompt_pages.transpose(0, 1, 3, 2)
    stored = {
        "gain": norm_gain,
        "feature_w": feature_w,
        "state": lin_state.transpose(0, 2, 1, 3).reshape(-1, HD),
        "lin_norm": lin_norm,
        "conv_w": conv_w,
        "conv_state": conv_state,
        "value_w": value_w.transpose(0, 2, 1)[0],
        "out_w": out_w[0],
    }

    section_index = lax.axis_index("section")
    page = window_page(pages_first)
    far_page = z_shift(page, ZN // 2)
    received = [head_shift(tokens, k) for k in (1, 3, 2)]
    far_page, received = lax.optimization_barrier((far_page, received))
    page = jnp.where(section_index == 0, far_page, page)
    stored, page = lax.optimization_barrier((stored, page))
    near = bring_near(stored)
    other, near = lax.optimization_barrier((x_swap(page, 1), near))
    two_pages = jnp.stack([page, other])
    update = linear_layer([tokens] + received, near)
    next_pages, update = lax.optimization_barrier((x_swap(two_pages, 2), update))
    near_pages = jnp.concatenate([two_pages, next_pages])
    far_pages = lax.ppermute(near_pages, "section", [(0, 1), (1, 0)])
    own_pages = own_pages.transpose(0, 1, 3, 2)
    query_key_w, own_pages, table, ends, update = lax.optimization_barrier(
        (query_key_w, own_pages, page_table, lengths, update)
    )
    near["query_key_w"], near["own_pages"], tags = bring_windows(
        table, ends, query_key_w, own_pages
    )
    swapped = [section_swap(update, k) for k in (0, 1, 3, 2)]
    one_share, packed, key_new, value_new = project(tags, swapped, near)
    asked = [packed] + [z_shift(packed, k) for k in (1, 7, 2)]
    own = own_attention(lengths, packed, key_new, value_new, near)
    asked, own = lax.optimization_barrier((asked, own))
    answers = prompt_attention(asked, near_pages, far_pages)
    answers, one_share = lax.optimization_barrier((answers, one_share))
    parts = [answers[0]] + [z_shift(answers[at], -k) for at, k in ((1, 1), (2, 7), (3, 2))]
    one_back = lax.ppermute(one_share, "section", [(1, 0), (0, 1)])
    parts, one_back = lax.optimization_barrier((parts, one_back))
    slabs = combine(own, parts, near)
    total = one_share.astype(jnp.float32) + slabs[0]
    for piece in [head_shift(slabs[k], k) for k in (1, 3, 2)]:
        total = total + piece
    output = jnp.where(section_index == 0, one_back, total.astype(jnp.bfloat16))
    return output[None]


def solution(mesh):
    placed = (
        P("req", "head"),
        P("section", None),
        P(None, "head"),
        P(None, "head"),
        P("section", None, "head"),
        P("section", "head", None),
        P(None, "head"),
        P("req", None, "head"),
        P("req", "head", None, None),
        P("req", "head", None),
        P("req", None, None, "head"),
        P("req", None, None, "head"),
        P("req", None),
        P("req"),
    )
    return jax.shard_map(
        body, mesh=mesh, in_specs=placed, out_specs=P("section", "req", "head"), check_vma=False
    )
```

```python
import jax
import jax.numpy as jnp
from jax import lax
from jax.experimental import pallas as pl
from jax.experimental.pallas import tpu as pltpu
from jax.sharding import PartitionSpec as P

HD = 112
FEAT = 16
WINDOW = 64
PAGE = 128
HALF = 64
MAXP = 256
GROUPS = 32
XN = 4
ZN = 8
LANES = 512
TAYLOR = 273
TAYLOR_LANES = 384
SPREAD = 1152

EPSILON = 1e-06
MASKED = -1e30


def head_shift(value, steps):
    count = lax.axis_size("head")
    return lax.ppermute(value, "head", [(i, (i + steps) % count) for i in range(count)])


def z_shift(value, steps):
    return lax.ppermute(
        value,
        "req",
        [(z * XN + i, (z + steps) % ZN * XN + i) for z in range(ZN) for i in range(XN)],
    )


def x_shift(value, steps):
    return lax.ppermute(
        value,
        "req",
        [(z * XN + i, z * XN + (i + steps) % XN) for z in range(ZN) for i in range(XN)],
    )


def far_swap(value):
    count = XN * ZN
    return lax.ppermute(
        value,
        ("section", "req"),
        [(count + i, count + (i + count // 2) % count) for i in range(count)],
    )


def section_swap(value, steps):
    count = lax.axis_size("head")
    there = [(i, count + (i + steps) % count) for i in range(count)]
    return lax.ppermute(value, ("section", "head"), there + [(b, a) for a, b in there])


VMEM = pl.BlockSpec(memory_space=pltpu.VMEM)
SMEM = pl.BlockSpec(memory_space=pltpu.SMEM)
HBM = pl.BlockSpec(memory_space=pltpu.HBM)
FLAT = (((1,), (1,)), ((), ()))


def normed_rows(values, gain_row):
    factor = lax.rsqrt(jnp.mean(values * values, axis=-1, keepdims=True) + EPSILON)
    return (values * factor * gain_row).astype(jnp.bfloat16)


def lanes_of(shape):
    return lax.broadcasted_iota(jnp.int32, shape, len(shape) - 1)


def in_head(lane, h):
    return (lane >= h * HD) & (lane < (h + 1) * HD)


def place():
    return lax.axis_index("section"), lax.axis_index("req"), lax.axis_index("head")


def kernel_call(
    kernel,
    section,
    name,
    out_shape,
    in_specs,
    scratch_shapes,
    args,
    vmem=6 << 20,
    cost=None,
    elsewhere=None,
):
    def run(*refs):
        ids = place()

        @pl.when(ids[0] == section)
        def _():
            kernel(ids, *refs)

        if elsewhere is not None:

            @pl.when(ids[0] != section)
            def _():
                elsewhere(ids, *refs)

    args = [
        pltpu.with_memory_space_constraint(arg, pltpu.HBM) if spec is HBM else arg
        for arg, spec in zip(args, in_specs, strict=True)
    ]
    return pl.pallas_call(
        run,
        out_shape=out_shape,
        in_specs=in_specs,
        out_specs=jax.tree.map(lambda _: VMEM, out_shape),
        scratch_shapes=scratch_shapes,
        compiler_params=pltpu.CompilerParams(vmem_limit_bytes=vmem),
        cost_estimate=cost,
        name=name,
    )(*args)


def expansion(features, width, repeat):
    lane = lax.broadcasted_iota(jnp.int32, (features, 2 * width), 1)
    source = lax.broadcasted_iota(jnp.int32, (features, 2 * width), 0)
    left = lane < width
    at = jnp.where(left, lane, lane - width) >> (repeat.bit_length() - 1)
    linear = left & (at > 0) & (at <= FEAT) & (source == at - 1)
    pair = at - (FEAT + 1)
    wanted = jnp.where(left, pair >> 4, pair & (FEAT - 1))
    quad = (pair >= 0) & (pair < FEAT * FEAT) & (source == wanted)
    return jnp.where(linear | quad, 1.0, 0.0).astype(jnp.bfloat16)


def taylor_rows(left, right, feature):
    scale = FEAT ** (-0.25)
    left, right = left * scale, right * scale
    return jnp.where(
        feature == 0, 1.0, jnp.where(feature <= FEAT, left, left * right * 0.5**0.5)
    )


def linear_kernel(
    ids,
    t0,
    t1,
    t2,
    t3,
    gain,
    feature_w,
    state,
    lin_norm,
    conv_w,
    conv_state,
    value_w,
    out_w,
    update,
):
    rows, share = t0.shape
    heads = share // HD
    span = TAYLOR * heads
    by_state = expansion(128, SPREAD, heads)
    by_norm = expansion(128, TAYLOR_LANES, 1)
    expand = jnp.concatenate([by_state, by_norm], axis=1)

    own = ids[2]
    got = [ref[...].astype(jnp.float32) for ref in (t0, t1, t3, t2)]
    whole = []
    for place in range(heads):
        piece = got[0]
        for back in range(1, heads):
            piece = jnp.where(((own - back) & (heads - 1)) == place, got[back], piece)
        whole.append(piece)
    tokens = jnp.concatenate(whole, axis=1)
    normed = normed_rows(tokens, gain[...])
    feats = jnp.dot(normed, feature_w[...], preferred_element_type=jnp.float32)
    by_head = jnp.concatenate(
        [feats] + [pltpu.roll(feats, 128 - 2 * FEAT * h, 1) for h in range(1, heads)], axis=0
    )
    high = by_head.astype(jnp.bfloat16)
    rest = by_head - high.astype(jnp.float32)
    middle = rest.astype(jnp.bfloat16)
    low = (rest - middle.astype(jnp.float32)).astype(jnp.bfloat16)
    spread = jnp.dot(
        jnp.concatenate([high, middle, low], axis=0), expand, preferred_element_type=jnp.float32
    )
    count = heads * rows
    spread = spread[:count] + spread[count : 2 * count] + spread[2 * count :]
    lane = lanes_of((count, SPREAD))
    head = lax.broadcasted_iota(jnp.int32, (count, SPREAD), 0) >> 3
    query_wide = taylor_rows(spread[:, :SPREAD], spread[:, SPREAD : 2 * SPREAD], lane >> 2)
    query_wide = jnp.where(((lane & (heads - 1)) == head) & (lane < span), query_wide, 0.0)
    query_feats = taylor_rows(
        spread[:, 2 * SPREAD : 2 * SPREAD + TAYLOR_LANES],
        spread[:, 2 * SPREAD + TAYLOR_LANES :],
        lanes_of((count, TAYLOR_LANES)),
    )[:, :TAYLOR]
    both = by_head * pltpu.roll(by_head, 128 - FEAT, 1)
    near = jnp.sum(
        jnp.where(lanes_of(both.shape) < FEAT, both, 0.0), axis=-1, keepdims=True
    ) * FEAT ** (-0.5)
    intersection = 1.0 + near + 0.5 * near * near

    length = span + 12
    queries = []
    for shift in range(0, 16, 4):
        moved = query_wide if shift == 0 else pltpu.roll(query_wide, shift, 1)
        queries.append(moved[:, :length].astype(jnp.bfloat16))
    row = lax.broadcasted_iota(jnp.int32, (count, HD), 0) & (rows - 1)
    found = jnp.zeros((count, HD), jnp.float32)
    for r in range(rows):
        first = span * r
        shift = first % 16
        product = jnp.dot(
            queries[shift // 4],
            state[first - shift : first - shift + length, :],
            preferred_element_type=jnp.float32,
        )
        found = jnp.where(row == r, product, found)
    fresh = lax.dot_general(normed, value_w[...], FLAT, preferred_element_type=jnp.float32)
    older = conv_state[...].astype(jnp.float32)
    mixed = conv_w[0:1] * older[:, 0] + conv_w[1:2] * older[:, 1] + conv_w[2:3] * fresh
    total = tokens * 0.25
    for h in range(heads):
        here = slice(h * rows, (h + 1) * rows)
        denominator = (
            jnp.sum(query_feats[here] * lin_norm[:, h, :], axis=-1, keepdims=True)
            + intersection[here]
        )
        attended = (
            (found[here] + intersection[here] * mixed[:, h * HD : (h + 1) * HD]) / denominator
        ).astype(jnp.bfloat16)
        total = total + jnp.dot(
            attended, out_w[h * HD : (h + 1) * HD, :], preferred_element_type=jnp.float32
        )
    update[...] = total


def linear_layer(pieces, near):
    return kernel_call(
        linear_kernel,
        0,
        "linear_layer",
        jax.ShapeDtypeStruct((pieces[0].shape[0], near["out_w"].shape[1]), jnp.float32),
        [VMEM] * 12,
        [],
        (*pieces, *(near[name] for name in LINEAR_NEAR)),
    )


def project_kernel(
    ids,
    tags,
    p0,
    p1,
    p2,
    p3,
    gain,
    v_w,
    qk_w,
    one,
    asked,
    key_new,
    value_new,
):
    rows, share = one.shape
    heads = share // HD
    layer_one = (p0[...] + p1[...] + p2[...] + p3[...]).astype(jnp.bfloat16)
    rounded = layer_one.astype(jnp.float32)
    mine = rounded[:, :share]
    for h in range(1, heads):
        mine = jnp.where(ids[2] == h, rounded[:, h * share : (h + 1) * share], mine)
    one[...] = mine.astype(jnp.bfloat16)
    normed = normed_rows(rounded, gain[...])
    value_new[...] = lax.dot_general(
        normed, v_w[...], FLAT, preferred_element_type=jnp.float32
    ).astype(jnp.bfloat16)
    query_key = jnp.dot(normed, qk_w[...], preferred_element_type=jnp.float32)
    width = query_key.shape[1]
    lane = lanes_of((rows, LANES))
    query = jnp.where(in_head(lane, 0), query_key[:, :LANES], 0.0)
    key = query
    for h in range(heads):
        if h:
            moved = pltpu.roll(query_key, width - h * HD, 1)[:, :LANES]
            query = jnp.where(in_head(lane, h), moved, query)
        moved = pltpu.roll(query_key, width - (h + 1) * HD, 1)[:, :LANES]
        key = jnp.where(in_head(lane, h), moved, key)
    query = jnp.where(lane == share, tags[:, 0:1], query)
    query = jnp.where(lane == share + 1, tags[:, 1:2], query)
    asked[...] = query.astype(jnp.bfloat16)
    key_new[...] = key[:, :share].astype(jnp.bfloat16)


def project(tags, pieces, near):
    rows = pieces[0].shape[0]
    share = near["value_w"].shape[0]
    return kernel_call(
        project_kernel,
        1,
        "project",
        [
            jax.ShapeDtypeStruct((rows, share), jnp.bfloat16),
            jax.ShapeDtypeStruct((rows, LANES), jnp.bfloat16),
            jax.ShapeDtypeStruct((rows, share), jnp.bfloat16),
            jax.ShapeDtypeStruct((rows, share), jnp.bfloat16),
        ],
        [VMEM] * 8,
        [],
        (tags, *pieces, near["gain"], near["value_w"], near["query_key_w"]),
    )


def window_pages(lengths, r):
    length = lengths[r]
    return jnp.maximum((length - WINDOW) // PAGE, 1), jnp.maximum((length - 2) // PAGE, 1)


def own_kernel(
    ids, lengths, asked, key_new, value_new, pages, summed_out, highest_out, total_out
):
    rows, share = key_new.shape
    bounds = [(lengths[r], *window_pages(lengths, r)) for r in range(rows)]
    head = lax.broadcasted_iota(jnp.int32, (8, share), 0)
    lane = lanes_of((8, share))
    mine = (lane >= head * HD) & (lane < (head + 1) * HD)
    scale = HD ** (-0.5)
    query = asked[:, :share].astype(jnp.float32)
    new_key = key_new[...].astype(jnp.float32)
    new_value = value_new[...].astype(jnp.float32)
    wide = jnp.concatenate([jnp.where(mine, query[r : r + 1], 0.0) for r in range(rows)], axis=0)
    keys = jnp.concatenate(
        [jnp.broadcast_to(new_key[r : r + 1], (8, share)) for r in range(rows)], axis=0
    )
    new_score = jnp.sum(wide * keys, axis=-1, keepdims=True) * scale
    token = lanes_of((8 * rows, 2 * PAGE))
    request = lax.broadcasted_iota(jnp.int32, (8 * rows, 2 * PAGE), 0) >> 3
    length = jnp.zeros(token.shape, jnp.int32)
    base = jnp.zeros(token.shape, jnp.int32)
    for r in range(rows):
        length = jnp.where(request == r, bounds[r][0], length)
        second = jnp.where(bounds[r][1] != bounds[r][2], bounds[r][2] - 1, -MAXP) * PAGE
        base = jnp.where(request == r, jnp.where(token < PAGE, bounds[r][1] * PAGE, second), base)
    position = base + token
    usable = (position >= length - WINDOW) & (position <= length - 2)
    scores = []
    for r in range(rows):
        low = wide[8 * r : 8 * r + 8].astype(jnp.bfloat16)
        scores.append(
            jnp.concatenate(
                [
                    jnp.dot(low, pages[r, slot, 0], preferred_element_type=jnp.float32)
                    for slot in range(2)
                ],
                axis=1,
            )
        )
    scores = jnp.where(usable, jnp.concatenate(scores, axis=0) * scale, MASKED)
    highest = jnp.maximum(jnp.max(scores, axis=-1, keepdims=True), new_score)
    exps = jnp.where(usable, jnp.exp(scores - highest), 0.0)
    exp_new = jnp.exp(new_score - highest)
    total = jnp.sum(exps, axis=-1, keepdims=True) + exp_new
    for r in range(rows):
        here = slice(8 * r, 8 * r + 8)
        low = exps[here].astype(jnp.bfloat16)
        found = exp_new[here] * new_value[r : r + 1]
        for slot in range(2):
            found = found + lax.dot_general(
                low[:, slot * PAGE : (slot + 1) * PAGE],
                pages[r, slot, 1],
                FLAT,
                preferred_element_type=jnp.float32,
            )
        for ref, value in (
            (summed_out, found),
            (highest_out, highest[here]),
            (total_out, total[here]),
        ):
            ref[r : r + 1, :] = jnp.sum(jnp.where(mine, value, 0.0), axis=0, keepdims=True)


def own_attention(lengths, asked, key_new, value_new, near):
    rows, share = key_new.shape
    return kernel_call(
        own_kernel,
        1,
        "own_attention",
        [jax.ShapeDtypeStruct((rows, share), jnp.float32)] * 3,
        [SMEM] + [VMEM] * 4,
        [],
        (lengths, asked, key_new, value_new, near["own_pages"]),
    )


def prompt_kernel(ids, a0, a1, a2, a3, near_pages, far_pages, o0, o1, o2, o3):
    rows = a0.shape[0]
    share = near_pages.shape[1]
    heads = share // HD
    pages = jnp.concatenate(
        [near_pages[i] for i in range(XN)] + [far_pages[i] for i in range(XN)], axis=1
    )
    asked = jnp.concatenate([ref[...].astype(jnp.float32) for ref in (a0, a1, a2, a3)], axis=0)
    count = asked.shape[0]
    lane = lanes_of(asked.shape)
    group = jnp.sum(jnp.where(lane == share, asked, 0.0), axis=-1, keepdims=True)
    start = jnp.sum(jnp.where(lane == share + 1, asked, 0.0), axis=-1, keepdims=True)
    group, start = group.astype(jnp.int32), start.astype(jnp.int32)
    query = jnp.concatenate(
        [jnp.where(in_head(lane, h), asked, 0.0)[:, :share] for h in range(heads)], axis=0
    ).astype(jnp.bfloat16)
    scores = jnp.dot(query, pages, preferred_element_type=jnp.float32) * HD ** (-0.5)
    token = lanes_of((count, 2 * XN * PAGE))
    z, x = ids[1] // XN, ids[1] % XN
    slot = token >> 7
    slot_group = jnp.where(slot < XN, z, (z + ZN // 2) & (ZN - 1)) * XN
    slot_group = slot_group + ((slot + x + XN - 1) & (XN - 1))
    offset = token & (PAGE - 1)
    usable = (slot_group == group) & (offset < HALF) & (offset + HALF >= start)
    lane = lanes_of((count, share))
    stat_lane = lanes_of((count, 128))
    weights = []
    stats = jnp.zeros((count, 128), jnp.float32)
    for h in range(heads):
        here = jnp.where(usable, scores[h * count : (h + 1) * count], MASKED)
        highest = jnp.max(here, axis=-1, keepdims=True)
        exps = jnp.where(usable, jnp.exp(here - highest), 0.0)
        total = jnp.sum(exps, axis=-1, keepdims=True)
        stats = jnp.where(stat_lane == h, highest, stats)
        stats = jnp.where(stat_lane == heads + h, total, stats)
        weights.append(pltpu.roll(exps, HALF, 1))
    found = lax.dot_general(
        jnp.concatenate(weights, axis=0).astype(jnp.bfloat16),
        pages,
        FLAT,
        preferred_element_type=jnp.float32,
    )
    summed = jnp.zeros((count, share), jnp.float32)
    for h in range(heads):
        summed = jnp.where(in_head(lane, h), found[h * count : (h + 1) * count], summed)
    for at, ref in enumerate((o0, o1, o2, o3)):
        ref[:, :share] = summed[at * rows : (at + 1) * rows]
        ref[:, share:LANES] = jnp.zeros((rows, LANES - share), jnp.float32)
        ref[:, LANES:] = stats[at * rows : (at + 1) * rows]


def prompt_attention(asked, near_pages, far_pages):
    rows = asked[0].shape[0]
    return kernel_call(
        prompt_kernel,
        1,
        "prompt_attention",
        [jax.ShapeDtypeStruct((rows, LANES + 128), jnp.float32)] * 4,
        [VMEM] * 6,
        [],
        (*asked, near_pages, far_pages),
    )


def combine_kernel(ids, summed, highest, total, r0, r1, r2, r3, out_w, s0, s1, s2, s3):
    rows, share = summed.shape
    heads = share // HD
    refs = (r0, r1, r2, r3)
    prompt_summed = sum(ref[:, :share] for ref in refs)
    stats = [ref[:, LANES:] for ref in refs]
    top = jnp.maximum(jnp.maximum(stats[0], stats[1]), jnp.maximum(stats[2], stats[3]))
    added = stats[0] + stats[1] + stats[2] + stats[3]
    lane = lanes_of((rows, share))
    prompt_highest = jnp.zeros((rows, share), jnp.float32)
    prompt_total = jnp.zeros((rows, share), jnp.float32)
    for h in range(heads):
        here = in_head(lane, h)
        prompt_highest = jnp.where(here, top[:, h : h + 1], prompt_highest)
        prompt_total = jnp.where(here, added[:, heads + h : heads + h + 1], prompt_total)
    peak = jnp.maximum(highest[...], prompt_highest)
    own_factor = jnp.exp(highest[...] - peak)
    prompt_factor = jnp.exp(prompt_highest - peak)
    whole = total[...] * own_factor + prompt_total * prompt_factor
    attended = (summed[...] * own_factor + prompt_summed * prompt_factor) / whole
    second = jnp.dot(attended.astype(jnp.bfloat16), out_w[...], preferred_element_type=jnp.float32)
    for steps, ref in enumerate((s0, s1, s2, s3)):
        slab = second[:, :share]
        for h in range(1, heads):
            slab = jnp.where(
                ((ids[2] + steps) & (heads - 1)) == h, second[:, h * share : (h + 1) * share], slab
            )
        ref[...] = slab


def combine(own, parts, near):
    return kernel_call(
        combine_kernel,
        1,
        "combine",
        [jax.ShapeDtypeStruct(own[0].shape, jnp.float32)] * 4,
        [VMEM] * 8,
        [],
        (*own, *parts, near["out_w"]),
    )


LINEAR_NEAR = (
    "gain",
    "feature_w",
    "state",
    "lin_norm",
    "conv_w",
    "conv_state",
    "value_w",
    "out_w",
)
SHARED_NEAR = ("gain", "value_w", "out_w")


def bring_near(arrays):
    names = list(arrays)
    count = len(names)
    both = [at for at, name in enumerate(names) if name in SHARED_NEAR]

    def copy_some(chosen, refs):
        sems = refs[-1]
        copies = [
            pltpu.make_async_copy(refs[at], refs[count + at], sems.at[at]) for at in chosen
        ]
        for copy in copies:
            copy.start()
        for copy in copies:
            copy.wait()

    near = kernel_call(
        lambda ids, *refs: copy_some(range(count), refs),
        0,
        "bring_near",
        [jax.ShapeDtypeStruct(array.shape, array.dtype) for array in arrays.values()],
        [HBM] * count,
        [pltpu.SemaphoreType.DMA((count,))],
        tuple(arrays.values()),
        4 << 20,
        bytes_only(arrays.values()),
        lambda ids, *refs: copy_some(both, refs),
    )
    return dict(zip(names, near))


def bytes_only(arrays):
    moved = sum(array.size * array.dtype.itemsize for array in arrays)
    return pl.CostEstimate(flops=0, bytes_accessed=2 * moved, transcendentals=0)


def window_kernel(
    ids, table, lengths, query_key_hbm, own_hbm, query_key_near, own_near, tags, key_sem, sems
):
    rows = tags.shape[0]
    total = own_hbm.shape[0]
    copies = [pltpu.make_async_copy(query_key_hbm, query_key_near, key_sem)]
    for r in range(rows):
        for slot, logical in enumerate(window_pages(lengths, r)):
            page = jnp.clip(table[r, logical] - GROUPS - ids[1] * total, 0, total - 1)
            copies.append(
                pltpu.make_async_copy(own_hbm.at[page], own_near.at[r, slot], sems.at[r, slot])
            )
    for copy in copies:
        copy.start()
    row = lax.broadcasted_iota(jnp.int32, tags.shape, 0)
    first = lanes_of(tags.shape) == 0
    marks = jnp.zeros(tags.shape, jnp.int32)
    for r in range(rows):
        start = jnp.minimum(lengths[r] - WINDOW, PAGE)
        marks = jnp.where(row == r, jnp.where(first, table[r, 0], start), marks)
    tags[...] = marks.astype(jnp.float32)
    for copy in copies:
        copy.wait()


def bring_windows(table, lengths, query_key_w, own_pages):
    rows = lengths.shape[0]
    windows = jax.ShapeDtypeStruct((rows, 2) + own_pages.shape[1:], own_pages.dtype)
    return kernel_call(
        window_kernel,
        1,
        "bring_windows",
        [
            jax.ShapeDtypeStruct(query_key_w.shape, query_key_w.dtype),
            windows,
            jax.ShapeDtypeStruct((rows, 128), jnp.float32),
        ],
        [SMEM] * 2 + [HBM] * 2,
        [pltpu.SemaphoreType.DMA, pltpu.SemaphoreType.DMA((rows, 2))],
        (table, lengths, query_key_w, own_pages),
        1 << 20,
        bytes_only([query_key_w, windows]),
    )


def page_kernel(ids, pages_hbm, page, pages, sem):
    copy = pltpu.make_async_copy(pages_hbm.at[0], pages, sem)
    copy.start()
    copy.wait()
    lane = lanes_of(page.shape)
    keys = pltpu.roll(pages[0].astype(jnp.float32), HALF, 1)
    page[...] = jnp.where(lane < HALF, keys, pages[1].astype(jnp.float32)).astype(jnp.bfloat16)


def window_page(prompt_pages):
    shape = prompt_pages.shape[1:]
    return kernel_call(
        page_kernel,
        1,
        "window_page",
        jax.ShapeDtypeStruct(shape[1:], jnp.bfloat16),
        [HBM],
        [pltpu.VMEM(shape, jnp.bfloat16), pltpu.SemaphoreType.DMA],
        (prompt_pages,),
        cost=pl.CostEstimate(flops=0, bytes_accessed=16 << 20, transcendentals=0),
    )


def body(
    tokens,
    norm_gain,
    feature_w,
    query_key_w,
    value_w,
    out_w,
    conv_w,
    conv_state,
    lin_state,
    lin_norm,
    own_pages,
    prompt_pages,
    page_table,
    lengths,
):
    pages_first = prompt_pages.transpose(0, 1, 3, 2)
    stored = {
        "gain": norm_gain,
        "feature_w": feature_w,
        "state": lin_state.transpose(0, 2, 1, 3).reshape(-1, HD),
        "lin_norm": lin_norm,
        "conv_w": conv_w,
        "conv_state": conv_state,
        "value_w": value_w.transpose(0, 2, 1)[0],
        "out_w": out_w[0],
    }

    page = window_page(pages_first)
    row_pages = [x_shift(page, k) for k in (1, 3, 2)]
    row_pages[0], last_tokens = lax.optimization_barrier((row_pages[0], tokens))
    received = [head_shift(tokens, 1), head_shift(tokens, 3), head_shift(last_tokens, 2)]
    near, received = lax.optimization_barrier((bring_near(stored), received))
    near_pages = jnp.stack([row_pages[0], page, row_pages[1], row_pages[2]])
    near_pages, received = lax.optimization_barrier((near_pages, received))
    far_pages = far_swap(near_pages)
    update = linear_layer([tokens] + received, near)
    own_pages = own_pages.transpose(0, 1, 3, 2)
    query_key_w, own_pages, table, ends, update = lax.optimization_barrier(
        (query_key_w, own_pages, page_table, lengths, update)
    )
    near["query_key_w"], near["own_pages"], tags = bring_windows(
        table, ends, query_key_w, own_pages
    )
    swapped = [section_swap(update, k) for k in (0, 1, 3, 2)]
    one_share, packed, key_new, value_new = project(tags, swapped, near)
    asked = [packed] + [z_shift(packed, k) for k in (1, 7, 2)]
    own = own_attention(lengths, packed, key_new, value_new, near)
    asked, own = lax.optimization_barrier((asked, own))
    answers = prompt_attention(asked, near_pages, far_pages)
    answers, one_share = lax.optimization_barrier((answers, one_share))
    parts = [answers[0]] + [z_shift(answers[at], -k) for at, k in ((1, 1), (2, 7), (3, 2))]
    one_back = lax.ppermute(one_share, "section", [(1, 0), (0, 1)])
    parts, one_back = lax.optimization_barrier((parts, one_back))
    slabs = combine(own, parts, near)
    section_index = lax.axis_index("section")
    total = one_share.astype(jnp.float32) + slabs[0]
    for piece in [head_shift(slabs[k], k) for k in (1, 3, 2)]:
        total = total + piece
    output = jnp.where(section_index == 0, one_back, total.astype(jnp.bfloat16))
    return output[None]


def solution(mesh):
    placed = (
        P("req", "head"),
        P("section", None),
        P(None, "head"),
        P(None, "head"),
        P("section", None, "head"),
        P("section", "head", None),
        P(None, "head"),
        P("req", None, "head"),
        P("req", "head", None, None),
        P("req", "head", None),
        P("req", None, None, "head"),
        P("req", None, None, "head"),
        P("req", None),
        P("req"),
    )
    return jax.shard_map(
        body, mesh=mesh, in_specs=placed, out_specs=P("section", "req", "head"), check_vma=False
    )
```

```python
import jax
import jax.numpy as jnp
from jax import lax
from jax.experimental import pallas as pl
from jax.experimental.pallas import tpu as pltpu
from jax.sharding import PartitionSpec as P

HD = 112
FEAT = 16
WINDOW = 64
PAGE = 128
HALF = 64
MAXP = 256
GROUPS = 32
XN = 4
ZN = 8
LANES = 512
TAYLOR = 273
TAYLOR_LANES = 384
SPREAD = 1152

EPSILON = 1e-06
MASKED = -1e30


def head_shift(value, steps):
    count = lax.axis_size("head")
    return lax.ppermute(value, "head", [(i, (i + steps) % count) for i in range(count)])


def z_shift(value, steps):
    return lax.ppermute(
        value,
        "req",
        [(z * XN + i, (z + steps) % ZN * XN + i) for z in range(ZN) for i in range(XN)],
    )


def x_shift(value, steps):
    return lax.ppermute(
        value,
        "req",
        [(z * XN + i, z * XN + (i + steps) % XN) for z in range(ZN) for i in range(XN)],
    )


def far_swap(value):
    count = XN * ZN
    return lax.ppermute(
        value,
        ("section", "req"),
        [(count + i, count + (i + count // 2) % count) for i in range(count)],
    )


def section_swap(value, steps):
    count = lax.axis_size("head")
    there = [(i, count + (i + steps) % count) for i in range(count)]
    return lax.ppermute(value, ("section", "head"), there + [(b, a) for a, b in there])


VMEM = pl.BlockSpec(memory_space=pltpu.VMEM)
SMEM = pl.BlockSpec(memory_space=pltpu.SMEM)
HBM = pl.BlockSpec(memory_space=pltpu.HBM)
FLAT = (((1,), (1,)), ((), ()))


def normed_rows(values, gain_row):
    factor = lax.rsqrt(jnp.mean(values * values, axis=-1, keepdims=True) + EPSILON)
    return (values * factor * gain_row).astype(jnp.bfloat16)


def lanes_of(shape):
    return lax.broadcasted_iota(jnp.int32, shape, len(shape) - 1)


def in_head(lane, h):
    return (lane >= h * HD) & (lane < (h + 1) * HD)


def place():
    return lax.axis_index("section"), lax.axis_index("req"), lax.axis_index("head")


def kernel_call(
    kernel,
    section,
    name,
    out_shape,
    in_specs,
    scratch_shapes,
    args,
    vmem=6 << 20,
    cost=None,
    elsewhere=None,
):
    def run(*refs):
        ids = place()

        @pl.when(ids[0] == section)
        def _():
            kernel(ids, *refs)

        if elsewhere is not None:

            @pl.when(ids[0] != section)
            def _():
                elsewhere(ids, *refs)

    args = [
        pltpu.with_memory_space_constraint(arg, pltpu.HBM) if spec is HBM else arg
        for arg, spec in zip(args, in_specs, strict=True)
    ]
    return pl.pallas_call(
        run,
        out_shape=out_shape,
        in_specs=in_specs,
        out_specs=jax.tree.map(lambda _: VMEM, out_shape),
        scratch_shapes=scratch_shapes,
        compiler_params=pltpu.CompilerParams(vmem_limit_bytes=vmem),
        cost_estimate=cost,
        name=name,
    )(*args)


def expansion(features, width, repeat):
    lane = lax.broadcasted_iota(jnp.int32, (features, 2 * width), 1)
    source = lax.broadcasted_iota(jnp.int32, (features, 2 * width), 0)
    left = lane < width
    at = jnp.where(left, lane, lane - width) >> (repeat.bit_length() - 1)
    linear = left & (at > 0) & (at <= FEAT) & (source == at - 1)
    pair = at - (FEAT + 1)
    wanted = jnp.where(left, pair >> 4, pair & (FEAT - 1))
    quad = (pair >= 0) & (pair < FEAT * FEAT) & (source == wanted)
    return jnp.where(linear | quad, 1.0, 0.0).astype(jnp.bfloat16)


def taylor_rows(left, right, feature):
    scale = FEAT ** (-0.25)
    left, right = left * scale, right * scale
    return jnp.where(
        feature == 0, 1.0, jnp.where(feature <= FEAT, left, left * right * 0.5**0.5)
    )


def linear_kernel(
    ids,
    t0,
    t1,
    t2,
    t3,
    gain,
    feature_w,
    state,
    lin_norm,
    conv_w,
    conv_state,
    value_w,
    out_w,
    update,
):
    rows, share = t0.shape
    heads = share // HD
    span = TAYLOR * heads
    by_state = expansion(128, SPREAD, heads)
    by_norm = expansion(128, TAYLOR_LANES, 1)
    expand = jnp.concatenate([by_state, by_norm], axis=1)

    own = ids[2]
    got = [ref[...].astype(jnp.float32) for ref in (t0, t1, t3, t2)]
    whole = []
    for place in range(heads):
        piece = got[0]
        for back in range(1, heads):
            piece = jnp.where(((own - back) & (heads - 1)) == place, got[back], piece)
        whole.append(piece)
    tokens = jnp.concatenate(whole, axis=1)
    normed = normed_rows(tokens, gain[...])
    feats = jnp.dot(normed, feature_w[...], preferred_element_type=jnp.float32)
    by_head = jnp.concatenate(
        [feats] + [pltpu.roll(feats, 128 - 2 * FEAT * h, 1) for h in range(1, heads)], axis=0
    )
    high = by_head.astype(jnp.bfloat16)
    rest = by_head - high.astype(jnp.float32)
    middle = rest.astype(jnp.bfloat16)
    low = (rest - middle.astype(jnp.float32)).astype(jnp.bfloat16)
    spread = jnp.dot(
        jnp.concatenate([high, middle, low], axis=0), expand, preferred_element_type=jnp.float32
    )
    count = heads * rows
    spread = spread[:count] + spread[count : 2 * count] + spread[2 * count :]
    lane = lanes_of((count, SPREAD))
    head = lax.broadcasted_iota(jnp.int32, (count, SPREAD), 0) >> 3
    query_wide = taylor_rows(spread[:, :SPREAD], spread[:, SPREAD : 2 * SPREAD], lane >> 2)
    query_wide = jnp.where(((lane & (heads - 1)) == head) & (lane < span), query_wide, 0.0)
    query_feats = taylor_rows(
        spread[:, 2 * SPREAD : 2 * SPREAD + TAYLOR_LANES],
        spread[:, 2 * SPREAD + TAYLOR_LANES :],
        lanes_of((count, TAYLOR_LANES)),
    )[:, :TAYLOR]
    both = by_head * pltpu.roll(by_head, 128 - FEAT, 1)
    near = jnp.sum(
        jnp.where(lanes_of(both.shape) < FEAT, both, 0.0), axis=-1, keepdims=True
    ) * FEAT ** (-0.5)
    intersection = 1.0 + near + 0.5 * near * near

    length = span + 12
    queries = []
    for shift in range(0, 16, 4):
        moved = query_wide if shift == 0 else pltpu.roll(query_wide, shift, 1)
        queries.append(moved[:, :length].astype(jnp.bfloat16))
    row = lax.broadcasted_iota(jnp.int32, (count, HD), 0) & (rows - 1)
    found = jnp.zeros((count, HD), jnp.float32)
    for r in range(rows):
        first = span * r
        shift = first % 16
        product = jnp.dot(
            queries[shift // 4],
            state[first - shift : first - shift + length, :],
            preferred_element_type=jnp.float32,
        )
        found = jnp.where(row == r, product, found)
    fresh = lax.dot_general(normed, value_w[...], FLAT, preferred_element_type=jnp.float32)
    older = conv_state[...].astype(jnp.float32)
    mixed = conv_w[0:1] * older[:, 0] + conv_w[1:2] * older[:, 1] + conv_w[2:3] * fresh
    total = tokens * 0.25
    for h in range(heads):
        here = slice(h * rows, (h + 1) * rows)
        denominator = (
            jnp.sum(query_feats[here] * lin_norm[:, h, :], axis=-1, keepdims=True)
            + intersection[here]
        )
        attended = (
            (found[here] + intersection[here] * mixed[:, h * HD : (h + 1) * HD]) / denominator
        ).astype(jnp.bfloat16)
        total = total + jnp.dot(
            attended, out_w[h * HD : (h + 1) * HD, :], preferred_element_type=jnp.float32
        )
    update[...] = total.astype(jnp.bfloat16)


def linear_layer(pieces, near):
    return kernel_call(
        linear_kernel,
        0,
        "linear_layer",
        jax.ShapeDtypeStruct((pieces[0].shape[0], near["out_w"].shape[1]), jnp.bfloat16),
        [VMEM] * 12,
        [],
        (*pieces, *(near[name] for name in LINEAR_NEAR)),
    )


def project_kernel(
    ids,
    tags,
    p0,
    p1,
    p2,
    p3,
    gain,
    v_w,
    qk_w,
    one,
    asked,
    key_new,
    value_new,
):
    rows, share = one.shape
    heads = share // HD
    layer_one = sum(ref[...].astype(jnp.float32) for ref in (p0, p1, p2, p3)).astype(jnp.bfloat16)
    rounded = layer_one.astype(jnp.float32)
    mine = rounded[:, :share]
    for h in range(1, heads):
        mine = jnp.where(ids[2] == h, rounded[:, h * share : (h + 1) * share], mine)
    one[...] = mine.astype(jnp.bfloat16)
    normed = normed_rows(rounded, gain[...])
    value_new[...] = lax.dot_general(
        normed, v_w[...], FLAT, preferred_element_type=jnp.float32
    ).astype(jnp.bfloat16)
    query_key = jnp.dot(normed, qk_w[...], preferred_element_type=jnp.float32)
    width = query_key.shape[1]
    lane = lanes_of((rows, LANES))
    query = jnp.where(in_head(lane, 0), query_key[:, :LANES], 0.0)
    key = query
    for h in range(heads):
        if h:
            moved = pltpu.roll(query_key, width - h * HD, 1)[:, :LANES]
            query = jnp.where(in_head(lane, h), moved, query)
        moved = pltpu.roll(query_key, width - (h + 1) * HD, 1)[:, :LANES]
        key = jnp.where(in_head(lane, h), moved, key)
    query = jnp.where(lane == share, tags[:, 0:1], query)
    query = jnp.where(lane == share + 1, tags[:, 1:2], query)
    asked[...] = query.astype(jnp.bfloat16)
    key_new[...] = key[:, :share].astype(jnp.bfloat16)


def project(tags, pieces, near):
    rows = pieces[0].shape[0]
    share = near["value_w"].shape[0]
    return kernel_call(
        project_kernel,
        1,
        "project",
        [
            jax.ShapeDtypeStruct((rows, share), jnp.bfloat16),
            jax.ShapeDtypeStruct((rows, LANES), jnp.bfloat16),
            jax.ShapeDtypeStruct((rows, share), jnp.bfloat16),
            jax.ShapeDtypeStruct((rows, share), jnp.bfloat16),
        ],
        [VMEM] * 8,
        [],
        (tags, *pieces, near["gain"], near["value_w"], near["query_key_w"]),
    )


def window_pages(lengths, r):
    length = lengths[r]
    return jnp.maximum((length - WINDOW) // PAGE, 1), jnp.maximum((length - 2) // PAGE, 1)


def own_kernel(
    ids, lengths, asked, key_new, value_new, pages, summed_out, highest_out, total_out
):
    rows, share = key_new.shape
    bounds = [(lengths[r], *window_pages(lengths, r)) for r in range(rows)]
    head = lax.broadcasted_iota(jnp.int32, (8, share), 0)
    lane = lanes_of((8, share))
    mine = (lane >= head * HD) & (lane < (head + 1) * HD)
    scale = HD ** (-0.5)
    query = asked[:, :share].astype(jnp.float32)
    new_key = key_new[...].astype(jnp.float32)
    new_value = value_new[...].astype(jnp.float32)
    wide = jnp.concatenate([jnp.where(mine, query[r : r + 1], 0.0) for r in range(rows)], axis=0)
    keys = jnp.concatenate(
        [jnp.broadcast_to(new_key[r : r + 1], (8, share)) for r in range(rows)], axis=0
    )
    new_score = jnp.sum(wide * keys, axis=-1, keepdims=True) * scale
    token = lanes_of((8 * rows, 2 * PAGE))
    request = lax.broadcasted_iota(jnp.int32, (8 * rows, 2 * PAGE), 0) >> 3
    length = jnp.zeros(token.shape, jnp.int32)
    base = jnp.zeros(token.shape, jnp.int32)
    for r in range(rows):
        length = jnp.where(request == r, bounds[r][0], length)
        second = jnp.where(bounds[r][1] != bounds[r][2], bounds[r][2] - 1, -MAXP) * PAGE
        base = jnp.where(request == r, jnp.where(token < PAGE, bounds[r][1] * PAGE, second), base)
    position = base + token
    usable = (position >= length - WINDOW) & (position <= length - 2)
    scores = []
    for r in range(rows):
        low = wide[8 * r : 8 * r + 8].astype(jnp.bfloat16)
        scores.append(
            jnp.concatenate(
                [
                    jnp.dot(low, pages[r, slot, 0], preferred_element_type=jnp.float32)
                    for slot in range(2)
                ],
                axis=1,
            )
        )
    scores = jnp.where(usable, jnp.concatenate(scores, axis=0) * scale, MASKED)
    highest = jnp.maximum(jnp.max(scores, axis=-1, keepdims=True), new_score)
    exps = jnp.where(usable, jnp.exp(scores - highest), 0.0)
    exp_new = jnp.exp(new_score - highest)
    total = jnp.sum(exps, axis=-1, keepdims=True) + exp_new
    for r in range(rows):
        here = slice(8 * r, 8 * r + 8)
        low = exps[here].astype(jnp.bfloat16)
        found = exp_new[here] * new_value[r : r + 1]
        for slot in range(2):
            found = found + lax.dot_general(
                low[:, slot * PAGE : (slot + 1) * PAGE],
                pages[r, slot, 1],
                FLAT,
                preferred_element_type=jnp.float32,
            )
        for ref, value in (
            (summed_out, found),
            (highest_out, highest[here]),
            (total_out, total[here]),
        ):
            ref[r : r + 1, :] = jnp.sum(jnp.where(mine, value, 0.0), axis=0, keepdims=True)


def own_attention(lengths, asked, key_new, value_new, near):
    rows, share = key_new.shape
    return kernel_call(
        own_kernel,
        1,
        "own_attention",
        [jax.ShapeDtypeStruct((rows, share), jnp.float32)] * 3,
        [SMEM] + [VMEM] * 4,
        [],
        (lengths, asked, key_new, value_new, near["own_pages"]),
    )


def prompt_kernel(ids, a0, a1, a2, a3, near_pages, far_pages, o0, o1, o2, o3):
    rows = a0.shape[0]
    share = near_pages.shape[1]
    heads = share // HD
    pages = jnp.concatenate(
        [near_pages[i] for i in range(XN)] + [far_pages[i] for i in range(XN)], axis=1
    )
    asked = jnp.concatenate([ref[...].astype(jnp.float32) for ref in (a0, a1, a2, a3)], axis=0)
    count = asked.shape[0]
    lane = lanes_of(asked.shape)
    group = jnp.sum(jnp.where(lane == share, asked, 0.0), axis=-1, keepdims=True)
    start = jnp.sum(jnp.where(lane == share + 1, asked, 0.0), axis=-1, keepdims=True)
    group, start = group.astype(jnp.int32), start.astype(jnp.int32)
    query = jnp.concatenate(
        [jnp.where(in_head(lane, h), asked, 0.0)[:, :share] for h in range(heads)], axis=0
    ).astype(jnp.bfloat16)
    scores = jnp.dot(query, pages, preferred_element_type=jnp.float32) * HD ** (-0.5)
    token = lanes_of((count, 2 * XN * PAGE))
    z, x = ids[1] // XN, ids[1] % XN
    slot = token >> 7
    slot_group = jnp.where(slot < XN, z, (z + ZN // 2) & (ZN - 1)) * XN
    slot_group = slot_group + ((slot + x + XN - 1) & (XN - 1))
    offset = token & (PAGE - 1)
    usable = (slot_group == group) & (offset < HALF) & (offset + HALF >= start)
    lane = lanes_of((count, share))
    stat_lane = lanes_of((count, 128))
    weights = []
    stats = jnp.zeros((count, 128), jnp.float32)
    for h in range(heads):
        here = jnp.where(usable, scores[h * count : (h + 1) * count], MASKED)
        highest = jnp.max(here, axis=-1, keepdims=True)
        exps = jnp.where(usable, jnp.exp(here - highest), 0.0)
        total = jnp.sum(exps, axis=-1, keepdims=True)
        stats = jnp.where(stat_lane == h, highest, stats)
        stats = jnp.where(stat_lane == heads + h, total, stats)
        weights.append(pltpu.roll(exps, HALF, 1))
    found = lax.dot_general(
        jnp.concatenate(weights, axis=0).astype(jnp.bfloat16),
        pages,
        FLAT,
        preferred_element_type=jnp.float32,
    )
    summed = jnp.zeros((count, share), jnp.float32)
    for h in range(heads):
        summed = jnp.where(in_head(lane, h), found[h * count : (h + 1) * count], summed)
    for at, ref in enumerate((o0, o1, o2, o3)):
        ref[:, :share] = summed[at * rows : (at + 1) * rows]
        ref[:, share:LANES] = jnp.zeros((rows, LANES - share), jnp.float32)
        ref[:, LANES:] = stats[at * rows : (at + 1) * rows]


def prompt_attention(asked, near_pages, far_pages):
    rows = asked[0].shape[0]
    return kernel_call(
        prompt_kernel,
        1,
        "prompt_attention",
        [jax.ShapeDtypeStruct((rows, LANES + 128), jnp.float32)] * 4,
        [VMEM] * 6,
        [],
        (*asked, near_pages, far_pages),
    )


def combine_kernel(ids, summed, highest, total, r0, r1, r2, r3, out_w, s0, s1, s2, s3):
    rows, share = summed.shape
    heads = share // HD
    refs = (r0, r1, r2, r3)
    prompt_summed = sum(ref[:, :share] for ref in refs)
    stats = [ref[:, LANES:] for ref in refs]
    top = jnp.maximum(jnp.maximum(stats[0], stats[1]), jnp.maximum(stats[2], stats[3]))
    added = stats[0] + stats[1] + stats[2] + stats[3]
    lane = lanes_of((rows, share))
    prompt_highest = jnp.zeros((rows, share), jnp.float32)
    prompt_total = jnp.zeros((rows, share), jnp.float32)
    for h in range(heads):
        here = in_head(lane, h)
        prompt_highest = jnp.where(here, top[:, h : h + 1], prompt_highest)
        prompt_total = jnp.where(here, added[:, heads + h : heads + h + 1], prompt_total)
    peak = jnp.maximum(highest[...], prompt_highest)
    own_factor = jnp.exp(highest[...] - peak)
    prompt_factor = jnp.exp(prompt_highest - peak)
    whole = total[...] * own_factor + prompt_total * prompt_factor
    attended = (summed[...] * own_factor + prompt_summed * prompt_factor) / whole
    second = jnp.dot(attended.astype(jnp.bfloat16), out_w[0], preferred_element_type=jnp.float32)
    for steps, ref in enumerate((s0, s1, s2, s3)):
        slab = second[:, :share]
        for h in range(1, heads):
            slab = jnp.where(
                ((ids[2] + steps) & (heads - 1)) == h, second[:, h * share : (h + 1) * share], slab
            )
        ref[...] = slab


def combine(own, parts, out_w):
    return kernel_call(
        combine_kernel,
        1,
        "combine",
        [jax.ShapeDtypeStruct(own[0].shape, jnp.float32)] * 4,
        [VMEM] * 8,
        [],
        (*own, *parts, out_w),
    )


LINEAR_NEAR = (
    "gain",
    "feature_w",
    "state",
    "lin_norm",
    "conv_w",
    "conv_state",
    "value_w",
    "out_w",
)
WINDOW_NEAR = ("gain", "value_w", "query_key_w")


def bring_near(arrays):
    names = list(arrays)
    count = len(names)
    first = [at for at, name in enumerate(names) if name in LINEAR_NEAR]
    second = [at for at, name in enumerate(names) if name in WINDOW_NEAR]

    def copy_some(chosen, refs):
        sems = refs[-1]
        copies = [
            pltpu.make_async_copy(refs[at], refs[count + at], sems.at[at]) for at in chosen
        ]
        for copy in copies:
            copy.start()
        for copy in copies:
            copy.wait()

    near = kernel_call(
        lambda ids, *refs: copy_some(first, refs),
        0,
        "bring_near",
        [jax.ShapeDtypeStruct(array.shape, array.dtype) for array in arrays.values()],
        [HBM] * count,
        [pltpu.SemaphoreType.DMA((count,))],
        tuple(arrays.values()),
        4 << 20,
        bytes_only(arrays.values()),
        lambda ids, *refs: copy_some(second, refs),
    )
    return dict(zip(names, near))


def bytes_only(arrays):
    moved = sum(array.size * array.dtype.itemsize for array in arrays)
    return pl.CostEstimate(flops=0, bytes_accessed=2 * moved, transcendentals=0)


def window_kernel(
    ids, table, lengths, own_hbm, own_near, tags, sems
):
    rows = tags.shape[0]
    total = own_hbm.shape[0]
    copies = []
    for r in range(rows):
        for slot, logical in enumerate(window_pages(lengths, r)):
            page = jnp.clip(table[r, logical] - GROUPS - ids[1] * total, 0, total - 1)
            copies.append(
                pltpu.make_async_copy(own_hbm.at[page], own_near.at[r, slot], sems.at[r, slot])
            )
    for copy in copies:
        copy.start()
    row = lax.broadcasted_iota(jnp.int32, tags.shape, 0)
    first = lanes_of(tags.shape) == 0
    marks = jnp.zeros(tags.shape, jnp.int32)
    for r in range(rows):
        start = jnp.minimum(lengths[r] - WINDOW, PAGE)
        marks = jnp.where(row == r, jnp.where(first, table[r, 0], start), marks)
    tags[...] = marks.astype(jnp.float32)
    for copy in copies:
        copy.wait()


def bring_windows(table, lengths, own_pages):
    rows = lengths.shape[0]
    windows = jax.ShapeDtypeStruct((rows, 2) + own_pages.shape[1:], own_pages.dtype)
    return kernel_call(
        window_kernel,
        1,
        "bring_windows",
        [
            windows,
            jax.ShapeDtypeStruct((rows, 128), jnp.float32),
        ],
        [SMEM] * 2 + [HBM],
        [pltpu.SemaphoreType.DMA((rows, 2))],
        (table, lengths, own_pages),
        1 << 20,
        bytes_only([windows]),
    )


def page_kernel(ids, pages_hbm, page, pages, sem):
    copy = pltpu.make_async_copy(pages_hbm.at[0], pages, sem)
    copy.start()
    copy.wait()
    lane = lanes_of(page.shape)
    keys = pltpu.roll(pages[0].astype(jnp.float32), HALF, 1)
    page[...] = jnp.where(lane < HALF, keys, pages[1].astype(jnp.float32)).astype(jnp.bfloat16)


def window_page(prompt_pages):
    shape = prompt_pages.shape[1:]
    return kernel_call(
        page_kernel,
        1,
        "window_page",
        jax.ShapeDtypeStruct(shape[1:], jnp.bfloat16),
        [HBM],
        [pltpu.VMEM(shape, jnp.bfloat16), pltpu.SemaphoreType.DMA],
        (prompt_pages,),
        cost=pl.CostEstimate(flops=0, bytes_accessed=16 << 20, transcendentals=0),
    )


def body(
    tokens,
    norm_gain,
    feature_w,
    query_key_w,
    value_w,
    out_w,
    conv_w,
    conv_state,
    lin_state,
    lin_norm,
    own_pages,
    prompt_pages,
    page_table,
    lengths,
):
    pages_first = prompt_pages.transpose(0, 1, 3, 2)
    stored = {
        "gain": norm_gain,
        "feature_w": feature_w,
        "state": lin_state.transpose(0, 2, 1, 3).reshape(-1, HD),
        "lin_norm": lin_norm,
        "conv_w": conv_w,
        "conv_state": conv_state,
        "value_w": value_w.transpose(0, 2, 1)[0],
        "out_w": out_w[0],
        "query_key_w": query_key_w,
    }

    page = window_page(pages_first)
    row_pages = [x_shift(page, k) for k in (1, 3, 2)]
    row_pages[0], last_tokens, stored = lax.optimization_barrier((row_pages[0], tokens, stored))
    received = [head_shift(tokens, 1), head_shift(tokens, 3), head_shift(last_tokens, 2)]
    near, received = lax.optimization_barrier((bring_near(stored), received))
    near_pages = jnp.stack([row_pages[0], page, row_pages[1], row_pages[2]])
    near_pages, received = lax.optimization_barrier((near_pages, received))
    far_pages = far_swap(near_pages)
    update = linear_layer([tokens] + received, near)
    own_pages = own_pages.transpose(0, 1, 3, 2)
    own_pages, table, ends, update = lax.optimization_barrier(
        (own_pages, page_table, lengths, update)
    )
    near["own_pages"], tags = bring_windows(table, ends, own_pages)
    swapped = [section_swap(update, k) for k in (0, 1, 3, 2)]
    one_share, packed, key_new, value_new = project(tags, swapped, near)
    asked = [packed] + [z_shift(packed, k) for k in (1, 7, 2)]
    own = own_attention(lengths, packed, key_new, value_new, near)
    asked, own = lax.optimization_barrier((asked, own))
    answers = prompt_attention(asked, near_pages, far_pages)
    answers, one_share = lax.optimization_barrier((answers, one_share))
    parts = [answers[0]] + [z_shift(answers[at], -k) for at, k in ((1, 1), (2, 7), (3, 2))]
    one_back = lax.ppermute(one_share, "section", [(1, 0), (0, 1)])
    parts, one_back = lax.optimization_barrier((parts, one_back))
    slabs = combine(own, parts, out_w)
    section_index = lax.axis_index("section")
    total = one_share.astype(jnp.float32) + slabs[0]
    for piece in [head_shift(slabs[k], k) for k in (1, 3, 2)]:
        total = total + piece
    output = jnp.where(section_index == 0, one_back, total.astype(jnp.bfloat16))
    return output[None]


def solution(mesh):
    placed = (
        P("req", "head"),
        P("section", None),
        P(None, "head"),
        P(None, "head"),
        P("section", None, "head"),
        P("section", "head", None),
        P(None, "head"),
        P("req", None, "head"),
        P("req", "head", None, None),
        P("req", "head", None),
        P("req", None, None, "head"),
        P("req", None, None, "head"),
        P("req", None),
        P("req"),
    )
    return jax.shard_map(
        body, mesh=mesh, in_specs=placed, out_specs=P("section", "req", "head"), check_vma=False
    )
```

```python
import jax
import jax.numpy as jnp
from jax import lax
from jax.experimental import pallas as pl
from jax.experimental.pallas import tpu as pltpu
from jax.sharding import PartitionSpec as P

HD = 112
FEAT = 16
WINDOW = 64
PAGE = 128
HALF = 64
MAXP = 256
GROUPS = 32
XN = 4
ZN = 8
LANES = 512
TAYLOR = 273
TAYLOR_LANES = 384
SPREAD = 1152

EPSILON = 1e-06
MASKED = -1e30


def head_shift(value, steps):
    count = lax.axis_size("head")
    return lax.ppermute(value, "head", [(i, (i + steps) % count) for i in range(count)])


def z_shift(value, steps):
    return lax.ppermute(
        value,
        "req",
        [(z * XN + i, (z + steps) % ZN * XN + i) for z in range(ZN) for i in range(XN)],
    )


def x_shift(value, steps):
    return lax.ppermute(
        value,
        "req",
        [(z * XN + i, z * XN + (i + steps) % XN) for z in range(ZN) for i in range(XN)],
    )


def far_swap(value):
    count = XN * ZN
    return lax.ppermute(
        value,
        ("section", "req"),
        [(count + i, count + (i + count // 2) % count) for i in range(count)],
    )


def section_swap(value, steps):
    count = lax.axis_size("head")
    there = [(i, count + (i + steps) % count) for i in range(count)]
    return lax.ppermute(value, ("section", "head"), there + [(b, a) for a, b in there])


VMEM = pl.BlockSpec(memory_space=pltpu.VMEM)
SMEM = pl.BlockSpec(memory_space=pltpu.SMEM)
HBM = pl.BlockSpec(memory_space=pltpu.HBM)
FLAT = (((1,), (1,)), ((), ()))


def normed_rows(values, gain_row):
    factor = lax.rsqrt(jnp.mean(values * values, axis=-1, keepdims=True) + EPSILON)
    return (values * factor * gain_row).astype(jnp.bfloat16)


def lanes_of(shape):
    return lax.broadcasted_iota(jnp.int32, shape, len(shape) - 1)


def in_head(lane, h):
    return (lane >= h * HD) & (lane < (h + 1) * HD)


def place():
    return lax.axis_index("section"), lax.axis_index("req"), lax.axis_index("head")


def kernel_call(
    kernel,
    section,
    name,
    out_shape,
    in_specs,
    scratch_shapes,
    args,
    vmem=6 << 20,
    cost=None,
    elsewhere=None,
):
    def run(*refs):
        ids = place()

        @pl.when(ids[0] == section)
        def _():
            kernel(ids, *refs)

        if elsewhere is not None:

            @pl.when(ids[0] != section)
            def _():
                elsewhere(ids, *refs)

    args = [
        pltpu.with_memory_space_constraint(arg, pltpu.HBM) if spec is HBM else arg
        for arg, spec in zip(args, in_specs, strict=True)
    ]
    return pl.pallas_call(
        run,
        out_shape=out_shape,
        in_specs=in_specs,
        out_specs=jax.tree.map(lambda _: VMEM, out_shape),
        scratch_shapes=scratch_shapes,
        compiler_params=pltpu.CompilerParams(vmem_limit_bytes=vmem),
        cost_estimate=cost,
        name=name,
    )(*args)


def expansion(features, width, repeat):
    lane = lax.broadcasted_iota(jnp.int32, (features, 2 * width), 1)
    source = lax.broadcasted_iota(jnp.int32, (features, 2 * width), 0)
    left = lane < width
    at = jnp.where(left, lane, lane - width) >> (repeat.bit_length() - 1)
    linear = left & (at > 0) & (at <= FEAT) & (source == at - 1)
    pair = at - (FEAT + 1)
    wanted = jnp.where(left, pair >> 4, pair & (FEAT - 1))
    quad = (pair >= 0) & (pair < FEAT * FEAT) & (source == wanted)
    return jnp.where(linear | quad, 1.0, 0.0).astype(jnp.bfloat16)


def taylor_rows(left, right, feature):
    scale = FEAT ** (-0.25)
    left, right = left * scale, right * scale
    return jnp.where(
        feature == 0, 1.0, jnp.where(feature <= FEAT, left, left * right * 0.5**0.5)
    )


def linear_kernel(
    ids,
    t0,
    t1,
    t2,
    t3,
    gain,
    feature_w,
    state,
    lin_norm,
    conv_w,
    conv_state,
    value_w,
    out_w,
    update,
):
    rows, share = t0.shape
    heads = share // HD
    span = TAYLOR * heads
    by_state = expansion(128, SPREAD, heads)
    by_norm = expansion(128, TAYLOR_LANES, 1)
    expand = jnp.concatenate([by_state, by_norm], axis=1)

    own = ids[2]
    got = [ref[...].astype(jnp.float32) for ref in (t0, t1, t3, t2)]
    whole = []
    for place in range(heads):
        piece = got[0]
        for back in range(1, heads):
            piece = jnp.where(((own - back) & (heads - 1)) == place, got[back], piece)
        whole.append(piece)
    tokens = jnp.concatenate(whole, axis=1)
    normed = normed_rows(tokens, gain[...])
    feats = jnp.dot(normed, feature_w[...], preferred_element_type=jnp.float32)
    by_head = jnp.concatenate(
        [feats] + [pltpu.roll(feats, 128 - 2 * FEAT * h, 1) for h in range(1, heads)], axis=0
    )
    high = by_head.astype(jnp.bfloat16)
    rest = by_head - high.astype(jnp.float32)
    middle = rest.astype(jnp.bfloat16)
    low = (rest - middle.astype(jnp.float32)).astype(jnp.bfloat16)
    spread = jnp.dot(
        jnp.concatenate([high, middle, low], axis=0), expand, preferred_element_type=jnp.float32
    )
    count = heads * rows
    spread = spread[:count] + spread[count : 2 * count] + spread[2 * count :]
    lane = lanes_of((count, SPREAD))
    head = lax.broadcasted_iota(jnp.int32, (count, SPREAD), 0) >> 3
    query_wide = taylor_rows(spread[:, :SPREAD], spread[:, SPREAD : 2 * SPREAD], lane >> 2)
    query_wide = jnp.where(((lane & (heads - 1)) == head) & (lane < span), query_wide, 0.0)
    query_feats = taylor_rows(
        spread[:, 2 * SPREAD : 2 * SPREAD + TAYLOR_LANES],
        spread[:, 2 * SPREAD + TAYLOR_LANES :],
        lanes_of((count, TAYLOR_LANES)),
    )[:, :TAYLOR]
    both = by_head * pltpu.roll(by_head, 128 - FEAT, 1)
    near = jnp.sum(
        jnp.where(lanes_of(both.shape) < FEAT, both, 0.0), axis=-1, keepdims=True
    ) * FEAT ** (-0.5)
    intersection = 1.0 + near + 0.5 * near * near

    length = span + 12
    queries = []
    for shift in range(0, 16, 4):
        moved = query_wide if shift == 0 else pltpu.roll(query_wide, shift, 1)
        queries.append(moved[:, :length].astype(jnp.bfloat16))
    row = lax.broadcasted_iota(jnp.int32, (count, HD), 0) & (rows - 1)
    found = jnp.zeros((count, HD), jnp.float32)
    for r in range(rows):
        first = span * r
        shift = first % 16
        product = jnp.dot(
            queries[shift // 4],
            state[first - shift : first - shift + length, :],
            preferred_element_type=jnp.float32,
        )
        found = jnp.where(row == r, product, found)
    fresh = lax.dot_general(normed, value_w[...], FLAT, preferred_element_type=jnp.float32)
    older = conv_state[...].astype(jnp.float32)
    mixed = conv_w[0:1] * older[:, 0] + conv_w[1:2] * older[:, 1] + conv_w[2:3] * fresh
    total = tokens * 0.25
    for h in range(heads):
        here = slice(h * rows, (h + 1) * rows)
        denominator = (
            jnp.sum(query_feats[here] * lin_norm[:, h, :], axis=-1, keepdims=True)
            + intersection[here]
        )
        attended = (
            (found[here] + intersection[here] * mixed[:, h * HD : (h + 1) * HD]) / denominator
        ).astype(jnp.bfloat16)
        total = total + jnp.dot(
            attended, out_w[h * HD : (h + 1) * HD, :], preferred_element_type=jnp.float32
        )
    update[...] = total.astype(jnp.bfloat16)


def linear_layer(pieces, near):
    return kernel_call(
        linear_kernel,
        0,
        "linear_layer",
        jax.ShapeDtypeStruct((pieces[0].shape[0], near["out_w"].shape[1]), jnp.bfloat16),
        [VMEM] * 12,
        [],
        (*pieces, *(near[name] for name in LINEAR_NEAR)),
    )


def project_kernel(
    ids,
    tags,
    p0,
    p1,
    p2,
    p3,
    gain,
    v_w,
    qk_w,
    one,
    asked,
    key_new,
    value_new,
):
    rows, share = one.shape
    heads = share // HD
    layer_one = sum(ref[...].astype(jnp.float32) for ref in (p0, p1, p2, p3)).astype(jnp.bfloat16)
    rounded = layer_one.astype(jnp.float32)
    mine = rounded[:, :share]
    for h in range(1, heads):
        mine = jnp.where(ids[2] == h, rounded[:, h * share : (h + 1) * share], mine)
    one[...] = mine.astype(jnp.bfloat16)
    normed = normed_rows(rounded, gain[...])
    value_new[...] = lax.dot_general(
        normed, v_w[...], FLAT, preferred_element_type=jnp.float32
    ).astype(jnp.bfloat16)
    query_key = jnp.dot(normed, qk_w[...], preferred_element_type=jnp.float32)
    width = query_key.shape[1]
    lane = lanes_of((rows, LANES))
    query = jnp.where(in_head(lane, 0), query_key[:, :LANES], 0.0)
    key = query
    for h in range(heads):
        if h:
            moved = pltpu.roll(query_key, width - h * HD, 1)[:, :LANES]
            query = jnp.where(in_head(lane, h), moved, query)
        moved = pltpu.roll(query_key, width - (h + 1) * HD, 1)[:, :LANES]
        key = jnp.where(in_head(lane, h), moved, key)
    query = jnp.where(lane == share, tags[:, 0:1], query)
    query = jnp.where(lane == share + 1, tags[:, 1:2], query)
    asked[...] = query.astype(jnp.bfloat16)
    key_new[...] = key[:, :share].astype(jnp.bfloat16)


def project(tags, pieces, near):
    rows = pieces[0].shape[0]
    share = near["value_w"].shape[0]
    return kernel_call(
        project_kernel,
        1,
        "project",
        [
            jax.ShapeDtypeStruct((rows, share), jnp.bfloat16),
            jax.ShapeDtypeStruct((rows, LANES), jnp.bfloat16),
            jax.ShapeDtypeStruct((rows, share), jnp.bfloat16),
            jax.ShapeDtypeStruct((rows, share), jnp.bfloat16),
        ],
        [VMEM] * 8,
        [],
        (tags, *pieces, near["gain"], near["value_w"], near["query_key_w"]),
    )


def window_pages(lengths, r):
    length = lengths[r]
    return jnp.maximum((length - WINDOW) // PAGE, 1), jnp.maximum((length - 2) // PAGE, 1)


def own_kernel(
    ids, lengths, asked, key_new, value_new, pages, summed_out, highest_out, total_out
):
    rows, share = key_new.shape
    bounds = [(lengths[r], *window_pages(lengths, r)) for r in range(rows)]
    head = lax.broadcasted_iota(jnp.int32, (8, share), 0)
    lane = lanes_of((8, share))
    mine = (lane >= head * HD) & (lane < (head + 1) * HD)
    scale = HD ** (-0.5)
    query = asked[:, :share].astype(jnp.float32)
    new_key = key_new[...].astype(jnp.float32)
    new_value = value_new[...].astype(jnp.float32)
    wide = jnp.concatenate([jnp.where(mine, query[r : r + 1], 0.0) for r in range(rows)], axis=0)
    keys = jnp.concatenate(
        [jnp.broadcast_to(new_key[r : r + 1], (8, share)) for r in range(rows)], axis=0
    )
    new_score = jnp.sum(wide * keys, axis=-1, keepdims=True) * scale
    token = lanes_of((8 * rows, 2 * PAGE))
    request = lax.broadcasted_iota(jnp.int32, (8 * rows, 2 * PAGE), 0) >> 3
    length = jnp.zeros(token.shape, jnp.int32)
    base = jnp.zeros(token.shape, jnp.int32)
    for r in range(rows):
        length = jnp.where(request == r, bounds[r][0], length)
        second = jnp.where(bounds[r][1] != bounds[r][2], bounds[r][2] - 1, -MAXP) * PAGE
        base = jnp.where(request == r, jnp.where(token < PAGE, bounds[r][1] * PAGE, second), base)
    position = base + token
    usable = (position >= length - WINDOW) & (position <= length - 2)
    scores = []
    for r in range(rows):
        low = wide[8 * r : 8 * r + 8].astype(jnp.bfloat16)
        scores.append(
            jnp.concatenate(
                [
                    jnp.dot(low, pages[r, slot, 0], preferred_element_type=jnp.float32)
                    for slot in range(2)
                ],
                axis=1,
            )
        )
    scores = jnp.where(usable, jnp.concatenate(scores, axis=0) * scale, MASKED)
    highest = jnp.maximum(jnp.max(scores, axis=-1, keepdims=True), new_score)
    exps = jnp.where(usable, jnp.exp(scores - highest), 0.0)
    exp_new = jnp.exp(new_score - highest)
    total = jnp.sum(exps, axis=-1, keepdims=True) + exp_new
    for r in range(rows):
        here = slice(8 * r, 8 * r + 8)
        low = exps[here].astype(jnp.bfloat16)
        found = exp_new[here] * new_value[r : r + 1]
        for slot in range(2):
            found = found + lax.dot_general(
                low[:, slot * PAGE : (slot + 1) * PAGE],
                pages[r, slot, 1],
                FLAT,
                preferred_element_type=jnp.float32,
            )
        for ref, value in (
            (summed_out, found),
            (highest_out, highest[here]),
            (total_out, total[here]),
        ):
            ref[r : r + 1, :] = jnp.sum(jnp.where(mine, value, 0.0), axis=0, keepdims=True)


def own_attention(lengths, asked, key_new, value_new, near):
    rows, share = key_new.shape
    return kernel_call(
        own_kernel,
        1,
        "own_attention",
        [jax.ShapeDtypeStruct((rows, share), jnp.float32)] * 3,
        [SMEM] + [VMEM] * 4,
        [],
        (lengths, asked, key_new, value_new, near["own_pages"]),
    )


def prompt_kernel(ids, a0, a1, a2, a3, near_pages, far_pages, o0, o1, o2, o3):
    rows = a0.shape[0]
    share = near_pages.shape[1]
    heads = share // HD
    pages = jnp.concatenate(
        [near_pages[i] for i in range(XN)] + [far_pages[i] for i in range(XN)], axis=1
    )
    asked = jnp.concatenate([ref[...].astype(jnp.float32) for ref in (a0, a1, a2, a3)], axis=0)
    count = asked.shape[0]
    lane = lanes_of(asked.shape)
    group = jnp.sum(jnp.where(lane == share, asked, 0.0), axis=-1, keepdims=True)
    start = jnp.sum(jnp.where(lane == share + 1, asked, 0.0), axis=-1, keepdims=True)
    group, start = group.astype(jnp.int32), start.astype(jnp.int32)
    query = jnp.concatenate(
        [jnp.where(in_head(lane, h), asked, 0.0)[:, :share] for h in range(heads)], axis=0
    ).astype(jnp.bfloat16)
    scores = jnp.dot(query, pages, preferred_element_type=jnp.float32) * HD ** (-0.5)
    token = lanes_of((count, 2 * XN * PAGE))
    z, x = ids[1] // XN, ids[1] % XN
    slot = token >> 7
    slot_group = jnp.where(slot < XN, z, (z + ZN // 2) & (ZN - 1)) * XN
    slot_group = slot_group + ((slot + x + XN - 1) & (XN - 1))
    offset = token & (PAGE - 1)
    usable = (slot_group == group) & (offset < HALF) & (offset + HALF >= start)
    lane = lanes_of((count, share))
    stat_lane = lanes_of((count, 128))
    weights = []
    stats = jnp.zeros((count, 128), jnp.float32)
    for h in range(heads):
        here = jnp.where(usable, scores[h * count : (h + 1) * count], MASKED)
        highest = jnp.max(here, axis=-1, keepdims=True)
        exps = jnp.where(usable, jnp.exp(here - highest), 0.0)
        total = jnp.sum(exps, axis=-1, keepdims=True)
        stats = jnp.where(stat_lane == h, highest, stats)
        stats = jnp.where(stat_lane == heads + h, total, stats)
        weights.append(pltpu.roll(exps, HALF, 1))
    found = lax.dot_general(
        jnp.concatenate(weights, axis=0).astype(jnp.bfloat16),
        pages,
        FLAT,
        preferred_element_type=jnp.float32,
    )
    summed = jnp.zeros((count, share), jnp.float32)
    for h in range(heads):
        summed = jnp.where(in_head(lane, h), found[h * count : (h + 1) * count], summed)
    for at, ref in enumerate((o0, o1, o2, o3)):
        ref[:, :share] = summed[at * rows : (at + 1) * rows]
        ref[:, share:LANES] = jnp.zeros((rows, LANES - share), jnp.float32)
        ref[:, LANES:] = stats[at * rows : (at + 1) * rows]


def prompt_attention(asked, near_pages, far_pages):
    rows = asked[0].shape[0]
    return kernel_call(
        prompt_kernel,
        1,
        "prompt_attention",
        [jax.ShapeDtypeStruct((rows, LANES + 128), jnp.float32)] * 4,
        [VMEM] * 6,
        [],
        (*asked, near_pages, far_pages),
    )


def combine_kernel(ids, summed, highest, total, r0, r1, r2, r3, out_w, s0, s1, s2, s3):
    rows, share = summed.shape
    heads = share // HD
    refs = (r0, r1, r2, r3)
    prompt_summed = sum(ref[:, :share] for ref in refs)
    stats = [ref[:, LANES:] for ref in refs]
    top = jnp.maximum(jnp.maximum(stats[0], stats[1]), jnp.maximum(stats[2], stats[3]))
    added = stats[0] + stats[1] + stats[2] + stats[3]
    lane = lanes_of((rows, share))
    prompt_highest = jnp.zeros((rows, share), jnp.float32)
    prompt_total = jnp.zeros((rows, share), jnp.float32)
    for h in range(heads):
        here = in_head(lane, h)
        prompt_highest = jnp.where(here, top[:, h : h + 1], prompt_highest)
        prompt_total = jnp.where(here, added[:, heads + h : heads + h + 1], prompt_total)
    peak = jnp.maximum(highest[...], prompt_highest)
    own_factor = jnp.exp(highest[...] - peak)
    prompt_factor = jnp.exp(prompt_highest - peak)
    whole = total[...] * own_factor + prompt_total * prompt_factor
    attended = (summed[...] * own_factor + prompt_summed * prompt_factor) / whole
    second = jnp.dot(attended.astype(jnp.bfloat16), out_w[0], preferred_element_type=jnp.float32)
    for steps, ref in enumerate((s0, s1, s2, s3)):
        slab = second[:, :share]
        for h in range(1, heads):
            slab = jnp.where(
                ((ids[2] + steps) & (heads - 1)) == h, second[:, h * share : (h + 1) * share], slab
            )
        ref[...] = slab


def combine(own, parts, out_w):
    return kernel_call(
        combine_kernel,
        1,
        "combine",
        [jax.ShapeDtypeStruct(own[0].shape, jnp.float32)] * 4,
        [VMEM] * 8,
        [],
        (*own, *parts, out_w),
    )


LINEAR_NEAR = (
    "gain",
    "feature_w",
    "state",
    "lin_norm",
    "conv_w",
    "conv_state",
    "value_w",
    "out_w",
)
WINDOW_NEAR = ("gain", "value_w", "query_key_w")


def bring_near(arrays):
    names = list(arrays)
    count = len(names)
    first = [at for at, name in enumerate(names) if name in LINEAR_NEAR]
    second = [at for at, name in enumerate(names) if name in WINDOW_NEAR]

    def copy_some(chosen, refs):
        sems = refs[-1]
        copies = [
            pltpu.make_async_copy(refs[at], refs[count + at], sems.at[at]) for at in chosen
        ]
        for copy in copies:
            copy.start()
        for copy in copies:
            copy.wait()

    near = kernel_call(
        lambda ids, *refs: copy_some(first, refs),
        0,
        "bring_near",
        [jax.ShapeDtypeStruct(array.shape, array.dtype) for array in arrays.values()],
        [HBM] * count,
        [pltpu.SemaphoreType.DMA((count,))],
        tuple(arrays.values()),
        4 << 20,
        bytes_only(arrays.values()),
        lambda ids, *refs: copy_some(second, refs),
    )
    return dict(zip(names, near))


def bytes_only(arrays):
    moved = sum(array.size * array.dtype.itemsize for array in arrays)
    return pl.CostEstimate(flops=0, bytes_accessed=2 * moved, transcendentals=0)


def window_kernel(
    ids, table, lengths, own_hbm, own_near, tags, sems
):
    rows = tags.shape[0]
    total = own_hbm.shape[0]
    copies = []
    for r in range(rows):
        for slot, logical in enumerate(window_pages(lengths, r)):
            page = jnp.clip(table[r, logical] - GROUPS - ids[1] * total, 0, total - 1)
            copies.append(
                pltpu.make_async_copy(own_hbm.at[page], own_near.at[r, slot], sems.at[r, slot])
            )
    for copy in copies:
        copy.start()
    row = lax.broadcasted_iota(jnp.int32, tags.shape, 0)
    first = lanes_of(tags.shape) == 0
    marks = jnp.zeros(tags.shape, jnp.int32)
    for r in range(rows):
        start = jnp.minimum(lengths[r] - WINDOW, PAGE)
        marks = jnp.where(row == r, jnp.where(first, table[r, 0], start), marks)
    tags[...] = marks.astype(jnp.float32)
    for copy in copies:
        copy.wait()


def bring_windows(table, lengths, own_pages):
    rows = lengths.shape[0]
    windows = jax.ShapeDtypeStruct((rows, 2) + own_pages.shape[1:], own_pages.dtype)
    return kernel_call(
        window_kernel,
        1,
        "bring_windows",
        [
            windows,
            jax.ShapeDtypeStruct((rows, 128), jnp.float32),
        ],
        [SMEM] * 2 + [HBM],
        [pltpu.SemaphoreType.DMA((rows, 2))],
        (table, lengths, own_pages),
        1 << 20,
        bytes_only([windows]),
    )


def page_kernel(ids, pages_hbm, page, pages, sem):
    copy = pltpu.make_async_copy(pages_hbm.at[0], pages, sem)
    copy.start()
    copy.wait()
    lane = lanes_of(page.shape)
    keys = pltpu.roll(pages[0].astype(jnp.float32), HALF, 1)
    page[...] = jnp.where(lane < HALF, keys, pages[1].astype(jnp.float32)).astype(jnp.bfloat16)


def window_page(prompt_pages):
    shape = prompt_pages.shape[1:]
    return kernel_call(
        page_kernel,
        1,
        "window_page",
        jax.ShapeDtypeStruct(shape[1:], jnp.bfloat16),
        [HBM],
        [pltpu.VMEM(shape, jnp.bfloat16), pltpu.SemaphoreType.DMA],
        (prompt_pages,),
        cost=pl.CostEstimate(flops=0, bytes_accessed=16 << 20, transcendentals=0),
    )


def body(
    tokens,
    norm_gain,
    feature_w,
    query_key_w,
    value_w,
    out_w,
    conv_w,
    conv_state,
    lin_state,
    lin_norm,
    own_pages,
    prompt_pages,
    page_table,
    lengths,
):
    pages_first = prompt_pages.transpose(0, 1, 3, 2)
    stored = {
        "gain": norm_gain,
        "feature_w": feature_w,
        "state": lin_state.transpose(0, 2, 1, 3).reshape(-1, HD),
        "lin_norm": lin_norm,
        "conv_w": conv_w,
        "conv_state": conv_state,
        "value_w": value_w.transpose(0, 2, 1)[0],
        "out_w": out_w[0],
        "query_key_w": query_key_w,
    }

    page = window_page(pages_first)
    row_pages = [x_shift(page, k) for k in (1, 3, 2)]
    row_pages[0], last_tokens, stored = lax.optimization_barrier((row_pages[0], tokens, stored))
    received = [head_shift(last_tokens, 1), head_shift(tokens, 3), head_shift(tokens, 2)]
    near, received, row_pages = lax.optimization_barrier((bring_near(stored), received, row_pages))
    near_pages = jnp.stack([row_pages[0], page, row_pages[1], row_pages[2]])
    near_pages, received = lax.optimization_barrier((near_pages, received))
    far_pages = far_swap(near_pages)
    update = linear_layer([tokens] + received, near)
    own_pages = own_pages.transpose(0, 1, 3, 2)
    own_pages, table, ends, update = lax.optimization_barrier(
        (own_pages, page_table, lengths, update)
    )
    near["own_pages"], tags = bring_windows(table, ends, own_pages)
    swapped = [section_swap(update, k) for k in (2, 1, 3, 0)]
    one_share, packed, key_new, value_new = project(tags, swapped, near)
    asked = [packed] + [z_shift(packed, k) for k in (2, 1, 7)]
    own = own_attention(lengths, packed, key_new, value_new, near)
    asked, own = lax.optimization_barrier((asked, own))
    answers = prompt_attention(asked, near_pages, far_pages)
    answers, one_share = lax.optimization_barrier((answers, one_share))
    parts = [answers[0]] + [z_shift(answers[at], -k) for at, k in ((1, 2), (2, 1), (3, 7))]
    one_back = lax.ppermute(one_share, "section", [(1, 0), (0, 1)])
    parts, one_back = lax.optimization_barrier((parts, one_back))
    slabs = combine(own, parts, out_w)
    section_index = lax.axis_index("section")
    total = one_share.astype(jnp.float32) + slabs[0]
    for piece in [head_shift(slabs[k], k) for k in (2, 1, 3)]:
        total = total + piece
    output = jnp.where(section_index == 0, one_back, total.astype(jnp.bfloat16))
    return output[None]


def solution(mesh):
    placed = (
        P("req", "head"),
        P("section", None),
        P(None, "head"),
        P(None, "head"),
        P("section", None, "head"),
        P("section", "head", None),
        P(None, "head"),
        P("req", None, "head"),
        P("req", "head", None, None),
        P("req", "head", None),
        P("req", None, None, "head"),
        P("req", None, None, "head"),
        P("req", None),
        P("req"),
    )
    return jax.shard_map(
        body, mesh=mesh, in_specs=placed, out_specs=P("section", "req", "head"), check_vma=False
    )
```

```python
import jax
import jax.numpy as jnp
from jax import lax
from jax.experimental import pallas as pl
from jax.experimental.pallas import tpu as pltpu
from jax.sharding import PartitionSpec as P

HD = 112
FEAT = 16
WINDOW = 64
PAGE = 128
HALF = 64
MAXP = 256
GROUPS = 32
XN = 4
ZN = 8
LANES = 512
TAYLOR = 273
TAYLOR_LANES = 384
SPREAD = 1152

EPSILON = 1e-06
MASKED = -1e30


def head_shift(value, steps):
    count = lax.axis_size("head")
    return lax.ppermute(value, "head", [(i, (i + steps) % count) for i in range(count)])


def z_shift(value, steps):
    return lax.ppermute(
        value,
        "req",
        [(z * XN + i, (z + steps) % ZN * XN + i) for z in range(ZN) for i in range(XN)],
    )


def x_shift(value, steps):
    return lax.ppermute(
        value,
        "req",
        [(z * XN + i, z * XN + (i + steps) % XN) for z in range(ZN) for i in range(XN)],
    )


def far_swap(value):
    count = XN * ZN
    return lax.ppermute(
        value,
        ("section", "req"),
        [(count + i, count + (i + count // 2) % count) for i in range(count)],
    )


def section_swap(value, steps):
    count = lax.axis_size("head")
    there = [(i, count + (i + steps) % count) for i in range(count)]
    return lax.ppermute(value, ("section", "head"), there + [(b, a) for a, b in there])


VMEM = pl.BlockSpec(memory_space=pltpu.VMEM)
SMEM = pl.BlockSpec(memory_space=pltpu.SMEM)
HBM = pl.BlockSpec(memory_space=pltpu.HBM)
FLAT = (((1,), (1,)), ((), ()))


def normed_rows(values, gain_row):
    factor = lax.rsqrt(jnp.mean(values * values, axis=-1, keepdims=True) + EPSILON)
    return (values * factor * gain_row).astype(jnp.bfloat16)


def lanes_of(shape):
    return lax.broadcasted_iota(jnp.int32, shape, len(shape) - 1)


def in_head(lane, h):
    return (lane >= h * HD) & (lane < (h + 1) * HD)


def place():
    return lax.axis_index("section"), lax.axis_index("req"), lax.axis_index("head")


def kernel_call(
    kernel,
    section,
    name,
    out_shape,
    in_specs,
    scratch_shapes,
    args,
    vmem=6 << 20,
    cost=None,
    elsewhere=None,
):
    def run(*refs):
        ids = place()

        @pl.when(ids[0] == section)
        def _():
            kernel(ids, *refs)

        if elsewhere is not None:

            @pl.when(ids[0] != section)
            def _():
                elsewhere(ids, *refs)

    args = [
        pltpu.with_memory_space_constraint(arg, pltpu.HBM) if spec is HBM else arg
        for arg, spec in zip(args, in_specs, strict=True)
    ]
    return pl.pallas_call(
        run,
        out_shape=out_shape,
        in_specs=in_specs,
        out_specs=jax.tree.map(lambda _: VMEM, out_shape),
        scratch_shapes=scratch_shapes,
        compiler_params=pltpu.CompilerParams(vmem_limit_bytes=vmem),
        cost_estimate=cost,
        name=name,
    )(*args)


def expansion(features, width, repeat):
    lane = lax.broadcasted_iota(jnp.int32, (features, 2 * width), 1)
    source = lax.broadcasted_iota(jnp.int32, (features, 2 * width), 0)
    left = lane < width
    at = jnp.where(left, lane, lane - width) >> (repeat.bit_length() - 1)
    linear = left & (at > 0) & (at <= FEAT) & (source == at - 1)
    pair = at - (FEAT + 1)
    wanted = jnp.where(left, pair >> 4, pair & (FEAT - 1))
    quad = (pair >= 0) & (pair < FEAT * FEAT) & (source == wanted)
    return jnp.where(linear | quad, 1.0, 0.0).astype(jnp.bfloat16)


def taylor_rows(left, right, feature):
    scale = FEAT ** (-0.25)
    left, right = left * scale, right * scale
    return jnp.where(
        feature == 0, 1.0, jnp.where(feature <= FEAT, left, left * right * 0.5**0.5)
    )


def linear_kernel(
    ids,
    t0,
    t1,
    t2,
    t3,
    gain,
    feature_w,
    state,
    lin_norm,
    conv_w,
    conv_state,
    value_w,
    out_hbm,
    update,
    out_w,
    sem,
):
    rows, share = t0.shape
    heads = share // HD
    span = TAYLOR * heads
    copy = pltpu.make_async_copy(out_hbm.at[0], out_w, sem)
    copy.start()
    by_state = expansion(128, SPREAD, heads)
    by_norm = expansion(128, TAYLOR_LANES, 1)
    expand = jnp.concatenate([by_state, by_norm], axis=1)

    own = ids[2]
    got = [ref[...].astype(jnp.float32) for ref in (t0, t1, t3, t2)]
    whole = []
    for place in range(heads):
        piece = got[0]
        for back in range(1, heads):
            piece = jnp.where(((own - back) & (heads - 1)) == place, got[back], piece)
        whole.append(piece)
    tokens = jnp.concatenate(whole, axis=1)
    normed = normed_rows(tokens, gain[...])
    feats = jnp.dot(normed, feature_w[...], preferred_element_type=jnp.float32)
    by_head = jnp.concatenate(
        [feats] + [pltpu.roll(feats, 128 - 2 * FEAT * h, 1) for h in range(1, heads)], axis=0
    )
    high = by_head.astype(jnp.bfloat16)
    rest = by_head - high.astype(jnp.float32)
    middle = rest.astype(jnp.bfloat16)
    low = (rest - middle.astype(jnp.float32)).astype(jnp.bfloat16)
    spread = jnp.dot(
        jnp.concatenate([high, middle, low], axis=0), expand, preferred_element_type=jnp.float32
    )
    count = heads * rows
    spread = spread[:count] + spread[count : 2 * count] + spread[2 * count :]
    lane = lanes_of((count, SPREAD))
    head = lax.broadcasted_iota(jnp.int32, (count, SPREAD), 0) >> 3
    query_wide = taylor_rows(spread[:, :SPREAD], spread[:, SPREAD : 2 * SPREAD], lane >> 2)
    query_wide = jnp.where(((lane & (heads - 1)) == head) & (lane < span), query_wide, 0.0)
    query_feats = taylor_rows(
        spread[:, 2 * SPREAD : 2 * SPREAD + TAYLOR_LANES],
        spread[:, 2 * SPREAD + TAYLOR_LANES :],
        lanes_of((count, TAYLOR_LANES)),
    )[:, :TAYLOR]
    both = by_head * pltpu.roll(by_head, 128 - FEAT, 1)
    near = jnp.sum(
        jnp.where(lanes_of(both.shape) < FEAT, both, 0.0), axis=-1, keepdims=True
    ) * FEAT ** (-0.5)
    intersection = 1.0 + near + 0.5 * near * near

    length = span + 12
    queries = []
    for shift in range(0, 16, 4):
        moved = query_wide if shift == 0 else pltpu.roll(query_wide, shift, 1)
        queries.append(moved[:, :length].astype(jnp.bfloat16))
    row = lax.broadcasted_iota(jnp.int32, (count, HD), 0) & (rows - 1)
    found = jnp.zeros((count, HD), jnp.float32)
    for r in range(rows):
        first = span * r
        shift = first % 16
        product = jnp.dot(
            queries[shift // 4],
            state[first - shift : first - shift + length, :],
            preferred_element_type=jnp.float32,
        )
        found = jnp.where(row == r, product, found)
    fresh = lax.dot_general(normed, value_w[...], FLAT, preferred_element_type=jnp.float32)
    older = conv_state[...].astype(jnp.float32)
    mixed = conv_w[0:1] * older[:, 0] + conv_w[1:2] * older[:, 1] + conv_w[2:3] * fresh
    total = tokens * 0.25
    copy.wait()
    for h in range(heads):
        here = slice(h * rows, (h + 1) * rows)
        denominator = (
            jnp.sum(query_feats[here] * lin_norm[:, h, :], axis=-1, keepdims=True)
            + intersection[here]
        )
        attended = (
            (found[here] + intersection[here] * mixed[:, h * HD : (h + 1) * HD]) / denominator
        ).astype(jnp.bfloat16)
        total = total + jnp.dot(
            attended, out_w[h * HD : (h + 1) * HD, :], preferred_element_type=jnp.float32
        )
    update[...] = total.astype(jnp.bfloat16)


def linear_layer(pieces, near, out_w):
    return kernel_call(
        linear_kernel,
        0,
        "linear_layer",
        jax.ShapeDtypeStruct((pieces[0].shape[0], out_w.shape[2]), jnp.bfloat16),
        [VMEM] * 11 + [HBM],
        [pltpu.VMEM(out_w.shape[1:], jnp.bfloat16), pltpu.SemaphoreType.DMA],
        (*pieces, *(near[name] for name in LINEAR_NEAR), out_w),
    )


def project_kernel(
    ids,
    tags,
    p0,
    p1,
    p2,
    p3,
    gain,
    qk_w,
    v_hbm,
    one,
    asked,
    key_new,
    value_new,
    v_w,
    sem,
):
    rows, share = one.shape
    copy = pltpu.make_async_copy(v_hbm.at[0], v_w, sem)
    copy.start()
    heads = share // HD
    layer_one = sum(ref[...].astype(jnp.float32) for ref in (p0, p1, p2, p3)).astype(jnp.bfloat16)
    rounded = layer_one.astype(jnp.float32)
    mine = rounded[:, :share]
    for h in range(1, heads):
        mine = jnp.where(ids[2] == h, rounded[:, h * share : (h + 1) * share], mine)
    one[...] = mine.astype(jnp.bfloat16)
    normed = normed_rows(rounded, gain[...])
    query_key = jnp.dot(normed, qk_w[...], preferred_element_type=jnp.float32)
    width = query_key.shape[1]
    lane = lanes_of((rows, LANES))
    query = jnp.where(in_head(lane, 0), query_key[:, :LANES], 0.0)
    key = query
    for h in range(heads):
        if h:
            moved = pltpu.roll(query_key, width - h * HD, 1)[:, :LANES]
            query = jnp.where(in_head(lane, h), moved, query)
        moved = pltpu.roll(query_key, width - (h + 1) * HD, 1)[:, :LANES]
        key = jnp.where(in_head(lane, h), moved, key)
    query = jnp.where(lane == share, tags[:, 0:1], query)
    query = jnp.where(lane == share + 1, tags[:, 1:2], query)
    asked[...] = query.astype(jnp.bfloat16)
    key_new[...] = key[:, :share].astype(jnp.bfloat16)
    copy.wait()
    value_new[...] = lax.dot_general(
        normed, v_w[...], FLAT, preferred_element_type=jnp.float32
    ).astype(jnp.bfloat16)


def project(tags, pieces, near, value_w):
    rows = pieces[0].shape[0]
    share = value_w.shape[1]
    return kernel_call(
        project_kernel,
        1,
        "project",
        [
            jax.ShapeDtypeStruct((rows, share), jnp.bfloat16),
            jax.ShapeDtypeStruct((rows, LANES), jnp.bfloat16),
            jax.ShapeDtypeStruct((rows, share), jnp.bfloat16),
            jax.ShapeDtypeStruct((rows, share), jnp.bfloat16),
        ],
        [VMEM] * 7 + [HBM],
        [pltpu.VMEM(value_w.shape[1:], jnp.bfloat16), pltpu.SemaphoreType.DMA],
        (tags, *pieces, near["gain"], near["query_key_w"], value_w),
    )


def window_pages(lengths, r):
    length = lengths[r]
    return jnp.maximum((length - WINDOW) // PAGE, 1), jnp.maximum((length - 2) // PAGE, 1)


def own_kernel(
    ids, tags, asked, key_new, value_new, pages, summed_out, highest_out, total_out
):
    rows, share = key_new.shape
    head = lax.broadcasted_iota(jnp.int32, (8, share), 0)
    lane = lanes_of((8, share))
    mine = (lane >= head * HD) & (lane < (head + 1) * HD)
    scale = HD ** (-0.5)
    query = asked[:, :share].astype(jnp.float32)
    new_key = key_new[...].astype(jnp.float32)
    new_value = value_new[...].astype(jnp.float32)
    wide = jnp.concatenate([jnp.where(mine, query[r : r + 1], 0.0) for r in range(rows)], axis=0)
    keys = jnp.concatenate(
        [jnp.broadcast_to(new_key[r : r + 1], (8, share)) for r in range(rows)], axis=0
    )
    new_score = jnp.sum(wide * keys, axis=-1, keepdims=True) * scale
    token = lanes_of((8 * rows, 2 * PAGE))

    def by_request(at):
        return jnp.concatenate(
            [jnp.broadcast_to(tags[r : r + 1, at : at + 1], (8, 2 * PAGE)) for r in range(rows)],
            axis=0,
        )

    length = by_request(2)
    position = token.astype(jnp.float32) + jnp.where(token < PAGE, by_request(3), by_request(4))
    usable = (position >= length - WINDOW) & (position <= length - 2)
    scores = []
    for r in range(rows):
        low = wide[8 * r : 8 * r + 8].astype(jnp.bfloat16)
        scores.append(
            jnp.concatenate(
                [
                    jnp.dot(low, pages[r, slot, 0], preferred_element_type=jnp.float32)
                    for slot in range(2)
                ],
                axis=1,
            )
        )
    scores = jnp.where(usable, jnp.concatenate(scores, axis=0) * scale, MASKED)
    highest = jnp.maximum(jnp.max(scores, axis=-1, keepdims=True), new_score)
    exps = jnp.where(usable, jnp.exp(scores - highest), 0.0)
    exp_new = jnp.exp(new_score - highest)
    total = jnp.sum(exps, axis=-1, keepdims=True) + exp_new
    for r in range(rows):
        here = slice(8 * r, 8 * r + 8)
        low = exps[here].astype(jnp.bfloat16)
        found = exp_new[here] * new_value[r : r + 1]
        for slot in range(2):
            found = found + lax.dot_general(
                low[:, slot * PAGE : (slot + 1) * PAGE],
                pages[r, slot, 1],
                FLAT,
                preferred_element_type=jnp.float32,
            )
        for ref, value in (
            (summed_out, found),
            (highest_out, highest[here]),
            (total_out, total[here]),
        ):
            ref[r : r + 1, :] = jnp.sum(jnp.where(mine, value, 0.0), axis=0, keepdims=True)


def own_attention(tags, asked, key_new, value_new, near):
    rows, share = key_new.shape
    return kernel_call(
        own_kernel,
        1,
        "own_attention",
        [jax.ShapeDtypeStruct((rows, share), jnp.float32)] * 3,
        [VMEM] * 5,
        [],
        (tags, asked, key_new, value_new, near["own_pages"]),
    )


def prompt_kernel(ids, a0, a1, a2, a3, near_pages, far_pages, o0, o1, o2, o3):
    rows = a0.shape[0]
    share = near_pages.shape[1]
    heads = share // HD
    pages = jnp.concatenate(
        [near_pages[i] for i in range(XN)] + [far_pages[i] for i in range(XN)], axis=1
    )
    asked = jnp.concatenate([ref[...].astype(jnp.float32) for ref in (a0, a1, a2, a3)], axis=0)
    count = asked.shape[0]
    lane = lanes_of(asked.shape)
    group = jnp.sum(jnp.where(lane == share, asked, 0.0), axis=-1, keepdims=True)
    start = jnp.sum(jnp.where(lane == share + 1, asked, 0.0), axis=-1, keepdims=True)
    group, start = group.astype(jnp.int32), start.astype(jnp.int32)
    query = jnp.concatenate(
        [jnp.where(in_head(lane, h), asked, 0.0)[:, :share] for h in range(heads)], axis=0
    ).astype(jnp.bfloat16)
    scores = jnp.dot(query, pages, preferred_element_type=jnp.float32) * HD ** (-0.5)
    token = lanes_of((count, 2 * XN * PAGE))
    z, x = ids[1] // XN, ids[1] % XN
    slot = token >> 7
    slot_group = jnp.where(slot < XN, z, (z + ZN // 2) & (ZN - 1)) * XN
    slot_group = slot_group + ((slot + x + XN - 1) & (XN - 1))
    offset = token & (PAGE - 1)
    usable = (slot_group == group) & (offset < HALF) & (offset + HALF >= start)
    lane = lanes_of((count, share))
    stat_lane = lanes_of((count, 128))
    weights = []
    stats = jnp.zeros((count, 128), jnp.float32)
    for h in range(heads):
        here = jnp.where(usable, scores[h * count : (h + 1) * count], MASKED)
        highest = jnp.max(here, axis=-1, keepdims=True)
        exps = jnp.where(usable, jnp.exp(here - highest), 0.0)
        total = jnp.sum(exps, axis=-1, keepdims=True)
        stats = jnp.where(stat_lane == h, highest, stats)
        stats = jnp.where(stat_lane == heads + h, total, stats)
        weights.append(pltpu.roll(exps, HALF, 1))
    found = lax.dot_general(
        jnp.concatenate(weights, axis=0).astype(jnp.bfloat16),
        pages,
        FLAT,
        preferred_element_type=jnp.float32,
    )
    summed = jnp.zeros((count, share), jnp.float32)
    for h in range(heads):
        summed = jnp.where(in_head(lane, h), found[h * count : (h + 1) * count], summed)
    for at, ref in enumerate((o0, o1, o2, o3)):
        ref[:, :share] = summed[at * rows : (at + 1) * rows]
        ref[:, share:LANES] = jnp.zeros((rows, LANES - share), jnp.float32)
        ref[:, LANES:] = stats[at * rows : (at + 1) * rows]


def prompt_attention(asked, near_pages, far_pages):
    rows = asked[0].shape[0]
    return kernel_call(
        prompt_kernel,
        1,
        "prompt_attention",
        [jax.ShapeDtypeStruct((rows, LANES + 128), jnp.float32)] * 4,
        [VMEM] * 6,
        [],
        (*asked, near_pages, far_pages),
    )


def combine_kernel(ids, summed, highest, total, r0, r1, r2, r3, update, out_w, s0, s1, s2, s3):
    rows, share = summed.shape
    heads = share // HD
    refs = (r0, r1, r2, r3)
    prompt_summed = sum(ref[:, :share] for ref in refs)
    stats = [ref[:, LANES:] for ref in refs]
    top = jnp.maximum(jnp.maximum(stats[0], stats[1]), jnp.maximum(stats[2], stats[3]))
    added = stats[0] + stats[1] + stats[2] + stats[3]
    lane = lanes_of((rows, share))
    prompt_highest = jnp.zeros((rows, share), jnp.float32)
    prompt_total = jnp.zeros((rows, share), jnp.float32)
    for h in range(heads):
        here = in_head(lane, h)
        prompt_highest = jnp.where(here, top[:, h : h + 1], prompt_highest)
        prompt_total = jnp.where(here, added[:, heads + h : heads + h + 1], prompt_total)
    peak = jnp.maximum(highest[...], prompt_highest)
    own_factor = jnp.exp(highest[...] - peak)
    prompt_factor = jnp.exp(prompt_highest - peak)
    whole = total[...] * own_factor + prompt_total * prompt_factor
    attended = (summed[...] * own_factor + prompt_summed * prompt_factor) / whole
    second = jnp.dot(attended.astype(jnp.bfloat16), out_w[0], preferred_element_type=jnp.float32)
    write_slabs(ids, second, (s0, s1, s2, s3))


def write_slabs(ids, rows_whole, refs):
    heads = len(refs)
    share = refs[0].shape[1]
    for steps, ref in enumerate(refs):
        slab = rows_whole[:, :share]
        for h in range(1, heads):
            there = rows_whole[:, h * share : (h + 1) * share]
            slab = jnp.where(((ids[2] + steps) & (heads - 1)) == h, there, slab)
        ref[...] = slab


def own_slabs(ids, *refs):
    write_slabs(ids, refs[7][...].astype(jnp.float32), refs[9:])


def combine(own, parts, update, out_w):
    return kernel_call(
        combine_kernel,
        1,
        "combine",
        [jax.ShapeDtypeStruct(own[0].shape, jnp.float32)] * 4,
        [VMEM] * 9,
        [],
        (*own, *parts, update, out_w),
        elsewhere=own_slabs,
    )


LINEAR_NEAR = (
    "gain",
    "feature_w",
    "state",
    "lin_norm",
    "conv_w",
    "conv_state",
    "value_w",
)
WINDOW_NEAR = ("gain", "query_key_w")


def bring_near(arrays):
    names = list(arrays)
    count = len(names)
    first = [at for at, name in enumerate(names) if name in LINEAR_NEAR]
    second = [at for at, name in enumerate(names) if name in WINDOW_NEAR]

    def copy_some(chosen, refs):
        sems = refs[-1]
        copies = [
            pltpu.make_async_copy(refs[at], refs[count + at], sems.at[at]) for at in chosen
        ]
        for copy in copies:
            copy.start()
        for copy in copies:
            copy.wait()

    near = kernel_call(
        lambda ids, *refs: copy_some(first, refs),
        0,
        "bring_near",
        [jax.ShapeDtypeStruct(array.shape, array.dtype) for array in arrays.values()],
        [HBM] * count,
        [pltpu.SemaphoreType.DMA((count,))],
        tuple(arrays.values()),
        4 << 20,
        bytes_only(arrays.values()),
        lambda ids, *refs: copy_some(second, refs),
    )
    return dict(zip(names, near))


def bytes_only(arrays):
    moved = sum(array.size * array.dtype.itemsize for array in arrays)
    return pl.CostEstimate(flops=0, bytes_accessed=2 * moved, transcendentals=0)


def window_kernel(
    ids, table, lengths, own_hbm, own_near, tags, sems
):
    rows = tags.shape[0]
    total = own_hbm.shape[0]
    copies = []
    for r in range(rows):
        for slot, logical in enumerate(window_pages(lengths, r)):
            page = jnp.clip(table[r, logical] - GROUPS - ids[1] * total, 0, total - 1)
            copies.append(
                pltpu.make_async_copy(own_hbm.at[page], own_near.at[r, slot], sems.at[r, slot])
            )
    for copy in copies:
        copy.start()
    row = lax.broadcasted_iota(jnp.int32, tags.shape, 0)
    lane = lanes_of(tags.shape)
    marks = jnp.zeros(tags.shape, jnp.int32)
    for r in range(rows):
        length = lengths[r]
        first, last = window_pages(lengths, r)
        second = jnp.where(first != last, last - 1, -MAXP) * PAGE
        start = jnp.minimum(length - WINDOW, PAGE)
        for at, mark in enumerate((table[r, 0], start, length, first * PAGE, second)):
            marks = jnp.where((row == r) & (lane == at), mark, marks)
    tags[...] = marks.astype(jnp.float32)
    for copy in copies:
        copy.wait()


def bring_windows(table, lengths, own_pages):
    rows = lengths.shape[0]
    windows = jax.ShapeDtypeStruct((rows, 2) + own_pages.shape[1:], own_pages.dtype)
    return kernel_call(
        window_kernel,
        1,
        "bring_windows",
        [
            windows,
            jax.ShapeDtypeStruct((rows, 128), jnp.float32),
        ],
        [SMEM] * 2 + [HBM],
        [pltpu.SemaphoreType.DMA((rows, 2))],
        (table, lengths, own_pages),
        1 << 20,
        bytes_only([windows]),
    )


def page_kernel(ids, pages_hbm, page, pages, sem):
    copy = pltpu.make_async_copy(pages_hbm.at[0], pages, sem)
    copy.start()
    copy.wait()
    lane = lanes_of(page.shape)
    keys = pltpu.roll(pages[0].astype(jnp.float32), HALF, 1)
    page[...] = jnp.where(lane < HALF, keys, pages[1].astype(jnp.float32)).astype(jnp.bfloat16)


def window_page(prompt_pages):
    shape = prompt_pages.shape[1:]
    return kernel_call(
        page_kernel,
        1,
        "window_page",
        jax.ShapeDtypeStruct(shape[1:], jnp.bfloat16),
        [HBM],
        [pltpu.VMEM(shape, jnp.bfloat16), pltpu.SemaphoreType.DMA],
        (prompt_pages,),
        cost=pl.CostEstimate(flops=0, bytes_accessed=16 << 20, transcendentals=0),
    )


def body(
    tokens,
    norm_gain,
    feature_w,
    query_key_w,
    value_w,
    out_w,
    conv_w,
    conv_state,
    lin_state,
    lin_norm,
    own_pages,
    prompt_pages,
    page_table,
    lengths,
):
    pages_first = prompt_pages.transpose(0, 1, 3, 2)
    value_w = value_w.transpose(0, 2, 1)
    stored = {
        "gain": norm_gain,
        "feature_w": feature_w,
        "state": lin_state.transpose(0, 2, 1, 3).reshape(-1, HD),
        "lin_norm": lin_norm,
        "conv_w": conv_w,
        "conv_state": conv_state,
        "value_w": value_w[0],
        "query_key_w": query_key_w,
    }

    page = window_page(pages_first)
    row_pages = [x_shift(page, k) for k in (1, 3, 2)]
    row_pages[0], last_tokens, stored = lax.optimization_barrier((row_pages[0], tokens, stored))
    received = [head_shift(last_tokens, 1), head_shift(tokens, 3), head_shift(tokens, 2)]
    near, received, row_pages = lax.optimization_barrier((bring_near(stored), received, row_pages))
    near_pages = jnp.stack([row_pages[0], page, row_pages[1], row_pages[2]])
    near_pages, received = lax.optimization_barrier((near_pages, received))
    far_pages = far_swap(near_pages)
    update = linear_layer([tokens] + received, near, out_w)
    own_pages = own_pages.transpose(0, 1, 3, 2)
    own_pages, table, ends, update = lax.optimization_barrier(
        (own_pages, page_table, lengths, update)
    )
    near["own_pages"], tags = bring_windows(table, ends, own_pages)
    swapped = [section_swap(update, k) for k in (2, 1, 3, 0)]
    one_share, packed, key_new, value_new = project(tags, swapped, near, value_w)
    asked = [packed] + [z_shift(packed, k) for k in (2, 1, 7)]
    own = own_attention(tags, packed, key_new, value_new, near)
    asked, own = lax.optimization_barrier((asked, own))
    answers = prompt_attention(asked, near_pages, far_pages)
    parts = [answers[0]] + [z_shift(answers[at], -k) for at, k in ((1, 2), (2, 1), (3, 7))]
    slabs = combine(own, parts, update, out_w)
    here = lax.axis_index("section") == 1
    total = jnp.where(here, one_share.astype(jnp.float32), 0.0) + slabs[0]
    for piece in [head_shift(slabs[k], k) for k in (2, 1, 3)]:
        total = total + piece
    return total.astype(jnp.bfloat16)[None]


def solution(mesh):
    placed = (
        P("req", "head"),
        P("section", None),
        P(None, "head"),
        P(None, "head"),
        P("section", None, "head"),
        P("section", "head", None),
        P(None, "head"),
        P("req", None, "head"),
        P("req", "head", None, None),
        P("req", "head", None),
        P("req", None, None, "head"),
        P("req", None, None, "head"),
        P("req", None),
        P("req"),
    )
    return jax.shard_map(
        body, mesh=mesh, in_specs=placed, out_specs=P("section", "req", "head"), check_vma=False
    )
```

```python
import jax
import jax.numpy as jnp
from jax import lax
from jax.experimental import pallas as pl
from jax.experimental.pallas import tpu as pltpu
from jax.sharding import PartitionSpec as P

HD = 112
FEAT = 16
WINDOW = 64
PAGE = 128
HALF = 64
MAXP = 256
GROUPS = 32
XN = 4
ZN = 8
LANES = 512
TAYLOR = 273
TAYLOR_LANES = 384
SPREAD = 1152

EPSILON = 1e-06
MASKED = -1e30


def head_shift(value, steps):
    count = lax.axis_size("head")
    return lax.ppermute(value, "head", [(i, (i + steps) % count) for i in range(count)])


def z_shift(value, steps):
    return lax.ppermute(
        value,
        "req",
        [(z * XN + i, (z + steps) % ZN * XN + i) for z in range(ZN) for i in range(XN)],
    )


def x_shift(value, steps):
    return lax.ppermute(
        value,
        "req",
        [(z * XN + i, z * XN + (i + steps) % XN) for z in range(ZN) for i in range(XN)],
    )


def far_swap(value):
    count = XN * ZN
    return lax.ppermute(
        value,
        ("section", "req"),
        [(count + i, count + (i + count // 2) % count) for i in range(count)],
    )


def section_swap(value, steps):
    count = lax.axis_size("head")
    there = [(i, count + (i + steps) % count) for i in range(count)]
    return lax.ppermute(value, ("section", "head"), there + [(b, a) for a, b in there])


VMEM = pl.BlockSpec(memory_space=pltpu.VMEM)
SMEM = pl.BlockSpec(memory_space=pltpu.SMEM)
HBM = pl.BlockSpec(memory_space=pltpu.HBM)
FLAT = (((1,), (1,)), ((), ()))


def normed_rows(values, gain_row):
    factor = lax.rsqrt(jnp.mean(values * values, axis=-1, keepdims=True) + EPSILON)
    return (values * factor * gain_row).astype(jnp.bfloat16)


def lanes_of(shape):
    return lax.broadcasted_iota(jnp.int32, shape, len(shape) - 1)


def in_head(lane, h):
    return (lane >= h * HD) & (lane < (h + 1) * HD)


def place():
    return lax.axis_index("section"), lax.axis_index("req"), lax.axis_index("head")


def kernel_call(
    kernel,
    section,
    name,
    out_shape,
    in_specs,
    scratch_shapes,
    args,
    vmem=6 << 20,
    cost=None,
    elsewhere=None,
):
    def run(*refs):
        ids = place()

        @pl.when(ids[0] == section)
        def _():
            kernel(ids, *refs)

        if elsewhere is not None:

            @pl.when(ids[0] != section)
            def _():
                elsewhere(ids, *refs)

    args = [
        pltpu.with_memory_space_constraint(arg, pltpu.HBM) if spec is HBM else arg
        for arg, spec in zip(args, in_specs, strict=True)
    ]
    return pl.pallas_call(
        run,
        out_shape=out_shape,
        in_specs=in_specs,
        out_specs=jax.tree.map(lambda _: VMEM, out_shape),
        scratch_shapes=scratch_shapes,
        compiler_params=pltpu.CompilerParams(vmem_limit_bytes=vmem),
        cost_estimate=cost,
        name=name,
    )(*args)


def expansion(features, width, repeat):
    lane = lax.broadcasted_iota(jnp.int32, (features, 2 * width), 1)
    source = lax.broadcasted_iota(jnp.int32, (features, 2 * width), 0)
    left = lane < width
    at = jnp.where(left, lane, lane - width) >> (repeat.bit_length() - 1)
    linear = left & (at > 0) & (at <= FEAT) & (source == at - 1)
    pair = at - (FEAT + 1)
    wanted = jnp.where(left, pair >> 4, pair & (FEAT - 1))
    quad = (pair >= 0) & (pair < FEAT * FEAT) & (source == wanted)
    return jnp.where(linear | quad, 1.0, 0.0).astype(jnp.bfloat16)


def taylor_rows(left, right, feature):
    scale = FEAT ** (-0.25)
    left, right = left * scale, right * scale
    return jnp.where(
        feature == 0, 1.0, jnp.where(feature <= FEAT, left, left * right * 0.5**0.5)
    )


def linear_kernel(
    ids,
    t0,
    t1,
    t2,
    t3,
    gain,
    feature_w,
    state,
    lin_norm,
    conv_w,
    conv_state,
    value_w,
    out_hbm,
    update,
    out_w,
    sem,
):
    rows, share = t0.shape
    heads = share // HD
    span = TAYLOR * heads
    copy = pltpu.make_async_copy(out_hbm.at[0], out_w, sem)
    copy.start()
    by_state = expansion(128, SPREAD, heads)
    by_norm = expansion(128, TAYLOR_LANES, 1)
    expand = jnp.concatenate([by_state, by_norm], axis=1)

    own = ids[2]
    got = [ref[...].astype(jnp.float32) for ref in (t0, t1, t3, t2)]
    whole = []
    for place in range(heads):
        piece = got[0]
        for back in range(1, heads):
            piece = jnp.where(((own - back) & (heads - 1)) == place, got[back], piece)
        whole.append(piece)
    tokens = jnp.concatenate(whole, axis=1)
    normed = normed_rows(tokens, gain[...])
    feats = jnp.dot(normed, feature_w[...], preferred_element_type=jnp.float32)
    by_head = jnp.concatenate(
        [feats] + [pltpu.roll(feats, 128 - 2 * FEAT * h, 1) for h in range(1, heads)], axis=0
    )
    high = by_head.astype(jnp.bfloat16)
    rest = by_head - high.astype(jnp.float32)
    middle = rest.astype(jnp.bfloat16)
    low = (rest - middle.astype(jnp.float32)).astype(jnp.bfloat16)
    spread = jnp.dot(
        jnp.concatenate([high, middle, low], axis=0), expand, preferred_element_type=jnp.float32
    )
    count = heads * rows
    spread = spread[:count] + spread[count : 2 * count] + spread[2 * count :]
    lane = lanes_of((count, SPREAD))
    head = lax.broadcasted_iota(jnp.int32, (count, SPREAD), 0) >> 3
    query_wide = taylor_rows(spread[:, :SPREAD], spread[:, SPREAD : 2 * SPREAD], lane >> 2)
    query_wide = jnp.where(((lane & (heads - 1)) == head) & (lane < span), query_wide, 0.0)
    query_feats = taylor_rows(
        spread[:, 2 * SPREAD : 2 * SPREAD + TAYLOR_LANES],
        spread[:, 2 * SPREAD + TAYLOR_LANES :],
        lanes_of((count, TAYLOR_LANES)),
    )[:, :TAYLOR]
    both = by_head * pltpu.roll(by_head, 128 - FEAT, 1)
    near = jnp.sum(
        jnp.where(lanes_of(both.shape) < FEAT, both, 0.0), axis=-1, keepdims=True
    ) * FEAT ** (-0.5)
    intersection = 1.0 + near + 0.5 * near * near

    length = span + 12
    queries = []
    for shift in range(0, 16, 4):
        moved = query_wide if shift == 0 else pltpu.roll(query_wide, shift, 1)
        queries.append(moved[:, :length].astype(jnp.bfloat16))
    row = lax.broadcasted_iota(jnp.int32, (count, HD), 0) & (rows - 1)
    found = jnp.zeros((count, HD), jnp.float32)
    for r in range(rows):
        first = span * r
        shift = first % 16
        product = jnp.dot(
            queries[shift // 4],
            state[first - shift : first - shift + length, :],
            preferred_element_type=jnp.float32,
        )
        found = jnp.where(row == r, product, found)
    fresh = lax.dot_general(normed, value_w[...], FLAT, preferred_element_type=jnp.float32)
    older = conv_state[...].astype(jnp.float32)
    mixed = conv_w[0:1] * older[:, 0] + conv_w[1:2] * older[:, 1] + conv_w[2:3] * fresh
    total = tokens * 0.25
    copy.wait()
    for h in range(heads):
        here = slice(h * rows, (h + 1) * rows)
        denominator = (
            jnp.sum(query_feats[here] * lin_norm[:, h, :], axis=-1, keepdims=True)
            + intersection[here]
        )
        attended = (
            (found[here] + intersection[here] * mixed[:, h * HD : (h + 1) * HD]) / denominator
        ).astype(jnp.bfloat16)
        total = total + jnp.dot(
            attended, out_w[h * HD : (h + 1) * HD, :], preferred_element_type=jnp.float32
        )
    update[...] = total.astype(jnp.bfloat16)


def linear_layer(pieces, near, out_w):
    return kernel_call(
        linear_kernel,
        0,
        "linear_layer",
        jax.ShapeDtypeStruct((pieces[0].shape[0], out_w.shape[2]), jnp.bfloat16),
        [VMEM] * 11 + [HBM],
        [pltpu.VMEM(out_w.shape[1:], jnp.bfloat16), pltpu.SemaphoreType.DMA],
        (*pieces, *(near[name] for name in LINEAR_NEAR), out_w),
    )


def project_kernel(
    ids,
    tags,
    p0,
    p1,
    p2,
    p3,
    gain,
    qk_w,
    v_w,
    one,
    asked,
    key_new,
    value_new,
):
    rows, share = one.shape
    heads = share // HD
    layer_one = sum(ref[...].astype(jnp.float32) for ref in (p0, p1, p2, p3)).astype(jnp.bfloat16)
    rounded = layer_one.astype(jnp.float32)
    mine = rounded[:, :share]
    for h in range(1, heads):
        mine = jnp.where(ids[2] == h, rounded[:, h * share : (h + 1) * share], mine)
    one[...] = mine.astype(jnp.bfloat16)
    normed = normed_rows(rounded, gain[...])
    query_key = jnp.dot(normed, qk_w[...], preferred_element_type=jnp.float32)
    width = query_key.shape[1]
    lane = lanes_of((rows, LANES))
    query = jnp.where(in_head(lane, 0), query_key[:, :LANES], 0.0)
    key = query
    for h in range(heads):
        if h:
            moved = pltpu.roll(query_key, width - h * HD, 1)[:, :LANES]
            query = jnp.where(in_head(lane, h), moved, query)
        moved = pltpu.roll(query_key, width - (h + 1) * HD, 1)[:, :LANES]
        key = jnp.where(in_head(lane, h), moved, key)
    query = jnp.where(lane == share, tags[:, 0:1], query)
    query = jnp.where(lane == share + 1, tags[:, 1:2], query)
    asked[...] = query.astype(jnp.bfloat16)
    key_new[...] = key[:, :share].astype(jnp.bfloat16)
    value_new[...] = lax.dot_general(
        normed, v_w[...], FLAT, preferred_element_type=jnp.float32
    ).astype(jnp.bfloat16)


def project(tags, pieces, near):
    rows = pieces[0].shape[0]
    share = near["value_w"].shape[0]
    return kernel_call(
        project_kernel,
        1,
        "project",
        [
            jax.ShapeDtypeStruct((rows, share), jnp.bfloat16),
            jax.ShapeDtypeStruct((rows, LANES), jnp.bfloat16),
            jax.ShapeDtypeStruct((rows, share), jnp.bfloat16),
            jax.ShapeDtypeStruct((rows, share), jnp.bfloat16),
        ],
        [VMEM] * 8,
        [],
        (tags, *pieces, near["gain"], near["query_key_w"], near["value_w"]),
    )


def window_pages(lengths, r):
    length = lengths[r]
    return jnp.maximum((length - WINDOW) // PAGE, 1), jnp.maximum((length - 2) // PAGE, 1)


def own_kernel(
    ids,
    table,
    lengths,
    tags,
    asked,
    key_new,
    value_new,
    key_pages,
    own_hbm,
    summed_out,
    highest_out,
    total_out,
    value_pages,
    sems,
):
    rows, share = key_new.shape
    total_pages = own_hbm.shape[0]
    copies = []
    for r in range(rows):
        for slot, logical in enumerate(window_pages(lengths, r)):
            page = jnp.clip(table[r, logical] - GROUPS - ids[1] * total_pages, 0, total_pages - 1)
            copies.append(
                pltpu.make_async_copy(
                    own_hbm.at[page, 1], value_pages.at[r, slot], sems.at[r, slot]
                )
            )
            copies[-1].start()
    head = lax.broadcasted_iota(jnp.int32, (8, share), 0)
    lane = lanes_of((8, share))
    mine = (lane >= head * HD) & (lane < (head + 1) * HD)
    scale = HD ** (-0.5)
    query = asked[:, :share].astype(jnp.float32)
    new_key = key_new[...].astype(jnp.float32)
    new_value = value_new[...].astype(jnp.float32)
    wide = jnp.concatenate([jnp.where(mine, query[r : r + 1], 0.0) for r in range(rows)], axis=0)
    keys = jnp.concatenate(
        [jnp.broadcast_to(new_key[r : r + 1], (8, share)) for r in range(rows)], axis=0
    )
    new_score = jnp.sum(wide * keys, axis=-1, keepdims=True) * scale
    token = lanes_of((8 * rows, 2 * PAGE))

    def by_request(at):
        return jnp.concatenate(
            [jnp.broadcast_to(tags[r : r + 1, at : at + 1], (8, 2 * PAGE)) for r in range(rows)],
            axis=0,
        )

    length = by_request(2)
    position = token.astype(jnp.float32) + jnp.where(token < PAGE, by_request(3), by_request(4))
    usable = (position >= length - WINDOW) & (position <= length - 2)
    scores = []
    for r in range(rows):
        low = wide[8 * r : 8 * r + 8].astype(jnp.bfloat16)
        scores.append(
            jnp.concatenate(
                [
                    jnp.dot(low, key_pages[r, slot], preferred_element_type=jnp.float32)
                    for slot in range(2)
                ],
                axis=1,
            )
        )
    scores = jnp.where(usable, jnp.concatenate(scores, axis=0) * scale, MASKED)
    highest = jnp.maximum(jnp.max(scores, axis=-1, keepdims=True), new_score)
    exps = jnp.where(usable, jnp.exp(scores - highest), 0.0)
    exp_new = jnp.exp(new_score - highest)
    total = jnp.sum(exps, axis=-1, keepdims=True) + exp_new
    for r in range(rows):
        here = slice(8 * r, 8 * r + 8)
        low = exps[here].astype(jnp.bfloat16)
        found = exp_new[here] * new_value[r : r + 1]
        for slot in range(2):
            copies[2 * r + slot].wait()
            found = found + lax.dot_general(
                low[:, slot * PAGE : (slot + 1) * PAGE],
                value_pages[r, slot],
                FLAT,
                preferred_element_type=jnp.float32,
            )
        for ref, value in (
            (summed_out, found),
            (highest_out, highest[here]),
            (total_out, total[here]),
        ):
            ref[r : r + 1, :] = jnp.sum(jnp.where(mine, value, 0.0), axis=0, keepdims=True)


def own_attention(table, lengths, tags, asked, key_new, value_new, near, own_pages):
    rows, share = key_new.shape
    return kernel_call(
        own_kernel,
        1,
        "own_attention",
        [jax.ShapeDtypeStruct((rows, share), jnp.float32)] * 3,
        [SMEM] * 2 + [VMEM] * 5 + [HBM],
        [
            pltpu.VMEM((rows, 2) + own_pages.shape[2:], jnp.bfloat16),
            pltpu.SemaphoreType.DMA((rows, 2)),
        ],
        (table, lengths, tags, asked, key_new, value_new, near["own_keys"], own_pages),
    )


def prompt_kernel(ids, a0, a1, a2, a3, near_pages, far_pages, o0, o1, o2, o3):
    rows = a0.shape[0]
    share = near_pages.shape[1]
    heads = share // HD
    pages = jnp.concatenate(
        [near_pages[i] for i in range(XN)] + [far_pages[i] for i in range(XN)], axis=1
    )
    asked = jnp.concatenate([ref[...].astype(jnp.float32) for ref in (a0, a1, a2, a3)], axis=0)
    count = asked.shape[0]
    lane = lanes_of(asked.shape)
    group = jnp.sum(jnp.where(lane == share, asked, 0.0), axis=-1, keepdims=True)
    start = jnp.sum(jnp.where(lane == share + 1, asked, 0.0), axis=-1, keepdims=True)
    group, start = group.astype(jnp.int32), start.astype(jnp.int32)
    query = jnp.concatenate(
        [jnp.where(in_head(lane, h), asked, 0.0)[:, :share] for h in range(heads)], axis=0
    ).astype(jnp.bfloat16)
    scores = jnp.dot(query, pages, preferred_element_type=jnp.float32) * HD ** (-0.5)
    token = lanes_of((count, 2 * XN * PAGE))
    z, x = ids[1] // XN, ids[1] % XN
    slot = token >> 7
    slot_group = jnp.where(slot < XN, z, (z + ZN // 2) & (ZN - 1)) * XN
    slot_group = slot_group + ((slot + x + XN - 1) & (XN - 1))
    offset = token & (PAGE - 1)
    usable = (slot_group == group) & (offset < HALF) & (offset + HALF >= start)
    lane = lanes_of((count, share))
    stat_lane = lanes_of((count, 128))
    weights = []
    stats = jnp.zeros((count, 128), jnp.float32)
    for h in range(heads):
        here = jnp.where(usable, scores[h * count : (h + 1) * count], MASKED)
        highest = jnp.max(here, axis=-1, keepdims=True)
        exps = jnp.where(usable, jnp.exp(here - highest), 0.0)
        total = jnp.sum(exps, axis=-1, keepdims=True)
        stats = jnp.where(stat_lane == h, highest, stats)
        stats = jnp.where(stat_lane == heads + h, total, stats)
        weights.append(pltpu.roll(exps, HALF, 1))
    found = lax.dot_general(
        jnp.concatenate(weights, axis=0).astype(jnp.bfloat16),
        pages,
        FLAT,
        preferred_element_type=jnp.float32,
    )
    summed = jnp.zeros((count, share), jnp.float32)
    for h in range(heads):
        summed = jnp.where(in_head(lane, h), found[h * count : (h + 1) * count], summed)
    for at, ref in enumerate((o0, o1, o2, o3)):
        ref[:, :share] = summed[at * rows : (at + 1) * rows]
        ref[:, share:LANES] = jnp.zeros((rows, LANES - share), jnp.float32)
        ref[:, LANES:] = stats[at * rows : (at + 1) * rows]


def prompt_attention(asked, near_pages, far_pages):
    rows = asked[0].shape[0]
    return kernel_call(
        prompt_kernel,
        1,
        "prompt_attention",
        [jax.ShapeDtypeStruct((rows, LANES + 128), jnp.float32)] * 4,
        [VMEM] * 6,
        [],
        (*asked, near_pages, far_pages),
    )


def combine_kernel(ids, summed, highest, total, r0, r1, r2, r3, update, out_w, s0, s1, s2, s3):
    rows, share = summed.shape
    heads = share // HD
    refs = (r0, r1, r2, r3)
    prompt_summed = sum(ref[:, :share] for ref in refs)
    stats = [ref[:, LANES:] for ref in refs]
    top = jnp.maximum(jnp.maximum(stats[0], stats[1]), jnp.maximum(stats[2], stats[3]))
    added = stats[0] + stats[1] + stats[2] + stats[3]
    lane = lanes_of((rows, share))
    prompt_highest = jnp.zeros((rows, share), jnp.float32)
    prompt_total = jnp.zeros((rows, share), jnp.float32)
    for h in range(heads):
        here = in_head(lane, h)
        prompt_highest = jnp.where(here, top[:, h : h + 1], prompt_highest)
        prompt_total = jnp.where(here, added[:, heads + h : heads + h + 1], prompt_total)
    peak = jnp.maximum(highest[...], prompt_highest)
    own_factor = jnp.exp(highest[...] - peak)
    prompt_factor = jnp.exp(prompt_highest - peak)
    whole = total[...] * own_factor + prompt_total * prompt_factor
    attended = (summed[...] * own_factor + prompt_summed * prompt_factor) / whole
    second = jnp.dot(attended.astype(jnp.bfloat16), out_w[0], preferred_element_type=jnp.float32)
    write_slabs(ids, second, (s0, s1, s2, s3))


def write_slabs(ids, rows_whole, refs):
    heads = len(refs)
    share = refs[0].shape[1]
    for steps, ref in enumerate(refs):
        slab = rows_whole[:, :share]
        for h in range(1, heads):
            there = rows_whole[:, h * share : (h + 1) * share]
            slab = jnp.where(((ids[2] + steps) & (heads - 1)) == h, there, slab)
        ref[...] = slab


def own_slabs(ids, *refs):
    write_slabs(ids, refs[7][...].astype(jnp.float32), refs[9:])


def combine(own, parts, update, out_w):
    return kernel_call(
        combine_kernel,
        1,
        "combine",
        [jax.ShapeDtypeStruct(own[0].shape, jnp.float32)] * 4,
        [VMEM] * 9,
        [],
        (*own, *parts, update, out_w),
        elsewhere=own_slabs,
    )


LINEAR_NEAR = (
    "gain",
    "feature_w",
    "state",
    "lin_norm",
    "conv_w",
    "conv_state",
    "value_w",
)
WINDOW_NEAR = ("gain", "value_w", "query_key_w")


def bring_near(arrays):
    names = list(arrays)
    count = len(names)
    first = [at for at, name in enumerate(names) if name in LINEAR_NEAR]
    second = [at for at, name in enumerate(names) if name in WINDOW_NEAR]

    def copy_some(chosen, refs):
        sems = refs[-1]
        copies = [
            pltpu.make_async_copy(refs[at], refs[count + at], sems.at[at]) for at in chosen
        ]
        for copy in copies:
            copy.start()
        for copy in copies:
            copy.wait()

    near = kernel_call(
        lambda ids, *refs: copy_some(first, refs),
        0,
        "bring_near",
        [jax.ShapeDtypeStruct(array.shape, array.dtype) for array in arrays.values()],
        [HBM] * count,
        [pltpu.SemaphoreType.DMA((count,))],
        tuple(arrays.values()),
        4 << 20,
        bytes_only(arrays.values()),
        lambda ids, *refs: copy_some(second, refs),
    )
    return dict(zip(names, near))


def bytes_only(arrays):
    moved = sum(array.size * array.dtype.itemsize for array in arrays)
    return pl.CostEstimate(flops=0, bytes_accessed=2 * moved, transcendentals=0)


def window_kernel(
    ids, table, lengths, own_hbm, own_near, tags, sems
):
    rows = tags.shape[0]
    total = own_hbm.shape[0]
    copies = []
    for r in range(rows):
        for slot, logical in enumerate(window_pages(lengths, r)):
            page = jnp.clip(table[r, logical] - GROUPS - ids[1] * total, 0, total - 1)
            copies.append(
                pltpu.make_async_copy(own_hbm.at[page, 0], own_near.at[r, slot], sems.at[r, slot])
            )
    for copy in copies:
        copy.start()
    row = lax.broadcasted_iota(jnp.int32, tags.shape, 0)
    lane = lanes_of(tags.shape)
    marks = jnp.zeros(tags.shape, jnp.int32)
    for r in range(rows):
        length = lengths[r]
        first, last = window_pages(lengths, r)
        second = jnp.where(first != last, last - 1, -MAXP) * PAGE
        start = jnp.minimum(length - WINDOW, PAGE)
        for at, mark in enumerate((table[r, 0], start, length, first * PAGE, second)):
            marks = jnp.where((row == r) & (lane == at), mark, marks)
    tags[...] = marks.astype(jnp.float32)
    for copy in copies:
        copy.wait()


def bring_windows(table, lengths, own_pages):
    rows = lengths.shape[0]
    windows = jax.ShapeDtypeStruct((rows, 2) + own_pages.shape[2:], own_pages.dtype)
    return kernel_call(
        window_kernel,
        1,
        "bring_windows",
        [
            windows,
            jax.ShapeDtypeStruct((rows, 128), jnp.float32),
        ],
        [SMEM] * 2 + [HBM],
        [pltpu.SemaphoreType.DMA((rows, 2))],
        (table, lengths, own_pages),
        1 << 20,
        bytes_only([windows]),
    )


def page_kernel(ids, pages_hbm, page, pages, sem):
    copy = pltpu.make_async_copy(pages_hbm.at[0], pages, sem)
    copy.start()
    copy.wait()
    lane = lanes_of(page.shape)
    keys = pltpu.roll(pages[0].astype(jnp.float32), HALF, 1)
    page[...] = jnp.where(lane < HALF, keys, pages[1].astype(jnp.float32)).astype(jnp.bfloat16)


def window_page(prompt_pages):
    shape = prompt_pages.shape[1:]
    return kernel_call(
        page_kernel,
        1,
        "window_page",
        jax.ShapeDtypeStruct(shape[1:], jnp.bfloat16),
        [HBM],
        [pltpu.VMEM(shape, jnp.bfloat16), pltpu.SemaphoreType.DMA],
        (prompt_pages,),
        cost=pl.CostEstimate(flops=0, bytes_accessed=16 << 20, transcendentals=0),
    )


def body(
    tokens,
    norm_gain,
    feature_w,
    query_key_w,
    value_w,
    out_w,
    conv_w,
    conv_state,
    lin_state,
    lin_norm,
    own_pages,
    prompt_pages,
    page_table,
    lengths,
):
    pages_first = prompt_pages.transpose(0, 1, 3, 2)
    value_w = value_w.transpose(0, 2, 1)
    stored = {
        "gain": norm_gain,
        "feature_w": feature_w,
        "state": lin_state.transpose(0, 2, 1, 3).reshape(-1, HD),
        "lin_norm": lin_norm,
        "conv_w": conv_w,
        "conv_state": conv_state,
        "value_w": value_w[0],
        "query_key_w": query_key_w,
    }

    page = window_page(pages_first)
    row_pages = [x_shift(page, k) for k in (1, 3, 2)]
    row_pages[0], last_tokens, stored = lax.optimization_barrier((row_pages[0], tokens, stored))
    received = [head_shift(last_tokens, 1), head_shift(tokens, 3), head_shift(tokens, 2)]
    near, received, row_pages = lax.optimization_barrier((bring_near(stored), received, row_pages))
    near_pages = jnp.stack([row_pages[0], page, row_pages[1], row_pages[2]])
    near_pages, received = lax.optimization_barrier((near_pages, received))
    far_pages = far_swap(near_pages)
    update = linear_layer([tokens] + received, near, out_w)
    own_pages = own_pages.transpose(0, 1, 3, 2)
    own_pages, table, ends, update = lax.optimization_barrier(
        (own_pages, page_table, lengths, update)
    )
    near["own_keys"], tags = bring_windows(table, ends, own_pages)
    swapped = [section_swap(update, k) for k in (2, 1, 3, 0)]
    one_share, packed, key_new, value_new = project(tags, swapped, near)
    asked = [packed] + [z_shift(packed, k) for k in (2, 1, 7)]
    own = own_attention(table, ends, tags, packed, key_new, value_new, near, own_pages)
    asked, own = lax.optimization_barrier((asked, own))
    answers = prompt_attention(asked, near_pages, far_pages)
    parts = [answers[0]] + [z_shift(answers[at], -k) for at, k in ((1, 2), (2, 1), (3, 7))]
    slabs = combine(own, parts, update, out_w)
    here = lax.axis_index("section") == 1
    total = jnp.where(here, one_share.astype(jnp.float32), 0.0) + slabs[0]
    for piece in [head_shift(slabs[k], k) for k in (2, 1, 3)]:
        total = total + piece
    return total.astype(jnp.bfloat16)[None]


def solution(mesh):
    placed = (
        P("req", "head"),
        P("section", None),
        P(None, "head"),
        P(None, "head"),
        P("section", None, "head"),
        P("section", "head", None),
        P(None, "head"),
        P("req", None, "head"),
        P("req", "head", None, None),
        P("req", "head", None),
        P("req", None, None, "head"),
        P("req", None, None, "head"),
        P("req", None),
        P("req"),
    )
    return jax.shard_map(
        body, mesh=mesh, in_specs=placed, out_specs=P("section", "req", "head"), check_vma=False
    )
```

```python
import jax
import jax.numpy as jnp
from jax import lax
from jax.experimental import pallas as pl
from jax.experimental.pallas import tpu as pltpu
from jax.sharding import PartitionSpec as P

HD = 112
FEAT = 16
WINDOW = 64
PAGE = 128
HALF = 64
MAXP = 256
GROUPS = 32
XN = 4
ZN = 8
LANES = 512
TAYLOR = 273
TAYLOR_LANES = 384
SPREAD = 1152

EPSILON = 1e-06
MASKED = -1e30


def head_shift(value, steps):
    count = lax.axis_size("head")
    return lax.ppermute(value, "head", [(i, (i + steps) % count) for i in range(count)])


def z_shift(value, steps):
    return lax.ppermute(
        value,
        "req",
        [(z * XN + i, (z + steps) % ZN * XN + i) for z in range(ZN) for i in range(XN)],
    )


def x_shift(value, steps):
    return lax.ppermute(
        value,
        "req",
        [(z * XN + i, z * XN + (i + steps) % XN) for z in range(ZN) for i in range(XN)],
    )


def far_swap(value):
    count = XN * ZN
    return lax.ppermute(
        value,
        ("section", "req"),
        [(count + i, count + (i + count // 2) % count) for i in range(count)],
    )


def section_swap(value, steps):
    count = lax.axis_size("head")
    there = [(i, count + (i + steps) % count) for i in range(count)]
    return lax.ppermute(value, ("section", "head"), there + [(b, a) for a, b in there])


VMEM = pl.BlockSpec(memory_space=pltpu.VMEM)
SMEM = pl.BlockSpec(memory_space=pltpu.SMEM)
HBM = pl.BlockSpec(memory_space=pltpu.HBM)
FLAT = (((1,), (1,)), ((), ()))


def normed_rows(values, gain_row):
    factor = lax.rsqrt(jnp.mean(values * values, axis=-1, keepdims=True) + EPSILON)
    return (values * factor * gain_row).astype(jnp.bfloat16)


def lanes_of(shape):
    return lax.broadcasted_iota(jnp.int32, shape, len(shape) - 1)


def in_head(lane, h):
    return (lane >= h * HD) & (lane < (h + 1) * HD)


def place():
    return lax.axis_index("section"), lax.axis_index("req"), lax.axis_index("head")


def kernel_call(
    kernel,
    section,
    name,
    out_shape,
    in_specs,
    scratch_shapes,
    args,
    vmem=6 << 20,
    cost=None,
    elsewhere=None,
):
    def run(*refs):
        ids = place()

        @pl.when(ids[0] == section)
        def _():
            kernel(ids, *refs)

        if elsewhere is not None:

            @pl.when(ids[0] != section)
            def _():
                elsewhere(ids, *refs)

    args = [
        pltpu.with_memory_space_constraint(arg, pltpu.HBM) if spec is HBM else arg
        for arg, spec in zip(args, in_specs, strict=True)
    ]
    return pl.pallas_call(
        run,
        out_shape=out_shape,
        in_specs=in_specs,
        out_specs=jax.tree.map(lambda _: VMEM, out_shape),
        scratch_shapes=scratch_shapes,
        compiler_params=pltpu.CompilerParams(vmem_limit_bytes=vmem),
        cost_estimate=cost,
        name=name,
    )(*args)


def expansion(features, width, repeat):
    lane = lax.broadcasted_iota(jnp.int32, (features, 2 * width), 1)
    source = lax.broadcasted_iota(jnp.int32, (features, 2 * width), 0)
    left = lane < width
    at = jnp.where(left, lane, lane - width) >> (repeat.bit_length() - 1)
    linear = left & (at > 0) & (at <= FEAT) & (source == at - 1)
    pair = at - (FEAT + 1)
    wanted = jnp.where(left, pair >> 4, pair & (FEAT - 1))
    quad = (pair >= 0) & (pair < FEAT * FEAT) & (source == wanted)
    return jnp.where(linear | quad, 1.0, 0.0).astype(jnp.bfloat16)


def taylor_rows(left, right, feature):
    scale = FEAT ** (-0.25)
    left, right = left * scale, right * scale
    return jnp.where(
        feature == 0, 1.0, jnp.where(feature <= FEAT, left, left * right * 0.5**0.5)
    )


def linear_kernel(
    ids,
    t0,
    t1,
    t2,
    t3,
    gain,
    feature_w,
    state,
    lin_norm,
    conv_w,
    conv_state,
    value_w,
    out_hbm,
    update,
    out_w,
    sem,
):
    rows, share = t0.shape
    heads = share // HD
    span = TAYLOR * heads
    copy = pltpu.make_async_copy(out_hbm.at[0], out_w, sem)
    copy.start()
    by_state = expansion(128, SPREAD, heads)
    by_norm = expansion(128, TAYLOR_LANES, 1)
    expand = jnp.concatenate([by_state, by_norm], axis=1)

    own = ids[2]
    got = [ref[...].astype(jnp.float32) for ref in (t0, t1, t3, t2)]
    whole = []
    for place in range(heads):
        piece = got[0]
        for back in range(1, heads):
            piece = jnp.where(((own - back) & (heads - 1)) == place, got[back], piece)
        whole.append(piece)
    tokens = jnp.concatenate(whole, axis=1)
    normed = normed_rows(tokens, gain[...])
    feats = jnp.dot(normed, feature_w[...], preferred_element_type=jnp.float32)
    by_head = jnp.concatenate(
        [feats] + [pltpu.roll(feats, 128 - 2 * FEAT * h, 1) for h in range(1, heads)], axis=0
    )
    high = by_head.astype(jnp.bfloat16)
    rest = by_head - high.astype(jnp.float32)
    middle = rest.astype(jnp.bfloat16)
    low = (rest - middle.astype(jnp.float32)).astype(jnp.bfloat16)
    spread = jnp.dot(
        jnp.concatenate([high, middle, low], axis=0), expand, preferred_element_type=jnp.float32
    )
    count = heads * rows
    spread = spread[:count] + spread[count : 2 * count] + spread[2 * count :]
    lane = lanes_of((count, SPREAD))
    head = lax.broadcasted_iota(jnp.int32, (count, SPREAD), 0) >> 3
    query_wide = taylor_rows(spread[:, :SPREAD], spread[:, SPREAD : 2 * SPREAD], lane >> 2)
    query_wide = jnp.where(((lane & (heads - 1)) == head) & (lane < span), query_wide, 0.0)
    query_feats = taylor_rows(
        spread[:, 2 * SPREAD : 2 * SPREAD + TAYLOR_LANES],
        spread[:, 2 * SPREAD + TAYLOR_LANES :],
        lanes_of((count, TAYLOR_LANES)),
    )[:, :TAYLOR]
    both = by_head * pltpu.roll(by_head, 128 - FEAT, 1)
    near = jnp.sum(
        jnp.where(lanes_of(both.shape) < FEAT, both, 0.0), axis=-1, keepdims=True
    ) * FEAT ** (-0.5)
    intersection = 1.0 + near + 0.5 * near * near

    length = span + 12
    queries = []
    for shift in range(0, 16, 4):
        moved = query_wide if shift == 0 else pltpu.roll(query_wide, shift, 1)
        queries.append(moved[:, :length].astype(jnp.bfloat16))
    row = lax.broadcasted_iota(jnp.int32, (count, HD), 0) & (rows - 1)
    found = jnp.zeros((count, HD), jnp.float32)
    for r in range(rows):
        first = span * r
        shift = first % 16
        product = jnp.dot(
            queries[shift // 4],
            state[first - shift : first - shift + length, :],
            preferred_element_type=jnp.float32,
        )
        found = jnp.where(row == r, product, found)
    fresh = lax.dot_general(normed, value_w[...], FLAT, preferred_element_type=jnp.float32)
    older = conv_state[...].astype(jnp.float32)
    mixed = conv_w[0:1] * older[:, 0] + conv_w[1:2] * older[:, 1] + conv_w[2:3] * fresh
    total = tokens * 0.25
    copy.wait()
    for h in range(heads):
        here = slice(h * rows, (h + 1) * rows)
        denominator = (
            jnp.sum(query_feats[here] * lin_norm[:, h, :], axis=-1, keepdims=True)
            + intersection[here]
        )
        attended = (
            (found[here] + intersection[here] * mixed[:, h * HD : (h + 1) * HD]) / denominator
        ).astype(jnp.bfloat16)
        total = total + jnp.dot(
            attended, out_w[h * HD : (h + 1) * HD, :], preferred_element_type=jnp.float32
        )
    update[...] = total.astype(jnp.bfloat16)


def linear_layer(pieces, near, out_w):
    return kernel_call(
        linear_kernel,
        0,
        "linear_layer",
        jax.ShapeDtypeStruct((pieces[0].shape[0], out_w.shape[2]), jnp.bfloat16),
        [VMEM] * 11 + [HBM],
        [pltpu.VMEM(out_w.shape[1:], jnp.bfloat16), pltpu.SemaphoreType.DMA],
        (*pieces, *(near[name] for name in LINEAR_NEAR), out_w),
    )


def project_kernel(
    ids,
    tags,
    p0,
    p1,
    p2,
    p3,
    gain,
    qk_w,
    v_w,
    one,
    asked,
    key_new,
    value_new,
):
    rows, share = one.shape
    heads = share // HD
    layer_one = sum(ref[...].astype(jnp.float32) for ref in (p0, p1, p2, p3)).astype(jnp.bfloat16)
    rounded = layer_one.astype(jnp.float32)
    mine = rounded[:, :share]
    for h in range(1, heads):
        mine = jnp.where(ids[2] == h, rounded[:, h * share : (h + 1) * share], mine)
    one[...] = mine.astype(jnp.bfloat16)
    normed = normed_rows(rounded, gain[...])
    query_key = jnp.dot(normed, qk_w[...], preferred_element_type=jnp.float32)
    width = query_key.shape[1]
    lane = lanes_of((rows, LANES))
    query = jnp.where(in_head(lane, 0), query_key[:, :LANES], 0.0)
    key = query
    for h in range(heads):
        if h:
            moved = pltpu.roll(query_key, width - h * HD, 1)[:, :LANES]
            query = jnp.where(in_head(lane, h), moved, query)
        moved = pltpu.roll(query_key, width - (h + 1) * HD, 1)[:, :LANES]
        key = jnp.where(in_head(lane, h), moved, key)
    query = jnp.where(lane == share, tags[:, 0:1], query)
    query = jnp.where(lane == share + 1, tags[:, 1:2], query)
    asked[...] = query.astype(jnp.bfloat16)
    key_new[...] = key[:, :share].astype(jnp.bfloat16)
    value_new[...] = lax.dot_general(
        normed, v_w[...], FLAT, preferred_element_type=jnp.float32
    ).astype(jnp.bfloat16)


def project(tags, pieces, near):
    rows = pieces[0].shape[0]
    share = near["value_w"].shape[0]
    return kernel_call(
        project_kernel,
        1,
        "project",
        [
            jax.ShapeDtypeStruct((rows, share), jnp.bfloat16),
            jax.ShapeDtypeStruct((rows, LANES), jnp.bfloat16),
            jax.ShapeDtypeStruct((rows, share), jnp.bfloat16),
            jax.ShapeDtypeStruct((rows, share), jnp.bfloat16),
        ],
        [VMEM] * 8,
        [],
        (tags, *pieces, near["gain"], near["query_key_w"], near["value_w"]),
    )


def window_pages(lengths, r):
    length = lengths[r]
    return jnp.maximum((length - WINDOW) // PAGE, 1), jnp.maximum((length - 2) // PAGE, 1)


def own_kernel(
    ids, tags, asked, key_new, value_new, pages, summed_out, highest_out, total_out
):
    rows, share = key_new.shape
    head = lax.broadcasted_iota(jnp.int32, (8, share), 0)
    lane = lanes_of((8, share))
    mine = (lane >= head * HD) & (lane < (head + 1) * HD)
    scale = HD ** (-0.5)
    query = asked[:, :share].astype(jnp.float32)
    new_key = key_new[...].astype(jnp.float32)
    new_value = value_new[...].astype(jnp.float32)
    wide = jnp.concatenate([jnp.where(mine, query[r : r + 1], 0.0) for r in range(rows)], axis=0)
    keys = jnp.concatenate(
        [jnp.broadcast_to(new_key[r : r + 1], (8, share)) for r in range(rows)], axis=0
    )
    new_score = jnp.sum(wide * keys, axis=-1, keepdims=True) * scale
    token = lanes_of((8 * rows, 2 * PAGE))

    def by_request(at):
        return jnp.concatenate(
            [jnp.broadcast_to(tags[r : r + 1, at : at + 1], (8, 2 * PAGE)) for r in range(rows)],
            axis=0,
        )

    length = by_request(2)
    position = token.astype(jnp.float32) + jnp.where(token < PAGE, by_request(3), by_request(4))
    usable = (position >= length - WINDOW) & (position <= length - 2)
    scores = []
    for r in range(rows):
        low = wide[8 * r : 8 * r + 8].astype(jnp.bfloat16)
        scores.append(
            jnp.concatenate(
                [
                    jnp.dot(low, pages[r, slot, 0], preferred_element_type=jnp.float32)
                    for slot in range(2)
                ],
                axis=1,
            )
        )
    scores = jnp.where(usable, jnp.concatenate(scores, axis=0) * scale, MASKED)
    highest = jnp.maximum(jnp.max(scores, axis=-1, keepdims=True), new_score)
    exps = jnp.where(usable, jnp.exp(scores - highest), 0.0)
    exp_new = jnp.exp(new_score - highest)
    total = jnp.sum(exps, axis=-1, keepdims=True) + exp_new
    for r in range(rows):
        here = slice(8 * r, 8 * r + 8)
        low = exps[here].astype(jnp.bfloat16)
        found = exp_new[here] * new_value[r : r + 1]
        for slot in range(2):
            found = found + lax.dot_general(
                low[:, slot * PAGE : (slot + 1) * PAGE],
                pages[r, slot, 1],
                FLAT,
                preferred_element_type=jnp.float32,
            )
        for ref, value in (
            (summed_out, found),
            (highest_out, highest[here]),
            (total_out, total[here]),
        ):
            ref[r : r + 1, :] = jnp.sum(jnp.where(mine, value, 0.0), axis=0, keepdims=True)


def own_attention(tags, asked, key_new, value_new, near):
    rows, share = key_new.shape
    return kernel_call(
        own_kernel,
        1,
        "own_attention",
        [jax.ShapeDtypeStruct((rows, share), jnp.float32)] * 3,
        [VMEM] * 5,
        [],
        (tags, asked, key_new, value_new, near["own_pages"]),
    )


def prompt_kernel(ids, a0, a1, a2, a3, near_pages, far_pages, o0, o1, o2, o3):
    rows = a0.shape[0]
    share = near_pages.shape[1]
    heads = share // HD
    pages = jnp.concatenate(
        [near_pages[i] for i in range(XN)] + [far_pages[i] for i in range(XN)], axis=1
    )
    asked = jnp.concatenate([ref[...].astype(jnp.float32) for ref in (a0, a1, a2, a3)], axis=0)
    count = asked.shape[0]
    lane = lanes_of(asked.shape)
    group = jnp.sum(jnp.where(lane == share, asked, 0.0), axis=-1, keepdims=True)
    start = jnp.sum(jnp.where(lane == share + 1, asked, 0.0), axis=-1, keepdims=True)
    group, start = group.astype(jnp.int32), start.astype(jnp.int32)
    query = jnp.concatenate(
        [jnp.where(in_head(lane, h), asked, 0.0)[:, :share] for h in range(heads)], axis=0
    ).astype(jnp.bfloat16)
    scores = jnp.dot(query, pages, preferred_element_type=jnp.float32) * HD ** (-0.5)
    token = lanes_of((count, 2 * XN * PAGE))
    z, x = ids[1] // XN, ids[1] % XN
    slot = token >> 7
    slot_group = jnp.where(slot < XN, z, (z + ZN // 2) & (ZN - 1)) * XN
    slot_group = slot_group + ((slot + x + XN - 1) & (XN - 1))
    offset = token & (PAGE - 1)
    usable = (slot_group == group) & (offset < HALF) & (offset + HALF >= start)
    lane = lanes_of((count, share))
    stat_lane = lanes_of((count, 128))
    weights = []
    stats = jnp.zeros((count, 128), jnp.float32)
    for h in range(heads):
        here = jnp.where(usable, scores[h * count : (h + 1) * count], MASKED)
        highest = jnp.max(here, axis=-1, keepdims=True)
        exps = jnp.where(usable, jnp.exp(here - highest), 0.0)
        total = jnp.sum(exps, axis=-1, keepdims=True)
        stats = jnp.where(stat_lane == h, highest, stats)
        stats = jnp.where(stat_lane == heads + h, total, stats)
        weights.append(pltpu.roll(exps, HALF, 1))
    found = lax.dot_general(
        jnp.concatenate(weights, axis=0).astype(jnp.bfloat16),
        pages,
        FLAT,
        preferred_element_type=jnp.float32,
    )
    summed = jnp.zeros((count, share), jnp.float32)
    for h in range(heads):
        summed = jnp.where(in_head(lane, h), found[h * count : (h + 1) * count], summed)
    for at, ref in enumerate((o0, o1, o2, o3)):
        ref[:, :share] = summed[at * rows : (at + 1) * rows]
        ref[:, share:LANES] = jnp.zeros((rows, LANES - share), jnp.float32)
        ref[:, LANES:] = stats[at * rows : (at + 1) * rows]


def prompt_attention(asked, near_pages, far_pages):
    rows = asked[0].shape[0]
    return kernel_call(
        prompt_kernel,
        1,
        "prompt_attention",
        [jax.ShapeDtypeStruct((rows, LANES + 128), jnp.float32)] * 4,
        [VMEM] * 6,
        [],
        (*asked, near_pages, far_pages),
    )


def combine_kernel(ids, summed, highest, total, r0, r1, r2, r3, update, out_w, s0, s1, s2, s3):
    rows, share = summed.shape
    heads = share // HD
    refs = (r0, r1, r2, r3)
    prompt_summed = sum(ref[:, :share] for ref in refs)
    stats = [ref[:, LANES:] for ref in refs]
    top = jnp.maximum(jnp.maximum(stats[0], stats[1]), jnp.maximum(stats[2], stats[3]))
    added = stats[0] + stats[1] + stats[2] + stats[3]
    lane = lanes_of((rows, share))
    prompt_highest = jnp.zeros((rows, share), jnp.float32)
    prompt_total = jnp.zeros((rows, share), jnp.float32)
    for h in range(heads):
        here = in_head(lane, h)
        prompt_highest = jnp.where(here, top[:, h : h + 1], prompt_highest)
        prompt_total = jnp.where(here, added[:, heads + h : heads + h + 1], prompt_total)
    peak = jnp.maximum(highest[...], prompt_highest)
    own_factor = jnp.exp(highest[...] - peak)
    prompt_factor = jnp.exp(prompt_highest - peak)
    whole = total[...] * own_factor + prompt_total * prompt_factor
    attended = (summed[...] * own_factor + prompt_summed * prompt_factor) / whole
    second = jnp.dot(attended.astype(jnp.bfloat16), out_w[0], preferred_element_type=jnp.float32)
    write_slabs(ids, second, (s0, s1, s2, s3))


def write_slabs(ids, rows_whole, refs):
    heads = len(refs)
    share = refs[0].shape[1]
    for steps, ref in enumerate(refs):
        slab = rows_whole[:, :share]
        for h in range(1, heads):
            there = rows_whole[:, h * share : (h + 1) * share]
            slab = jnp.where(((ids[2] + steps) & (heads - 1)) == h, there, slab)
        ref[...] = slab.astype(jnp.bfloat16)


def own_slabs(ids, *refs):
    write_slabs(ids, refs[7][...].astype(jnp.float32), refs[9:])


def combine(own, parts, update, out_w):
    return kernel_call(
        combine_kernel,
        1,
        "combine",
        [jax.ShapeDtypeStruct(own[0].shape, jnp.bfloat16)] * 4,
        [VMEM] * 9,
        [],
        (*own, *parts, update, out_w),
        elsewhere=own_slabs,
    )


LINEAR_NEAR = (
    "gain",
    "feature_w",
    "state",
    "lin_norm",
    "conv_w",
    "conv_state",
    "value_w",
)
WINDOW_NEAR = ("gain", "value_w", "query_key_w")


def bring_near(arrays):
    names = list(arrays)
    count = len(names)
    first = [at for at, name in enumerate(names) if name in LINEAR_NEAR]
    second = [at for at, name in enumerate(names) if name in WINDOW_NEAR]

    def copy_some(chosen, refs):
        sems = refs[-1]
        copies = [
            pltpu.make_async_copy(refs[at], refs[count + at], sems.at[at]) for at in chosen
        ]
        for copy in copies:
            copy.start()
        for copy in copies:
            copy.wait()

    near = kernel_call(
        lambda ids, *refs: copy_some(first, refs),
        0,
        "bring_near",
        [jax.ShapeDtypeStruct(array.shape, array.dtype) for array in arrays.values()],
        [HBM] * count,
        [pltpu.SemaphoreType.DMA((count,))],
        tuple(arrays.values()),
        4 << 20,
        bytes_only(arrays.values()),
        lambda ids, *refs: copy_some(second, refs),
    )
    return dict(zip(names, near))


def bytes_only(arrays):
    moved = sum(array.size * array.dtype.itemsize for array in arrays)
    return pl.CostEstimate(flops=0, bytes_accessed=2 * moved, transcendentals=0)


def window_kernel(
    ids, table, lengths, own_hbm, own_near, tags, sems
):
    rows = tags.shape[0]
    total = own_hbm.shape[0]
    copies = []
    for r in range(rows):
        for slot, logical in enumerate(window_pages(lengths, r)):
            page = jnp.clip(table[r, logical] - GROUPS - ids[1] * total, 0, total - 1)
            copies.append(
                pltpu.make_async_copy(own_hbm.at[page], own_near.at[r, slot], sems.at[r, slot])
            )
    for copy in copies:
        copy.start()
    row = lax.broadcasted_iota(jnp.int32, tags.shape, 0)
    lane = lanes_of(tags.shape)
    marks = jnp.zeros(tags.shape, jnp.int32)
    for r in range(rows):
        length = lengths[r]
        first, last = window_pages(lengths, r)
        second = jnp.where(first != last, last - 1, -MAXP) * PAGE
        start = jnp.minimum(length - WINDOW, PAGE)
        for at, mark in enumerate((table[r, 0], start, length, first * PAGE, second)):
            marks = jnp.where((row == r) & (lane == at), mark, marks)
    tags[...] = marks.astype(jnp.float32)
    for copy in copies:
        copy.wait()


def bring_windows(table, lengths, own_pages):
    rows = lengths.shape[0]
    windows = jax.ShapeDtypeStruct((rows, 2) + own_pages.shape[1:], own_pages.dtype)
    return kernel_call(
        window_kernel,
        1,
        "bring_windows",
        [
            windows,
            jax.ShapeDtypeStruct((rows, 128), jnp.float32),
        ],
        [SMEM] * 2 + [HBM],
        [pltpu.SemaphoreType.DMA((rows, 2))],
        (table, lengths, own_pages),
        1 << 20,
        bytes_only([windows]),
    )


def page_kernel(ids, pages_hbm, page, pages, sem):
    copy = pltpu.make_async_copy(pages_hbm.at[0], pages, sem)
    copy.start()
    copy.wait()
    lane = lanes_of(page.shape)
    keys = pltpu.roll(pages[0].astype(jnp.float32), HALF, 1)
    page[...] = jnp.where(lane < HALF, keys, pages[1].astype(jnp.float32)).astype(jnp.bfloat16)


def window_page(prompt_pages):
    shape = prompt_pages.shape[1:]
    return kernel_call(
        page_kernel,
        1,
        "window_page",
        jax.ShapeDtypeStruct(shape[1:], jnp.bfloat16),
        [HBM],
        [pltpu.VMEM(shape, jnp.bfloat16), pltpu.SemaphoreType.DMA],
        (prompt_pages,),
        cost=pl.CostEstimate(flops=0, bytes_accessed=16 << 20, transcendentals=0),
    )


def body(
    tokens,
    norm_gain,
    feature_w,
    query_key_w,
    value_w,
    out_w,
    conv_w,
    conv_state,
    lin_state,
    lin_norm,
    own_pages,
    prompt_pages,
    page_table,
    lengths,
):
    pages_first = prompt_pages.transpose(0, 1, 3, 2)
    value_w = value_w.transpose(0, 2, 1)
    stored = {
        "gain": norm_gain,
        "feature_w": feature_w,
        "state": lin_state.transpose(0, 2, 1, 3).reshape(-1, HD),
        "lin_norm": lin_norm,
        "conv_w": conv_w,
        "conv_state": conv_state,
        "value_w": value_w[0],
        "query_key_w": query_key_w,
    }

    page = window_page(pages_first)
    row_pages = [x_shift(page, k) for k in (1, 3, 2)]
    row_pages[0], last_tokens, stored = lax.optimization_barrier((row_pages[0], tokens, stored))
    received = [head_shift(last_tokens, 1), head_shift(tokens, 3), head_shift(tokens, 2)]
    near, received, row_pages = lax.optimization_barrier((bring_near(stored), received, row_pages))
    near_pages = jnp.stack([row_pages[0], page, row_pages[1], row_pages[2]])
    near_pages, received = lax.optimization_barrier((near_pages, received))
    far_pages = far_swap(near_pages)
    update = linear_layer([tokens] + received, near, out_w)
    own_pages = own_pages.transpose(0, 1, 3, 2)
    own_pages, table, ends, update = lax.optimization_barrier(
        (own_pages, page_table, lengths, update)
    )
    near["own_pages"], tags = bring_windows(table, ends, own_pages)
    swapped = [section_swap(update, k) for k in (2, 1, 3, 0)]
    one_share, packed, key_new, value_new = project(tags, swapped, near)
    asked = [packed] + [z_shift(packed, k) for k in (2, 1, 7)]
    own = own_attention(tags, packed, key_new, value_new, near)
    asked, own = lax.optimization_barrier((asked, own))
    answers = prompt_attention(asked, near_pages, far_pages)
    parts = [answers[0]] + [z_shift(answers[at], -k) for at, k in ((1, 2), (2, 1), (3, 7))]
    slabs = combine(own, parts, update, out_w)
    here = lax.axis_index("section") == 1
    total = jnp.where(here, one_share.astype(jnp.float32), 0.0) + slabs[0].astype(jnp.float32)
    for piece in [head_shift(slabs[k], k) for k in (2, 1, 3)]:
        total = total + piece.astype(jnp.float32)
    return total.astype(jnp.bfloat16)[None]


def solution(mesh):
    placed = (
        P("req", "head"),
        P("section", None),
        P(None, "head"),
        P(None, "head"),
        P("section", None, "head"),
        P("section", "head", None),
        P(None, "head"),
        P("req", None, "head"),
        P("req", "head", None, None),
        P("req", "head", None),
        P("req", None, None, "head"),
        P("req", None, None, "head"),
        P("req", None),
        P("req"),
    )
    return jax.shard_map(
        body, mesh=mesh, in_specs=placed, out_specs=P("section", "req", "head"), check_vma=False
    )
```

```python
import jax
import jax.numpy as jnp
from jax import lax
from jax.experimental import pallas as pl
from jax.experimental.pallas import tpu as pltpu
from jax.sharding import PartitionSpec as P

HD = 112
FEAT = 16
WINDOW = 64
PAGE = 128
HALF = 64
MAXP = 256
GROUPS = 32
XN = 4
ZN = 8
LANES = 512
TAYLOR = 273
TAYLOR_LANES = 384
SPREAD = 1152

EPSILON = 1e-06
MASKED = -1e30


def head_shift(value, steps):
    count = lax.axis_size("head")
    return lax.ppermute(value, "head", [(i, (i + steps) % count) for i in range(count)])


def z_shift(value, steps):
    return lax.ppermute(
        value,
        "req",
        [(z * XN + i, (z + steps) % ZN * XN + i) for z in range(ZN) for i in range(XN)],
    )


def x_shift(value, steps):
    return lax.ppermute(
        value,
        "req",
        [(z * XN + i, z * XN + (i + steps) % XN) for z in range(ZN) for i in range(XN)],
    )


def far_swap(value):
    count = XN * ZN
    return lax.ppermute(
        value,
        ("section", "req"),
        [(count + i, count + (i + count // 2) % count) for i in range(count)],
    )


def section_swap(value, steps):
    count = lax.axis_size("head")
    there = [(i, count + (i + steps) % count) for i in range(count)]
    return lax.ppermute(value, ("section", "head"), there + [(b, a) for a, b in there])


VMEM = pl.BlockSpec(memory_space=pltpu.VMEM)
SMEM = pl.BlockSpec(memory_space=pltpu.SMEM)
HBM = pl.BlockSpec(memory_space=pltpu.HBM)
FLAT = (((1,), (1,)), ((), ()))


def normed_rows(values, gain_row):
    factor = lax.rsqrt(jnp.mean(values * values, axis=-1, keepdims=True) + EPSILON)
    return (values * factor * gain_row).astype(jnp.bfloat16)


def lanes_of(shape):
    return lax.broadcasted_iota(jnp.int32, shape, len(shape) - 1)


def in_head(lane, h):
    return (lane >= h * HD) & (lane < (h + 1) * HD)


def place():
    return lax.axis_index("section"), lax.axis_index("req"), lax.axis_index("head")


def kernel_call(
    kernel,
    section,
    name,
    out_shape,
    in_specs,
    scratch_shapes,
    args,
    vmem=6 << 20,
    cost=None,
    elsewhere=None,
):
    def run(*refs):
        ids = place()

        @pl.when(ids[0] == section)
        def _():
            kernel(ids, *refs)

        if elsewhere is not None:

            @pl.when(ids[0] != section)
            def _():
                elsewhere(ids, *refs)

    args = [
        pltpu.with_memory_space_constraint(arg, pltpu.HBM) if spec is HBM else arg
        for arg, spec in zip(args, in_specs, strict=True)
    ]
    return pl.pallas_call(
        run,
        out_shape=out_shape,
        in_specs=in_specs,
        out_specs=jax.tree.map(lambda _: VMEM, out_shape),
        scratch_shapes=scratch_shapes,
        compiler_params=pltpu.CompilerParams(vmem_limit_bytes=vmem),
        cost_estimate=cost,
        name=name,
    )(*args)


def expansion(features, width, repeat):
    lane = lax.broadcasted_iota(jnp.int32, (features, 2 * width), 1)
    source = lax.broadcasted_iota(jnp.int32, (features, 2 * width), 0)
    left = lane < width
    at = jnp.where(left, lane, lane - width) >> (repeat.bit_length() - 1)
    linear = left & (at > 0) & (at <= FEAT) & (source == at - 1)
    pair = at - (FEAT + 1)
    wanted = jnp.where(left, pair >> 4, pair & (FEAT - 1))
    quad = (pair >= 0) & (pair < FEAT * FEAT) & (source == wanted)
    return jnp.where(linear | quad, 1.0, 0.0).astype(jnp.bfloat16)


def taylor_rows(left, right, feature):
    scale = FEAT ** (-0.25)
    left, right = left * scale, right * scale
    return jnp.where(
        feature == 0, 1.0, jnp.where(feature <= FEAT, left, left * right * 0.5**0.5)
    )


def linear_kernel(
    ids,
    t0,
    t1,
    t2,
    t3,
    gain,
    feature_w,
    state,
    lin_norm,
    conv_w,
    conv_state,
    value_w,
    out_hbm,
    update,
    out_w,
    sem,
):
    rows, share = t0.shape
    heads = share // HD
    span = TAYLOR * heads
    copy = pltpu.make_async_copy(out_hbm.at[0], out_w, sem)
    copy.start()
    by_state = expansion(128, SPREAD, heads)
    by_norm = expansion(128, TAYLOR_LANES, 1)
    expand = jnp.concatenate([by_state, by_norm], axis=1)

    own = ids[2]
    got = [ref[...].astype(jnp.float32) for ref in (t0, t1, t3, t2)]
    whole = []
    for place in range(heads):
        piece = got[0]
        for back in range(1, heads):
            piece = jnp.where(((own - back) & (heads - 1)) == place, got[back], piece)
        whole.append(piece)
    tokens = jnp.concatenate(whole, axis=1)
    normed = normed_rows(tokens, gain[...])
    feats = jnp.dot(normed, feature_w[...], preferred_element_type=jnp.float32)
    by_head = jnp.concatenate(
        [feats] + [pltpu.roll(feats, 128 - 2 * FEAT * h, 1) for h in range(1, heads)], axis=0
    )
    high = by_head.astype(jnp.bfloat16)
    rest = by_head - high.astype(jnp.float32)
    middle = rest.astype(jnp.bfloat16)
    low = (rest - middle.astype(jnp.float32)).astype(jnp.bfloat16)
    spread = jnp.dot(
        jnp.concatenate([high, middle, low], axis=0), expand, preferred_element_type=jnp.float32
    )
    count = heads * rows
    spread = spread[:count] + spread[count : 2 * count] + spread[2 * count :]
    lane = lanes_of((count, SPREAD))
    head = lax.broadcasted_iota(jnp.int32, (count, SPREAD), 0) >> 3
    query_wide = taylor_rows(spread[:, :SPREAD], spread[:, SPREAD : 2 * SPREAD], lane >> 2)
    query_wide = jnp.where(((lane & (heads - 1)) == head) & (lane < span), query_wide, 0.0)
    query_feats = taylor_rows(
        spread[:, 2 * SPREAD : 2 * SPREAD + TAYLOR_LANES],
        spread[:, 2 * SPREAD + TAYLOR_LANES :],
        lanes_of((count, TAYLOR_LANES)),
    )[:, :TAYLOR]
    both = by_head * pltpu.roll(by_head, 128 - FEAT, 1)
    near = jnp.sum(
        jnp.where(lanes_of(both.shape) < FEAT, both, 0.0), axis=-1, keepdims=True
    ) * FEAT ** (-0.5)
    intersection = 1.0 + near + 0.5 * near * near

    length = span + 12
    queries = []
    for shift in range(0, 16, 4):
        moved = query_wide if shift == 0 else pltpu.roll(query_wide, shift, 1)
        queries.append(moved[:, :length].astype(jnp.bfloat16))
    row = lax.broadcasted_iota(jnp.int32, (count, HD), 0) & (rows - 1)
    found = jnp.zeros((count, HD), jnp.float32)
    for r in range(rows):
        first = span * r
        shift = first % 16
        product = jnp.dot(
            queries[shift // 4],
            state[first - shift : first - shift + length, :],
            preferred_element_type=jnp.float32,
        )
        found = jnp.where(row == r, product, found)
    fresh = lax.dot_general(normed, value_w[...], FLAT, preferred_element_type=jnp.float32)
    older = conv_state[...].astype(jnp.float32)
    mixed = conv_w[0:1] * older[:, 0] + conv_w[1:2] * older[:, 1] + conv_w[2:3] * fresh
    total = tokens * 0.25
    copy.wait()
    for h in range(heads):
        here = slice(h * rows, (h + 1) * rows)
        denominator = (
            jnp.sum(query_feats[here] * lin_norm[:, h, :], axis=-1, keepdims=True)
            + intersection[here]
        )
        attended = (
            (found[here] + intersection[here] * mixed[:, h * HD : (h + 1) * HD]) / denominator
        ).astype(jnp.bfloat16)
        total = total + jnp.dot(
            attended, out_w[h * HD : (h + 1) * HD, :], preferred_element_type=jnp.float32
        )
    update[...] = total.astype(jnp.bfloat16)


def linear_layer(pieces, near, out_w):
    return kernel_call(
        linear_kernel,
        0,
        "linear_layer",
        jax.ShapeDtypeStruct((pieces[0].shape[0], out_w.shape[2]), jnp.bfloat16),
        [VMEM] * 11 + [HBM],
        [pltpu.VMEM(out_w.shape[1:], jnp.bfloat16), pltpu.SemaphoreType.DMA],
        (*pieces, *(near[name] for name in LINEAR_NEAR), out_w),
    )


def project_kernel(
    ids,
    tags,
    p0,
    p1,
    p2,
    p3,
    gain,
    qk_w,
    v_w,
    one,
    asked,
    key_new,
    value_new,
):
    rows, share = one.shape
    heads = share // HD
    layer_one = sum(ref[...].astype(jnp.float32) for ref in (p0, p1, p2, p3)).astype(jnp.bfloat16)
    rounded = layer_one.astype(jnp.float32)
    mine = rounded[:, :share]
    for h in range(1, heads):
        mine = jnp.where(ids[2] == h, rounded[:, h * share : (h + 1) * share], mine)
    one[...] = mine.astype(jnp.bfloat16)
    normed = normed_rows(rounded, gain[...])
    query_key = jnp.dot(normed, qk_w[...], preferred_element_type=jnp.float32)
    width = query_key.shape[1]
    lane = lanes_of((rows, LANES))
    query = jnp.where(in_head(lane, 0), query_key[:, :LANES], 0.0)
    key = query
    for h in range(heads):
        if h:
            moved = pltpu.roll(query_key, width - h * HD, 1)[:, :LANES]
            query = jnp.where(in_head(lane, h), moved, query)
        moved = pltpu.roll(query_key, width - (h + 1) * HD, 1)[:, :LANES]
        key = jnp.where(in_head(lane, h), moved, key)
    query = jnp.where(lane == share, tags[:, 0:1], query)
    query = jnp.where(lane == share + 1, tags[:, 1:2], query)
    asked[...] = query.astype(jnp.bfloat16)
    key_new[...] = key[:, :share].astype(jnp.bfloat16)
    value_new[...] = lax.dot_general(
        normed, v_w[...], FLAT, preferred_element_type=jnp.float32
    ).astype(jnp.bfloat16)


def project(tags, pieces, near):
    rows = pieces[0].shape[0]
    share = near["value_w"].shape[0]
    return kernel_call(
        project_kernel,
        1,
        "project",
        [
            jax.ShapeDtypeStruct((rows, share), jnp.bfloat16),
            jax.ShapeDtypeStruct((rows, LANES), jnp.bfloat16),
            jax.ShapeDtypeStruct((rows, share), jnp.bfloat16),
            jax.ShapeDtypeStruct((rows, share), jnp.bfloat16),
        ],
        [VMEM] * 8,
        [],
        (tags, *pieces, near["gain"], near["query_key_w"], near["value_w"]),
    )


def window_pages(lengths, r):
    length = lengths[r]
    return jnp.maximum((length - WINDOW) // PAGE, 1), jnp.maximum((length - 2) // PAGE, 1)


def own_kernel(
    ids, tags, asked, key_new, value_new, pages, summed_out, highest_out, total_out
):
    rows, share = key_new.shape
    head = lax.broadcasted_iota(jnp.int32, (8, share), 0)
    lane = lanes_of((8, share))
    mine = (lane >= head * HD) & (lane < (head + 1) * HD)
    scale = HD ** (-0.5)
    query = asked[:, :share].astype(jnp.float32)
    new_key = key_new[...].astype(jnp.float32)
    new_value = value_new[...].astype(jnp.float32)
    wide = jnp.concatenate([jnp.where(mine, query[r : r + 1], 0.0) for r in range(rows)], axis=0)
    keys = jnp.concatenate(
        [jnp.broadcast_to(new_key[r : r + 1], (8, share)) for r in range(rows)], axis=0
    )
    new_score = jnp.sum(wide * keys, axis=-1, keepdims=True) * scale
    token = lanes_of((8 * rows, 2 * PAGE))

    def by_request(at):
        return jnp.concatenate(
            [jnp.broadcast_to(tags[r : r + 1, at : at + 1], (8, 2 * PAGE)) for r in range(rows)],
            axis=0,
        )

    length = by_request(2)
    position = token.astype(jnp.float32) + jnp.where(token < PAGE, by_request(3), by_request(4))
    usable = (position >= length - WINDOW) & (position <= length - 2)
    scores = []
    for r in range(rows):
        low = wide[8 * r : 8 * r + 8].astype(jnp.bfloat16)
        scores.append(
            jnp.concatenate(
                [
                    jnp.dot(low, pages[r, slot, 0], preferred_element_type=jnp.float32)
                    for slot in range(2)
                ],
                axis=1,
            )
        )
    scores = jnp.where(usable, jnp.concatenate(scores, axis=0) * scale, MASKED)
    highest = jnp.maximum(jnp.max(scores, axis=-1, keepdims=True), new_score)
    exps = jnp.where(usable, jnp.exp(scores - highest), 0.0)
    exp_new = jnp.exp(new_score - highest)
    total = jnp.sum(exps, axis=-1, keepdims=True) + exp_new
    for r in range(rows):
        here = slice(8 * r, 8 * r + 8)
        low = exps[here].astype(jnp.bfloat16)
        found = exp_new[here] * new_value[r : r + 1]
        for slot in range(2):
            found = found + lax.dot_general(
                low[:, slot * PAGE : (slot + 1) * PAGE],
                pages[r, slot, 1],
                FLAT,
                preferred_element_type=jnp.float32,
            )
        for ref, value in (
            (summed_out, found),
            (highest_out, highest[here]),
            (total_out, total[here]),
        ):
            ref[r : r + 1, :] = jnp.sum(jnp.where(mine, value, 0.0), axis=0, keepdims=True)


def own_attention(tags, asked, key_new, value_new, near):
    rows, share = key_new.shape
    return kernel_call(
        own_kernel,
        1,
        "own_attention",
        [jax.ShapeDtypeStruct((rows, share), jnp.float32)] * 3,
        [VMEM] * 5,
        [],
        (tags, asked, key_new, value_new, near["own_pages"]),
    )


def prompt_kernel(ids, a0, a1, a2, a3, near_pages, far_pages, o0, o1, o2, o3):
    rows = a0.shape[0]
    share = near_pages.shape[1]
    heads = share // HD
    pages = jnp.concatenate(
        [near_pages[i] for i in range(XN)] + [far_pages[i] for i in range(XN)], axis=1
    )
    asked = jnp.concatenate([ref[...].astype(jnp.float32) for ref in (a0, a1, a2, a3)], axis=0)
    count = asked.shape[0]
    lane = lanes_of(asked.shape)
    group = jnp.sum(jnp.where(lane == share, asked, 0.0), axis=-1, keepdims=True)
    start = jnp.sum(jnp.where(lane == share + 1, asked, 0.0), axis=-1, keepdims=True)
    group, start = group.astype(jnp.int32), start.astype(jnp.int32)
    query = jnp.concatenate(
        [jnp.where(in_head(lane, h), asked, 0.0)[:, :share] for h in range(heads)], axis=0
    ).astype(jnp.bfloat16)
    scores = jnp.dot(query, pages, preferred_element_type=jnp.float32) * HD ** (-0.5)
    token = lanes_of((count, 2 * XN * PAGE))
    z, x = ids[1] // XN, ids[1] % XN
    slot = token >> 7
    slot_group = jnp.where(slot < XN, z, (z + ZN // 2) & (ZN - 1)) * XN
    slot_group = slot_group + ((slot + x + XN - 1) & (XN - 1))
    offset = token & (PAGE - 1)
    usable = (slot_group == group) & (offset < HALF) & (offset + HALF >= start)
    lane = lanes_of((count, share))
    stat_lane = lanes_of((count, 128))
    weights = []
    stats = jnp.zeros((count, 128), jnp.float32)
    for h in range(heads):
        here = jnp.where(usable, scores[h * count : (h + 1) * count], MASKED)
        highest = jnp.max(here, axis=-1, keepdims=True)
        exps = jnp.where(usable, jnp.exp(here - highest), 0.0)
        total = jnp.sum(exps, axis=-1, keepdims=True)
        stats = jnp.where(stat_lane == h, highest, stats)
        stats = jnp.where(stat_lane == heads + h, total, stats)
        weights.append(pltpu.roll(exps, HALF, 1))
    found = lax.dot_general(
        jnp.concatenate(weights, axis=0).astype(jnp.bfloat16),
        pages,
        FLAT,
        preferred_element_type=jnp.float32,
    )
    summed = jnp.zeros((count, share), jnp.float32)
    for h in range(heads):
        summed = jnp.where(in_head(lane, h), found[h * count : (h + 1) * count], summed)
    for at, ref in enumerate((o0, o1, o2, o3)):
        ref[:, :share] = summed[at * rows : (at + 1) * rows]
        ref[:, share:LANES] = jnp.zeros((rows, LANES - share), jnp.float32)
        ref[:, LANES:] = stats[at * rows : (at + 1) * rows]


def prompt_attention(asked, near_pages, far_pages):
    rows = asked[0].shape[0]
    return kernel_call(
        prompt_kernel,
        1,
        "prompt_attention",
        [jax.ShapeDtypeStruct((rows, LANES + 128), jnp.float32)] * 4,
        [VMEM] * 6,
        [],
        (*asked, near_pages, far_pages),
    )


def combine_kernel(ids, summed, highest, total, r0, r1, r2, r3, update, out_w, s0, s1, s2, s3):
    rows, share = summed.shape
    heads = share // HD
    refs = (r0, r1, r2, r3)
    prompt_summed = sum(ref[:, :share] for ref in refs)
    stats = [ref[:, LANES:] for ref in refs]
    top = jnp.maximum(jnp.maximum(stats[0], stats[1]), jnp.maximum(stats[2], stats[3]))
    added = stats[0] + stats[1] + stats[2] + stats[3]
    lane = lanes_of((rows, share))
    prompt_highest = jnp.zeros((rows, share), jnp.float32)
    prompt_total = jnp.zeros((rows, share), jnp.float32)
    for h in range(heads):
        here = in_head(lane, h)
        prompt_highest = jnp.where(here, top[:, h : h + 1], prompt_highest)
        prompt_total = jnp.where(here, added[:, heads + h : heads + h + 1], prompt_total)
    peak = jnp.maximum(highest[...], prompt_highest)
    own_factor = jnp.exp(highest[...] - peak)
    prompt_factor = jnp.exp(prompt_highest - peak)
    whole = total[...] * own_factor + prompt_total * prompt_factor
    attended = (summed[...] * own_factor + prompt_summed * prompt_factor) / whole
    second = jnp.dot(attended.astype(jnp.bfloat16), out_w[0], preferred_element_type=jnp.float32)
    write_slabs(ids, second, (s0, s1, s2, s3))


def write_slabs(ids, rows_whole, refs):
    heads = len(refs)
    share = refs[0].shape[1]
    for steps, ref in enumerate(refs):
        slab = rows_whole[:, :share]
        for h in range(1, heads):
            there = rows_whole[:, h * share : (h + 1) * share]
            slab = jnp.where(((ids[2] + steps) & (heads - 1)) == h, there, slab)
        ref[...] = slab.astype(jnp.bfloat16)


def own_slabs(ids, *refs):
    write_slabs(ids, refs[7][...].astype(jnp.float32), refs[9:])


def combine(own, parts, update, out_w):
    return kernel_call(
        combine_kernel,
        1,
        "combine",
        [jax.ShapeDtypeStruct(own[0].shape, jnp.bfloat16)] * 4,
        [VMEM] * 9,
        [],
        (*own, *parts, update, out_w),
        elsewhere=own_slabs,
    )


LINEAR_NEAR = (
    "gain",
    "feature_w",
    "state",
    "lin_norm",
    "conv_w",
    "conv_state",
    "value_w",
)
WINDOW_NEAR = ("gain", "value_w", "query_key_w")


def bring_near(arrays):
    names = list(arrays)
    count = len(names)
    first = [at for at, name in enumerate(names) if name in LINEAR_NEAR]
    second = [at for at, name in enumerate(names) if name in WINDOW_NEAR]

    def copy_some(chosen, refs):
        sems = refs[-1]
        copies = [
            pltpu.make_async_copy(refs[at], refs[count + at], sems.at[at]) for at in chosen
        ]
        for copy in copies:
            copy.start()
        for copy in copies:
            copy.wait()

    near = kernel_call(
        lambda ids, *refs: copy_some(first, refs),
        0,
        "bring_near",
        [jax.ShapeDtypeStruct(array.shape, array.dtype) for array in arrays.values()],
        [HBM] * count,
        [pltpu.SemaphoreType.DMA((count,))],
        tuple(arrays.values()),
        4 << 20,
        bytes_only(arrays.values()),
        lambda ids, *refs: copy_some(second, refs),
    )
    return dict(zip(names, near))


def bytes_only(arrays):
    moved = sum(array.size * array.dtype.itemsize for array in arrays)
    return pl.CostEstimate(flops=0, bytes_accessed=2 * moved, transcendentals=0)


def window_kernel(
    ids, table, lengths, own_hbm, own_near, tags, sems
):
    rows = tags.shape[0]
    total = own_hbm.shape[0]
    copies = []
    spans = []
    for r in range(rows):
        first, last = window_pages(lengths, r)
        spans.append(first != last)
        for slot, logical in enumerate((first, last)):
            page = jnp.clip(table[r, logical] - GROUPS - ids[1] * total, 0, total - 1)
            copies.append(
                pltpu.make_async_copy(own_hbm.at[page], own_near.at[r, slot], sems.at[r, slot])
            )
        copies[2 * r].start()
        pl.when(spans[r])(copies[2 * r + 1].start)

        @pl.when(jnp.logical_not(spans[r]))
        def _():
            own_near[r, 1] = jnp.zeros(own_near.shape[2:], own_near.dtype)

    row = lax.broadcasted_iota(jnp.int32, tags.shape, 0)
    lane = lanes_of(tags.shape)
    marks = jnp.zeros(tags.shape, jnp.int32)
    for r in range(rows):
        length = lengths[r]
        first, last = window_pages(lengths, r)
        second = jnp.where(first != last, last - 1, -MAXP) * PAGE
        start = jnp.minimum(length - WINDOW, PAGE)
        for at, mark in enumerate((table[r, 0], start, length, first * PAGE, second)):
            marks = jnp.where((row == r) & (lane == at), mark, marks)
    tags[...] = marks.astype(jnp.float32)
    for r in range(rows):
        copies[2 * r].wait()
        pl.when(spans[r])(copies[2 * r + 1].wait)


def bring_windows(table, lengths, own_pages):
    rows = lengths.shape[0]
    windows = jax.ShapeDtypeStruct((rows, 2) + own_pages.shape[1:], own_pages.dtype)
    return kernel_call(
        window_kernel,
        1,
        "bring_windows",
        [
            windows,
            jax.ShapeDtypeStruct((rows, 128), jnp.float32),
        ],
        [SMEM] * 2 + [HBM],
        [pltpu.SemaphoreType.DMA((rows, 2))],
        (table, lengths, own_pages),
        1 << 20,
        bytes_only([windows]),
    )


def page_kernel(ids, pages_hbm, page, pages, sem):
    copy = pltpu.make_async_copy(pages_hbm.at[0], pages, sem)
    copy.start()
    copy.wait()
    lane = lanes_of(page.shape)
    keys = pltpu.roll(pages[0].astype(jnp.float32), HALF, 1)
    page[...] = jnp.where(lane < HALF, keys, pages[1].astype(jnp.float32)).astype(jnp.bfloat16)


def window_page(prompt_pages):
    shape = prompt_pages.shape[1:]
    return kernel_call(
        page_kernel,
        1,
        "window_page",
        jax.ShapeDtypeStruct(shape[1:], jnp.bfloat16),
        [HBM],
        [pltpu.VMEM(shape, jnp.bfloat16), pltpu.SemaphoreType.DMA],
        (prompt_pages,),
        cost=pl.CostEstimate(flops=0, bytes_accessed=16 << 20, transcendentals=0),
    )


def body(
    tokens,
    norm_gain,
    feature_w,
    query_key_w,
    value_w,
    out_w,
    conv_w,
    conv_state,
    lin_state,
    lin_norm,
    own_pages,
    prompt_pages,
    page_table,
    lengths,
):
    pages_first = prompt_pages.transpose(0, 1, 3, 2)
    value_w = value_w.transpose(0, 2, 1)
    stored = {
        "gain": norm_gain,
        "feature_w": feature_w,
        "state": lin_state.transpose(0, 2, 1, 3).reshape(-1, HD),
        "lin_norm": lin_norm,
        "conv_w": conv_w,
        "conv_state": conv_state,
        "value_w": value_w[0],
        "query_key_w": query_key_w,
    }

    page = window_page(pages_first)
    row_pages = [x_shift(page, k) for k in (1, 3, 2)]
    row_pages[0], last_tokens, stored = lax.optimization_barrier((row_pages[0], tokens, stored))
    received = [head_shift(last_tokens, 1), head_shift(tokens, 3), head_shift(tokens, 2)]
    near, received, row_pages = lax.optimization_barrier((bring_near(stored), received, row_pages))
    near_pages = jnp.stack([row_pages[0], page, row_pages[1], row_pages[2]])
    near_pages, received = lax.optimization_barrier((near_pages, received))
    far_pages = far_swap(near_pages)
    update = linear_layer([tokens] + received, near, out_w)
    own_pages = own_pages.transpose(0, 1, 3, 2)
    own_pages, table, ends, update = lax.optimization_barrier(
        (own_pages, page_table, lengths, update)
    )
    near["own_pages"], tags = bring_windows(table, ends, own_pages)
    swapped = [section_swap(update, k) for k in (2, 1, 3, 0)]
    one_share, packed, key_new, value_new = project(tags, swapped, near)
    asked = [packed] + [z_shift(packed, k) for k in (2, 1, 7)]
    own = own_attention(tags, packed, key_new, value_new, near)
    asked, own = lax.optimization_barrier((asked, own))
    answers = prompt_attention(asked, near_pages, far_pages)
    parts = [answers[0]] + [z_shift(answers[at], -k) for at, k in ((1, 2), (2, 1), (3, 7))]
    slabs = combine(own, parts, update, out_w)
    here = lax.axis_index("section") == 1
    total = jnp.where(here, one_share.astype(jnp.float32), 0.0) + slabs[0].astype(jnp.float32)
    for piece in [head_shift(slabs[k], k) for k in (2, 1, 3)]:
        total = total + piece.astype(jnp.float32)
    return total.astype(jnp.bfloat16)[None]


def solution(mesh):
    placed = (
        P("req", "head"),
        P("section", None),
        P(None, "head"),
        P(None, "head"),
        P("section", None, "head"),
        P("section", "head", None),
        P(None, "head"),
        P("req", None, "head"),
        P("req", "head", None, None),
        P("req", "head", None),
        P("req", None, None, "head"),
        P("req", None, None, "head"),
        P("req", None),
        P("req"),
    )
    return jax.shard_map(
        body, mesh=mesh, in_specs=placed, out_specs=P("section", "req", "head"), check_vma=False
    )
```

```python
import jax
import jax.numpy as jnp
from jax import lax
from jax.experimental import pallas as pl
from jax.experimental.pallas import tpu as pltpu
from jax.sharding import PartitionSpec as P

HD = 112
FEAT = 16
WINDOW = 64
PAGE = 128
HALF = 64
MAXP = 256
GROUPS = 32
XN = 4
ZN = 8
LANES = 512
TAYLOR = 273
TAYLOR_LANES = 384
SPREAD = 1152

EPSILON = 1e-06
MASKED = -1e30


def head_shift(value, steps):
    count = lax.axis_size("head")
    return lax.ppermute(value, "head", [(i, (i + steps) % count) for i in range(count)])


def z_shift(value, steps):
    return lax.ppermute(
        value,
        "req",
        [(z * XN + i, (z + steps) % ZN * XN + i) for z in range(ZN) for i in range(XN)],
    )


def x_shift(value, steps):
    return lax.ppermute(
        value,
        "req",
        [(z * XN + i, z * XN + (i + steps) % XN) for z in range(ZN) for i in range(XN)],
    )


def far_swap(value):
    count = XN * ZN
    return lax.ppermute(
        value,
        ("section", "req"),
        [(count + i, count + (i + count // 2) % count) for i in range(count)],
    )


def section_swap(value, steps):
    count = lax.axis_size("head")
    there = [(i, count + (i + steps) % count) for i in range(count)]
    return lax.ppermute(value, ("section", "head"), there + [(b, a) for a, b in there])


VMEM = pl.BlockSpec(memory_space=pltpu.VMEM)
SMEM = pl.BlockSpec(memory_space=pltpu.SMEM)
HBM = pl.BlockSpec(memory_space=pltpu.HBM)
FLAT = (((1,), (1,)), ((), ()))


def normed_rows(values, gain_row):
    factor = lax.rsqrt(jnp.mean(values * values, axis=-1, keepdims=True) + EPSILON)
    return (values * factor * gain_row).astype(jnp.bfloat16)


def lanes_of(shape):
    return lax.broadcasted_iota(jnp.int32, shape, len(shape) - 1)


def in_head(lane, h):
    return (lane >= h * HD) & (lane < (h + 1) * HD)


def place():
    return lax.axis_index("section"), lax.axis_index("req"), lax.axis_index("head")


def kernel_call(
    kernel,
    section,
    name,
    out_shape,
    in_specs,
    scratch_shapes,
    args,
    vmem=6 << 20,
    cost=None,
    elsewhere=None,
):
    def run(*refs):
        ids = place()

        @pl.when(ids[0] == section)
        def _():
            kernel(ids, *refs)

        if elsewhere is not None:

            @pl.when(ids[0] != section)
            def _():
                elsewhere(ids, *refs)

    args = [
        pltpu.with_memory_space_constraint(arg, pltpu.HBM) if spec is HBM else arg
        for arg, spec in zip(args, in_specs, strict=True)
    ]
    return pl.pallas_call(
        run,
        out_shape=out_shape,
        in_specs=in_specs,
        out_specs=jax.tree.map(lambda _: VMEM, out_shape),
        scratch_shapes=scratch_shapes,
        compiler_params=pltpu.CompilerParams(vmem_limit_bytes=vmem),
        cost_estimate=cost,
        name=name,
    )(*args)


def expansion(features, width, repeat):
    lane = lax.broadcasted_iota(jnp.int32, (features, 2 * width), 1)
    source = lax.broadcasted_iota(jnp.int32, (features, 2 * width), 0)
    left = lane < width
    at = jnp.where(left, lane, lane - width) >> (repeat.bit_length() - 1)
    linear = left & (at > 0) & (at <= FEAT) & (source == at - 1)
    pair = at - (FEAT + 1)
    wanted = jnp.where(left, pair >> 4, pair & (FEAT - 1))
    quad = (pair >= 0) & (pair < FEAT * FEAT) & (source == wanted)
    return jnp.where(linear | quad, 1.0, 0.0).astype(jnp.bfloat16)


def taylor_rows(left, right, feature):
    scale = FEAT ** (-0.25)
    left, right = left * scale, right * scale
    return jnp.where(
        feature == 0, 1.0, jnp.where(feature <= FEAT, left, left * right * 0.5**0.5)
    )


def linear_kernel(
    ids,
    t0,
    t1,
    t2,
    t3,
    gain,
    feature_w,
    state,
    lin_norm,
    conv_w,
    conv_state,
    value_w,
    out_hbm,
    update,
    out_w,
    sem,
):
    rows, share = t0.shape
    heads = share // HD
    span = TAYLOR * heads
    copy = pltpu.make_async_copy(out_hbm.at[0], out_w, sem)
    copy.start()
    by_state = expansion(128, SPREAD, heads)
    by_norm = expansion(128, TAYLOR_LANES, 1)
    expand = jnp.concatenate([by_state, by_norm], axis=1)

    own = ids[2]
    got = [ref[...].astype(jnp.float32) for ref in (t0, t1, t3, t2)]
    whole = []
    for place in range(heads):
        piece = got[0]
        for back in range(1, heads):
            piece = jnp.where(((own - back) & (heads - 1)) == place, got[back], piece)
        whole.append(piece)
    tokens = jnp.concatenate(whole, axis=1)
    normed = normed_rows(tokens, gain[...])
    feats = jnp.dot(normed, feature_w[...], preferred_element_type=jnp.float32)
    by_head = jnp.concatenate(
        [feats] + [pltpu.roll(feats, 128 - 2 * FEAT * h, 1) for h in range(1, heads)], axis=0
    )
    high = by_head.astype(jnp.bfloat16)
    rest = by_head - high.astype(jnp.float32)
    middle = rest.astype(jnp.bfloat16)
    low = (rest - middle.astype(jnp.float32)).astype(jnp.bfloat16)
    spread = jnp.dot(
        jnp.concatenate([high, middle, low], axis=0), expand, preferred_element_type=jnp.float32
    )
    count = heads * rows
    spread = spread[:count] + spread[count : 2 * count] + spread[2 * count :]
    lane = lanes_of((count, SPREAD))
    head = lax.broadcasted_iota(jnp.int32, (count, SPREAD), 0) >> 3
    query_wide = taylor_rows(spread[:, :SPREAD], spread[:, SPREAD : 2 * SPREAD], lane >> 2)
    query_wide = jnp.where(((lane & (heads - 1)) == head) & (lane < span), query_wide, 0.0)
    query_feats = taylor_rows(
        spread[:, 2 * SPREAD : 2 * SPREAD + TAYLOR_LANES],
        spread[:, 2 * SPREAD + TAYLOR_LANES :],
        lanes_of((count, TAYLOR_LANES)),
    )[:, :TAYLOR]
    both = by_head * pltpu.roll(by_head, 128 - FEAT, 1)
    near = jnp.sum(
        jnp.where(lanes_of(both.shape) < FEAT, both, 0.0), axis=-1, keepdims=True
    ) * FEAT ** (-0.5)
    intersection = 1.0 + near + 0.5 * near * near

    length = span + 12
    queries = []
    for shift in range(0, 16, 4):
        moved = query_wide if shift == 0 else pltpu.roll(query_wide, shift, 1)
        queries.append(moved[:, :length].astype(jnp.bfloat16))
    row = lax.broadcasted_iota(jnp.int32, (count, HD), 0) & (rows - 1)
    found = jnp.zeros((count, HD), jnp.float32)
    for r in range(rows):
        first = span * r
        shift = first % 16
        product = jnp.dot(
            queries[shift // 4],
            state[first - shift : first - shift + length, :],
            preferred_element_type=jnp.float32,
        )
        found = jnp.where(row == r, product, found)
    fresh = lax.dot_general(normed, value_w[...], FLAT, preferred_element_type=jnp.float32)
    older = conv_state[...].astype(jnp.float32)
    mixed = conv_w[0:1] * older[:, 0] + conv_w[1:2] * older[:, 1] + conv_w[2:3] * fresh
    total = tokens * 0.25
    copy.wait()
    for h in range(heads):
        here = slice(h * rows, (h + 1) * rows)
        denominator = (
            jnp.sum(query_feats[here] * lin_norm[:, h, :], axis=-1, keepdims=True)
            + intersection[here]
        )
        attended = (
            (found[here] + intersection[here] * mixed[:, h * HD : (h + 1) * HD]) / denominator
        ).astype(jnp.bfloat16)
        total = total + jnp.dot(
            attended, out_w[h * HD : (h + 1) * HD, :], preferred_element_type=jnp.float32
        )
    update[...] = total.astype(jnp.bfloat16)


def linear_layer(pieces, near, out_w):
    return kernel_call(
        linear_kernel,
        0,
        "linear_layer",
        jax.ShapeDtypeStruct((pieces[0].shape[0], out_w.shape[2]), jnp.bfloat16),
        [VMEM] * 11 + [HBM],
        [pltpu.VMEM(out_w.shape[1:], jnp.bfloat16), pltpu.SemaphoreType.DMA],
        (*pieces, *(near[name] for name in LINEAR_NEAR), out_w),
    )


def project_kernel(
    ids,
    tags,
    p0,
    p1,
    p2,
    p3,
    gain,
    qk_w,
    v_w,
    one,
    asked,
    key_new,
    value_new,
):
    rows, share = one.shape
    heads = share // HD
    layer_one = sum(ref[...].astype(jnp.float32) for ref in (p0, p1, p2, p3)).astype(jnp.bfloat16)
    rounded = layer_one.astype(jnp.float32)
    mine = rounded[:, :share]
    for h in range(1, heads):
        mine = jnp.where(ids[2] == h, rounded[:, h * share : (h + 1) * share], mine)
    one[...] = mine.astype(jnp.bfloat16)
    normed = normed_rows(rounded, gain[...])
    query_key = jnp.dot(normed, qk_w[...], preferred_element_type=jnp.float32)
    width = query_key.shape[1]
    lane = lanes_of((rows, LANES))
    query = jnp.where(in_head(lane, 0), query_key[:, :LANES], 0.0)
    key = query
    for h in range(heads):
        if h:
            moved = pltpu.roll(query_key, width - h * HD, 1)[:, :LANES]
            query = jnp.where(in_head(lane, h), moved, query)
        moved = pltpu.roll(query_key, width - (h + 1) * HD, 1)[:, :LANES]
        key = jnp.where(in_head(lane, h), moved, key)
    query = jnp.where(lane == share, tags[:, 0:1], query)
    query = jnp.where(lane == share + 1, tags[:, 1:2], query)
    asked[...] = query.astype(jnp.bfloat16)
    key_new[...] = key[:, :share].astype(jnp.bfloat16)
    value_new[...] = lax.dot_general(
        normed, v_w[...], FLAT, preferred_element_type=jnp.float32
    ).astype(jnp.bfloat16)


def project(tags, pieces, near):
    rows = pieces[0].shape[0]
    share = near["value_w"].shape[0]
    return kernel_call(
        project_kernel,
        1,
        "project",
        [
            jax.ShapeDtypeStruct((rows, share), jnp.bfloat16),
            jax.ShapeDtypeStruct((rows, LANES), jnp.bfloat16),
            jax.ShapeDtypeStruct((rows, share), jnp.bfloat16),
            jax.ShapeDtypeStruct((rows, share), jnp.bfloat16),
        ],
        [VMEM] * 8,
        [],
        (tags, *pieces, near["gain"], near["query_key_w"], near["value_w"]),
    )


def window_pages(lengths, r):
    length = lengths[r]
    return jnp.maximum((length - WINDOW) // PAGE, 1), jnp.maximum((length - 2) // PAGE, 1)


def own_kernel(
    ids, tags, asked, key_new, value_new, pages, summed_out, highest_out, total_out
):
    rows, share = key_new.shape
    head = lax.broadcasted_iota(jnp.int32, (8, share), 0)
    lane = lanes_of((8, share))
    mine = (lane >= head * HD) & (lane < (head + 1) * HD)
    scale = HD ** (-0.5)
    query = asked[:, :share].astype(jnp.float32)
    new_key = key_new[...].astype(jnp.float32)
    new_value = value_new[...].astype(jnp.float32)
    wide = jnp.concatenate([jnp.where(mine, query[r : r + 1], 0.0) for r in range(rows)], axis=0)
    keys = jnp.concatenate(
        [jnp.broadcast_to(new_key[r : r + 1], (8, share)) for r in range(rows)], axis=0
    )
    new_score = jnp.sum(wide * keys, axis=-1, keepdims=True) * scale
    token = lanes_of((8 * rows, 2 * PAGE))

    def by_request(at):
        return jnp.concatenate(
            [jnp.broadcast_to(tags[r : r + 1, at : at + 1], (8, 2 * PAGE)) for r in range(rows)],
            axis=0,
        )

    length = by_request(2)
    position = token.astype(jnp.float32) + jnp.where(token < PAGE, by_request(3), by_request(4))
    usable = (position >= length - WINDOW) & (position <= length - 2)
    scores = []
    for r in range(rows):
        low = wide[8 * r : 8 * r + 8].astype(jnp.bfloat16)
        scores.append(
            jnp.concatenate(
                [
                    jnp.dot(low, pages[r, slot, 0], preferred_element_type=jnp.float32)
                    for slot in range(2)
                ],
                axis=1,
            )
        )
    scores = jnp.where(usable, jnp.concatenate(scores, axis=0) * scale, MASKED)
    highest = jnp.maximum(jnp.max(scores, axis=-1, keepdims=True), new_score)
    exps = jnp.where(usable, jnp.exp(scores - highest), 0.0)
    exp_new = jnp.exp(new_score - highest)
    total = jnp.sum(exps, axis=-1, keepdims=True) + exp_new
    for r in range(rows):
        here = slice(8 * r, 8 * r + 8)
        low = exps[here].astype(jnp.bfloat16)
        found = exp_new[here] * new_value[r : r + 1]
        for slot in range(2):
            found = found + lax.dot_general(
                low[:, slot * PAGE : (slot + 1) * PAGE],
                pages[r, slot, 1],
                FLAT,
                preferred_element_type=jnp.float32,
            )
        for ref, value in (
            (summed_out, found),
            (highest_out, highest[here]),
            (total_out, total[here]),
        ):
            ref[r : r + 1, :] = jnp.sum(jnp.where(mine, value, 0.0), axis=0, keepdims=True)


def own_attention(tags, asked, key_new, value_new, near):
    rows, share = key_new.shape
    return kernel_call(
        own_kernel,
        1,
        "own_attention",
        [jax.ShapeDtypeStruct((rows, share), jnp.float32)] * 3,
        [VMEM] * 5,
        [],
        (tags, asked, key_new, value_new, near["own_pages"]),
    )


def prompt_kernel(ids, a0, a1, a2, a3, near_pages, far_pages, o0, o1, o2, o3):
    rows = a0.shape[0]
    share = near_pages.shape[1]
    heads = share // HD
    pages = jnp.concatenate(
        [near_pages[i] for i in range(XN)] + [far_pages[i] for i in range(XN)], axis=1
    )
    asked = jnp.concatenate([ref[...].astype(jnp.float32) for ref in (a0, a1, a2, a3)], axis=0)
    count = asked.shape[0]
    lane = lanes_of(asked.shape)
    group = jnp.sum(jnp.where(lane == share, asked, 0.0), axis=-1, keepdims=True)
    start = jnp.sum(jnp.where(lane == share + 1, asked, 0.0), axis=-1, keepdims=True)
    group, start = group.astype(jnp.int32), start.astype(jnp.int32)
    query = jnp.concatenate(
        [jnp.where(in_head(lane, h), asked, 0.0)[:, :share] for h in range(heads)], axis=0
    ).astype(jnp.bfloat16)
    scores = jnp.dot(query, pages, preferred_element_type=jnp.float32) * HD ** (-0.5)
    token = lanes_of((count, 2 * XN * PAGE))
    z, x = ids[1] // XN, ids[1] % XN
    slot = token >> 7
    slot_group = jnp.where(slot < XN, z, (z + ZN // 2) & (ZN - 1)) * XN
    slot_group = slot_group + ((slot + x + XN - 1) & (XN - 1))
    offset = token & (PAGE - 1)
    usable = (slot_group == group) & (offset < HALF) & (offset + HALF >= start)
    lane = lanes_of((count, share))
    stat_lane = lanes_of((count, 128))
    weights = []
    stats = jnp.zeros((count, 128), jnp.float32)
    for h in range(heads):
        here = jnp.where(usable, scores[h * count : (h + 1) * count], MASKED)
        highest = jnp.max(here, axis=-1, keepdims=True)
        exps = jnp.where(usable, jnp.exp(here - highest), 0.0)
        total = jnp.sum(exps, axis=-1, keepdims=True)
        stats = jnp.where(stat_lane == h, highest, stats)
        stats = jnp.where(stat_lane == heads + h, total, stats)
        weights.append(pltpu.roll(exps, HALF, 1))
    found = lax.dot_general(
        jnp.concatenate(weights, axis=0).astype(jnp.bfloat16),
        pages,
        FLAT,
        preferred_element_type=jnp.float32,
    )
    summed = jnp.zeros((count, share), jnp.float32)
    for h in range(heads):
        summed = jnp.where(in_head(lane, h), found[h * count : (h + 1) * count], summed)
    for at, ref in enumerate((o0, o1, o2, o3)):
        ref[:, :share] = summed[at * rows : (at + 1) * rows]
        ref[:, share:LANES] = jnp.zeros((rows, LANES - share), jnp.float32)
        ref[:, LANES:] = stats[at * rows : (at + 1) * rows]


def prompt_attention(asked, near_pages, far_pages):
    rows = asked[0].shape[0]
    return kernel_call(
        prompt_kernel,
        1,
        "prompt_attention",
        [jax.ShapeDtypeStruct((rows, LANES + 128), jnp.float32)] * 4,
        [VMEM] * 6,
        [],
        (*asked, near_pages, far_pages),
    )


def combine_kernel(ids, summed, highest, total, r0, r1, r2, r3, update, out_w, s0, s1, s2, s3):
    rows, share = summed.shape
    heads = share // HD
    refs = (r0, r1, r2, r3)
    prompt_summed = sum(ref[:, :share] for ref in refs)
    stats = [ref[:, LANES:] for ref in refs]
    top = jnp.maximum(jnp.maximum(stats[0], stats[1]), jnp.maximum(stats[2], stats[3]))
    added = stats[0] + stats[1] + stats[2] + stats[3]
    lane = lanes_of((rows, share))
    prompt_highest = jnp.zeros((rows, share), jnp.float32)
    prompt_total = jnp.zeros((rows, share), jnp.float32)
    for h in range(heads):
        here = in_head(lane, h)
        prompt_highest = jnp.where(here, top[:, h : h + 1], prompt_highest)
        prompt_total = jnp.where(here, added[:, heads + h : heads + h + 1], prompt_total)
    peak = jnp.maximum(highest[...], prompt_highest)
    own_factor = jnp.exp(highest[...] - peak)
    prompt_factor = jnp.exp(prompt_highest - peak)
    whole = total[...] * own_factor + prompt_total * prompt_factor
    attended = (summed[...] * own_factor + prompt_summed * prompt_factor) / whole
    second = jnp.dot(attended.astype(jnp.bfloat16), out_w[0], preferred_element_type=jnp.float32)
    write_slabs(ids, second, (s0, s1, s2, s3))


def write_slabs(ids, rows_whole, refs):
    heads = len(refs)
    share = refs[0].shape[1]
    for steps, ref in enumerate(refs):
        slab = rows_whole[:, :share]
        for h in range(1, heads):
            there = rows_whole[:, h * share : (h + 1) * share]
            slab = jnp.where(((ids[2] + steps) & (heads - 1)) == h, there, slab)
        ref[...] = slab.astype(jnp.bfloat16)


def own_slabs(ids, *refs):
    write_slabs(ids, refs[7][...].astype(jnp.float32), refs[9:])


def combine(own, parts, update, out_w):
    return kernel_call(
        combine_kernel,
        1,
        "combine",
        [jax.ShapeDtypeStruct(own[0].shape, jnp.bfloat16)] * 4,
        [VMEM] * 9,
        [],
        (*own, *parts, update, out_w),
        elsewhere=own_slabs,
    )


LINEAR_NEAR = (
    "gain",
    "feature_w",
    "state",
    "lin_norm",
    "conv_w",
    "conv_state",
    "value_w",
)
WINDOW_NEAR = ("gain", "value_w", "query_key_w")


def bring_near(arrays):
    names = list(arrays)
    count = len(names)
    first = [at for at, name in enumerate(names) if name in LINEAR_NEAR]
    second = [at for at, name in enumerate(names) if name in WINDOW_NEAR]

    def copy_some(chosen, refs):
        sems = refs[-1]
        copies = [
            pltpu.make_async_copy(refs[at], refs[count + at], sems.at[at]) for at in chosen
        ]
        for copy in copies:
            copy.start()
        for copy in copies:
            copy.wait()

    near = kernel_call(
        lambda ids, *refs: copy_some(first, refs),
        0,
        "bring_near",
        [jax.ShapeDtypeStruct(array.shape, array.dtype) for array in arrays.values()],
        [HBM] * count,
        [pltpu.SemaphoreType.DMA((count,))],
        tuple(arrays.values()),
        4 << 20,
        bytes_only(arrays.values()),
        lambda ids, *refs: copy_some(second, refs),
    )
    return dict(zip(names, near))


def bytes_only(arrays):
    moved = sum(array.size * array.dtype.itemsize for array in arrays)
    return pl.CostEstimate(flops=0, bytes_accessed=2 * moved, transcendentals=0)


def window_kernel(
    ids, table, lengths, own_hbm, own_near, tags, sems
):
    rows = tags.shape[0]
    total = own_hbm.shape[0]
    copies = []
    spans = []
    for r in range(rows):
        first, last = window_pages(lengths, r)
        spans.append(first != last)
        for slot, logical in enumerate((first, last)):
            page = jnp.clip(table[r, logical] - GROUPS - ids[1] * total, 0, total - 1)
            copies.append(
                pltpu.make_async_copy(own_hbm.at[page], own_near.at[r, slot], sems.at[r, slot])
            )
        copies[2 * r].start()
        pl.when(spans[r])(copies[2 * r + 1].start)

        @pl.when(jnp.logical_not(spans[r]))
        def _():
            own_near[r, 1] = jnp.zeros(own_near.shape[2:], own_near.dtype)

    row = lax.broadcasted_iota(jnp.int32, tags.shape, 0)
    lane = lanes_of(tags.shape)
    marks = jnp.zeros(tags.shape, jnp.int32)
    for r in range(rows):
        length = lengths[r]
        first, last = window_pages(lengths, r)
        second = jnp.where(first != last, last - 1, -MAXP) * PAGE
        start = jnp.minimum(length - WINDOW, PAGE)
        for at, mark in enumerate((table[r, 0], start, length, first * PAGE, second)):
            marks = jnp.where((row == r) & (lane == at), mark, marks)
    tags[...] = marks.astype(jnp.float32)
    for r in range(rows):
        copies[2 * r].wait()
        pl.when(spans[r])(copies[2 * r + 1].wait)


def bring_windows(table, lengths, own_pages):
    rows = lengths.shape[0]
    windows = jax.ShapeDtypeStruct((rows, 2) + own_pages.shape[1:], own_pages.dtype)
    return kernel_call(
        window_kernel,
        1,
        "bring_windows",
        [
            windows,
            jax.ShapeDtypeStruct((rows, 128), jnp.float32),
        ],
        [SMEM] * 2 + [HBM],
        [pltpu.SemaphoreType.DMA((rows, 2))],
        (table, lengths, own_pages),
        1 << 20,
        bytes_only([windows]),
    )


def page_kernel(ids, pages_hbm, page, pages, sem):
    copy = pltpu.make_async_copy(pages_hbm.at[0], pages, sem)
    copy.start()
    copy.wait()
    lane = lanes_of(page.shape)
    keys = pltpu.roll(pages[0].astype(jnp.float32), HALF, 1)
    page[...] = jnp.where(lane < HALF, keys, pages[1].astype(jnp.float32)).astype(jnp.bfloat16)


def window_page(prompt_pages):
    shape = prompt_pages.shape[1:]
    return kernel_call(
        page_kernel,
        1,
        "window_page",
        jax.ShapeDtypeStruct(shape[1:], jnp.bfloat16),
        [HBM],
        [pltpu.VMEM(shape, jnp.bfloat16), pltpu.SemaphoreType.DMA],
        (prompt_pages,),
        cost=pl.CostEstimate(flops=0, bytes_accessed=16 << 20, transcendentals=0),
    )


def body(
    tokens,
    norm_gain,
    feature_w,
    query_key_w,
    value_w,
    out_w,
    conv_w,
    conv_state,
    lin_state,
    lin_norm,
    own_pages,
    prompt_pages,
    page_table,
    lengths,
):
    pages_first = prompt_pages.transpose(0, 1, 3, 2)
    value_w = value_w.transpose(0, 2, 1)
    stored = {
        "gain": norm_gain,
        "feature_w": feature_w,
        "state": lin_state.transpose(0, 2, 1, 3).reshape(-1, HD),
        "lin_norm": lin_norm,
        "conv_w": conv_w,
        "conv_state": conv_state,
        "value_w": value_w[0],
        "query_key_w": query_key_w,
    }

    page = window_page(pages_first)
    far_first = [x_shift(page, k) for k in (2, 1, 3)]
    row_pages = [far_first[1], far_first[2], far_first[0]]
    row_pages[0], last_tokens, stored = lax.optimization_barrier((row_pages[0], tokens, stored))
    received = [head_shift(last_tokens, 1), head_shift(tokens, 3), head_shift(tokens, 2)]
    near, received, row_pages = lax.optimization_barrier((bring_near(stored), received, row_pages))
    near_pages = jnp.stack([row_pages[0], page, row_pages[1], row_pages[2]])
    near_pages, received = lax.optimization_barrier((near_pages, received))
    far_pages = far_swap(near_pages)
    update = linear_layer([tokens] + received, near, out_w)
    own_pages = own_pages.transpose(0, 1, 3, 2)
    own_pages, table, ends, update = lax.optimization_barrier(
        (own_pages, page_table, lengths, update)
    )
    near["own_pages"], tags = bring_windows(table, ends, own_pages)
    swapped = [section_swap(update, k) for k in (2, 1, 3, 0)]
    one_share, packed, key_new, value_new = project(tags, swapped, near)
    asked = [packed] + [z_shift(packed, k) for k in (2, 1, 7)]
    own = own_attention(tags, packed, key_new, value_new, near)
    asked, own = lax.optimization_barrier((asked, own))
    answers = prompt_attention(asked, near_pages, far_pages)
    parts = [answers[0]] + [z_shift(answers[at], -k) for at, k in ((1, 2), (2, 1), (3, 7))]
    slabs = combine(own, parts, update, out_w)
    here = lax.axis_index("section") == 1
    total = jnp.where(here, one_share.astype(jnp.float32), 0.0) + slabs[0].astype(jnp.float32)
    for piece in [head_shift(slabs[k], k) for k in (2, 1, 3)]:
        total = total + piece.astype(jnp.float32)
    return total.astype(jnp.bfloat16)[None]


def solution(mesh):
    placed = (
        P("req", "head"),
        P("section", None),
        P(None, "head"),
        P(None, "head"),
        P("section", None, "head"),
        P("section", "head", None),
        P(None, "head"),
        P("req", None, "head"),
        P("req", "head", None, None),
        P("req", "head", None),
        P("req", None, None, "head"),
        P("req", None, None, "head"),
        P("req", None),
        P("req"),
    )
    return jax.shard_map(
        body, mesh=mesh, in_specs=placed, out_specs=P("section", "req", "head"), check_vma=False
    )
```
